32 devices in a mesh: ctx: 4 (over x, core), fsdp: 8 (over z, y).
Axes of the slice: x: 2, y: 2, z: 4, core: 2. Of those that a mesh axis runs over, the one named last changes fastest.
Arguments:
- tokens: bfloat16 [2, 8, 1024, 1024], P(None, 'fsdp', 'ctx'), may hold values from -8 to 8
- cotangent: bfloat16 [2, 8, 1024, 1024], P(None, 'fsdp', 'ctx'), may hold values from -6 to 6
- random_blocks: int32 [2, 8, 16, 16, 3], P(None, 'fsdp', None, 'ctx'), may hold values from 0 to 15
- global_blocks: int32 [2, 8, 2], P(None, 'fsdp'), may hold values from 0 to 15, as said below
- attend_gain: bfloat16 [1024], P('fsdp'), may hold values from 0.099609375 to 1.8984375
- attend_bias: bfloat16 [1024], P('fsdp'), may hold values from -1.75 to 1.75
- triple_weight: bfloat16 [1024, 3072], P('fsdp'), may hold values from -0.1875 to 0.1875
- output_weight: bfloat16 [1024, 1024], P('fsdp'), may hold values from -1.5 to 1.5
- hidden_gain: bfloat16 [1024], P('fsdp'), may hold values from 0.099609375 to 1.8984375
- hidden_bias: bfloat16 [1024], P('fsdp'), may hold values from -1.75 to 1.75
- expand_weight: bfloat16 [1024, 4096], P('fsdp'), may hold values from -0.1875 to 0.1875
- expand_bias: bfloat16 [4096], P('fsdp'), may hold values from -3 to 3
- shrink_weight: bfloat16 [4096, 1024], P('fsdp'), may hold values from -0.09375 to 0.09375
- shrink_bias: bfloat16 [1024], P('fsdp'), may hold values from -1.75 to 1.75
Outputs:
- result: bfloat16 [2, 8, 1024, 1024], P(None, 'fsdp', 'ctx')
- token_grad: bfloat16 [2, 8, 1024, 1024], P(None, 'fsdp', 'ctx')
- attend_gain_grad: float32 [1024], P('fsdp')
- attend_bias_grad: float32 [1024], P('fsdp')
- triple_weight_grad: float32 [1024, 3072], P('fsdp')
- output_weight_grad: float32 [1024, 1024], P('fsdp')
- hidden_gain_grad: float32 [1024], P('fsdp')
- hidden_bias_grad: float32 [1024], P('fsdp')
- expand_weight_grad: float32 [1024, 4096], P('fsdp')
- expand_bias_grad: float32 [4096], P('fsdp')
- shrink_weight_grad: float32 [4096, 1024], P('fsdp')
- shrink_bias_grad: float32 [1024], P('fsdp')
The draws below stay inside these ranges and needn't reach their ends.
Inputs may be any that keep to these rules, and one draw needn't show every extreme that they name: `global_blocks`: the 2 global blocks of one sequence are different.
All inputs are finite; a program needn't handle non-finite values.
Results may differ from the reference program's by a relative error of at most 0.017.
Values may be sent and summed in bfloat16 or wider, within the bound.
A program may use at most 320 MiB of HBM per device.

```python
import jax
import jax.numpy as jnp
from jax import lax

D = 1024
HEADS = 16
HEAD_DIM = 64
FF = 4096
BLOCK = 64
RAND = 3
GLOBALS = 2
MICRO = 2
LENGTH = 1024
BLOCKS = 16
SEQS = 8


def draw_global_blocks(key, part):
    count = MICRO * SEQS
    ranking = jax.random.randint(key, (count, BLOCKS), 0, 1 << 16) * BLOCKS + jnp.arange(BLOCKS, dtype=jnp.int32)[None, :]
    order = jnp.argsort(ranking, axis=1)[:, :GLOBALS].astype(jnp.int32)
    pinned = jnp.where(jnp.arange(GLOBALS) == 0, 0, BLOCKS - 1).astype(jnp.int32)
    order = order.at[0].set(pinned)
    return order.reshape(MICRO, SEQS, GLOBALS)


def with_ends(array, key, low, largest):
    longest = array.shape.index(max(array.shape))
    spots = []
    for shift in (0, 1):
        where = [jax.random.randint(jax.random.fold_in(key, axis), (), 0, length) for axis, length in enumerate(array.shape)]
        where[longest] = (where[longest] + shift) % array.shape[longest]
        spots.append(tuple(where))
    return array.at[spots[0]].set(low).at[spots[1]].set(largest)


def with_spikes(result, own_key, source, target, shards_of, factor):
    def block_of(position):
        return (jnp.arange(result.shape[position]) // (result.shape[position] // shards_of)).reshape((-1,) + (1,) * (result.ndim - 1 - position))

    near = jax.random.permutation(own_key, shards_of)[block_of(target)]
    far = (block_of(target) + shards_of // 2) % shards_of
    return jnp.where((block_of(source) == near) | (block_of(source) == far), factor * result, result)


def steps_of(stream_key, dims, split, low, high):
    loudness, own = 1.0, jax.random.fold_in(stream_key, 6)
    for axis_at, blocks in split:
        draws = jnp.exp(jax.random.uniform(jax.random.fold_in(own, axis_at), (blocks,), jnp.float32, low / len(split), high / len(split)))
        loudness = loudness * jnp.repeat(draws, dims[axis_at] // blocks).reshape([-1 if axis == axis_at else 1 for axis in range(len(dims))])
    return loudness


def noise(key, extent, deviation, limit, shards=(), held_as=jnp.bfloat16):
    entries = deviation * jax.random.normal(key, extent, jnp.float32)
    if shards:
        entries = entries * steps_of(key, extent, shards, -0.22, 0.18)
    return jnp.clip(entries, -limit, limit).astype(held_as)


def noise_with(key, shape, width, reach, shards, heavy, kind=jnp.bfloat16):
    result = width * jax.random.normal(key, shape, jnp.float32)
    if shards:
        result = result * steps_of(key, shape, shards, -0.22, 0.18)
    return jnp.clip(with_spikes(result, jax.random.fold_in(key, 3), *heavy), -reach, reach).astype(kind)


def setup_inputs(seed: int = 0) -> dict:
    arg_keys = jax.random.split(jax.random.key(seed), 15)
    tokens = noise_with(arg_keys[0], (MICRO, SEQS, LENGTH, D), 1.0, 8.0, ((1, 8), (2, 4)), (1, 3, 8, 2.0))
    cotangent = noise(arg_keys[1], (MICRO, SEQS, LENGTH, D), 1.0, 6.0, ((1, 8), (2, 4)))
    random_blocks = with_ends(jax.random.randint(arg_keys[2], (MICRO, SEQS, HEADS, BLOCKS, RAND), 0, BLOCKS), jax.random.fold_in(arg_keys[2], 1), 0, BLOCKS - 1).astype(jnp.int32)
    global_blocks = draw_global_blocks(jax.random.fold_in(arg_keys[14], 71), 0)
    attend_gain = jnp.clip(1.0 + 0.18 * jax.random.normal(arg_keys[4], (D,), jnp.float32), 0.099609375, 1.8984375).astype(jnp.bfloat16)
    attend_bias = noise(arg_keys[5], (D,), 0.3, 1.75, ((0, 8),))
    triple_weight = noise(arg_keys[6], (D, 3 * D), D ** -0.5, 0.1875, ((0, 8),))
    output_weight = noise(arg_keys[7], (D, D), (max(D // 64, 1)) ** -0.5, 1.5, ((0, 8),))
    hidden_gain = jnp.clip(1.0 + 0.18 * jax.random.normal(arg_keys[8], (D,), jnp.float32), 0.099609375, 1.8984375).astype(jnp.bfloat16)
    hidden_bias = noise(arg_keys[9], (D,), 0.3, 1.75, ((0, 8),))
    expand_weight = noise(arg_keys[10], (D, FF), D ** -0.5, 0.1875, ((0, 8),))
    expand_bias = noise(arg_keys[11], (FF,), 0.5, 3.0, ((0, 8),))
    shrink_weight = noise(arg_keys[12], (FF, D), FF ** -0.5, 0.09375, ((0, 8),))
    shrink_bias = noise(arg_keys[13], (D,), 0.3, 1.75, ((0, 8),))
    return dict(tokens=tokens, cotangent=cotangent, random_blocks=random_blocks, global_blocks=global_blocks, attend_gain=attend_gain, attend_bias=attend_bias, triple_weight=triple_weight, output_weight=output_weight, hidden_gain=hidden_gain, hidden_bias=hidden_bias, expand_weight=expand_weight, expand_bias=expand_bias, shrink_weight=shrink_weight, shrink_bias=shrink_bias)


@jax.custom_vjp
def low(v):
    return lax.optimization_barrier(v.astype(jnp.bfloat16)).astype(jnp.float32)

@jax.custom_vjp
def low_back(v):
    return v

def low_keep(v):
    return (low(v), None)

def low_pass(kept, grad):
    return (grad,)

def back_keep(v):
    return (v, None)

def back_low(kept, grad):
    return (low(grad),)
low.defvjp(low_keep, low_pass)
low_back.defvjp(back_keep, back_low)
highest = lax.Precision.HIGHEST
epsilon = 1e-05

def layer_norm(values, scale_vector, shift_vector):
    average = lax.optimization_barrier(jnp.mean(values, axis=-1, keepdims=True))
    centered = values - average
    variance = lax.optimization_barrier(jnp.mean(centered * centered, axis=-1, keepdims=True))
    return centered * lax.rsqrt(variance + epsilon) * scale_vector + shift_vector

def allowed_blocks(chosen_blocks, global_list):
    block_ids = jnp.arange(BLOCKS, dtype=jnp.int32)
    nearby = jnp.abs(block_ids[:, None] - block_ids[None, :]) <= 1
    picked = jnp.any(chosen_blocks[:, :, :, None] == block_ids[None, None, None, :], axis=2)
    global_mark = jnp.any(global_list[:, None] == block_ids[None, :], axis=0)
    return nearby[None] | picked | global_mark[None, None, :] | global_mark[None, :, None]

def forward(inputs, params, chosen_blocks, global_list):
    attend_gain, attend_bias, triple_weight, output_weight, hidden_gain, hidden_bias, expand_weight, expand_bias, shrink_weight, shrink_bias = params
    length = inputs.shape[0]
    normed = low(layer_norm(inputs, attend_gain, attend_bias))
    triple = low_back(low(jnp.dot(normed, triple_weight, precision=highest)))
    queries = triple[:, :D].reshape(length, HEADS, HEAD_DIM)
    keys_all = triple[:, D:2 * D].reshape(length, HEADS, HEAD_DIM)
    values_all = triple[:, 2 * D:].reshape(length, HEADS, HEAD_DIM)
    scores = low_back(jnp.einsum('qhd,khd->hqk', queries, keys_all, precision=highest) * HEAD_DIM ** (-0.5))
    allowed = allowed_blocks(chosen_blocks, global_list)
    blocked = jnp.where(allowed[:, :, None, :, None], scores.reshape(HEADS, BLOCKS, BLOCK, BLOCKS, BLOCK), -1e+30)
    blocked = blocked.reshape(HEADS, length, length)
    row_peak = lax.optimization_barrier(jnp.max(blocked, axis=-1, keepdims=True))
    powered = jnp.exp(blocked - row_peak)
    probs = low(powered / lax.optimization_barrier(jnp.sum(powered, axis=-1, keepdims=True)))
    mixed = jnp.einsum('hqk,khd->qhd', probs, values_all, precision=highest).reshape(length, D)
    mixed = low_back(low(mixed))
    attended = inputs + low_back(jnp.dot(mixed, output_weight, precision=highest))
    hidden_normed = low(layer_norm(attended, hidden_gain, hidden_bias))
    before = low_back(jnp.dot(hidden_normed, expand_weight, precision=highest) + expand_bias)
    activated = low(jax.nn.gelu(before, approximate=True))
    return attended + low_back(jnp.dot(activated, shrink_weight, precision=highest) + shrink_bias)

def reference(tokens, cotangent, random_blocks, global_blocks, attend_gain, attend_bias, triple_weight, output_weight, hidden_gain, hidden_bias, expand_weight, expand_bias, shrink_weight, shrink_bias):
    params = tuple((item.astype(jnp.float32) for item in (attend_gain, attend_bias, triple_weight, output_weight, hidden_gain, hidden_bias, expand_weight, expand_bias, shrink_weight, shrink_bias)))
    count = MICRO * SEQS
    inputs_all = tokens.reshape(count, LENGTH, D)
    tangents_all = cotangent.reshape(count, LENGTH, D)
    chosen_all = random_blocks.reshape(count, HEADS, BLOCKS, RAND)
    globals_all = global_blocks.reshape(count, GLOBALS)

    def one_sequence(running, packed):
        inputs, tangent, chosen_blocks, global_list = packed

        def apply(inputs_f, params_f):
            return forward(inputs_f, params_f, chosen_blocks, global_list)
        output, pull = jax.vjp(apply, inputs.astype(jnp.float32), params)
        input_part, param_part = pull(tangent.astype(jnp.float32))
        running = tuple((old_value + new_value for old_value, new_value in zip(running, param_part)))
        return (running, (output.astype(jnp.bfloat16), input_part.astype(jnp.bfloat16)))
    start = tuple((jnp.zeros_like(item) for item in params))
    totals, (outputs, input_grads) = lax.scan(one_sequence, start, (inputs_all, tangents_all, chosen_all, globals_all))
    shape = (MICRO, SEQS, LENGTH, D)
    return (outputs.reshape(shape), input_grads.reshape(shape), totals[0], totals[1], totals[2], totals[3], totals[4], totals[5], totals[6], totals[7], totals[8], totals[9])
```

```python
import functools

import jax
import jax.numpy as jnp
from jax import lax
from jax.experimental import pallas as pl
from jax.experimental.pallas import tpu as pltpu
from jax.sharding import PartitionSpec as P

HEAD_DIM = 64
BLOCK = 64
EPSILON = 1e-05
F32 = jnp.float32
BF16 = jnp.bfloat16
MIB = 1 << 20

VM = pl.BlockSpec(memory_space=pltpu.VMEM)
SM = pl.BlockSpec(memory_space=pltpu.SMEM)
ANY = pl.BlockSpec(memory_space=pl.ANY)

NN = (((1,), (0,)), ((), ()))
NT = (((1,), (1,)), ((), ()))
TN = (((0,), (0,)), ((), ()))


def dot(left, right, dims=NN):
    return lax.dot_general(left, right, dims, preferred_element_type=F32)


def shape(dims, kind):
    return jax.ShapeDtypeStruct(dims, kind)


def params(limit=56):
    return pltpu.CompilerParams(vmem_limit_bytes=limit * MIB)


def cost(flops, moved, special=0):
    return pl.CostEstimate(flops=flops, bytes_accessed=moved, transcendentals=special)


def swap(value, axis, step):
    size = lax.axis_size(axis)
    return lax.ppermute(value, axis, [(i, i ^ step) for i in range(size)])


def gather_rows(piece):
    size = lax.axis_size("fsdp")
    if size == 8:
        line = [piece] + [swap(piece, "fsdp", 2 * k) for k in range(1, 4)]
        return [block for mine in line for block in (mine, swap(mine, "fsdp", 1))]
    whole = lax.all_gather(piece, "fsdp", axis=0, tiled=True)
    rows = whole.shape[0] // 8
    return [whole[(1 ^ j) * rows : (1 ^ j) * rows + rows] for j in range(8)]


def place_id():
    return lax.axis_index("fsdp") if lax.axis_size("fsdp") == 8 else jnp.int32(1)


def wide_add(*terms):
    total = terms[0].astype(F32)
    for term in terms[1:]:
        total = total + term.astype(F32)
    return total


def scatter_rows(kept, sent):
    if lax.axis_size("fsdp") == 8:
        came = swap(sent, "fsdp", 1)
        sums = [wide_add(kept[k], came[k]).astype(BF16) for k in range(4)]
        return wide_add(sums[0], *(swap(sums[k], "fsdp", 2 * k) for k in range(1, 4)))
    whole = jnp.stack([sent, kept], axis=1)
    whole = whole.reshape((8 * kept.shape[1],) + kept.shape[2:])
    return lax.psum_scatter(whole.astype(F32), "fsdp", scatter_dimension=0, tiled=True)


def sum_everywhere(vector):
    if lax.axis_size("fsdp") == 8:
        for axis, step in (("ctx", 1), ("ctx", 2), ("fsdp", 1), ("fsdp", 2), ("fsdp", 4)):
            vector = vector + swap(vector, axis, step)
        return vector
    return lax.psum(vector, ("ctx", "fsdp"))


def norm_parts(values):
    average = jnp.mean(values, axis=-1, keepdims=True)
    centered = values - average
    variance = jnp.mean(centered * centered, axis=-1, keepdims=True)
    inverse = lax.rsqrt(variance + EPSILON)
    return centered * inverse, inverse


def norm_back(grad, unit, inverse, gain):
    scaled = grad * gain
    first = jnp.mean(scaled, axis=-1, keepdims=True)
    second = jnp.mean(scaled * unit, axis=-1, keepdims=True)
    return inverse * (scaled - first - unit * second)


def fetch(pieces, target, semaphores, base, rows):
    copies = []
    for j in range(8):
        start = pl.multiple_of((base ^ j) * rows, rows)
        copies.append(
            pltpu.make_async_copy(pieces[j], target.at[pl.ds(start, rows), :], semaphores.at[j])
        )
        copies[-1].start()
    return copies


def project_kernel(ids, t0, t1, t2, t3, gain, bias, *rest):
    pieces, (triple, normed), (held, semaphores) = rest[:8], rest[8:10], rest[10:]
    copies = fetch(pieces, held, semaphores, ids[0], pieces[0].shape[0])
    rows = t0.shape[0]
    for place, part in enumerate((t0, t1, t2, t3)):
        unit, _ = norm_parts(part[...].astype(F32))
        normed[place * rows : (place + 1) * rows, :] = (unit * gain[...] + bias[...]).astype(BF16)
    for copy in copies:
        copy.wait()
    for place in range(4):
        block = normed[place * rows : (place + 1) * rows, :]
        triple[place * rows : (place + 1) * rows, :] = dot(block, held[...]).astype(BF16)


def project(ids, parts, gain, bias, pieces):
    rows, width = parts[0].shape
    columns = pieces[0].shape[1]
    return pl.pallas_call(
        project_kernel,
        name="project",
        out_shape=(shape((4 * rows, columns), BF16), shape((4 * rows, width), BF16)),
        in_specs=[SM] + [VM] * 6 + [ANY] * 8,
        out_specs=(VM, VM),
        scratch_shapes=[pltpu.VMEM((width, columns), BF16), pltpu.SemaphoreType.DMA((8,))],
        compiler_params=params(),
        cost_estimate=cost(8 * rows * width * columns, 12 * rows * width + 2 * width * columns),
    )(ids, *parts, gain, bias, *pieces)


def head_mask(rows):
    return lax.broadcasted_iota(jnp.int32, (rows, 2 * HEAD_DIM), 1) // HEAD_DIM


def attend_kernel(triple, block_bias, m0, m1, m2, m3, lse):
    outs = (m0, m1, m2, m3)
    length = triple.shape[0]
    width = triple.shape[1] // 3
    rows = length // 4
    blocks = length // BLOCK
    lse[...] = jnp.zeros_like(lse)
    for pair in range(width // 128):
        keys = triple[:, width + pair * 128 : width + pair * 128 + 128]
        values = triple[:, 2 * width + pair * 128 : 2 * width + pair * 128 + 128]
        values_t = values.astype(F32).T.astype(BF16)
        for place in range(4):
            span = slice(place * rows, (place + 1) * rows)
            queries = triple[span, pair * 128 : pair * 128 + 128] * jnp.asarray(0.125, BF16)
            side = head_mask(rows)
            halves = []
            for which in range(2):
                head = 2 * pair + which
                one = jnp.where(side == which, queries, jnp.zeros_like(queries))
                scores = dot(keys, one, NT)
                scores = scores.reshape(blocks, BLOCK, rows) + block_bias[head, :, span][:, None, :]
                peak = jnp.max(jnp.max(scores, axis=0), axis=0, keepdims=True)
                powered = jnp.exp(scores - peak[None])
                total = jnp.sum(jnp.sum(powered, axis=0), axis=0, keepdims=True)
                lse[head : head + 1, span] = peak + jnp.log(total)
                low = powered.astype(BF16).reshape(length, rows)
                part = dot(values_t[which * HEAD_DIM : (which + 1) * HEAD_DIM, :], low)
                halves.append(part / total)
            joined = jnp.concatenate(halves, axis=0)
            outs[place][:, pair * 128 : pair * 128 + 128] = joined.T.astype(BF16)


def attend(triple, block_bias):
    length, columns = triple.shape
    width = columns // 3
    heads = width // HEAD_DIM
    rows = length // 4
    return pl.pallas_call(
        attend_kernel,
        name="attend",
        out_shape=tuple(shape((rows, width), BF16) for _ in range(4)) + (shape((8, length), F32),),
        in_specs=[VM, VM],
        out_specs=(VM,) * 5,
        compiler_params=params(),
        cost_estimate=cost(
            32 * heads * length * length * HEAD_DIM, 8 * length * width, heads * length * length
        ),
    )(triple, block_bias)


def attend_back_kernel(ids, triple, block_bias, lse, *rest):
    grads, mixed, pieces = rest[:4], rest[4:8], rest[8:16]
    d_triple, n0, n1, n2, n3 = rest[16:21]
    held, semaphores, key_total, value_total = rest[21:]
    copies = fetch(pieces, held, semaphores, ids[0], pieces[0].shape[0])
    length = triple.shape[0]
    width = triple.shape[1] // 3
    rows = length // 4
    blocks = length // BLOCK
    for pair in range(width // 128):
        lanes = slice(pair * 128, pair * 128 + 128)
        keys = triple[:, width + pair * 128 : width + pair * 128 + 128]
        values = triple[:, 2 * width + pair * 128 : 2 * width + pair * 128 + 128]
        keys_t = keys.astype(F32).T.astype(BF16)
        key_total[...] = jnp.zeros_like(key_total)
        value_total[...] = jnp.zeros_like(value_total)
        for place in range(4):
            span = slice(place * rows, (place + 1) * rows)
            queries = triple[span, lanes] * jnp.asarray(0.125, BF16)
            grad = grads[place][:, lanes]
            product = (grad.astype(F32) * mixed[place][:, lanes].astype(F32)).T
            side = head_mask(rows)
            halves = []
            for which in range(2):
                head = 2 * pair + which
                one = jnp.where(side == which, queries, jnp.zeros_like(queries))
                one_grad = jnp.where(side == which, grad, jnp.zeros_like(grad))
                delta = jnp.sum(
                    product[which * HEAD_DIM : (which + 1) * HEAD_DIM, :], axis=0, keepdims=True
                )
                scores = dot(keys, one, NT)
                shift = block_bias[head, :, span] - lse[head : head + 1, span]
                exact = jnp.exp(scores.reshape(blocks, BLOCK, rows) + shift[:, None, :])
                exact = exact.reshape(length, rows)
                value_total[...] += dot(exact.astype(BF16), one_grad)
                d_probs = dot(values, one_grad, NT)
                d_scores = (exact * (d_probs - delta)).astype(BF16)
                key_total[...] += dot(d_scores, one)
                halves.append(dot(keys_t[which * HEAD_DIM : (which + 1) * HEAD_DIM, :], d_scores))
            joined = jnp.concatenate(halves, axis=0) * 0.125
            d_triple[span, lanes] = joined.T.astype(BF16)
        d_triple[:, width + pair * 128 : width + pair * 128 + 128] = key_total[...].astype(BF16)
        d_triple[:, 2 * width + pair * 128 : 2 * width + pair * 128 + 128] = value_total[
            ...
        ].astype(BF16)
    for copy in copies:
        copy.wait()
    for place, out in enumerate((n0, n1, n2, n3)):
        out[...] = dot(d_triple[place * rows : (place + 1) * rows, :], held[...], NT).astype(BF16)


def attend_back(ids, triple, block_bias, lse, grads, mixed, pieces, width_all):
    length, columns = triple.shape
    width = columns // 3
    heads = width // HEAD_DIM
    rows = length // 4
    return pl.pallas_call(
        attend_back_kernel,
        name="attend_back",
        out_shape=(shape((length, columns), BF16),)
        + tuple(shape((rows, width_all), BF16) for _ in range(4)),
        in_specs=[SM] + [VM] * 11 + [ANY] * 8,
        out_specs=(VM,) * 5,
        scratch_shapes=[
            pltpu.VMEM((width_all, columns), BF16),
            pltpu.SemaphoreType.DMA((8,)),
            pltpu.VMEM((length, 128), F32),
            pltpu.VMEM((length, 128), F32),
        ],
        compiler_params=params(),
        cost_estimate=cost(
            80 * heads * length * length * HEAD_DIM, 16 * length * width, heads * length * length
        ),
    )(ids, triple, block_bias, lse, *grads, *mixed, *pieces)


def fetch_output(ids, own, other, held, semaphores):
    copies = []
    rows = own.shape[0] // 8
    half = own.shape[1]
    for j in range(8):
        block = ids[0] ^ j
        start = pl.multiple_of(((block // 2) ^ ids[1]) * (2 * rows) + (block % 2) * rows, rows)
        for side, source in enumerate((own, other)):
            column = pl.multiple_of((ids[2] ^ side) * half, half)
            copies.append(
                pltpu.make_async_copy(
                    source.at[pl.ds(j * rows, rows), :],
                    held.at[pl.ds(start, rows), pl.ds(column, half)],
                    semaphores.at[2 * j + side],
                )
            )
            copies[-1].start()
    return copies


def output_kernel(ids, tokens, *rest):
    mixed, (gain, bias, own, other) = rest[:8], rest[8:12]
    attended, normed, joined, held, semaphores = rest[12:]
    copies = fetch_output(ids, own, other, held, semaphores)
    rows, width = mixed[0].shape
    for micro in range(2):
        for place in range(4):
            joined[micro * rows : (micro + 1) * rows, place * width : (place + 1) * width] = mixed[
                4 * micro + place
            ][...]
    for copy in copies:
        copy.wait()
    for micro in range(2):
        span = slice(micro * rows, (micro + 1) * rows)
        value = tokens[micro].astype(F32) + dot(joined[span, :], held[...])
        attended[span, :] = value
        unit, _ = norm_parts(value)
        normed[span, :] = (unit * gain[...] + bias[...]).astype(BF16)


def output_project(ids, tokens, mixed, gain, bias, own, other):
    micro, rows, width = tokens.shape
    total = micro * rows
    return pl.pallas_call(
        output_kernel,
        name="output_project",
        out_shape=(
            shape((total, width), F32),
            shape((total, width), BF16),
            shape((total, width), BF16),
        ),
        in_specs=[SM] + [VM] * 11 + [ANY] * 2,
        out_specs=(VM, VM, VM),
        scratch_shapes=[
            pltpu.VMEM((width, width), BF16),
            pltpu.SemaphoreType.DMA((16,)),
        ],
        compiler_params=params(),
        cost_estimate=cost(2 * total * width * width, 12 * total * width + 2 * width * width),
    )(ids, tokens, *mixed, gain, bias, own, other)


CURVE = 0.7978845608028654
CUBIC = 0.044715


def feed_kernel(ids, h0, h1, c0, c1, shift, *rest):
    expand, shrink = rest[:8], rest[8:16]
    own_out, other_out, own_hidden, other_hidden, bias_grad = rest[16:21]
    shrink_sent, shrink_kept, expand_sent, expand_kept = rest[21:25]
    expand_held, hidden, tangent, hidden_t, out_total, hidden_total, semaphores = rest[25:]
    base = ids[0]
    copies = fetch(expand, expand_held, semaphores, base, expand[0].shape[0])
    rows, width = h0.shape
    tile = shrink[0].shape[0]
    deep = expand[0].shape[0]
    hidden[:rows, :] = h0[...]
    hidden[rows:, :] = h1[...]
    tangent[:rows, :] = c0[...]
    tangent[rows:, :] = c1[...]
    for j in range(8):
        source = pl.multiple_of((base ^ j) * deep, deep)
        hidden_t[j * deep : (j + 1) * deep, :] = (
            hidden[:, pl.ds(source, deep)].astype(F32).T.astype(BF16)
        )
    for copy in copies:
        copy.wait()
    for step, j in enumerate((1, 3, 5, 7, 0, 2, 4, 6)):
        column = pl.multiple_of((base ^ j) * tile, tile)
        up = expand_held[:, pl.ds(column, tile)]
        down = shrink[j][...]
        before = dot(hidden[...], up) + shift[:, pl.ds(column, tile)]
        d_active = dot(tangent[...], down, NT)
        square = before * before
        bend = jnp.tanh(CURVE * before * (1.0 + CUBIC * square))
        plus = 0.5 * (1.0 + bend)
        active = (before * plus).astype(BF16)
        slope = plus + (0.5 * CURVE) * before * (1.0 - bend * bend) * (1.0 + 3 * CUBIC * square)
        d_before = (d_active * slope).astype(BF16)
        bias_grad[:, pl.ds(column, tile)] = jnp.sum(d_before.astype(F32), axis=0, keepdims=True)
        out_part = dot(active, down)
        hidden_part = dot(d_before, up, NT)
        if step == 0:
            out_total[...] = out_part
            hidden_total[...] = hidden_part
        else:
            out_total[...] += out_part
            hidden_total[...] += hidden_part
        shrink_part = dot(active, tangent[...], TN).astype(BF16)
        (shrink_sent if j % 2 else shrink_kept)[j // 2] = shrink_part
        expand_part = dot(hidden_t[...], d_before).astype(BF16)
        for place in range(8):
            target = expand_sent if place % 2 else expand_kept
            target[place // 2, :, pl.ds(column, tile)] = expand_part[
                place * deep : (place + 1) * deep, :
            ]
    own_out[...] = out_total[:rows, :]
    other_out[...] = out_total[rows:, :].astype(BF16)
    own_hidden[...] = hidden_total[:rows, :]
    other_hidden[...] = hidden_total[rows:, :].astype(BF16)


def feed(ids, hidden, tangent, shift, expand, shrink):
    rows, width = hidden[0].shape
    deep, wide = expand[0].shape
    tile = shrink[0].shape[0]
    return pl.pallas_call(
        feed_kernel,
        name="feed",
        out_shape=(
            shape((rows, width), F32),
            shape((rows, width), BF16),
            shape((rows, width), F32),
            shape((rows, width), BF16),
            shape((1, wide), F32),
            shape((4, tile, width), BF16),
            shape((4, tile, width), BF16),
            shape((4, deep, wide), BF16),
            shape((4, deep, wide), BF16),
        ),
        in_specs=[SM] + [VM] * 5 + [ANY] * 8 + [VM] * 8,
        out_specs=(VM,) * 9,
        scratch_shapes=[
            pltpu.VMEM((width, wide), BF16),
            pltpu.VMEM((2 * rows, width), BF16),
            pltpu.VMEM((2 * rows, width), BF16),
            pltpu.VMEM((width, 2 * rows), BF16),
            pltpu.VMEM((2 * rows, width), F32),
            pltpu.VMEM((2 * rows, width), F32),
            pltpu.SemaphoreType.DMA((8,)),
        ],
        compiler_params=params(60),
        cost_estimate=cost(24 * rows * width * wide, 8 * width * wide + 20 * rows * width, 2 * rows * wide),
    )(ids, *hidden, *tangent, shift, *expand, *shrink)


def branch_kernel(
    ids, attended, own_hidden, came_hidden, tangent, own_out, came_out, gain, shift, own, other, *rest
):
    result, d_attended, d_branch = rest[:3]
    grads, (gain_grad, bias_grad, shift_grad), (held, semaphores) = rest[3:11], rest[11:14], rest[14:]
    copies = fetch_output(ids, own, other, held, semaphores)
    rows = tangent.shape[1]
    width = gain.shape[1] // 4
    gain_total = bias_total = shift_total = 0.0
    for micro in range(2):
        span = slice(micro * rows, (micro + 1) * rows)
        value = attended[span, :]
        cot = tangent[micro].astype(F32)
        branch = own_out[span, :] + came_out[span, :].astype(F32) + shift[...]
        result[micro] = (value + branch).astype(BF16)
        unit, inverse = norm_parts(value)
        grad = own_hidden[span, :] + came_hidden[span, :].astype(F32)
        gain_total = gain_total + jnp.sum(grad * unit, axis=0, keepdims=True)
        bias_total = bias_total + jnp.sum(grad, axis=0, keepdims=True)
        shift_total = shift_total + jnp.sum(cot, axis=0, keepdims=True)
        total = cot + norm_back(grad, unit, inverse, gain[...])
        d_attended[span, :] = total
        d_branch[span, :] = total.astype(BF16)
    gain_grad[...] = gain_total
    bias_grad[...] = bias_total
    shift_grad[...] = shift_total
    for copy in copies:
        copy.wait()
    for micro in range(2):
        mixed = dot(d_branch[micro * rows : (micro + 1) * rows, :], held[...], NT).astype(BF16)
        for place in range(4):
            grads[4 * micro + place][...] = mixed[:, place * width : (place + 1) * width]


def branch_back(ids, attended, own_hidden, came_hidden, tangent, own_out, came_out, gain, shift, own, other):
    micro, rows, width = tangent.shape
    total = micro * rows
    row = shape((1, width), F32)
    return pl.pallas_call(
        branch_kernel,
        name="branch_back",
        out_shape=(
            shape(tangent.shape, BF16),
            shape((total, width), F32),
            shape((total, width), BF16),
        )
        + tuple(shape((rows, width // 4), BF16) for _ in range(8))
        + (row, row, row),
        in_specs=[SM] + [VM] * 8 + [ANY] * 2,
        out_specs=(VM,) * 14,
        scratch_shapes=[pltpu.VMEM((width, width), BF16), pltpu.SemaphoreType.DMA((16,))],
        compiler_params=params(),
        cost_estimate=cost(2 * total * width * width, 32 * total * width),
    )(ids, attended, own_hidden, came_hidden, tangent, own_out, came_out, gain, shift, own, other)


def output_grad_kernel(ids, own_mixed, other_mixed, own_branch, other_branch, out):
    rows = out.shape[1]
    width = own_branch.shape[1]
    half = width // 2
    column = pl.multiple_of(ids[2] * half, half)
    right = own_branch[:, pl.ds(column, half)]
    for k in range(4):
        block = ids[0] ^ (2 * k + ids[3])
        first = ((block // 2) ^ ids[1]) * (2 * rows) + (block % 2) * rows
        second = ((block // 2) ^ ids[1] ^ 1) * (2 * rows) + (block % 2) * rows
        part = dot(own_mixed[:, pl.ds(pl.multiple_of(first, rows), rows)], right, TN)
        part += dot(other_mixed[:, pl.ds(pl.multiple_of(second, rows), rows)], other_branch[...], TN)
        out[k] = part.astype(BF16)


def output_grad(ids, own_mixed, other_mixed, own_branch, other_branch):
    total, width = own_mixed.shape
    return pl.pallas_call(
        output_grad_kernel,
        name="output_grad",
        out_shape=shape((4, width // 8, width // 2), BF16),
        in_specs=[SM] + [VM] * 4,
        out_specs=VM,
        compiler_params=params(),
        cost_estimate=cost(total * width * width, 8 * total * width),
    )(ids, own_mixed, other_mixed, own_branch, other_branch)


def triple_grad_kernel(ids, n0, n1, d0, d1, out):
    rows = out.shape[1]
    for k in range(4):
        column = pl.multiple_of((ids[0] ^ (2 * k + ids[3])) * rows, rows)
        part = dot(n0[:, pl.ds(column, rows)], d0[...], TN)
        part += dot(n1[:, pl.ds(column, rows)], d1[...], TN)
        out[k] = part.astype(BF16)


def triple_grad(ids, normed, grads):
    length, width = normed[0].shape
    columns = grads[0].shape[1]
    return pl.pallas_call(
        triple_grad_kernel,
        name="triple_grad",
        out_shape=shape((4, width // 8, columns), BF16),
        in_specs=[SM] + [VM] * 4,
        out_specs=VM,
        compiler_params=params(),
        cost_estimate=cost(2 * length * width * columns, 4 * length * (width + columns)),
    )(ids, *normed, *grads)


def first_back_kernel(tokens, d_attended, gain, *rest):
    parts, (grad_out, gain_grad, bias_grad) = rest[:6], rest[6:]
    rows = tokens.shape[1]
    gain_total = bias_total = 0.0
    for micro in range(2):
        one, two, three = parts[3 * micro : 3 * micro + 3]
        grad = one[...].astype(F32) + two[...].astype(F32) + three[...].astype(F32)
        unit, inverse = norm_parts(tokens[micro].astype(F32))
        gain_total = gain_total + jnp.sum(grad * unit, axis=0, keepdims=True)
        bias_total = bias_total + jnp.sum(grad, axis=0, keepdims=True)
        total = d_attended[micro * rows : (micro + 1) * rows, :]
        grad_out[micro] = (total + norm_back(grad, unit, inverse, gain[...])).astype(BF16)
    gain_grad[...] = gain_total
    bias_grad[...] = bias_total


def first_back(tokens, d_attended, gain, parts):
    micro, rows, width = tokens.shape
    row = shape((1, width), F32)
    return pl.pallas_call(
        first_back_kernel,
        name="first_back",
        out_shape=(shape(tokens.shape, BF16), row, row),
        in_specs=[VM] * 9,
        out_specs=(VM,) * 3,
        compiler_params=params(),
        cost_estimate=cost(20 * micro * rows * width, 16 * micro * rows * width),
    )(tokens, d_attended, gain, *parts)


def block_biases(chosen, globals_here, rank, local_blocks):
    heads, count, _ = chosen.shape
    place = jnp.arange(count, dtype=jnp.int32)
    true_block = ((place // local_blocks) ^ rank) * local_blocks + place % local_blocks
    near = jnp.abs(true_block[:, None] - true_block[None, :]) <= 1
    is_global = jnp.any(true_block[:, None] == globals_here[None, :], axis=1)
    picked = jnp.any(chosen[:, None, :, :] == true_block[None, :, None, None], axis=3)
    allowed = near[None] | picked | is_global[None, :, None] | is_global[None, None, :]
    bias = jnp.where(allowed, 0.0, -1e30).astype(F32)
    return jnp.repeat(bias, BLOCK, axis=2)


def on_device(
    tokens,
    cotangent,
    random_blocks,
    global_blocks,
    attend_gain,
    attend_bias,
    triple_weight,
    output_weight,
    hidden_gain,
    hidden_bias,
    expand_weight,
    expand_bias,
    shrink_weight,
    shrink_bias,
):
    tokens, cotangent = tokens[:, 0], cotangent[:, 0]
    micro, rows, width = tokens.shape
    total = micro * rows
    ways = lax.axis_size("fsdp")
    fsdp = lax.axis_index("fsdp")
    rank = lax.axis_index("ctx")
    core = rank % 2
    place = place_id()
    heads_all = random_blocks.shape[2]
    own_heads = heads_all // 4
    local_blocks = rows // BLOCK
    shard = width // ways
    wide = expand_weight.shape[1]
    deep = shrink_weight.shape[0]
    ids = jnp.stack([place, rank, core, jnp.int32(0)])
    ids_sent = jnp.stack([place, rank, core, jnp.int32(1)])

    small = jnp.concatenate(
        [attend_gain, attend_bias, hidden_gain, hidden_bias, shrink_bias, expand_bias]
    ).reshape(1, -1)
    small_rows = gather_rows(small) if ways == 8 else None
    triple_part = jnp.take(triple_weight.reshape(shard, 3, 4, width // 4), rank, axis=2)
    triple_pieces = gather_rows(triple_part.reshape(shard, 3 * width // 4))
    token_parts, chosen = [], None
    for step in range(micro):
        mine = tokens[step]
        far = swap(mine, "ctx", 2)
        token_parts.append((mine, swap(mine, "ctx", 1), far, swap(far, "ctx", 1)))
    picks = random_blocks[:, 0]
    far_picks = swap(picks, "ctx", 2)
    all_picks = jnp.stack([picks, swap(picks, "ctx", 1), far_picks, swap(far_picks, "ctx", 1)])
    chosen = lax.dynamic_slice_in_dim(all_picks, rank * own_heads, own_heads, 2)
    chosen = chosen.transpose(1, 2, 0, 3, 4).reshape(micro, own_heads, 4 * local_blocks, -1)
    output_part = lax.dynamic_slice_in_dim(output_weight, core * (width // 2), width // 2, 1)
    output_own = jnp.concatenate(gather_rows(output_part), axis=0)
    output_other = swap(output_own, "ctx", 1)
    if ways != 8:
        pass
    expand_part = jnp.take(expand_weight.reshape(shard, ways, 2, wide // (2 * ways)), core, axis=2)
    expand_pieces = gather_rows(expand_part.reshape(shard, wide // 2))
    shrink_part = lax.dynamic_slice_in_dim(shrink_weight, core * (deep // 2), deep // 2, 0)
    shrink_pieces = gather_rows(shrink_part)
    tangent_own = cotangent.reshape(total, width)
    tangent_other = swap(tangent_own, "ctx", 1)

    if ways == 8:
        table = jnp.concatenate(small_rows, axis=0)[jnp.arange(8) ^ fsdp].astype(F32)
    else:
        table = lax.all_gather(small, "fsdp", axis=0, tiled=True).astype(F32)
    gain_one, bias_one, gain_two, bias_two, shift_out = (
        table[:, k * shard : (k + 1) * shard].reshape(1, width) for k in range(5)
    )
    shift_in = jnp.take(table[:, 5 * shard :].reshape(ways, 2, wide // (2 * ways)), core, axis=1)
    shift_in = shift_in.reshape(1, wide // 2)

    biases, triples, normeds, lses, mixed_own, mixed_here = [], [], [], [], [], []
    for step in range(micro):
        biases.append(block_biases(chosen[step], global_blocks[step, 0], rank, local_blocks))
        triple, normed = project(ids, token_parts[step], gain_one, bias_one, triple_pieces)
        *mixed, lse = attend(triple, biases[step])
        triples.append(triple)
        normeds.append(normed)
        lses.append(lse)
        mixed_own.append(mixed)
        mixed_here += [mixed[0]] + [swap(mixed[p], "ctx", p) for p in range(1, 4)]
    attended, hidden, mixed_all = output_project(
        ids, tokens, mixed_here, gain_two, bias_two, output_own, output_other
    )

    hidden_other = swap(hidden, "ctx", 1)
    (
        own_out,
        other_out,
        own_hidden,
        other_hidden,
        shift_in_grad,
        shrink_sent,
        shrink_kept,
        expand_sent,
        expand_kept,
    ) = feed(ids, (hidden, hidden_other), (tangent_own, tangent_other), shift_in, expand_pieces, shrink_pieces)
    came_hidden = swap(other_hidden, "ctx", 1)
    came_out = swap(other_out, "ctx", 1)
    shrink_mine = scatter_rows(shrink_kept, shrink_sent)
    expand_mine = scatter_rows(expand_kept, expand_sent)
    result, d_attended, d_branch, *grads, gain_two_grad, bias_two_grad, shift_out_grad = branch_back(
        ids,
        attended,
        own_hidden,
        came_hidden,
        cotangent,
        own_out,
        came_out,
        gain_two,
        shift_out,
        output_own,
        output_other,
    )
    mixed_other = swap(mixed_all, "ctx", 1)
    half_sent = lax.dynamic_slice_in_dim(d_branch, (1 - core) * (width // 2), width // 2, 1)
    branch_other = swap(half_sent, "ctx", 1)
    output_sent = output_grad(ids_sent, mixed_all, mixed_other, d_branch, branch_other)
    output_kept = output_grad(ids, mixed_all, mixed_other, d_branch, branch_other)
    output_mine = scatter_rows(output_kept, output_sent)

    d_triples, norm_parts_here = [], []
    for step in range(micro):
        here = grads[4 * step : 4 * step + 4]
        here = [here[0]] + [swap(here[p], "ctx", p) for p in range(1, 4)]
        d_triple, *parts = attend_back(
            ids, triples[step], biases[step], lses[step], here, mixed_own[step], triple_pieces, width
        )
        d_triples.append(d_triple)
        near = swap(parts[1], "ctx", 1)
        far = wide_add(parts[2], swap(parts[3], "ctx", 1)).astype(BF16)
        norm_parts_here += [parts[0], near, swap(far, "ctx", 2)]
    triple_sent = triple_grad(ids_sent, normeds, d_triples)
    triple_kept = triple_grad(ids, normeds, d_triples)
    triple_mine = scatter_rows(triple_kept, triple_sent)
    token_grad, gain_one_grad, bias_one_grad = first_back(
        tokens, d_attended, gain_one, norm_parts_here
    )

    halves = shift_in_grad.reshape(ways, 1, wide // (2 * ways))
    blank = jnp.zeros_like(halves)
    spread = jnp.where(
        core == 0,
        jnp.concatenate([halves, blank], axis=1),
        jnp.concatenate([blank, halves], axis=1),
    )
    early = sum_everywhere(
        jnp.concatenate(
            [
                gain_two_grad.reshape(ways, shard),
                bias_two_grad.reshape(ways, shard),
                shift_out_grad.reshape(ways, shard),
                spread.reshape(ways, wide // ways),
            ],
            axis=1,
        )
    )
    late = sum_everywhere(
        jnp.concatenate([gain_one_grad.reshape(ways, shard), bias_one_grad.reshape(ways, shard)], axis=1)
    )
    early = lax.dynamic_index_in_dim(early, fsdp, 0, keepdims=False)
    late = lax.dynamic_index_in_dim(late, fsdp, 0, keepdims=False)

    def over_chips(part):
        low = part.astype(BF16)
        return wide_add(low, swap(low, "ctx", 2))

    def both(own, axis):
        other = swap(own, "ctx", 1)
        first = jnp.where(core == 0, own, other)
        second = jnp.where(core == 0, other, own)
        return jnp.stack([first, second], axis=axis)

    shrink_grad = both(over_chips(shrink_mine), 0).reshape(deep, width)
    expand_half = over_chips(expand_mine).reshape(shard, ways, wide // (2 * ways))
    expand_grad = both(expand_half, 2).reshape(shard, wide)
    output_grad_all = both(over_chips(output_mine), 1).reshape(shard, width)
    low = triple_mine.astype(BF16).reshape(shard, 3, width // 4)
    far = swap(low, "ctx", 2)
    pair = jnp.stack([jnp.where(rank < 2, low, far), jnp.where(rank < 2, far, low)], axis=2)
    triple_grad_all = both(pair, 3).reshape(shard, 3 * width).astype(F32)

    return (
        result[:, None],
        token_grad[:, None],
        late[:shard],
        late[shard:],
        triple_grad_all,
        output_grad_all,
        early[:shard],
        early[shard : 2 * shard],
        expand_grad,
        early[3 * shard :],
        shrink_grad,
        early[2 * shard : 3 * shard],
    )


def solution(mesh):
    token_spec = P(None, "fsdp", "ctx", None)
    flat, rows = P("fsdp"), P("fsdp", None)
    return jax.shard_map(
        on_device,
        mesh=mesh,
        in_specs=(
            token_spec,
            token_spec,
            P(None, "fsdp", None, "ctx", None),
            P(None, "fsdp", None),
            flat,
            flat,
            rows,
            rows,
            flat,
            flat,
            rows,
            flat,
            rows,
            flat,
        ),
        out_specs=(
            token_spec,
            token_spec,
            flat,
            flat,
            rows,
            rows,
            flat,
            flat,
            rows,
            flat,
            rows,
            flat,
        ),
        check_vma=False,
    )
```

```python
import functools

import jax
import jax.numpy as jnp
from jax import lax
from jax.experimental import pallas as pl
from jax.experimental.pallas import tpu as pltpu
from jax.sharding import PartitionSpec as P

HEAD_DIM = 64
BLOCK = 64
EPSILON = 1e-05
F32 = jnp.float32
BF16 = jnp.bfloat16
MIB = 1 << 20

VM = pl.BlockSpec(memory_space=pltpu.VMEM)
SM = pl.BlockSpec(memory_space=pltpu.SMEM)
ANY = pl.BlockSpec(memory_space=pl.ANY)

NN = (((1,), (0,)), ((), ()))
NT = (((1,), (1,)), ((), ()))
TN = (((0,), (0,)), ((), ()))


def dot(left, right, dims=NN):
    return lax.dot_general(left, right, dims, preferred_element_type=F32)


def shape(dims, kind):
    return jax.ShapeDtypeStruct(dims, kind)


def params(limit=56):
    return pltpu.CompilerParams(vmem_limit_bytes=limit * MIB)


def cost(flops, moved, special=0):
    return pl.CostEstimate(flops=flops, bytes_accessed=moved, transcendentals=special)


def swap(value, axis, step):
    size = lax.axis_size(axis)
    return lax.ppermute(value, axis, [(i, i ^ step) for i in range(size)])


def place_id():
    return lax.axis_index("fsdp") if lax.axis_size("fsdp") == 8 else jnp.int32(1)


def wide_add(*terms):
    total = terms[0].astype(F32)
    for term in terms[1:]:
        total = total + term.astype(F32)
    return total


def scatter_rows(kept, sent):
    if lax.axis_size("fsdp") == 8:
        came = swap(sent, "fsdp", 1)
        sums = [wide_add(kept[k], came[k]).astype(BF16) for k in range(4)]
        return wide_add(sums[0], *(swap(sums[k], "fsdp", 2 * k) for k in range(1, 4)))
    whole = jnp.stack([sent, kept], axis=1)
    whole = whole.reshape((8 * kept.shape[1],) + kept.shape[2:])
    return lax.psum_scatter(whole.astype(F32), "fsdp", scatter_dimension=0, tiled=True)


def sum_everywhere(vector):
    if lax.axis_size("fsdp") == 8:
        for axis, step in (("ctx", 1), ("ctx", 2), ("fsdp", 1), ("fsdp", 2), ("fsdp", 4)):
            vector = vector + swap(vector, axis, step)
        return vector
    return lax.psum(vector, ("ctx", "fsdp"))


def norm_parts(values):
    average = jnp.mean(values, axis=-1, keepdims=True)
    centered = values - average
    variance = jnp.mean(centered * centered, axis=-1, keepdims=True)
    inverse = lax.rsqrt(variance + EPSILON)
    return centered * inverse, inverse


def norm_back(grad, unit, inverse, gain):
    scaled = grad * gain
    first = jnp.mean(scaled, axis=-1, keepdims=True)
    second = jnp.mean(scaled * unit, axis=-1, keepdims=True)
    return inverse * (scaled - first - unit * second)


def normalize(source, gain, bias):
    unit, _ = norm_parts(source.astype(F32))
    return (unit * gain + bias).astype(BF16)


def project_kernel(t0, t1, t2, t3, gain, bias, weight, triple, normed):
    rows = t0.shape[0]
    for place, part in enumerate((t0, t1, t2, t3)):
        span = slice(place * rows, (place + 1) * rows)
        normed[span, :] = normalize(part[...], gain[...], bias[...])
        triple[span, :] = dot(normed[span, :], weight[...]).astype(BF16)


def project(parts, gain, bias, weight):
    rows, width = parts[0].shape
    columns = weight.shape[1]
    return pl.pallas_call(
        project_kernel,
        name="project",
        out_shape=(shape((4 * rows, columns), BF16), shape((4 * rows, width), BF16)),
        in_specs=[VM] * 7,
        out_specs=(VM, VM),
        compiler_params=params(),
        cost_estimate=cost(8 * rows * width * columns, 12 * rows * width + 2 * width * columns),
    )(*parts, gain, bias, weight)


def head_mask(rows):
    return lax.broadcasted_iota(jnp.int32, (rows, 2 * HEAD_DIM), 1) // HEAD_DIM


def attend_body(triple, block_bias, mixed, lse):
    length = triple.shape[0]
    width = triple.shape[1] // 3
    rows = length // 4
    blocks = length // BLOCK
    for pair in range(width // 128):
        keys = triple[:, width + pair * 128 : width + pair * 128 + 128]
        values = triple[:, 2 * width + pair * 128 : 2 * width + pair * 128 + 128]
        values_t = values.astype(F32).T.astype(BF16)

        def step(place, carry):
            start = pl.multiple_of(place * rows, rows)
            queries = triple[pl.ds(start, rows), pair * 128 : pair * 128 + 128]
            queries = queries * jnp.asarray(0.125, BF16)
            side = head_mask(rows)
            halves = []
            for which in range(2):
                head = 2 * pair + which
                one = jnp.where(side == which, queries, jnp.zeros_like(queries))
                scores = dot(keys, one, NT)
                shift = block_bias[head, :, pl.ds(start, rows)]
                scores = scores.reshape(blocks, BLOCK, rows) + shift[:, None, :]
                peak = jnp.max(jnp.max(scores, axis=0), axis=0, keepdims=True)
                powered = jnp.exp(scores - peak[None])
                total = jnp.sum(jnp.sum(powered, axis=0), axis=0, keepdims=True)
                lse[head : head + 1, pl.ds(start, rows)] = peak + jnp.log(total)
                low = powered.astype(BF16).reshape(length, rows)
                part = dot(values_t[which * HEAD_DIM : (which + 1) * HEAD_DIM, :], low)
                halves.append(part / total)
            joined = jnp.concatenate(halves, axis=0)
            mixed[place, :, pair * 128 : pair * 128 + 128] = joined.T.astype(BF16)
            return carry

        lax.fori_loop(0, 4, step, 0)


def attend(triple, block_bias):
    length, columns = triple.shape
    width = columns // 3
    heads = width // HEAD_DIM
    rows = length // 4
    return pl.pallas_call(
        attend_body,
        name="attend",
        out_shape=(shape((4, rows, width), BF16), shape((8, length), F32)),
        in_specs=[VM, VM],
        out_specs=(VM, VM),
        compiler_params=params(),
        cost_estimate=cost(
            32 * heads * length * length * HEAD_DIM, 8 * length * width, heads * length * length
        ),
    )(triple, block_bias)


def attend_back_body(triple, block_bias, lse, grads, mixed, d_triple, key_total, value_total):
    length = triple.shape[0]
    width = triple.shape[1] // 3
    rows = length // 4
    blocks = length // BLOCK
    for pair in range(width // 128):
        lanes = slice(pair * 128, pair * 128 + 128)
        keys = triple[:, width + pair * 128 : width + pair * 128 + 128]
        values = triple[:, 2 * width + pair * 128 : 2 * width + pair * 128 + 128]
        keys_t = keys.astype(F32).T.astype(BF16)
        key_total[...] = jnp.zeros_like(key_total)
        value_total[...] = jnp.zeros_like(value_total)

        def step(place, carry):
            start = pl.multiple_of(place * rows, rows)
            queries = triple[pl.ds(start, rows), lanes] * jnp.asarray(0.125, BF16)
            grad = grads[place, :, lanes]
            product = (grad.astype(F32) * mixed[place, :, lanes].astype(F32)).T
            side = head_mask(rows)
            halves = []
            for which in range(2):
                head = 2 * pair + which
                one = jnp.where(side == which, queries, jnp.zeros_like(queries))
                one_grad = jnp.where(side == which, grad, jnp.zeros_like(grad))
                delta = jnp.sum(
                    product[which * HEAD_DIM : (which + 1) * HEAD_DIM, :], axis=0, keepdims=True
                )
                scores = dot(keys, one, NT)
                shift = block_bias[head, :, pl.ds(start, rows)] - lse[head : head + 1, pl.ds(start, rows)]
                exact = jnp.exp(scores.reshape(blocks, BLOCK, rows) + shift[:, None, :])
                exact = exact.reshape(length, rows)
                value_total[...] += dot(exact.astype(BF16), one_grad)
                d_probs = dot(values, one_grad, NT)
                d_scores = (exact * (d_probs - delta)).astype(BF16)
                key_total[...] += dot(d_scores, one)
                halves.append(dot(keys_t[which * HEAD_DIM : (which + 1) * HEAD_DIM, :], d_scores))
            joined = jnp.concatenate(halves, axis=0) * 0.125
            d_triple[pl.ds(start, rows), lanes] = joined.T.astype(BF16)
            return carry

        lax.fori_loop(0, 4, step, 0)
        d_triple[:, width + pair * 128 : width + pair * 128 + 128] = key_total[...].astype(BF16)
        d_triple[:, 2 * width + pair * 128 : 2 * width + pair * 128 + 128] = value_total[
            ...
        ].astype(BF16)


def attend_back_kernel(triple, block_bias, lse, g0, g1, g2, g3, mixed, weight, d_triple, norm_grad, grads, key_total, value_total):
    rows = g0.shape[0]
    for place, part in enumerate((g0, g1, g2, g3)):
        grads[place] = part[...]
    attend_back_body(triple, block_bias, lse, grads, mixed, d_triple, key_total, value_total)
    for place in range(4):
        part = dot(d_triple[place * rows : (place + 1) * rows, :], weight[...], NT)
        norm_grad[place] = part.astype(BF16)


def attend_back(triple, block_bias, lse, grads, mixed, weight):
    length, columns = triple.shape
    width = columns // 3
    heads = width // HEAD_DIM
    rows = length // 4
    return pl.pallas_call(
        attend_back_kernel,
        name="attend_back",
        out_shape=(shape((length, columns), BF16), shape((4, rows, weight.shape[0]), BF16)),
        in_specs=[VM] * 9,
        out_specs=(VM,) * 2,
        scratch_shapes=[
            pltpu.VMEM((4, rows, width), BF16),
            pltpu.VMEM((length, 128), F32),
            pltpu.VMEM((length, 128), F32),
        ],
        compiler_params=params(),
        cost_estimate=cost(
            80 * heads * length * length * HEAD_DIM, 16 * length * width, heads * length * length
        ),
    )(triple, block_bias, lse, *grads, mixed, weight)


def output_kernel(tokens, joined, gain, bias, weight, attended, normed):
    rows = tokens.shape[1]
    for micro in range(2):
        span = slice(micro * rows, (micro + 1) * rows)
        value = tokens[micro].astype(F32) + dot(joined[span, :], weight[...])
        attended[span, :] = value
        normed[span, :] = normalize(value, gain[...], bias[...])


def output_project(tokens, joined, gain, bias, weight):
    micro, rows, width = tokens.shape
    total = micro * rows
    return pl.pallas_call(
        output_kernel,
        name="output_project",
        out_shape=(shape((total, width), F32), shape((total, width), BF16)),
        in_specs=[VM] * 5,
        out_specs=(VM, VM),
        compiler_params=params(),
        cost_estimate=cost(2 * total * width * width, 12 * total * width + 2 * width * width),
    )(tokens, joined, gain, bias, weight)


CURVE = 0.7978845608028654
CUBIC = 0.044715


def feed_kernel(ids, h0, h1, c0, c1, shift, *rest):
    expand_held, shrink_held = rest[:2]
    own_out, other_out, own_hidden, other_hidden, bias_grad = rest[2:7]
    shrink_sent, shrink_kept, expand_sent, expand_kept = rest[7:11]
    hidden, tangent, hidden_t, out_total, hidden_total = rest[11:]
    base = ids[0]
    rows, width = h0.shape
    tile = shrink_held.shape[0] // 8
    deep = width // 8
    hidden[:rows, :] = h0[...]
    hidden[rows:, :] = h1[...]
    tangent[:rows, :] = c0[...]
    tangent[rows:, :] = c1[...]
    for j in range(8):
        source = pl.multiple_of((base ^ j) * deep, deep)
        hidden_t[j * deep : (j + 1) * deep, :] = (
            hidden[:, pl.ds(source, deep)].astype(F32).T.astype(BF16)
        )
    for step, j in enumerate((1, 3, 5, 7, 0, 2, 4, 6)):
        column = pl.multiple_of((base ^ j) * tile, tile)
        up = expand_held[:, pl.ds(column, tile)]
        down = shrink_held[pl.ds(column, tile), :]
        before = dot(hidden[...], up) + shift[:, pl.ds(column, tile)]
        d_active = dot(tangent[...], down, NT)
        square = before * before
        bend = jnp.tanh(CURVE * before * (1.0 + CUBIC * square))
        plus = 0.5 * (1.0 + bend)
        active = (before * plus).astype(BF16)
        slope = plus + (0.5 * CURVE) * before * (1.0 - bend * bend) * (1.0 + 3 * CUBIC * square)
        d_before = (d_active * slope).astype(BF16)
        bias_grad[:, pl.ds(column, tile)] = jnp.sum(d_before.astype(F32), axis=0, keepdims=True)
        out_part = dot(active, down)
        hidden_part = dot(d_before, up, NT)
        if step == 0:
            out_total[...] = out_part
            hidden_total[...] = hidden_part
        else:
            out_total[...] += out_part
            hidden_total[...] += hidden_part
        shrink_part = dot(active, tangent[...], TN).astype(BF16)
        (shrink_sent if j % 2 else shrink_kept)[j // 2] = shrink_part
        expand_part = dot(hidden_t[...], d_before).astype(BF16)
        for place in range(8):
            target = expand_sent if place % 2 else expand_kept
            target[place // 2, :, pl.ds(column, tile)] = expand_part[
                place * deep : (place + 1) * deep, :
            ]
    own_out[...] = out_total[:rows, :]
    other_out[...] = out_total[rows:, :].astype(BF16)
    own_hidden[...] = hidden_total[:rows, :]
    other_hidden[...] = hidden_total[rows:, :].astype(BF16)


def feed(ids, hidden, tangent, shift, expand, shrink):
    rows, width = hidden[0].shape
    wide = expand.shape[1]
    deep, tile = width // 8, wide // 8
    return pl.pallas_call(
        feed_kernel,
        name="feed",
        out_shape=(
            shape((rows, width), F32),
            shape((rows, width), BF16),
            shape((rows, width), F32),
            shape((rows, width), BF16),
            shape((1, wide), F32),
            shape((4, tile, width), BF16),
            shape((4, tile, width), BF16),
            shape((4, deep, wide), BF16),
            shape((4, deep, wide), BF16),
        ),
        in_specs=[SM] + [VM] * 7,
        out_specs=(VM,) * 9,
        scratch_shapes=[
            pltpu.VMEM((2 * rows, width), BF16),
            pltpu.VMEM((2 * rows, width), BF16),
            pltpu.VMEM((width, 2 * rows), BF16),
            pltpu.VMEM((2 * rows, width), F32),
            pltpu.VMEM((2 * rows, width), F32),
        ],
        compiler_params=params(60),
        cost_estimate=cost(24 * rows * width * wide, 8 * width * wide + 20 * rows * width, 2 * rows * wide),
    )(ids, *hidden, *tangent, shift, expand, shrink)


def branch_kernel(
    ids, attended, own_hidden, came_hidden, tangent, own_out, came_out, gain, shift, weight, *rest
):
    result, d_attended, d_branch = rest[:3]
    grads, (gain_grad, bias_grad, shift_grad) = rest[3:11], rest[11:14]
    rows = tangent.shape[1]
    width = gain.shape[1] // 4
    gain_total = bias_total = shift_total = 0.0
    for micro in range(2):
        span = slice(micro * rows, (micro + 1) * rows)
        value = attended[span, :]
        cot = tangent[micro].astype(F32)
        branch = own_out[span, :] + came_out[span, :].astype(F32) + shift[...]
        result[micro] = (value + branch).astype(BF16)
        unit, inverse = norm_parts(value)
        grad = own_hidden[span, :] + came_hidden[span, :].astype(F32)
        gain_total = gain_total + jnp.sum(grad * unit, axis=0, keepdims=True)
        bias_total = bias_total + jnp.sum(grad, axis=0, keepdims=True)
        shift_total = shift_total + jnp.sum(cot, axis=0, keepdims=True)
        total = cot + norm_back(grad, unit, inverse, gain[...])
        d_attended[span, :] = total
        d_branch[span, :] = total.astype(BF16)
    gain_grad[...] = gain_total
    bias_grad[...] = bias_total
    shift_grad[...] = shift_total
    for micro in range(2):
        for place in range(4):
            start = pl.multiple_of((ids[1] ^ place) * width, width)
            part = dot(d_branch[micro * rows : (micro + 1) * rows, :], weight[pl.ds(start, width), :], NT)
            grads[4 * micro + place][...] = part.astype(BF16)


def branch_back(ids, attended, own_hidden, came_hidden, tangent, own_out, came_out, gain, shift, weight):
    micro, rows, width = tangent.shape
    total = micro * rows
    row = shape((1, width), F32)
    return pl.pallas_call(
        branch_kernel,
        name="branch_back",
        out_shape=(
            shape(tangent.shape, BF16),
            shape((total, width), F32),
            shape((total, width), BF16),
        )
        + tuple(shape((rows, width // 4), BF16) for _ in range(8))
        + (row, row, row),
        in_specs=[SM] + [VM] * 9,
        out_specs=(VM,) * 14,
        compiler_params=params(),
        cost_estimate=cost(2 * total * width * width, 32 * total * width),
    )(ids, attended, own_hidden, came_hidden, tangent, own_out, came_out, gain, shift, weight)


def output_grad_kernel(ids, own_mixed, other_mixed, own_branch, other_branch, out):
    rows = out.shape[1]
    width = own_branch.shape[1]
    half = width // 2
    column = pl.multiple_of(ids[2] * half, half)
    right = own_branch[:, pl.ds(column, half)]
    for k in range(4):
        start = pl.multiple_of((ids[0] ^ (2 * k + ids[3])) * rows, rows)
        part = dot(own_mixed[:, pl.ds(start, rows)], right, TN)
        part += dot(other_mixed[:, pl.ds(start, rows)], other_branch[...], TN)
        out[k] = part.astype(BF16)


def output_grad(ids, own_mixed, other_mixed, own_branch, other_branch):
    total, width = own_mixed.shape
    return pl.pallas_call(
        output_grad_kernel,
        name="output_grad",
        out_shape=shape((4, width // 8, width // 2), BF16),
        in_specs=[SM] + [VM] * 4,
        out_specs=VM,
        compiler_params=params(),
        cost_estimate=cost(total * width * width, 8 * total * width),
    )(ids, own_mixed, other_mixed, own_branch, other_branch)


def triple_grad_kernel(ids, n0, n1, d0, d1, out):
    rows = out.shape[1]
    for k in range(4):
        column = pl.multiple_of((ids[0] ^ (2 * k + ids[3])) * rows, rows)
        part = dot(n0[:, pl.ds(column, rows)], d0[...], TN)
        part += dot(n1[:, pl.ds(column, rows)], d1[...], TN)
        out[k] = part.astype(BF16)


def triple_grad(ids, normed, grads):
    length, width = normed[0].shape
    columns = grads[0].shape[1]
    return pl.pallas_call(
        triple_grad_kernel,
        name="triple_grad",
        out_shape=shape((4, width // 8, columns), BF16),
        in_specs=[SM] + [VM] * 4,
        out_specs=VM,
        compiler_params=params(),
        cost_estimate=cost(2 * length * width * columns, 4 * length * (width + columns)),
    )(ids, *normed, *grads)


def first_back_kernel(tokens, d_attended, gain, *rest):
    parts, (grad_out, gain_grad, bias_grad) = rest[:6], rest[6:]
    rows = tokens.shape[1]
    gain_total = bias_total = 0.0
    for micro in range(2):
        one, two, three = parts[3 * micro : 3 * micro + 3]
        grad = one[...].astype(F32) + two[...].astype(F32) + three[...].astype(F32)
        unit, inverse = norm_parts(tokens[micro].astype(F32))
        gain_total = gain_total + jnp.sum(grad * unit, axis=0, keepdims=True)
        bias_total = bias_total + jnp.sum(grad, axis=0, keepdims=True)
        total = d_attended[micro * rows : (micro + 1) * rows, :]
        grad_out[micro] = (total + norm_back(grad, unit, inverse, gain[...])).astype(BF16)
    gain_grad[...] = gain_total
    bias_grad[...] = bias_total


def first_back(tokens, d_attended, gain, parts):
    micro, rows, width = tokens.shape
    row = shape((1, width), F32)
    return pl.pallas_call(
        first_back_kernel,
        name="first_back",
        out_shape=(shape(tokens.shape, BF16), row, row),
        in_specs=[VM] * 9,
        out_specs=(VM,) * 3,
        compiler_params=params(),
        cost_estimate=cost(20 * micro * rows * width, 16 * micro * rows * width),
    )(tokens, d_attended, gain, *parts)


def flip(index, bits):
    out, bit = index, 1
    while bit <= bits:
        if bits & bit:
            out = out + bit * (1 - 2 * lax.rem(lax.div(index, jnp.int32(bit)), jnp.int32(2)))
        bit *= 2
    return out


class Moves:
    def __init__(self, send, recv):
        self.send, self.recv, self.started = send, recv, []
        self.place = {"ctx": lax.axis_index("ctx"), "fsdp": lax.axis_index("fsdp")}

    def greet(self):
        barrier = pltpu.get_barrier_semaphore()
        partners = [("ctx", 1), ("ctx", 2), ("ctx", 3), ("fsdp", 1), ("fsdp", 2), ("fsdp", 4), ("fsdp", 6)]
        for axis, bits in partners:
            pl.semaphore_signal(
                barrier,
                inc=1,
                device_id={axis: flip(self.place[axis], bits)},
                device_id_type=pl.DeviceIdType.MESH,
            )
        pl.semaphore_wait(barrier, len(partners))

    def go(self, source, target, axis, bits):
        slot = len(self.started)
        move = pltpu.make_async_remote_copy(
            src_ref=source,
            dst_ref=target,
            send_sem=self.send.at[slot],
            recv_sem=self.recv.at[slot],
            device_id={axis: flip(self.place[axis], bits)},
            device_id_type=pl.DeviceIdType.MESH,
        )
        move.start()
        self.started.append(move)
        return move

    def close(self):
        for move in self.started:
            move.wait_send()


class Gather:
    def __init__(self, moves, part, view, local):
        self.moves, self.view = moves, view
        me = moves.place["fsdp"]
        self.along = [moves.go(part, view(me), "fsdp", 2 * k) for k in range(1, 4)]
        self.across = [moves.go(part, view(me), "fsdp", 1)]
        self.own = pltpu.make_async_copy(part, view(me), local)
        self.own.start()

    def forward(self):
        me = self.moves.place["fsdp"]
        for k in range(1, 4):
            self.along[k - 1].wait_recv()
            block = self.view(flip(me, 2 * k))
            self.across.append(self.moves.go(block, block, "fsdp", 1))

    def finish(self):
        for move in self.across:
            move.wait_recv()
        self.own.wait()


FORWARD_MOVES = 6 * 7 + 7 + 6 + 3 + 1 + 1 + 6 + 2


def row_view(ref, rows, columns=slice(None)):
    return lambda index: ref.at[pl.ds(pl.multiple_of(index * rows, rows), rows), columns]


def forward_kernel(
    global_ids,
    tokens,
    small,
    picks,
    triple_part,
    output_part,
    expand_part,
    shrink_part,
    tangent,
    small_all,
    triple_out,
    output_out,
    expand_all,
    shrink_all,
    tangent_other,
    triple,
    normed,
    block_bias,
    lse,
    mixed,
    joined_out,
    mixed_other,
    attended,
    hidden,
    hidden_other,
    parts,
    small_held,
    picks_held,
    triple_held,
    output_held,
    joined,
    hidden_held,
    send,
    recv,
    local,
):
    moves = Moves(send, recv)
    rank, me = moves.place["ctx"], moves.place["fsdp"]
    core = lax.rem(rank, jnp.int32(2))
    micro, rows, width = tokens.shape
    half = width // 2
    quarter = width // 4
    shard = triple_part.shape[0]
    wide = expand_part.shape[1]
    deep = shrink_part.shape[0]
    moves.greet()

    small_gather = Gather(moves, small, lambda index: small_held.at[index], local.at[0])
    near = [moves.go(tokens.at[0], parts.at[0, 1], "ctx", 1)]
    far = [moves.go(tokens.at[0], parts.at[0, 2], "ctx", 2)]
    triple_gather = Gather(moves, triple_part, row_view(triple_held, shard), local.at[1])
    picked = [moves.go(picks.at[p], picks_held.at[p], "ctx", p) for p in range(1, 4)]
    near.append(moves.go(tokens.at[1], parts.at[1, 1], "ctx", 1))
    far.append(moves.go(tokens.at[1], parts.at[1, 2], "ctx", 2))
    small_gather.forward()
    triple_gather.forward()
    output_gather = Gather(
        moves, output_part, row_view(output_held, shard, pl.ds(core * half, half)), local.at[2]
    )
    cut = wide // 2
    chunks = [
        (shrink_part.at[: deep // 2, :], lambda i: shrink_all.at[pl.ds(pl.multiple_of(i * deep, deep), deep // 2), :]),
        (expand_part.at[:, :cut], row_view(expand_all, shard, slice(0, cut))),
        (
            shrink_part.at[deep // 2 :, :],
            lambda i: shrink_all.at[pl.ds(pl.multiple_of(i * deep + deep // 2, deep // 2), deep // 2), :],
        ),
        (expand_part.at[:, cut:], row_view(expand_all, shard, slice(cut, wide))),
    ]
    gathers = [Gather(moves, *chunks[0], local.at[3])]
    tangent_move = moves.go(tangent, tangent_other, "ctx", 1)

    for move in picked:
        move.wait_recv()
    count = block_bias.shape[2]
    each = count // 4
    ranks = [flip(rank, p) if p else rank for p in range(4)]
    key_row = lax.broadcasted_iota(jnp.int32, (count, rows), 0)
    key_place = key_row // each
    key_rank = ranks[0]
    for p in range(1, 4):
        key_rank = jnp.where(key_place == p, ranks[p], key_rank)
    key_block = key_rank * each + key_row % each
    lane = lax.broadcasted_iota(jnp.int32, (count, rows), 1) // BLOCK
    for step in range(micro):
        first, second = global_ids[step, 0], global_ids[step, 1]
        key_global = (key_block == first) | (key_block == second)
        for p in range(4):
            source = picks.at[0] if p == 0 else picks_held.at[p]
            query_block = ranks[p] * each + lane
            base = key_global | (jnp.abs(query_block - key_block) <= 1)
            base = base | (query_block == first) | (query_block == second)
            for head in range(block_bias.shape[1]):
                hit = base
                for pick in range(3):
                    hit = hit | (source[step, head, pick : pick + 1, :] == key_block)
                block_bias[step, head, :, p * rows : (p + 1) * rows] = jnp.where(hit, 0.0, -1e30)

    small_gather.finish()
    small_all[...] = small_held[...]

    def vector(line):
        return jnp.concatenate([small_held[b, line : line + 1, :] for b in range(8)], axis=1)

    gain_one, bias_one, gain_two, bias_two = (vector(line) for line in range(4))

    for step in range(micro):
        far[step].wait_recv()
        near.append(moves.go(parts.at[step, 2], parts.at[step, 3], "ctx", 1))
    mixed_moves = []
    for step in range(micro):
        near[step].wait_recv()
        near[2 + step].wait_recv()
        for p in range(4):
            source = tokens[step] if p == 0 else parts[step, p]
            normed[step, p * rows : (p + 1) * rows, :] = normalize(source, gain_one, bias_one)
        if step == 0:
            triple_gather.finish()
        for p in range(4):
            span = slice(p * rows, (p + 1) * rows)
            triple[step, span, :] = dot(normed[step, span, :], triple_held[...]).astype(BF16)
        if step == 0:
            output_gather.forward()
            gathers.append(Gather(moves, *chunks[1], local.at[4]))
        else:
            output_gather.finish()
            piece = output_held.at[:, pl.ds(core * half, half)]
            output_move = moves.go(piece, piece, "ctx", 1)
            gathers[1].forward()
            gathers.append(Gather(moves, *chunks[3], local.at[6]))
        attend_body(triple.at[step], block_bias.at[step], mixed.at[step], lse.at[step])
        own = pl.ds(pl.multiple_of(rank * quarter, quarter), quarter)
        span = slice(step * rows, (step + 1) * rows)
        joined[span, own] = mixed[step, 0]
        for p in range(1, 4):
            mixed_moves.append(moves.go(mixed.at[step, p], joined.at[span, own], "ctx", p))
        if step == 0:
            gathers[0].forward()
            gathers.append(Gather(moves, *chunks[2], local.at[5]))
    output_move.wait_recv()
    for move in mixed_moves:
        move.wait_recv()
    keep = [
        pltpu.make_async_copy(triple_held, triple_out, local.at[7]),
        pltpu.make_async_copy(output_held, output_out, local.at[8]),
    ]
    for copy in keep:
        copy.start()
    output_kernel(tokens, joined, gain_two, bias_two, output_held, attended, hidden_held)
    last = [
        moves.go(hidden_held, hidden_other, "ctx", 1),
        moves.go(joined, mixed_other, "ctx", 1),
    ]
    hidden[...] = hidden_held[...]
    joined_out[...] = joined[...]
    gathers[2].forward()
    gathers[3].forward()
    for gather in gathers:
        gather.finish()
    for move in [tangent_move] + last:
        move.wait_recv()
    for copy in keep:
        copy.wait()
    moves.close()


def forward_together(global_ids, tokens, small, picks, triple_part, output_part, expand_part, shrink_part, tangent):
    micro, rows, width = tokens.shape
    total = micro * rows
    columns = triple_part.shape[1]
    wide = expand_part.shape[1]
    length = 4 * rows
    heads = picks.shape[2]
    outs = (
        (VM, (8,) + small.shape, F32),
        (ANY, (width, columns), BF16),
        (ANY, (width, width), BF16),
        (ANY, (width, wide), BF16),
        (ANY, (wide, width), BF16),
        (ANY, (total, width), BF16),
        (VM, (micro, length, columns), BF16),
        (VM, (micro, length, width), BF16),
        (VM, (micro, heads, length // BLOCK, length), F32),
        (VM, (micro, 8, length), F32),
        (VM, (micro, 4, rows, width // 4), BF16),
        (VM, (total, width), BF16),
        (ANY, (total, width), BF16),
        (VM, (total, width), F32),
        (VM, (total, width), BF16),
        (ANY, (total, width), BF16),
    )
    return pl.pallas_call(
        forward_kernel,
        name="forward_together",
        out_shape=tuple(shape(dims, kind) for _, dims, kind in outs),
        in_specs=[SM] + [VM] * 3 + [ANY] * 5,
        out_specs=tuple(spec for spec, _, _ in outs),
        scratch_shapes=[
            pltpu.VMEM((micro, 4, rows, width), BF16),
            pltpu.VMEM((8,) + small.shape, F32),
            pltpu.VMEM(picks.shape, jnp.int32),
            pltpu.VMEM((width, columns), BF16),
            pltpu.VMEM((width, width), BF16),
            pltpu.VMEM((total, width), BF16),
            pltpu.VMEM((total, width), BF16),
            pltpu.SemaphoreType.DMA((FORWARD_MOVES,)),
            pltpu.SemaphoreType.DMA((FORWARD_MOVES,)),
            pltpu.SemaphoreType.DMA((9,)),
        ],
        compiler_params=pltpu.CompilerParams(
            collective_id=0, has_side_effects=True, vmem_limit_bytes=56 * MIB
        ),
        cost_estimate=cost(16 * total * width * width, 64 * MIB),
    )(global_ids, tokens, small, picks, triple_part, output_part, expand_part, shrink_part, tangent)


def block_biases(chosen, globals_here, rank, local_blocks):
    heads, count, _ = chosen.shape
    place = jnp.arange(count, dtype=jnp.int32)
    true_block = ((place // local_blocks) ^ rank) * local_blocks + place % local_blocks
    near = jnp.abs(true_block[:, None] - true_block[None, :]) <= 1
    is_global = jnp.any(true_block[:, None] == globals_here[None, :], axis=1)
    picked = jnp.any(chosen[:, None, :, :] == true_block[None, :, None, None], axis=3)
    allowed = near[None] | picked | is_global[None, :, None] | is_global[None, None, :]
    bias = jnp.where(allowed, 0.0, -1e30).astype(F32)
    return jnp.repeat(bias, BLOCK, axis=2)


def on_device(
    tokens,
    cotangent,
    random_blocks,
    global_blocks,
    attend_gain,
    attend_bias,
    triple_weight,
    output_weight,
    hidden_gain,
    hidden_bias,
    expand_weight,
    expand_bias,
    shrink_weight,
    shrink_bias,
):
    tokens, cotangent = tokens[:, 0], cotangent[:, 0]
    micro, rows, width = tokens.shape
    total = micro * rows
    ways = lax.axis_size("fsdp")
    fsdp = lax.axis_index("fsdp")
    rank = lax.axis_index("ctx")
    core = rank % 2
    place = place_id()
    heads_all = random_blocks.shape[2]
    own_heads = heads_all // 4
    local_blocks = rows // BLOCK
    shard = width // ways
    wide = expand_weight.shape[1]
    deep = shrink_weight.shape[0]
    ids = jnp.stack([place, rank, core, jnp.int32(0)])
    ids_sent = jnp.stack([place, rank, core, jnp.int32(1)])

    half_units = wide // (2 * ways)
    vectors = [attend_gain, attend_bias, hidden_gain, hidden_bias, shrink_bias]
    triple_part = jnp.concatenate(
        [
            lax.dynamic_slice_in_dim(triple_weight, k * width + rank * (width // 4), width // 4, 1)
            for k in range(3)
        ],
        axis=1,
    )
    output_part = lax.dynamic_slice_in_dim(output_weight, core * (width // 2), width // 2, 1)
    expand_part = jnp.concatenate(
        [
            lax.dynamic_slice_in_dim(expand_weight, (2 * k + core) * half_units, half_units, 1)
            for k in range(ways)
        ],
        axis=1,
    )
    shrink_part = lax.dynamic_slice_in_dim(shrink_weight, core * (deep // 2), deep // 2, 0)
    tangent_own = cotangent.reshape(total, width)
    picks = random_blocks[:, 0]
    if ways == 8:
        small = jnp.concatenate(
            [v.reshape(1, shard) for v in vectors]
            + [expand_bias.reshape(-1, shard), jnp.zeros((7, shard), BF16)]
        ).astype(F32)
        sets = picks.reshape(micro, 4, own_heads, local_blocks, -1).transpose(1, 0, 2, 4, 3)
        order = [rank ^ p for p in range(4)]
        sets = jnp.concatenate([lax.dynamic_slice_in_dim(sets, r, 1, 0) for r in order], axis=0)
        sets = jnp.pad(jnp.repeat(sets, BLOCK, axis=4), ((0, 0),) * 3 + ((0, 5), (0, 0)))
        (
            table,
            triple_full,
            output_full,
            expand_full,
            shrink_full,
            tangent_other,
            triples,
            normeds,
            biases,
            lses,
            mixed_own,
            mixed_all,
            mixed_other,
            attended,
            hidden,
            hidden_other,
        ) = forward_together(
            global_blocks[:, 0],
            tokens,
            small,
            sets,
            triple_part,
            output_part,
            expand_part,
            shrink_part,
            tangent_own,
        )
        gain_one, bias_one, gain_two, bias_two, shift_out = (
            table[:, k].reshape(1, width) for k in range(5)
        )
        shift_in = lax.dynamic_slice_in_dim(
            table[:, 5:9].reshape(8, 2, half_units), core, 1, 1
        ).reshape(1, wide // 2)
    else:

        def whole(part):
            return lax.all_gather(part, "fsdp", axis=0, tiled=True)

        gain_one, bias_one, gain_two, bias_two, shift_out = (
            whole(v).astype(F32).reshape(1, width) for v in vectors
        )
        halves = whole(expand_bias).astype(F32).reshape(ways, 2, half_units)
        shift_in = jnp.where(core == 0, halves[:, 0], halves[:, 1]).reshape(1, wide // 2)
        triple_full, expand_full, shrink_full = whole(triple_part), whole(expand_part), whole(shrink_part)
        output_full = whole(output_weight)
        tangent_other = swap(tangent_own, "ctx", 1)
        far_picks = swap(picks, "ctx", 2)
        all_picks = jnp.stack([picks, swap(picks, "ctx", 1), far_picks, swap(far_picks, "ctx", 1)])
        chosen = lax.dynamic_slice_in_dim(all_picks, rank * own_heads, own_heads, 2)
        chosen = chosen.transpose(1, 2, 0, 3, 4).reshape(micro, own_heads, 4 * local_blocks, -1)
        triples, normeds, biases, lses, mixed_own, joined = [], [], [], [], [], []
        for step in range(micro):
            biases.append(block_biases(chosen[step], global_blocks[step, 0], rank, local_blocks))
            near, far = swap(tokens[step], "ctx", 1), swap(tokens[step], "ctx", 2)
            places = (tokens[step], near, far, swap(far, "ctx", 1))
            triple, normed = project(places, gain_one, bias_one, triple_full)
            mixed, lse = attend(triple, biases[step])
            here = [mixed[0]] + [swap(mixed[p], "ctx", p) for p in range(1, 4)]
            for low_bit, high in ((core == 1, False), (rank >= 2, True)):
                pairs = ((0, 2), (1, 3)) if high else ((0, 1), (2, 3))
                for one, two in pairs:
                    first = jnp.where(low_bit, here[two], here[one])
                    here[two] = jnp.where(low_bit, here[one], here[two])
                    here[one] = first
            joined.append(jnp.concatenate(here, axis=1))
            for kept, value in zip(
                (triples, normeds, lses, mixed_own), (triple, normed, lse, mixed)
            ):
                kept.append(value)
        mixed_all = jnp.concatenate(joined, axis=0)
        mixed_other = swap(mixed_all, "ctx", 1)
        attended, hidden = output_project(tokens, mixed_all, gain_two, bias_two, output_full)
        hidden_other = swap(hidden, "ctx", 1)

    (
        own_out,
        other_out,
        own_hidden,
        other_hidden,
        shift_in_grad,
        shrink_sent,
        shrink_kept,
        expand_sent,
        expand_kept,
    ) = feed(ids, (hidden, hidden_other), (tangent_own, tangent_other), shift_in, expand_full, shrink_full)
    came_hidden = swap(other_hidden, "ctx", 1)
    came_out = swap(other_out, "ctx", 1)
    shrink_mine = scatter_rows(shrink_kept, shrink_sent)
    expand_mine = scatter_rows(expand_kept, expand_sent)
    result, d_attended, d_branch, *grads, gain_two_grad, bias_two_grad, shift_out_grad = branch_back(
        ids,
        attended,
        own_hidden,
        came_hidden,
        cotangent,
        own_out,
        came_out,
        gain_two,
        shift_out,
        output_full,
    )
    half_sent = lax.dynamic_slice_in_dim(d_branch, (1 - core) * (width // 2), width // 2, 1)
    branch_other = swap(half_sent, "ctx", 1)
    output_sent = output_grad(ids_sent, mixed_all, mixed_other, d_branch, branch_other)
    output_kept = output_grad(ids, mixed_all, mixed_other, d_branch, branch_other)
    output_mine = scatter_rows(output_kept, output_sent)

    d_triples, norm_parts_here = [], []
    for step in range(micro):
        here = grads[4 * step : 4 * step + 4]
        here = [here[0]] + [swap(here[p], "ctx", p) for p in range(1, 4)]
        d_triple, parts = attend_back(
            triples[step], biases[step], lses[step], here, mixed_own[step], triple_full
        )
        d_triples.append(d_triple)
        near = swap(parts[1], "ctx", 1)
        far = wide_add(parts[2], swap(parts[3], "ctx", 1)).astype(BF16)
        norm_parts_here += [parts[0], near, swap(far, "ctx", 2)]
    normed_pair = (normeds[0], normeds[1])
    triple_sent = triple_grad(ids_sent, normed_pair, d_triples)
    triple_kept = triple_grad(ids, normed_pair, d_triples)
    triple_mine = scatter_rows(triple_kept, triple_sent)
    token_grad, gain_one_grad, bias_one_grad = first_back(
        tokens, d_attended, gain_one, norm_parts_here
    )

    halves = shift_in_grad.reshape(ways, 1, wide // (2 * ways))
    blank = jnp.zeros_like(halves)
    spread = jnp.where(
        core == 0,
        jnp.concatenate([halves, blank], axis=1),
        jnp.concatenate([blank, halves], axis=1),
    )
    early = sum_everywhere(
        jnp.concatenate(
            [
                gain_two_grad.reshape(ways, shard),
                bias_two_grad.reshape(ways, shard),
                shift_out_grad.reshape(ways, shard),
                spread.reshape(ways, wide // ways),
            ],
            axis=1,
        )
    )
    late = sum_everywhere(
        jnp.concatenate([gain_one_grad.reshape(ways, shard), bias_one_grad.reshape(ways, shard)], axis=1)
    )
    early = lax.dynamic_index_in_dim(early, fsdp, 0, keepdims=False)
    late = lax.dynamic_index_in_dim(late, fsdp, 0, keepdims=False)

    def over_chips(part):
        low = part.astype(BF16)
        return wide_add(low, swap(low, "ctx", 2))

    def both(own, axis):
        other = swap(own, "ctx", 1)
        first = jnp.where(core == 0, own, other)
        second = jnp.where(core == 0, other, own)
        return jnp.stack([first, second], axis=axis)

    shrink_grad = both(over_chips(shrink_mine), 0).reshape(deep, width)
    expand_half = over_chips(expand_mine).reshape(shard, ways, wide // (2 * ways))
    expand_grad = both(expand_half, 2).reshape(shard, wide)
    output_grad_all = both(over_chips(output_mine), 1).reshape(shard, width)
    low = triple_mine.astype(BF16).reshape(shard, 3, width // 4)
    far = swap(low, "ctx", 2)
    pair = jnp.stack([jnp.where(rank < 2, low, far), jnp.where(rank < 2, far, low)], axis=2)
    triple_grad_all = both(pair, 3).reshape(shard, 3 * width).astype(F32)

    return (
        result[:, None],
        token_grad[:, None],
        late[:shard],
        late[shard:],
        triple_grad_all,
        output_grad_all,
        early[:shard],
        early[shard : 2 * shard],
        expand_grad,
        early[3 * shard :],
        shrink_grad,
        early[2 * shard : 3 * shard],
    )


def solution(mesh):
    token_spec = P(None, "fsdp", "ctx", None)
    flat, rows = P("fsdp"), P("fsdp", None)
    return jax.shard_map(
        on_device,
        mesh=mesh,
        in_specs=(
            token_spec,
            token_spec,
            P(None, "fsdp", None, "ctx", None),
            P(None, "fsdp", None),
            flat,
            flat,
            rows,
            rows,
            flat,
            flat,
            rows,
            flat,
            rows,
            flat,
        ),
        out_specs=(
            token_spec,
            token_spec,
            flat,
            flat,
            rows,
            rows,
            flat,
            flat,
            rows,
            flat,
            rows,
            flat,
        ),
        check_vma=False,
    )
```

```python
import functools

import jax
import jax.numpy as jnp
from jax import lax
from jax.experimental import pallas as pl
from jax.experimental.pallas import tpu as pltpu
from jax.sharding import PartitionSpec as P

HEAD_DIM = 64
BLOCK = 64
EPSILON = 1e-05
F32 = jnp.float32
BF16 = jnp.bfloat16
MIB = 1 << 20

VM = pl.BlockSpec(memory_space=pltpu.VMEM)
SM = pl.BlockSpec(memory_space=pltpu.SMEM)
ANY = pl.BlockSpec(memory_space=pl.ANY)

NN = (((1,), (0,)), ((), ()))
NT = (((1,), (1,)), ((), ()))
TN = (((0,), (0,)), ((), ()))


def dot(left, right, dims=NN):
    return lax.dot_general(left, right, dims, preferred_element_type=F32)


def shape(dims, kind):
    return jax.ShapeDtypeStruct(dims, kind)


def params(limit=56):
    return pltpu.CompilerParams(vmem_limit_bytes=limit * MIB)


def cost(flops, moved, special=0):
    return pl.CostEstimate(flops=flops, bytes_accessed=moved, transcendentals=special)


def swap(value, axis, step):
    size = lax.axis_size(axis)
    return lax.ppermute(value, axis, [(i, i ^ step) for i in range(size)])


def place_id():
    return lax.axis_index("fsdp") if lax.axis_size("fsdp") == 8 else jnp.int32(1)


def wide_add(*terms):
    total = terms[0].astype(F32)
    for term in terms[1:]:
        total = total + term.astype(F32)
    return total


def scatter_rows(kept, sent):
    whole = jnp.stack([sent, kept], axis=1)
    whole = whole.reshape((8 * kept.shape[1],) + kept.shape[2:])
    return lax.psum_scatter(whole.astype(F32), "fsdp", scatter_dimension=0, tiled=True)


def sum_everywhere(vector):
    return lax.psum(vector, ("ctx", "fsdp"))


def norm_parts(values):
    average = jnp.mean(values, axis=-1, keepdims=True)
    centered = values - average
    variance = jnp.mean(centered * centered, axis=-1, keepdims=True)
    inverse = lax.rsqrt(variance + EPSILON)
    return centered * inverse, inverse


def norm_back(grad, unit, inverse, gain):
    scaled = grad * gain
    first = jnp.mean(scaled, axis=-1, keepdims=True)
    second = jnp.mean(scaled * unit, axis=-1, keepdims=True)
    return inverse * (scaled - first - unit * second)


def normalize(source, gain, bias):
    unit, _ = norm_parts(source.astype(F32))
    return (unit * gain + bias).astype(BF16)


def project_kernel(t0, t1, t2, t3, gain, bias, weight, triple, normed):
    rows = t0.shape[0]
    for place, part in enumerate((t0, t1, t2, t3)):
        span = slice(place * rows, (place + 1) * rows)
        normed[span, :] = normalize(part[...], gain[...], bias[...])
        triple[span, :] = dot(normed[span, :], weight[...]).astype(BF16)


def project(parts, gain, bias, weight):
    rows, width = parts[0].shape
    columns = weight.shape[1]
    return pl.pallas_call(
        project_kernel,
        name="project",
        out_shape=(shape((4 * rows, columns), BF16), shape((4 * rows, width), BF16)),
        in_specs=[VM] * 7,
        out_specs=(VM, VM),
        compiler_params=params(),
        cost_estimate=cost(8 * rows * width * columns, 12 * rows * width + 2 * width * columns),
    )(*parts, gain, bias, weight)


def head_mask(rows):
    return lax.broadcasted_iota(jnp.int32, (rows, 2 * HEAD_DIM), 1) // HEAD_DIM


def attend_body(triple, block_bias, mixed, lse):
    length = triple.shape[0]
    width = triple.shape[1] // 3
    rows = length // 4
    blocks = length // BLOCK
    for pair in range(width // 128):
        keys = triple[:, width + pair * 128 : width + pair * 128 + 128]
        values = triple[:, 2 * width + pair * 128 : 2 * width + pair * 128 + 128]
        values_t = values.astype(F32).T.astype(BF16)

        def step(place, carry):
            start = pl.multiple_of(place * rows, rows)
            queries = triple[pl.ds(start, rows), pair * 128 : pair * 128 + 128]
            queries = queries * jnp.asarray(0.125, BF16)
            side = head_mask(rows)
            halves = []
            for which in range(2):
                head = 2 * pair + which
                one = jnp.where(side == which, queries, jnp.zeros_like(queries))
                scores = dot(keys, one, NT)
                shift = block_bias[head, :, pl.ds(start, rows)]
                scores = scores.reshape(blocks, BLOCK, rows) + shift[:, None, :]
                peak = jnp.max(jnp.max(scores, axis=0), axis=0, keepdims=True)
                powered = jnp.exp(scores - peak[None])
                total = jnp.sum(jnp.sum(powered, axis=0), axis=0, keepdims=True)
                lse[head : head + 1, pl.ds(start, rows)] = peak + jnp.log(total)
                low = powered.astype(BF16).reshape(length, rows)
                part = dot(values_t[which * HEAD_DIM : (which + 1) * HEAD_DIM, :], low)
                halves.append(part / total)
            joined = jnp.concatenate(halves, axis=0)
            mixed[place, :, pair * 128 : pair * 128 + 128] = joined.T.astype(BF16)
            return carry

        lax.fori_loop(0, 4, step, 0)


def attend(triple, block_bias):
    length, columns = triple.shape
    width = columns // 3
    heads = width // HEAD_DIM
    rows = length // 4
    return pl.pallas_call(
        attend_body,
        name="attend",
        out_shape=(shape((4, rows, width), BF16), shape((8, length), F32)),
        in_specs=[VM, VM],
        out_specs=(VM, VM),
        compiler_params=params(),
        cost_estimate=cost(
            32 * heads * length * length * HEAD_DIM, 8 * length * width, heads * length * length
        ),
    )(triple, block_bias)


def attend_back_body(triple, block_bias, lse, grads, mixed, d_triple, key_total, value_total):
    length = triple.shape[0]
    width = triple.shape[1] // 3
    rows = length // 4
    blocks = length // BLOCK
    for pair in range(width // 128):
        lanes = slice(pair * 128, pair * 128 + 128)
        keys = triple[:, width + pair * 128 : width + pair * 128 + 128]
        values = triple[:, 2 * width + pair * 128 : 2 * width + pair * 128 + 128]
        keys_t = keys.astype(F32).T.astype(BF16)
        key_total[...] = jnp.zeros_like(key_total)
        value_total[...] = jnp.zeros_like(value_total)

        def step(place, carry):
            start = pl.multiple_of(place * rows, rows)
            queries = triple[pl.ds(start, rows), lanes] * jnp.asarray(0.125, BF16)
            grad = grads[place, :, lanes]
            product = (grad.astype(F32) * mixed[place, :, lanes].astype(F32)).T
            side = head_mask(rows)
            halves = []
            for which in range(2):
                head = 2 * pair + which
                one = jnp.where(side == which, queries, jnp.zeros_like(queries))
                one_grad = jnp.where(side == which, grad, jnp.zeros_like(grad))
                delta = jnp.sum(
                    product[which * HEAD_DIM : (which + 1) * HEAD_DIM, :], axis=0, keepdims=True
                )
                scores = dot(keys, one, NT)
                shift = block_bias[head, :, pl.ds(start, rows)] - lse[head : head + 1, pl.ds(start, rows)]
                exact = jnp.exp(scores.reshape(blocks, BLOCK, rows) + shift[:, None, :])
                exact = exact.reshape(length, rows)
                value_total[...] += dot(exact.astype(BF16), one_grad)
                d_probs = dot(values, one_grad, NT)
                d_scores = (exact * (d_probs - delta)).astype(BF16)
                key_total[...] += dot(d_scores, one)
                halves.append(dot(keys_t[which * HEAD_DIM : (which + 1) * HEAD_DIM, :], d_scores))
            joined = jnp.concatenate(halves, axis=0) * 0.125
            d_triple[pl.ds(start, rows), lanes] = joined.T.astype(BF16)
            return carry

        lax.fori_loop(0, 4, step, 0)
        d_triple[:, width + pair * 128 : width + pair * 128 + 128] = key_total[...].astype(BF16)
        d_triple[:, 2 * width + pair * 128 : 2 * width + pair * 128 + 128] = value_total[
            ...
        ].astype(BF16)


def attend_back_kernel(triple, block_bias, lse, g0, g1, g2, g3, mixed, weight, d_triple, norm_grad, grads, key_total, value_total):
    rows = g0.shape[0]
    for place, part in enumerate((g0, g1, g2, g3)):
        grads[place] = part[...]
    attend_back_body(triple, block_bias, lse, grads, mixed, d_triple, key_total, value_total)
    for place in range(4):
        part = dot(d_triple[place * rows : (place + 1) * rows, :], weight[...], NT)
        norm_grad[place] = part.astype(BF16)


def attend_back(triple, block_bias, lse, grads, mixed, weight):
    length, columns = triple.shape
    width = columns // 3
    heads = width // HEAD_DIM
    rows = length // 4
    return pl.pallas_call(
        attend_back_kernel,
        name="attend_back",
        out_shape=(shape((length, columns), BF16), shape((4, rows, weight.shape[0]), BF16)),
        in_specs=[VM] * 9,
        out_specs=(VM,) * 2,
        scratch_shapes=[
            pltpu.VMEM((4, rows, width), BF16),
            pltpu.VMEM((length, 128), F32),
            pltpu.VMEM((length, 128), F32),
        ],
        compiler_params=params(),
        cost_estimate=cost(
            80 * heads * length * length * HEAD_DIM, 16 * length * width, heads * length * length
        ),
    )(triple, block_bias, lse, *grads, mixed, weight)


def output_kernel(tokens, joined, gain, bias, weight, attended, normed):
    rows = tokens.shape[1]
    for micro in range(2):
        span = slice(micro * rows, (micro + 1) * rows)
        value = tokens[micro].astype(F32) + dot(joined[span, :], weight[...])
        attended[span, :] = value
        normed[span, :] = normalize(value, gain[...], bias[...])


def output_project(tokens, joined, gain, bias, weight):
    micro, rows, width = tokens.shape
    total = micro * rows
    return pl.pallas_call(
        output_kernel,
        name="output_project",
        out_shape=(shape((total, width), F32), shape((total, width), BF16)),
        in_specs=[VM] * 5,
        out_specs=(VM, VM),
        compiler_params=params(),
        cost_estimate=cost(2 * total * width * width, 12 * total * width + 2 * width * width),
    )(tokens, joined, gain, bias, weight)


CURVE = 0.7978845608028654
CUBIC = 0.044715


def feed_kernel(ids, h0, h1, c0, c1, shift, *rest):
    expand_held, shrink_held = rest[:2]
    own_out, other_out, own_hidden, other_hidden, bias_grad = rest[2:7]
    shrink_sent, shrink_kept, expand_sent, expand_kept = rest[7:11]
    hidden, tangent, hidden_t, out_total, hidden_total = rest[11:]
    base = ids[0]
    rows, width = h0.shape
    tile = shrink_held.shape[0] // 8
    deep = width // 8
    hidden[:rows, :] = h0[...]
    hidden[rows:, :] = h1[...]
    tangent[:rows, :] = c0[...]
    tangent[rows:, :] = c1[...]
    for j in range(8):
        source = pl.multiple_of((base ^ j) * deep, deep)
        hidden_t[j * deep : (j + 1) * deep, :] = (
            hidden[:, pl.ds(source, deep)].astype(F32).T.astype(BF16)
        )
    for step, j in enumerate((1, 3, 5, 7, 0, 2, 4, 6)):
        column = pl.multiple_of((base ^ j) * tile, tile)
        up = expand_held[:, pl.ds(column, tile)]
        down = shrink_held[pl.ds(column, tile), :]
        before = dot(hidden[...], up) + shift[:, pl.ds(column, tile)]
        d_active = dot(tangent[...], down, NT)
        square = before * before
        bend = jnp.tanh(CURVE * before * (1.0 + CUBIC * square))
        plus = 0.5 * (1.0 + bend)
        active = (before * plus).astype(BF16)
        slope = plus + (0.5 * CURVE) * before * (1.0 - bend * bend) * (1.0 + 3 * CUBIC * square)
        d_before = (d_active * slope).astype(BF16)
        bias_grad[:, pl.ds(column, tile)] = jnp.sum(d_before.astype(F32), axis=0, keepdims=True)
        out_part = dot(active, down)
        hidden_part = dot(d_before, up, NT)
        if step == 0:
            out_total[...] = out_part
            hidden_total[...] = hidden_part
        else:
            out_total[...] += out_part
            hidden_total[...] += hidden_part
        shrink_part = dot(active, tangent[...], TN).astype(BF16)
        (shrink_sent if j % 2 else shrink_kept)[j // 2] = shrink_part
        expand_part = dot(hidden_t[...], d_before).astype(BF16)
        for place in range(8):
            target = expand_sent if place % 2 else expand_kept
            target[place // 2, :, pl.ds(column, tile)] = expand_part[
                place * deep : (place + 1) * deep, :
            ]
    own_out[...] = out_total[:rows, :]
    other_out[...] = out_total[rows:, :].astype(BF16)
    own_hidden[...] = hidden_total[:rows, :]
    other_hidden[...] = hidden_total[rows:, :].astype(BF16)


def feed(ids, hidden, tangent, shift, expand, shrink):
    rows, width = hidden[0].shape
    wide = expand.shape[1]
    deep, tile = width // 8, wide // 8
    return pl.pallas_call(
        feed_kernel,
        name="feed",
        out_shape=(
            shape((rows, width), F32),
            shape((rows, width), BF16),
            shape((rows, width), F32),
            shape((rows, width), BF16),
            shape((1, wide), F32),
            shape((4, tile, width), BF16),
            shape((4, tile, width), BF16),
            shape((4, deep, wide), BF16),
            shape((4, deep, wide), BF16),
        ),
        in_specs=[SM] + [VM] * 7,
        out_specs=(VM,) * 9,
        scratch_shapes=[
            pltpu.VMEM((2 * rows, width), BF16),
            pltpu.VMEM((2 * rows, width), BF16),
            pltpu.VMEM((width, 2 * rows), BF16),
            pltpu.VMEM((2 * rows, width), F32),
            pltpu.VMEM((2 * rows, width), F32),
        ],
        compiler_params=params(60),
        cost_estimate=cost(24 * rows * width * wide, 8 * width * wide + 20 * rows * width, 2 * rows * wide),
    )(ids, *hidden, *tangent, shift, expand, shrink)


def branch_kernel(
    ids, attended, own_hidden, came_hidden, tangent, own_out, came_out, gain, shift, weight, *rest
):
    result, d_attended, d_branch = rest[:3]
    grads, (gain_grad, bias_grad, shift_grad) = rest[3:11], rest[11:14]
    rows = tangent.shape[1]
    width = gain.shape[1] // 4
    gain_total = bias_total = shift_total = 0.0
    for micro in range(2):
        span = slice(micro * rows, (micro + 1) * rows)
        value = attended[span, :]
        cot = tangent[micro].astype(F32)
        branch = own_out[span, :] + came_out[span, :].astype(F32) + shift[...]
        result[micro] = (value + branch).astype(BF16)
        unit, inverse = norm_parts(value)
        grad = own_hidden[span, :] + came_hidden[span, :].astype(F32)
        gain_total = gain_total + jnp.sum(grad * unit, axis=0, keepdims=True)
        bias_total = bias_total + jnp.sum(grad, axis=0, keepdims=True)
        shift_total = shift_total + jnp.sum(cot, axis=0, keepdims=True)
        total = cot + norm_back(grad, unit, inverse, gain[...])
        d_attended[span, :] = total
        d_branch[span, :] = total.astype(BF16)
    gain_grad[...] = gain_total
    bias_grad[...] = bias_total
    shift_grad[...] = shift_total
    for micro in range(2):
        for place in range(4):
            start = pl.multiple_of((ids[1] ^ place) * width, width)
            part = dot(d_branch[micro * rows : (micro + 1) * rows, :], weight[pl.ds(start, width), :], NT)
            grads[4 * micro + place][...] = part.astype(BF16)


def branch_back(ids, attended, own_hidden, came_hidden, tangent, own_out, came_out, gain, shift, weight):
    micro, rows, width = tangent.shape
    total = micro * rows
    row = shape((1, width), F32)
    return pl.pallas_call(
        branch_kernel,
        name="branch_back",
        out_shape=(
            shape(tangent.shape, BF16),
            shape((total, width), F32),
            shape((total, width), BF16),
        )
        + tuple(shape((rows, width // 4), BF16) for _ in range(8))
        + (row, row, row),
        in_specs=[SM] + [VM] * 9,
        out_specs=(VM,) * 14,
        compiler_params=params(),
        cost_estimate=cost(2 * total * width * width, 32 * total * width),
    )(ids, attended, own_hidden, came_hidden, tangent, own_out, came_out, gain, shift, weight)


def output_grad_kernel(ids, own_mixed, other_mixed, own_branch, other_branch, out):
    rows = out.shape[1]
    width = own_branch.shape[1]
    half = width // 2
    column = pl.multiple_of(ids[2] * half, half)
    right = own_branch[:, pl.ds(column, half)]
    for k in range(4):
        start = pl.multiple_of((ids[0] ^ (2 * k + ids[3])) * rows, rows)
        part = dot(own_mixed[:, pl.ds(start, rows)], right, TN)
        part += dot(other_mixed[:, pl.ds(start, rows)], other_branch[...], TN)
        out[k] = part.astype(BF16)


def output_grad(ids, own_mixed, other_mixed, own_branch, other_branch):
    total, width = own_mixed.shape
    return pl.pallas_call(
        output_grad_kernel,
        name="output_grad",
        out_shape=shape((4, width // 8, width // 2), BF16),
        in_specs=[SM] + [VM] * 4,
        out_specs=VM,
        compiler_params=params(),
        cost_estimate=cost(total * width * width, 8 * total * width),
    )(ids, own_mixed, other_mixed, own_branch, other_branch)


def triple_grad_kernel(ids, n0, n1, d0, d1, out):
    rows = out.shape[1]
    for k in range(4):
        column = pl.multiple_of((ids[0] ^ (2 * k + ids[3])) * rows, rows)
        part = dot(n0[:, pl.ds(column, rows)], d0[...], TN)
        part += dot(n1[:, pl.ds(column, rows)], d1[...], TN)
        out[k] = part.astype(BF16)


def triple_grad(ids, normed, grads):
    length, width = normed[0].shape
    columns = grads[0].shape[1]
    return pl.pallas_call(
        triple_grad_kernel,
        name="triple_grad",
        out_shape=shape((4, width // 8, columns), BF16),
        in_specs=[SM] + [VM] * 4,
        out_specs=VM,
        compiler_params=params(),
        cost_estimate=cost(2 * length * width * columns, 4 * length * (width + columns)),
    )(ids, *normed, *grads)


def first_back_kernel(tokens, d_attended, gain, *rest):
    parts, (grad_out, gain_grad, bias_grad) = rest[:6], rest[6:]
    rows = tokens.shape[1]
    gain_total = bias_total = 0.0
    for micro in range(2):
        one, two, three = parts[3 * micro : 3 * micro + 3]
        grad = one[...].astype(F32) + two[...].astype(F32) + three[...].astype(F32)
        unit, inverse = norm_parts(tokens[micro].astype(F32))
        gain_total = gain_total + jnp.sum(grad * unit, axis=0, keepdims=True)
        bias_total = bias_total + jnp.sum(grad, axis=0, keepdims=True)
        total = d_attended[micro * rows : (micro + 1) * rows, :]
        grad_out[micro] = (total + norm_back(grad, unit, inverse, gain[...])).astype(BF16)
    gain_grad[...] = gain_total
    bias_grad[...] = bias_total


def first_back(tokens, d_attended, gain, parts):
    micro, rows, width = tokens.shape
    row = shape((1, width), F32)
    return pl.pallas_call(
        first_back_kernel,
        name="first_back",
        out_shape=(shape(tokens.shape, BF16), row, row),
        in_specs=[VM] * 9,
        out_specs=(VM,) * 3,
        compiler_params=params(),
        cost_estimate=cost(20 * micro * rows * width, 16 * micro * rows * width),
    )(tokens, d_attended, gain, *parts)


def flip(index, bits):
    out, bit = index, 1
    while bit <= bits:
        if bits & bit:
            out = out + bit * (1 - 2 * lax.rem(lax.div(index, jnp.int32(bit)), jnp.int32(2)))
        bit *= 2
    return out


class Moves:
    def __init__(self, send, recv):
        self.send, self.recv, self.started, self.freed = send, recv, [], []
        self.place = {"ctx": lax.axis_index("ctx"), "fsdp": lax.axis_index("fsdp")}

    def greet(self):
        barrier = pltpu.get_barrier_semaphore()
        partners = [("ctx", 1), ("ctx", 2), ("ctx", 3), ("fsdp", 1), ("fsdp", 2), ("fsdp", 4), ("fsdp", 6)]
        for axis, bits in partners:
            pl.semaphore_signal(
                barrier,
                inc=1,
                device_id={axis: flip(self.place[axis], bits)},
                device_id_type=pl.DeviceIdType.MESH,
            )
        pl.semaphore_wait(barrier, len(partners))

    def go(self, source, target, axis, bits):
        slot = len(self.started)
        move = pltpu.make_async_remote_copy(
            src_ref=source,
            dst_ref=target,
            send_sem=self.send.at[slot],
            recv_sem=self.recv.at[slot],
            device_id={axis: flip(self.place[axis], bits)},
            device_id_type=pl.DeviceIdType.MESH,
        )
        move.start()
        self.started.append(move)
        return move

    def sent(self, move):
        move.wait_send()
        self.freed.append(move)

    def close(self):
        for move in self.started:
            if not any(move is other for other in self.freed):
                move.wait_send()


class Gather:
    def __init__(self, moves, part, view, local):
        self.moves, self.view = moves, view
        me = moves.place["fsdp"]
        self.along = [moves.go(part, view(me), "fsdp", 2 * k) for k in range(1, 4)]
        self.across = [moves.go(part, view(me), "fsdp", 1)]
        self.own = pltpu.make_async_copy(part, view(me), local)
        self.own.start()

    def forward(self):
        me = self.moves.place["fsdp"]
        for k in range(1, 4):
            self.along[k - 1].wait_recv()
            block = self.view(flip(me, 2 * k))
            self.across.append(self.moves.go(block, block, "fsdp", 1))

    def finish(self):
        for move in self.across:
            move.wait_recv()
        self.own.wait()


FORWARD_MOVES = 6 * 7 + 7 + 6 + 3 + 1 + 1 + 6 + 2


def row_view(ref, rows, columns=slice(None)):
    return lambda index: ref.at[pl.ds(pl.multiple_of(index * rows, rows), rows), columns]


def forward_kernel(
    global_ids,
    tokens,
    small,
    picks,
    triple_part,
    output_part,
    expand_part,
    shrink_part,
    tangent,
    small_all,
    triple_out,
    output_out,
    expand_all,
    shrink_all,
    tangent_other,
    triple,
    normed,
    block_bias,
    lse,
    mixed,
    joined_out,
    mixed_other,
    attended,
    hidden,
    hidden_other,
    parts,
    small_held,
    picks_held,
    triple_held,
    output_held,
    joined,
    hidden_held,
    send,
    recv,
    local,
):
    moves = Moves(send, recv)
    rank, me = moves.place["ctx"], moves.place["fsdp"]
    core = lax.rem(rank, jnp.int32(2))
    micro, rows, width = tokens.shape
    half = width // 2
    quarter = width // 4
    shard = triple_part.shape[0]
    wide = expand_part.shape[1]
    deep = shrink_part.shape[0]
    moves.greet()

    small_gather = Gather(moves, small, lambda index: small_held.at[index], local.at[0])
    near = [moves.go(tokens.at[0], parts.at[0, 1], "ctx", 1)]
    far = [moves.go(tokens.at[0], parts.at[0, 2], "ctx", 2)]
    triple_gather = Gather(moves, triple_part, row_view(triple_held, shard), local.at[1])
    picked = [moves.go(picks.at[p], picks_held.at[p], "ctx", p) for p in range(1, 4)]
    near.append(moves.go(tokens.at[1], parts.at[1, 1], "ctx", 1))
    far.append(moves.go(tokens.at[1], parts.at[1, 2], "ctx", 2))
    small_gather.forward()
    triple_gather.forward()
    output_gather = Gather(
        moves, output_part, row_view(output_held, shard, pl.ds(core * half, half)), local.at[2]
    )
    cut = wide // 2
    chunks = [
        (shrink_part.at[: deep // 2, :], lambda i: shrink_all.at[pl.ds(pl.multiple_of(i * deep, deep), deep // 2), :]),
        (expand_part.at[:, :cut], row_view(expand_all, shard, slice(0, cut))),
        (
            shrink_part.at[deep // 2 :, :],
            lambda i: shrink_all.at[pl.ds(pl.multiple_of(i * deep + deep // 2, deep // 2), deep // 2), :],
        ),
        (expand_part.at[:, cut:], row_view(expand_all, shard, slice(cut, wide))),
    ]
    gathers = [Gather(moves, *chunks[0], local.at[3])]
    tangent_move = moves.go(tangent, tangent_other, "ctx", 1)

    for move in picked:
        move.wait_recv()
    count = block_bias.shape[2]
    each = count // 4
    ranks = [flip(rank, p) if p else rank for p in range(4)]
    key_row = lax.broadcasted_iota(jnp.int32, (count, rows), 0)
    key_place = key_row // each
    key_rank = ranks[0]
    for p in range(1, 4):
        key_rank = jnp.where(key_place == p, ranks[p], key_rank)
    key_block = key_rank * each + key_row % each
    lane = lax.broadcasted_iota(jnp.int32, (count, rows), 1) // BLOCK
    for step in range(micro):
        first, second = global_ids[step, 0], global_ids[step, 1]
        key_global = (key_block == first) | (key_block == second)
        for p in range(4):
            source = picks.at[0] if p == 0 else picks_held.at[p]
            query_block = ranks[p] * each + lane
            base = key_global | (jnp.abs(query_block - key_block) <= 1)
            base = base | (query_block == first) | (query_block == second)
            for head in range(block_bias.shape[1]):
                hit = base
                for pick in range(3):
                    hit = hit | (source[step, head, pick : pick + 1, :] == key_block)
                block_bias[step, head, :, p * rows : (p + 1) * rows] = jnp.where(hit, 0.0, -1e30)

    small_gather.finish()
    small_all[...] = small_held[...]

    def vector(line):
        return jnp.concatenate([small_held[b, line : line + 1, :] for b in range(8)], axis=1)

    gain_one, bias_one, gain_two, bias_two = (vector(line) for line in range(4))

    for step in range(micro):
        far[step].wait_recv()
        near.append(moves.go(parts.at[step, 2], parts.at[step, 3], "ctx", 1))
    mixed_moves = []
    for step in range(micro):
        near[step].wait_recv()
        near[2 + step].wait_recv()
        for p in range(4):
            source = tokens[step] if p == 0 else parts[step, p]
            normed[step, p * rows : (p + 1) * rows, :] = normalize(source, gain_one, bias_one)
        if step == 0:
            triple_gather.finish()
        for p in range(4):
            span = slice(p * rows, (p + 1) * rows)
            triple[step, span, :] = dot(normed[step, span, :], triple_held[...]).astype(BF16)
        if step == 0:
            output_gather.forward()
            gathers.append(Gather(moves, *chunks[1], local.at[4]))
        else:
            output_gather.finish()
            piece = output_held.at[:, pl.ds(core * half, half)]
            output_move = moves.go(piece, piece, "ctx", 1)
            gathers[1].forward()
            gathers.append(Gather(moves, *chunks[3], local.at[6]))
        attend_body(triple.at[step], block_bias.at[step], mixed.at[step], lse.at[step])
        own = pl.ds(pl.multiple_of(rank * quarter, quarter), quarter)
        span = slice(step * rows, (step + 1) * rows)
        joined[span, own] = mixed[step, 0]
        for p in range(1, 4):
            mixed_moves.append(moves.go(mixed.at[step, p], joined.at[span, own], "ctx", p))
        if step == 0:
            gathers[0].forward()
            gathers.append(Gather(moves, *chunks[2], local.at[5]))
    output_move.wait_recv()
    for move in mixed_moves:
        move.wait_recv()
    keep = [
        pltpu.make_async_copy(triple_held, triple_out, local.at[7]),
        pltpu.make_async_copy(output_held, output_out, local.at[8]),
    ]
    for copy in keep:
        copy.start()
    output_kernel(tokens, joined, gain_two, bias_two, output_held, attended, hidden_held)
    last = [
        moves.go(hidden_held, hidden_other, "ctx", 1),
        moves.go(joined, mixed_other, "ctx", 1),
    ]
    hidden[...] = hidden_held[...]
    joined_out[...] = joined[...]
    gathers[2].forward()
    gathers[3].forward()
    for gather in gathers:
        gather.finish()
    for move in [tangent_move] + last:
        move.wait_recv()
    for copy in keep:
        copy.wait()
    moves.close()


def forward_together(global_ids, tokens, small, picks, triple_part, output_part, expand_part, shrink_part, tangent):
    micro, rows, width = tokens.shape
    total = micro * rows
    columns = triple_part.shape[1]
    wide = expand_part.shape[1]
    length = 4 * rows
    heads = picks.shape[2]
    outs = (
        (VM, (8,) + small.shape, F32),
        (ANY, (width, columns), BF16),
        (ANY, (width, width), BF16),
        (ANY, (width, wide), BF16),
        (ANY, (wide, width), BF16),
        (ANY, (total, width), BF16),
        (VM, (micro, length, columns), BF16),
        (VM, (micro, length, width), BF16),
        (VM, (micro, heads, length // BLOCK, length), F32),
        (VM, (micro, 8, length), F32),
        (VM, (micro, 4, rows, width // 4), BF16),
        (VM, (total, width), BF16),
        (ANY, (total, width), BF16),
        (VM, (total, width), F32),
        (VM, (total, width), BF16),
        (ANY, (total, width), BF16),
    )
    return pl.pallas_call(
        forward_kernel,
        name="forward_together",
        out_shape=tuple(shape(dims, kind) for _, dims, kind in outs),
        in_specs=[SM] + [VM] * 3 + [ANY] * 5,
        out_specs=tuple(spec for spec, _, _ in outs),
        scratch_shapes=[
            pltpu.VMEM((micro, 4, rows, width), BF16),
            pltpu.VMEM((8,) + small.shape, F32),
            pltpu.VMEM(picks.shape, jnp.int32),
            pltpu.VMEM((width, columns), BF16),
            pltpu.VMEM((width, width), BF16),
            pltpu.VMEM((total, width), BF16),
            pltpu.VMEM((total, width), BF16),
            pltpu.SemaphoreType.DMA((FORWARD_MOVES,)),
            pltpu.SemaphoreType.DMA((FORWARD_MOVES,)),
            pltpu.SemaphoreType.DMA((9,)),
        ],
        compiler_params=pltpu.CompilerParams(
            collective_id=0, has_side_effects=True, vmem_limit_bytes=56 * MIB
        ),
        cost_estimate=cost(16 * total * width * width, 64 * MIB),
    )(global_ids, tokens, small, picks, triple_part, output_part, expand_part, shrink_part, tangent)


class Reduce:
    def __init__(self, moves, sent, came, line):
        self.moves, self.came, self.line = moves, came, line
        self.across = moves.go(sent, came, "fsdp", 1)

    def forward(self, kept):
        self.across.wait_recv()
        for k in range(4):
            self.came[k] = wide_add(kept[k], self.came[k]).astype(BF16)
        self.along = [
            self.moves.go(self.came.at[k], self.line.at[k - 1], "fsdp", 2 * k) for k in range(1, 4)
        ]

    def finish(self):
        for move in self.along:
            move.wait_recv()
        return wide_add(self.came[0], *(self.line[k] for k in range(3)))


class Spread:
    hops = (("ctx", 1), ("ctx", 2), ("fsdp", 1), ("fsdp", 2), ("fsdp", 4))

    def __init__(self, moves, totals, came):
        self.moves, self.totals, self.came, self.done, self.move = moves, totals, came, 0, None

    def hop(self):
        if self.move is not None:
            self.move.wait_recv()
            self.totals[self.done + 1] = self.totals[self.done] + self.came[self.done]
            self.done += 1
            self.move = None
        if self.done < 5:
            axis, bits = self.hops[self.done]
            self.move = self.moves.go(self.totals.at[self.done], self.came.at[self.done], axis, bits)

    def finish(self):
        while self.move is not None:
            self.hop()
        return self.totals[5]


BACKWARD_MOVES = 68


def backward_kernel(
    vectors,
    tangent,
    output_weight,
    triple_weight,
    triples,
    biases,
    lses,
    mixed_own,
    shift_in_grad,
    own_hidden,
    other_hidden,
    own_out,
    other_out,
    attended,
    tokens,
    mixed_all,
    mixed_other,
    normeds,
    shrink_sent,
    shrink_kept,
    expand_sent,
    expand_kept,
    result,
    token_grad,
    shrink_out,
    expand_out,
    output_out,
    triple_out,
    early_out,
    late_out,
    came_out,
    came_hidden,
    d_attended,
    stage,
    held,
    d_branch,
    branch_other,
    d_mixed,
    grads,
    d_triples,
    key_total,
    value_total,
    near_parts,
    own_parts,
    near_came,
    far_sent,
    far_came,
    kept_ring,
    feed_came,
    feed_line,
    output_sent,
    output_kept,
    output_came,
    output_line,
    triple_sent,
    triple_kept,
    triple_came,
    triple_line,
    chip_sent,
    chip_came,
    final,
    triple_all,
    early_totals,
    early_came,
    late_totals,
    late_came,
    send,
    recv,
    local,
):
    moves = Moves(send, recv)
    rank, me = moves.place["ctx"], moves.place["fsdp"]
    core = lax.rem(rank, jnp.int32(2))
    micro, rows, width = tangent.shape
    half, quarter, shard = width // 2, width // 4, width // 8
    moves.greet()
    used = []

    def load(source, target):
        copy = pltpu.make_async_copy(source, target, local.at[len(used)])
        copy.start()
        used.append(copy)
        return copy

    hidden_move = moves.go(other_hidden, came_hidden, "ctx", 1)
    out_move = moves.go(other_out, came_out, "ctx", 1)
    deep = shrink_sent.shape[1] // 2
    wide = expand_sent.shape[2] // 2
    cuts = [
        (lambda ref: ref.at[:, :deep, :], shrink_sent, shrink_kept),
        (lambda ref: ref.at[:, :, :wide], expand_sent, expand_kept),
        (lambda ref: ref.at[:, deep:, :], shrink_sent, shrink_kept),
        (lambda ref: ref.at[:, :, wide:], expand_sent, expand_kept),
    ]

    def begin(i):
        view, sent, _ = cuts[i]
        return Reduce(moves, view(sent), feed_came.at[i], feed_line.at[i])

    def load_kept(i):
        view, _, kept = cuts[i]
        return load(view(kept), kept_ring.at[i % 2])

    feeds = [begin(0), begin(1)]
    loads = [load(own_hidden, d_attended), load(attended, stage)]
    kept_loads = [load_kept(0), load_kept(1)]
    mixed_loads = [load(mixed_all, held.at[0, : 2 * rows, :]), load(mixed_other, held.at[0, 2 * rows :, :])]

    gain_two, gain_one, shift_out = vectors[0:1, :], vectors[1:2, :], vectors[2:3, :]
    for copy in loads:
        copy.wait()
    hidden_move.wait_recv()
    gain_total = bias_total = shift_total = 0.0
    for step in range(micro):
        span = slice(step * rows, (step + 1) * rows)
        cot = tangent[step].astype(F32)
        unit, inverse = norm_parts(stage[span, :])
        grad = d_attended[span, :] + came_hidden[span, :].astype(F32)
        gain_total = gain_total + jnp.sum(grad * unit, axis=0, keepdims=True)
        bias_total = bias_total + jnp.sum(grad, axis=0, keepdims=True)
        shift_total = shift_total + jnp.sum(cot, axis=0, keepdims=True)
        total = cot + norm_back(grad, unit, inverse, gain_two)
        d_attended[span, :] = total
        d_branch[span, :] = total.astype(BF16)
    theirs = d_branch.at[:, pl.ds(pl.multiple_of((1 - core) * half, half), half)]
    branch_move = moves.go(theirs, branch_other, "ctx", 1)
    grad_moves = []
    for step in range(micro):
        for p in (2, 3, 1, 0):
            start = pl.multiple_of((flip(rank, p) if p else rank) * quarter, quarter)
            part = dot(d_branch[step * rows : (step + 1) * rows, :], output_weight[pl.ds(start, quarter), :], NT)
            if p:
                d_mixed[step, p] = part.astype(BF16)
                grad_moves.append(moves.go(d_mixed.at[step, p], grads.at[step, p], "ctx", p))
            else:
                grads[step, 0] = part.astype(BF16)

    early_totals[0] = jnp.zeros_like(early_totals[0])
    for b in range(8):
        lanes = slice(b * shard, (b + 1) * shard)
        early_totals[0, b : b + 1, 0:shard] = gain_total[:, lanes]
        early_totals[0, b : b + 1, shard : 2 * shard] = bias_total[:, lanes]
        early_totals[0, b : b + 1, 2 * shard : 3 * shard] = shift_total[:, lanes]
        unit_lanes = shift_in_grad.shape[1] // 8
        early_totals[
            0, b : b + 1, pl.ds(pl.multiple_of(3 * shard + core * unit_lanes, shard), unit_lanes)
        ] = shift_in_grad[:, b * unit_lanes : (b + 1) * unit_lanes]
    early = Spread(moves, early_totals, early_came)
    early.hop()

    for copy in mixed_loads:
        copy.wait()
    branch_move.wait_recv()
    mine = pl.ds(pl.multiple_of(core * half, half), half)

    def output_part(index):
        lanes = pl.ds(pl.multiple_of(index * shard, shard), shard)
        part = dot(held[0, : 2 * rows, lanes], d_branch[:, mine], TN)
        return part + dot(held[0, 2 * rows :, lanes], branch_other[...], TN)

    for k in range(4):
        output_sent[k] = output_part(flip(me, 2 * k + 1)).astype(BF16)
    early.hop()
    output_reduce = Reduce(moves, output_sent, output_came, output_line)
    for k in range(4):
        output_kept[k] = output_part(flip(me, 2 * k) if k else me).astype(BF16)
    feeds.append(begin(2))
    normed_loads = [load(normeds.at[step], held.at[step]) for step in range(1, micro)]

    norm_moves, far_moves = [], []

    def attention(step):
        for move in grad_moves[3 * step : 3 * step + 3]:
            move.wait_recv()
        attend_back_body(
            triples.at[step],
            biases.at[step],
            lses.at[step],
            grads.at[step],
            mixed_own.at[step],
            d_triples.at[step],
            key_total,
            value_total,
        )
        for p in (3, 1, 2, 0):
            span = slice(p * rows, (p + 1) * rows)
            part = dot(d_triples[step, span, :], triple_weight[...], NT).astype(BF16)
            if p:
                near_parts[step, p - 1] = part
            else:
                own_parts[step] = part
            if p % 2:
                norm_moves.append(moves.go(near_parts.at[step, p - 1], near_came.at[step, p // 2], "ctx", 1))

    def far_part(step):
        norm_moves[2 * step].wait_recv()
        far_sent[step] = wide_add(near_parts[step, 1], near_came[step, 1]).astype(BF16)
        far_moves.append(moves.go(far_sent.at[step], far_came.at[step], "ctx", 2))

    def feed_forward(i):
        kept_loads[i].wait()
        feeds[i].forward(kept_ring.at[i % 2])
        if i < 2:
            kept_loads.append(load_kept(i + 2))

    attention(0)
    feed_forward(0)
    feeds.append(begin(3))
    early.hop()
    far_part(0)
    normed_loads.insert(0, load(normeds.at[0], held.at[0]))
    feed_forward(1)
    attention(1)
    early.hop()
    output_reduce.forward(output_kept)
    feed_forward(2)
    far_part(1)

    for copy in normed_loads:
        copy.wait()

    def triple_part(index):
        lanes = pl.ds(pl.multiple_of(index * shard, shard), shard)
        part = dot(held[0, :, lanes], d_triples[0], TN)
        return part + dot(held[1, :, lanes], d_triples[1], TN)

    for k in range(4):
        triple_sent[k] = triple_part(flip(me, 2 * k + 1)).astype(BF16)
    triple_reduce = Reduce(moves, triple_sent, triple_came, triple_line)
    for k in range(4):
        triple_kept[k] = triple_part(flip(me, 2 * k) if k else me).astype(BF16)
    early.hop()
    early_out[...] = early.finish()

    token_load = load(tokens, held.at[0, : 2 * rows, :])
    out_load = load(own_out, stage)
    out_move.wait_recv()
    came_load = load(came_out, came_hidden)

    chips = {}

    def chip_begin(i, value):
        columns = value.shape[1]
        chip_sent[i, :, :columns] = value.astype(BF16)
        chips[i] = moves.go(chip_sent.at[i, :, pl.ds(0, columns)], chip_came.at[i, :, pl.ds(0, columns)], "ctx", 2)

    ends, stays = [], []

    def place(source, target):
        ends.append(moves.go(source, target, "ctx", 1))
        stays.append(load(source, target))

    def chip_end(i):
        chips[i].wait_recv()
        if i < 4:
            final[i] = wide_add(chip_sent[i], chip_came[i])
        else:
            final[i, :, :half] = wide_add(chip_sent[i, :, :half], chip_came[i, :, :half])
        if i in (0, 2):
            start = pl.multiple_of((2 * core + i // 2) * deep, deep)
            place(final.at[i], shrink_out.at[pl.ds(start, deep), :])
        elif i < 4:
            block = wide // 4
            for q in range(4):
                start = pl.multiple_of(((4 * (i // 2) + q) * 2 + core) * block, block)
                place(final.at[i, :, q * block : (q + 1) * block], expand_out.at[:, pl.ds(start, block)])
        else:
            place(final.at[i, :, :half], output_out.at[:, mine])

    chip_begin(0, feeds[0].finish())
    feed_forward(3)
    chip_begin(1, feeds[1].finish())
    chip_end(0)

    token_load.wait()
    for move in norm_moves[1::2] + far_moves:
        move.wait_recv()
    gain_total = bias_total = 0.0
    for step in range(micro):
        span = slice(step * rows, (step + 1) * rows)
        grad = wide_add(own_parts[step], near_came[step, 0], far_came[step])
        unit, inverse = norm_parts(held[0, span, :].astype(F32))
        gain_total = gain_total + jnp.sum(grad * unit, axis=0, keepdims=True)
        bias_total = bias_total + jnp.sum(grad, axis=0, keepdims=True)
        token_grad[step] = (d_attended[span, :] + norm_back(grad, unit, inverse, gain_one)).astype(BF16)
    for b in range(8):
        lanes = slice(b * shard, (b + 1) * shard)
        late_totals[0, b : b + 1, 0:shard] = gain_total[:, lanes]
        late_totals[0, b : b + 1, shard : 2 * shard] = bias_total[:, lanes]
    late = Spread(moves, late_totals, late_came)
    late.hop()
    out_load.wait()
    sum_load = load(attended, d_attended)
    came_load.wait()
    for step in range(micro):
        span = slice(step * rows, (step + 1) * rows)
        stage[span, :] = stage[span, :] + came_hidden[span, :].astype(F32) + shift_out
    sum_load.wait()
    moves.sent(branch_move)
    for step in range(micro):
        span = slice(step * rows, (step + 1) * rows)
        d_branch[span, :] = (d_attended[span, :] + stage[span, :]).astype(BF16)
    result_load = load(d_branch, result)
    late.hop()
    chip_begin(4, output_reduce.finish())
    chip_begin(2, feeds[2].finish())
    chip_end(1)
    late.hop()
    triple_reduce.forward(triple_kept)
    chip_end(4)
    chip_end(2)
    late.hop()
    chip_begin(3, feeds[3].finish())
    late.hop()
    triple_all[0] = triple_reduce.finish().astype(BF16)
    peers = [moves.go(triple_all.at[0], triple_all.at[p], "ctx", p) for p in range(1, 4)]
    chip_end(3)
    late_out[...] = late.finish()
    for p in range(4):
        if p:
            peers[p - 1].wait_recv()
        target = flip(rank, p) if p else rank
        for k in range(3):
            start = pl.multiple_of(k * width + target * quarter, quarter)
            triple_out[:, pl.ds(start, quarter)] = triple_all[p, :, k * quarter : (k + 1) * quarter].astype(F32)
    for move in ends:
        move.wait_recv()
    for copy in stays + [result_load]:
        copy.wait()
    moves.close()


def backward_together(vectors, tangent, output_weight, triple_weight, triples, biases, lses, mixed_own, shift_in_grad, *late_arrays):
    micro, rows, width = tangent.shape
    total, half, quarter, shard = micro * rows, width // 2, width // 4, width // 8
    columns = triple_weight.shape[1]
    shrink_sent, expand_sent = late_arrays[-4], late_arrays[-2]
    deep, wide = shrink_sent.shape[1], expand_sent.shape[2]
    small = 3 * shard + deep * 2
    length = 4 * rows
    outs = (
        (ANY, (total, width), BF16),
        (VM, tangent.shape, BF16),
        (ANY, (2 * deep, width), F32),
        (ANY, (shard, 2 * wide), F32),
        (ANY, (shard, width), F32),
        (VM, (shard, 4 * columns), F32),
        (VM, (8, small), F32),
        (VM, (8, 2 * shard), F32),
        (ANY, (total, width), BF16),
    )
    scratch = (
        ((total, width), BF16),
        ((total, width), F32),
        ((total, width), F32),
        ((2, length, width), BF16),
        ((total, width), BF16),
        ((total, half), BF16),
        ((micro, 4, rows, quarter), BF16),
        ((micro, 4, rows, quarter), BF16),
        ((micro, length, columns), BF16),
        ((length, 128), F32),
        ((length, 128), F32),
        ((micro, 3, rows, width), BF16),
        ((micro, rows, width), BF16),
        ((micro, 2, rows, width), BF16),
        ((micro, rows, width), BF16),
        ((micro, rows, width), BF16),
        ((2, 4, shard, width), BF16),
        ((4, 4, shard, width), BF16),
        ((4, 3, shard, width), BF16),
        ((4, shard, half), BF16),
        ((4, shard, half), BF16),
        ((4, shard, half), BF16),
        ((3, shard, half), BF16),
        ((4, shard, columns), BF16),
        ((4, shard, columns), BF16),
        ((4, shard, columns), BF16),
        ((3, shard, columns), BF16),
        ((5, shard, width), BF16),
        ((5, shard, width), BF16),
        ((5, shard, width), F32),
        ((4, shard, columns), BF16),
        ((6, 8, small), F32),
        ((5, 8, small), F32),
        ((6, 8, 2 * shard), F32),
        ((5, 8, 2 * shard), F32),
    )
    return pl.pallas_call(
        backward_kernel,
        name="backward_together",
        out_shape=tuple(shape(dims, kind) for _, dims, kind in outs),
        in_specs=[VM] * 9 + [ANY] * 13,
        out_specs=tuple(spec for spec, _, _ in outs),
        scratch_shapes=[pltpu.VMEM(dims, kind) for dims, kind in scratch]
        + [
            pltpu.SemaphoreType.DMA((BACKWARD_MOVES,)),
            pltpu.SemaphoreType.DMA((BACKWARD_MOVES,)),
            pltpu.SemaphoreType.DMA((26,)),
        ],
        compiler_params=pltpu.CompilerParams(
            collective_id=1, has_side_effects=True, vmem_limit_bytes=63 * MIB
        ),
        cost_estimate=cost(24 * total * width * width, 64 * MIB),
    )(vectors, tangent, output_weight, triple_weight, triples, biases, lses, mixed_own, shift_in_grad, *late_arrays)


def block_biases(chosen, globals_here, rank, local_blocks):
    heads, count, _ = chosen.shape
    place = jnp.arange(count, dtype=jnp.int32)
    true_block = ((place // local_blocks) ^ rank) * local_blocks + place % local_blocks
    near = jnp.abs(true_block[:, None] - true_block[None, :]) <= 1
    is_global = jnp.any(true_block[:, None] == globals_here[None, :], axis=1)
    picked = jnp.any(chosen[:, None, :, :] == true_block[None, :, None, None], axis=3)
    allowed = near[None] | picked | is_global[None, :, None] | is_global[None, None, :]
    bias = jnp.where(allowed, 0.0, -1e30).astype(F32)
    return jnp.repeat(bias, BLOCK, axis=2)


def on_device(
    tokens,
    cotangent,
    random_blocks,
    global_blocks,
    attend_gain,
    attend_bias,
    triple_weight,
    output_weight,
    hidden_gain,
    hidden_bias,
    expand_weight,
    expand_bias,
    shrink_weight,
    shrink_bias,
):
    tokens, cotangent = tokens[:, 0], cotangent[:, 0]
    micro, rows, width = tokens.shape
    total = micro * rows
    ways = lax.axis_size("fsdp")
    fsdp = lax.axis_index("fsdp")
    rank = lax.axis_index("ctx")
    core = rank % 2
    place = place_id()
    heads_all = random_blocks.shape[2]
    own_heads = heads_all // 4
    local_blocks = rows // BLOCK
    shard = width // ways
    wide = expand_weight.shape[1]
    deep = shrink_weight.shape[0]
    ids = jnp.stack([place, rank, core, jnp.int32(0)])
    ids_sent = jnp.stack([place, rank, core, jnp.int32(1)])

    half_units = wide // (2 * ways)
    vectors = [attend_gain, attend_bias, hidden_gain, hidden_bias, shrink_bias]
    triple_part = jnp.concatenate(
        [
            lax.dynamic_slice_in_dim(triple_weight, k * width + rank * (width // 4), width // 4, 1)
            for k in range(3)
        ],
        axis=1,
    )
    output_part = lax.dynamic_slice_in_dim(output_weight, core * (width // 2), width // 2, 1)
    expand_part = jnp.concatenate(
        [
            lax.dynamic_slice_in_dim(expand_weight, (2 * k + core) * half_units, half_units, 1)
            for k in range(ways)
        ],
        axis=1,
    )
    shrink_part = lax.dynamic_slice_in_dim(shrink_weight, core * (deep // 2), deep // 2, 0)
    tangent_own = cotangent.reshape(total, width)
    picks = random_blocks[:, 0]
    if ways == 8:
        small = jnp.concatenate(
            [v.reshape(1, shard) for v in vectors]
            + [expand_bias.reshape(-1, shard), jnp.zeros((7, shard), BF16)]
        ).astype(F32)
        sets = picks.reshape(micro, 4, own_heads, local_blocks, -1).transpose(1, 0, 2, 4, 3)
        order = [rank ^ p for p in range(4)]
        sets = jnp.concatenate([lax.dynamic_slice_in_dim(sets, r, 1, 0) for r in order], axis=0)
        sets = jnp.pad(jnp.repeat(sets, BLOCK, axis=4), ((0, 0),) * 3 + ((0, 5), (0, 0)))
        (
            table,
            triple_full,
            output_full,
            expand_full,
            shrink_full,
            tangent_other,
            triples,
            normeds,
            biases,
            lses,
            mixed_own,
            mixed_all,
            mixed_other,
            attended,
            hidden,
            hidden_other,
        ) = forward_together(
            global_blocks[:, 0],
            tokens,
            small,
            sets,
            triple_part,
            output_part,
            expand_part,
            shrink_part,
            tangent_own,
        )
        gain_one, bias_one, gain_two, bias_two, shift_out = (
            table[:, k].reshape(1, width) for k in range(5)
        )
        shift_in = lax.dynamic_slice_in_dim(
            table[:, 5:9].reshape(8, 2, half_units), core, 1, 1
        ).reshape(1, wide // 2)
    else:

        def whole(part):
            return lax.all_gather(part, "fsdp", axis=0, tiled=True)

        gain_one, bias_one, gain_two, bias_two, shift_out = (
            whole(v).astype(F32).reshape(1, width) for v in vectors
        )
        halves = whole(expand_bias).astype(F32).reshape(ways, 2, half_units)
        shift_in = jnp.where(core == 0, halves[:, 0], halves[:, 1]).reshape(1, wide // 2)
        triple_full, expand_full, shrink_full = whole(triple_part), whole(expand_part), whole(shrink_part)
        output_full = whole(output_weight)
        tangent_other = swap(tangent_own, "ctx", 1)
        far_picks = swap(picks, "ctx", 2)
        all_picks = jnp.stack([picks, swap(picks, "ctx", 1), far_picks, swap(far_picks, "ctx", 1)])
        chosen = lax.dynamic_slice_in_dim(all_picks, rank * own_heads, own_heads, 2)
        chosen = chosen.transpose(1, 2, 0, 3, 4).reshape(micro, own_heads, 4 * local_blocks, -1)
        triples, normeds, biases, lses, mixed_own, joined = [], [], [], [], [], []
        for step in range(micro):
            biases.append(block_biases(chosen[step], global_blocks[step, 0], rank, local_blocks))
            near, far = swap(tokens[step], "ctx", 1), swap(tokens[step], "ctx", 2)
            places = (tokens[step], near, far, swap(far, "ctx", 1))
            triple, normed = project(places, gain_one, bias_one, triple_full)
            mixed, lse = attend(triple, biases[step])
            here = [mixed[0]] + [swap(mixed[p], "ctx", p) for p in range(1, 4)]
            for low_bit, high in ((core == 1, False), (rank >= 2, True)):
                pairs = ((0, 2), (1, 3)) if high else ((0, 1), (2, 3))
                for one, two in pairs:
                    first = jnp.where(low_bit, here[two], here[one])
                    here[two] = jnp.where(low_bit, here[one], here[two])
                    here[one] = first
            joined.append(jnp.concatenate(here, axis=1))
            for kept, value in zip(
                (triples, normeds, lses, mixed_own), (triple, normed, lse, mixed)
            ):
                kept.append(value)
        mixed_all = jnp.concatenate(joined, axis=0)
        mixed_other = swap(mixed_all, "ctx", 1)
        attended, hidden = output_project(tokens, mixed_all, gain_two, bias_two, output_full)
        hidden_other = swap(hidden, "ctx", 1)

    (
        own_out,
        other_out,
        own_hidden,
        other_hidden,
        shift_in_grad,
        shrink_sent,
        shrink_kept,
        expand_sent,
        expand_kept,
    ) = feed(ids, (hidden, hidden_other), (tangent_own, tangent_other), shift_in, expand_full, shrink_full)
    if ways == 8:
        rows_of = jnp.concatenate([gain_two, gain_one, shift_out, jnp.zeros((5, width), F32)])
        (
            result,
            token_grad,
            shrink_grad,
            expand_grad,
            output_grad_all,
            triple_grad_all,
            early,
            late,
            _,
        ) = backward_together(
            rows_of,
            cotangent,
            output_full,
            triple_full,
            triples,
            biases,
            lses,
            mixed_own,
            shift_in_grad,
            own_hidden,
            other_hidden,
            own_out,
            other_out,
            attended,
            tokens.reshape(total, width),
            mixed_all,
            mixed_other,
            normeds,
            shrink_sent,
            shrink_kept,
            expand_sent,
            expand_kept,
        )
        result = result.reshape(micro, rows, width)
    else:
        came_hidden = swap(other_hidden, "ctx", 1)
        came_out = swap(other_out, "ctx", 1)
        shrink_mine = scatter_rows(shrink_kept, shrink_sent)
        expand_mine = scatter_rows(expand_kept, expand_sent)
        result, d_attended, d_branch, *grads, gain_two_grad, bias_two_grad, shift_out_grad = branch_back(
            ids,
            attended,
            own_hidden,
            came_hidden,
            cotangent,
            own_out,
            came_out,
            gain_two,
            shift_out,
            output_full,
        )
        half_sent = lax.dynamic_slice_in_dim(d_branch, (1 - core) * (width // 2), width // 2, 1)
        branch_other = swap(half_sent, "ctx", 1)
        output_sent = output_grad(ids_sent, mixed_all, mixed_other, d_branch, branch_other)
        output_kept = output_grad(ids, mixed_all, mixed_other, d_branch, branch_other)
        output_mine = scatter_rows(output_kept, output_sent)

        d_triples, norm_parts_here = [], []
        for step in range(micro):
            here = grads[4 * step : 4 * step + 4]
            here = [here[0]] + [swap(here[p], "ctx", p) for p in range(1, 4)]
            d_triple, parts = attend_back(
                triples[step], biases[step], lses[step], here, mixed_own[step], triple_full
            )
            d_triples.append(d_triple)
            near = swap(parts[1], "ctx", 1)
            far = wide_add(parts[2], swap(parts[3], "ctx", 1)).astype(BF16)
            norm_parts_here += [parts[0], near, swap(far, "ctx", 2)]
        normed_pair = (normeds[0], normeds[1])
        triple_sent = triple_grad(ids_sent, normed_pair, d_triples)
        triple_kept = triple_grad(ids, normed_pair, d_triples)
        triple_mine = scatter_rows(triple_kept, triple_sent)
        token_grad, gain_one_grad, bias_one_grad = first_back(
            tokens, d_attended, gain_one, norm_parts_here
        )

        halves = shift_in_grad.reshape(ways, 1, wide // (2 * ways))
        blank = jnp.zeros_like(halves)
        spread = jnp.where(
            core == 0,
            jnp.concatenate([halves, blank], axis=1),
            jnp.concatenate([blank, halves], axis=1),
        )
        early = sum_everywhere(
            jnp.concatenate(
                [
                    gain_two_grad.reshape(ways, shard),
                    bias_two_grad.reshape(ways, shard),
                    shift_out_grad.reshape(ways, shard),
                    spread.reshape(ways, wide // ways),
                ],
                axis=1,
            )
        )
        late = sum_everywhere(
            jnp.concatenate([gain_one_grad.reshape(ways, shard), bias_one_grad.reshape(ways, shard)], axis=1)
        )

        def over_chips(part):
            low = part.astype(BF16)
            return wide_add(low, swap(low, "ctx", 2))

        def both(own, axis):
            other = swap(own, "ctx", 1)
            first = jnp.where(core == 0, own, other)
            second = jnp.where(core == 0, other, own)
            return jnp.stack([first, second], axis=axis)

        shrink_grad = both(over_chips(shrink_mine), 0).reshape(deep, width)
        expand_half = over_chips(expand_mine).reshape(shard, ways, wide // (2 * ways))
        expand_grad = both(expand_half, 2).reshape(shard, wide)
        output_grad_all = both(over_chips(output_mine), 1).reshape(shard, width)
        low = triple_mine.astype(BF16).reshape(shard, 3, width // 4)
        far = swap(low, "ctx", 2)
        pair = jnp.stack([jnp.where(rank < 2, low, far), jnp.where(rank < 2, far, low)], axis=2)
        triple_grad_all = both(pair, 3).reshape(shard, 3 * width).astype(F32)


    early = lax.dynamic_index_in_dim(early, fsdp, 0, keepdims=False)
    late = lax.dynamic_index_in_dim(late, fsdp, 0, keepdims=False)
    return (
        result[:, None],
        token_grad[:, None],
        late[:shard],
        late[shard:],
        triple_grad_all,
        output_grad_all,
        early[:shard],
        early[shard : 2 * shard],
        expand_grad,
        early[3 * shard :],
        shrink_grad,
        early[2 * shard : 3 * shard],
    )


def solution(mesh):
    token_spec = P(None, "fsdp", "ctx", None)
    flat, rows = P("fsdp"), P("fsdp", None)
    return jax.shard_map(
        on_device,
        mesh=mesh,
        in_specs=(
            token_spec,
            token_spec,
            P(None, "fsdp", None, "ctx", None),
            P(None, "fsdp", None),
            flat,
            flat,
            rows,
            rows,
            flat,
            flat,
            rows,
            flat,
            rows,
            flat,
        ),
        out_specs=(
            token_spec,
            token_spec,
            flat,
            flat,
            rows,
            rows,
            flat,
            flat,
            rows,
            flat,
            rows,
            flat,
        ),
        check_vma=False,
    )
```

```python
import functools

import jax
import jax.numpy as jnp
from jax import lax
from jax.experimental import pallas as pl
from jax.experimental.pallas import tpu as pltpu
from jax.sharding import PartitionSpec as P

HEAD_DIM = 64
BLOCK = 64
EPSILON = 1e-05
F32 = jnp.float32
BF16 = jnp.bfloat16
MIB = 1 << 20

VM = pl.BlockSpec(memory_space=pltpu.VMEM)
SM = pl.BlockSpec(memory_space=pltpu.SMEM)
ANY = pl.BlockSpec(memory_space=pl.ANY)

NN = (((1,), (0,)), ((), ()))
NT = (((1,), (1,)), ((), ()))
TN = (((0,), (0,)), ((), ()))


def dot(left, right, dims=NN):
    return lax.dot_general(left, right, dims, preferred_element_type=F32)


def shape(dims, kind):
    return jax.ShapeDtypeStruct(dims, kind)


def params(limit=56):
    return pltpu.CompilerParams(vmem_limit_bytes=limit * MIB)


def cost(flops, moved, special=0):
    return pl.CostEstimate(flops=flops, bytes_accessed=moved, transcendentals=special)


def swap(value, axis, step):
    size = lax.axis_size(axis)
    return lax.ppermute(value, axis, [(i, i ^ step) for i in range(size)])


def place_id():
    return lax.axis_index("fsdp") if lax.axis_size("fsdp") == 8 else jnp.int32(1)


def wide_add(*terms):
    total = terms[0].astype(F32)
    for term in terms[1:]:
        total = total + term.astype(F32)
    return total


def scatter_rows(kept, sent):
    whole = jnp.stack([sent, kept], axis=1)
    whole = whole.reshape((8 * kept.shape[1],) + kept.shape[2:])
    return lax.psum_scatter(whole.astype(F32), "fsdp", scatter_dimension=0, tiled=True)


def sum_everywhere(vector):
    return lax.psum(vector, ("ctx", "fsdp"))


def norm_parts(values):
    average = jnp.mean(values, axis=-1, keepdims=True)
    centered = values - average
    variance = jnp.mean(centered * centered, axis=-1, keepdims=True)
    inverse = lax.rsqrt(variance + EPSILON)
    return centered * inverse, inverse


def norm_back(grad, unit, inverse, gain):
    scaled = grad * gain
    first = jnp.mean(scaled, axis=-1, keepdims=True)
    second = jnp.mean(scaled * unit, axis=-1, keepdims=True)
    return inverse * (scaled - first - unit * second)


def normalize(source, gain, bias):
    unit, _ = norm_parts(source.astype(F32))
    return (unit * gain + bias).astype(BF16)


def project_kernel(t0, t1, t2, t3, gain, bias, weight, triple, normed):
    rows = t0.shape[0]
    for place, part in enumerate((t0, t1, t2, t3)):
        span = slice(place * rows, (place + 1) * rows)
        normed[span, :] = normalize(part[...], gain[...], bias[...])
        triple[span, :] = dot(normed[span, :], weight[...]).astype(BF16)


def project(parts, gain, bias, weight):
    rows, width = parts[0].shape
    columns = weight.shape[1]
    return pl.pallas_call(
        project_kernel,
        name="project",
        out_shape=(shape((4 * rows, columns), BF16), shape((4 * rows, width), BF16)),
        in_specs=[VM] * 7,
        out_specs=(VM, VM),
        compiler_params=params(),
        cost_estimate=cost(8 * rows * width * columns, 12 * rows * width + 2 * width * columns),
    )(*parts, gain, bias, weight)


def head_mask(rows):
    return lax.broadcasted_iota(jnp.int32, (rows, 2 * HEAD_DIM), 1) // HEAD_DIM


def attend_body(triple, block_bias, mixed, lse, between=None):
    length = triple.shape[0]
    width = triple.shape[1] // 3
    rows = length // 4
    blocks = length // BLOCK
    for pair in range(width // 128):
        keys = triple[:, width + pair * 128 : width + pair * 128 + 128]
        values = triple[:, 2 * width + pair * 128 : 2 * width + pair * 128 + 128]
        values_t = values.astype(F32).T.astype(BF16)

        def step(place, carry):
            start = pl.multiple_of(place * rows, rows)
            queries = triple[pl.ds(start, rows), pair * 128 : pair * 128 + 128]
            queries = queries * jnp.asarray(0.125, BF16)
            side = head_mask(rows)
            halves = []
            for which in range(2):
                head = 2 * pair + which
                one = jnp.where(side == which, queries, jnp.zeros_like(queries))
                scores = dot(keys, one, NT)
                shift = block_bias[head, :, pl.ds(start, rows)]
                scores = scores.reshape(blocks, BLOCK, rows) + shift[:, None, :]
                peak = jnp.max(jnp.max(scores, axis=0), axis=0, keepdims=True)
                powered = jnp.exp(scores - peak[None])
                total = jnp.sum(jnp.sum(powered, axis=0), axis=0, keepdims=True)
                lse[head : head + 1, pl.ds(start, rows)] = peak + jnp.log(total)
                low = powered.astype(BF16).reshape(length, rows)
                part = dot(values_t[which * HEAD_DIM : (which + 1) * HEAD_DIM, :], low)
                halves.append(part / total)
            joined = jnp.concatenate(halves, axis=0)
            mixed[place, :, pair * 128 : pair * 128 + 128] = joined.T.astype(BF16)
            return carry

        lax.fori_loop(0, 4, step, 0)
        if between is not None and pair == 0:
            between()


def attend(triple, block_bias):
    length, columns = triple.shape
    width = columns // 3
    heads = width // HEAD_DIM
    rows = length // 4
    return pl.pallas_call(
        attend_body,
        name="attend",
        out_shape=(shape((4, rows, width), BF16), shape((8, length), F32)),
        in_specs=[VM, VM],
        out_specs=(VM, VM),
        compiler_params=params(),
        cost_estimate=cost(
            32 * heads * length * length * HEAD_DIM, 8 * length * width, heads * length * length
        ),
    )(triple, block_bias)


def attend_back_body(triple, block_bias, lse, grads, mixed, d_triple, key_total, value_total):
    length = triple.shape[0]
    width = triple.shape[1] // 3
    rows = length // 4
    blocks = length // BLOCK
    for pair in range(width // 128):
        lanes = slice(pair * 128, pair * 128 + 128)
        keys = triple[:, width + pair * 128 : width + pair * 128 + 128]
        values = triple[:, 2 * width + pair * 128 : 2 * width + pair * 128 + 128]
        keys_t = keys.astype(F32).T.astype(BF16)
        key_total[...] = jnp.zeros_like(key_total)
        value_total[...] = jnp.zeros_like(value_total)

        def step(place, carry):
            start = pl.multiple_of(place * rows, rows)
            queries = triple[pl.ds(start, rows), lanes] * jnp.asarray(0.125, BF16)
            grad = grads[place, :, lanes]
            product = (grad.astype(F32) * mixed[place, :, lanes].astype(F32)).T
            side = head_mask(rows)
            halves = []
            for which in range(2):
                head = 2 * pair + which
                one = jnp.where(side == which, queries, jnp.zeros_like(queries))
                one_grad = jnp.where(side == which, grad, jnp.zeros_like(grad))
                delta = jnp.sum(
                    product[which * HEAD_DIM : (which + 1) * HEAD_DIM, :], axis=0, keepdims=True
                )
                scores = dot(keys, one, NT)
                shift = block_bias[head, :, pl.ds(start, rows)] - lse[head : head + 1, pl.ds(start, rows)]
                exact = jnp.exp(scores.reshape(blocks, BLOCK, rows) + shift[:, None, :])
                exact = exact.reshape(length, rows)
                value_total[...] += dot(exact.astype(BF16), one_grad)
                d_probs = dot(values, one_grad, NT)
                d_scores = (exact * (d_probs - delta)).astype(BF16)
                key_total[...] += dot(d_scores, one)
                halves.append(dot(keys_t[which * HEAD_DIM : (which + 1) * HEAD_DIM, :], d_scores))
            joined = jnp.concatenate(halves, axis=0) * 0.125
            d_triple[pl.ds(start, rows), lanes] = joined.T.astype(BF16)
            return carry

        lax.fori_loop(0, 4, step, 0)
        d_triple[:, width + pair * 128 : width + pair * 128 + 128] = key_total[...].astype(BF16)
        d_triple[:, 2 * width + pair * 128 : 2 * width + pair * 128 + 128] = value_total[
            ...
        ].astype(BF16)


def attend_back_kernel(triple, block_bias, lse, g0, g1, g2, g3, mixed, weight, d_triple, norm_grad, grads, key_total, value_total):
    rows = g0.shape[0]
    for place, part in enumerate((g0, g1, g2, g3)):
        grads[place] = part[...]
    attend_back_body(triple, block_bias, lse, grads, mixed, d_triple, key_total, value_total)
    for place in range(4):
        part = dot(d_triple[place * rows : (place + 1) * rows, :], weight[...], NT)
        norm_grad[place] = part.astype(BF16)


def attend_back(triple, block_bias, lse, grads, mixed, weight):
    length, columns = triple.shape
    width = columns // 3
    heads = width // HEAD_DIM
    rows = length // 4
    return pl.pallas_call(
        attend_back_kernel,
        name="attend_back",
        out_shape=(shape((length, columns), BF16), shape((4, rows, weight.shape[0]), BF16)),
        in_specs=[VM] * 9,
        out_specs=(VM,) * 2,
        scratch_shapes=[
            pltpu.VMEM((4, rows, width), BF16),
            pltpu.VMEM((length, 128), F32),
            pltpu.VMEM((length, 128), F32),
        ],
        compiler_params=params(),
        cost_estimate=cost(
            80 * heads * length * length * HEAD_DIM, 16 * length * width, heads * length * length
        ),
    )(triple, block_bias, lse, *grads, mixed, weight)


def output_kernel(tokens, joined, gain, bias, weight, attended, normed):
    rows = tokens.shape[1]
    for micro in range(2):
        span = slice(micro * rows, (micro + 1) * rows)
        value = tokens[micro].astype(F32) + dot(joined[span, :], weight[...])
        attended[span, :] = value
        normed[span, :] = normalize(value, gain[...], bias[...])


def output_project(tokens, joined, gain, bias, weight):
    micro, rows, width = tokens.shape
    total = micro * rows
    return pl.pallas_call(
        output_kernel,
        name="output_project",
        out_shape=(shape((total, width), F32), shape((total, width), BF16)),
        in_specs=[VM] * 5,
        out_specs=(VM, VM),
        compiler_params=params(),
        cost_estimate=cost(2 * total * width * width, 12 * total * width + 2 * width * width),
    )(tokens, joined, gain, bias, weight)


CURVE = 0.7978845608028654
CUBIC = 0.044715


def feed_kernel(ids, h0, h1, c0, c1, shift, *rest):
    expand_held, shrink_held = rest[:2]
    own_out, other_out, own_hidden, other_hidden, bias_grad = rest[2:7]
    shrink_sent, shrink_kept, expand_sent, expand_kept = rest[7:11]
    hidden, tangent, hidden_t, out_total, hidden_total = rest[11:]
    base = ids[0]
    rows, width = h0.shape
    tile = shrink_held.shape[0] // 8
    deep = width // 8
    hidden[:rows, :] = h0[...]
    hidden[rows:, :] = h1[...]
    tangent[:rows, :] = c0[...]
    tangent[rows:, :] = c1[...]
    for j in range(8):
        source = pl.multiple_of((base ^ j) * deep, deep)
        hidden_t[j * deep : (j + 1) * deep, :] = (
            hidden[:, pl.ds(source, deep)].astype(F32).T.astype(BF16)
        )
    for step, j in enumerate((1, 3, 5, 7, 0, 2, 4, 6)):
        column = pl.multiple_of((base ^ j) * tile, tile)
        up = expand_held[:, pl.ds(column, tile)]
        down = shrink_held[pl.ds(column, tile), :]
        before = dot(hidden[...], up) + shift[:, pl.ds(column, tile)]
        d_active = dot(tangent[...], down, NT)
        square = before * before
        bend = jnp.tanh(CURVE * before * (1.0 + CUBIC * square))
        plus = 0.5 * (1.0 + bend)
        active = (before * plus).astype(BF16)
        slope = plus + (0.5 * CURVE) * before * (1.0 - bend * bend) * (1.0 + 3 * CUBIC * square)
        d_before = (d_active * slope).astype(BF16)
        bias_grad[:, pl.ds(column, tile)] = jnp.sum(d_before.astype(F32), axis=0, keepdims=True)
        out_part = dot(active, down)
        hidden_part = dot(d_before, up, NT)
        if step == 0:
            out_total[...] = out_part
            hidden_total[...] = hidden_part
        else:
            out_total[...] += out_part
            hidden_total[...] += hidden_part
        shrink_part = dot(active, tangent[...], TN).astype(BF16)
        (shrink_sent if j % 2 else shrink_kept)[j // 2] = shrink_part
        expand_part = dot(hidden_t[...], d_before).astype(BF16)
        for place in range(8):
            target = expand_sent if place % 2 else expand_kept
            target[place // 2, :, pl.ds(column, tile)] = expand_part[
                place * deep : (place + 1) * deep, :
            ]
    own_out[...] = out_total[:rows, :]
    other_out[...] = out_total[rows:, :].astype(BF16)
    own_hidden[...] = hidden_total[:rows, :]
    other_hidden[...] = hidden_total[rows:, :].astype(BF16)


def feed(ids, hidden, tangent, shift, expand, shrink):
    rows, width = hidden[0].shape
    wide = expand.shape[1]
    deep, tile = width // 8, wide // 8
    return pl.pallas_call(
        feed_kernel,
        name="feed",
        out_shape=(
            shape((rows, width), F32),
            shape((rows, width), BF16),
            shape((rows, width), F32),
            shape((rows, width), BF16),
            shape((1, wide), F32),
            shape((4, tile, width), BF16),
            shape((4, tile, width), BF16),
            shape((4, deep, wide), BF16),
            shape((4, deep, wide), BF16),
        ),
        in_specs=[SM] + [VM] * 7,
        out_specs=(VM,) * 9,
        scratch_shapes=[
            pltpu.VMEM((2 * rows, width), BF16),
            pltpu.VMEM((2 * rows, width), BF16),
            pltpu.VMEM((width, 2 * rows), BF16),
            pltpu.VMEM((2 * rows, width), F32),
            pltpu.VMEM((2 * rows, width), F32),
        ],
        compiler_params=params(60),
        cost_estimate=cost(24 * rows * width * wide, 8 * width * wide + 20 * rows * width, 2 * rows * wide),
    )(ids, *hidden, *tangent, shift, expand, shrink)


def branch_kernel(
    ids, attended, own_hidden, came_hidden, tangent, own_out, came_out, gain, shift, weight, *rest
):
    result, d_attended, d_branch = rest[:3]
    grads, (gain_grad, bias_grad, shift_grad) = rest[3:11], rest[11:14]
    rows = tangent.shape[1]
    width = gain.shape[1] // 4
    gain_total = bias_total = shift_total = 0.0
    for micro in range(2):
        span = slice(micro * rows, (micro + 1) * rows)
        value = attended[span, :]
        cot = tangent[micro].astype(F32)
        branch = own_out[span, :] + came_out[span, :].astype(F32) + shift[...]
        result[micro] = (value + branch).astype(BF16)
        unit, inverse = norm_parts(value)
        grad = own_hidden[span, :] + came_hidden[span, :].astype(F32)
        gain_total = gain_total + jnp.sum(grad * unit, axis=0, keepdims=True)
        bias_total = bias_total + jnp.sum(grad, axis=0, keepdims=True)
        shift_total = shift_total + jnp.sum(cot, axis=0, keepdims=True)
        total = cot + norm_back(grad, unit, inverse, gain[...])
        d_attended[span, :] = total
        d_branch[span, :] = total.astype(BF16)
    gain_grad[...] = gain_total
    bias_grad[...] = bias_total
    shift_grad[...] = shift_total
    for micro in range(2):
        for place in range(4):
            start = pl.multiple_of((ids[1] ^ place) * width, width)
            part = dot(d_branch[micro * rows : (micro + 1) * rows, :], weight[pl.ds(start, width), :], NT)
            grads[4 * micro + place][...] = part.astype(BF16)


def branch_back(ids, attended, own_hidden, came_hidden, tangent, own_out, came_out, gain, shift, weight):
    micro, rows, width = tangent.shape
    total = micro * rows
    row = shape((1, width), F32)
    return pl.pallas_call(
        branch_kernel,
        name="branch_back",
        out_shape=(
            shape(tangent.shape, BF16),
            shape((total, width), F32),
            shape((total, width), BF16),
        )
        + tuple(shape((rows, width // 4), BF16) for _ in range(8))
        + (row, row, row),
        in_specs=[SM] + [VM] * 9,
        out_specs=(VM,) * 14,
        compiler_params=params(),
        cost_estimate=cost(2 * total * width * width, 32 * total * width),
    )(ids, attended, own_hidden, came_hidden, tangent, own_out, came_out, gain, shift, weight)


def output_grad_kernel(ids, own_mixed, other_mixed, own_branch, other_branch, out):
    rows = out.shape[1]
    width = own_branch.shape[1]
    half = width // 2
    column = pl.multiple_of(ids[2] * half, half)
    right = own_branch[:, pl.ds(column, half)]
    for k in range(4):
        start = pl.multiple_of((ids[0] ^ (2 * k + ids[3])) * rows, rows)
        part = dot(own_mixed[:, pl.ds(start, rows)], right, TN)
        part += dot(other_mixed[:, pl.ds(start, rows)], other_branch[...], TN)
        out[k] = part.astype(BF16)


def output_grad(ids, own_mixed, other_mixed, own_branch, other_branch):
    total, width = own_mixed.shape
    return pl.pallas_call(
        output_grad_kernel,
        name="output_grad",
        out_shape=shape((4, width // 8, width // 2), BF16),
        in_specs=[SM] + [VM] * 4,
        out_specs=VM,
        compiler_params=params(),
        cost_estimate=cost(total * width * width, 8 * total * width),
    )(ids, own_mixed, other_mixed, own_branch, other_branch)


def triple_grad_kernel(ids, n0, n1, d0, d1, out):
    rows = out.shape[1]
    for k in range(4):
        column = pl.multiple_of((ids[0] ^ (2 * k + ids[3])) * rows, rows)
        part = dot(n0[:, pl.ds(column, rows)], d0[...], TN)
        part += dot(n1[:, pl.ds(column, rows)], d1[...], TN)
        out[k] = part.astype(BF16)


def triple_grad(ids, normed, grads):
    length, width = normed[0].shape
    columns = grads[0].shape[1]
    return pl.pallas_call(
        triple_grad_kernel,
        name="triple_grad",
        out_shape=shape((4, width // 8, columns), BF16),
        in_specs=[SM] + [VM] * 4,
        out_specs=VM,
        compiler_params=params(),
        cost_estimate=cost(2 * length * width * columns, 4 * length * (width + columns)),
    )(ids, *normed, *grads)


def first_back_kernel(tokens, d_attended, gain, *rest):
    parts, (grad_out, gain_grad, bias_grad) = rest[:6], rest[6:]
    rows = tokens.shape[1]
    gain_total = bias_total = 0.0
    for micro in range(2):
        one, two, three = parts[3 * micro : 3 * micro + 3]
        grad = one[...].astype(F32) + two[...].astype(F32) + three[...].astype(F32)
        unit, inverse = norm_parts(tokens[micro].astype(F32))
        gain_total = gain_total + jnp.sum(grad * unit, axis=0, keepdims=True)
        bias_total = bias_total + jnp.sum(grad, axis=0, keepdims=True)
        total = d_attended[micro * rows : (micro + 1) * rows, :]
        grad_out[micro] = (total + norm_back(grad, unit, inverse, gain[...])).astype(BF16)
    gain_grad[...] = gain_total
    bias_grad[...] = bias_total


def first_back(tokens, d_attended, gain, parts):
    micro, rows, width = tokens.shape
    row = shape((1, width), F32)
    return pl.pallas_call(
        first_back_kernel,
        name="first_back",
        out_shape=(shape(tokens.shape, BF16), row, row),
        in_specs=[VM] * 9,
        out_specs=(VM,) * 3,
        compiler_params=params(),
        cost_estimate=cost(20 * micro * rows * width, 16 * micro * rows * width),
    )(tokens, d_attended, gain, *parts)


def flip(index, bits):
    out, bit = index, 1
    while bit <= bits:
        if bits & bit:
            out = out + bit * (1 - 2 * lax.rem(lax.div(index, jnp.int32(bit)), jnp.int32(2)))
        bit *= 2
    return out


class Moves:
    def __init__(self, send, recv):
        self.send, self.recv, self.started, self.freed = send, recv, [], []
        self.place = {"ctx": lax.axis_index("ctx"), "fsdp": lax.axis_index("fsdp")}

    def greet(self):
        barrier = pltpu.get_barrier_semaphore()
        partners = [("ctx", 1), ("ctx", 2), ("ctx", 3), ("fsdp", 1), ("fsdp", 2), ("fsdp", 4), ("fsdp", 6)]
        for axis, bits in partners:
            pl.semaphore_signal(
                barrier,
                inc=1,
                device_id={axis: flip(self.place[axis], bits)},
                device_id_type=pl.DeviceIdType.MESH,
            )
        pl.semaphore_wait(barrier, len(partners))

    def go(self, source, target, axis, bits):
        slot = len(self.started)
        move = pltpu.make_async_remote_copy(
            src_ref=source,
            dst_ref=target,
            send_sem=self.send.at[slot],
            recv_sem=self.recv.at[slot],
            device_id={axis: flip(self.place[axis], bits)},
            device_id_type=pl.DeviceIdType.MESH,
        )
        move.start()
        self.started.append(move)
        return move

    def sent(self, move):
        move.wait_send()
        self.freed.append(move)

    def close(self):
        for move in self.started:
            if not any(move is other for other in self.freed):
                move.wait_send()


class Gather:
    def __init__(self, moves, part, view, own, shared=False):
        self.moves, self.view, self.own, self.shared = moves, view, own, shared
        self.part = part

    def start(self):
        moves, part, view, me = self.moves, self.part, self.view, self.moves.place["fsdp"]
        self.along = [moves.go(part, view(me), "fsdp", 2 * k) for k in range(1, 4)]
        self.across = [moves.go(part, view(me), "fsdp", 1)]
        self.over = [moves.go(part, view(me), "ctx", 2)] if self.shared else []
        return self

    def pass_on(self, index):
        if self.shared:
            block = self.view(index)
            self.over.append(self.moves.go(block, block, "ctx", 2))

    def forward(self):
        me = self.moves.place["fsdp"]
        for k in range(1, 4):
            self.along[k - 1].wait_recv()
            block = self.view(flip(me, 2 * k))
            self.across.append(self.moves.go(block, block, "fsdp", 1))
            self.pass_on(flip(me, 2 * k))

    def second(self):
        for k, move in enumerate(self.across):
            move.wait_recv()
            self.pass_on(flip(self.moves.place["fsdp"], 2 * k + 1))

    def finish(self):
        if not self.shared:
            self.second()
        for move in self.over:
            move.wait_recv()
        for copy in self.own:
            copy.wait()


FORWARD_MOVES = 106


def row_view(ref, rows, columns=slice(None)):
    return lambda index: ref.at[pl.ds(pl.multiple_of(index * rows, rows), rows), columns]


def forward_kernel(
    global_ids,
    tokens,
    small,
    picks,
    triple_weight,
    output_weight,
    expand_weight,
    shrink_weight,
    tangent,
    small_all,
    triple_out,
    output_out,
    expand_all,
    shrink_all,
    tangent_other,
    triple,
    normed,
    block_bias,
    lse,
    mixed,
    joined_out,
    mixed_other,
    attended,
    hidden,
    hidden_other,
    parts,
    small_held,
    picks_held,
    triple_held,
    output_held,
    joined,
    hidden_held,
    send,
    recv,
    local,
):
    moves = Moves(send, recv)
    rank, me = moves.place["ctx"], moves.place["fsdp"]
    core = lax.rem(rank, jnp.int32(2))
    micro, rows, width = tokens.shape
    half = width // 2
    quarter = width // 4
    shard = triple_weight.shape[0]
    wide = expand_all.shape[1] // 2
    deep = shrink_weight.shape[0] // 8
    chip = lax.div(rank, jnp.int32(2))
    locals_used = []

    def copy_here(source, target):
        copy = pltpu.make_async_copy(source, target, local.at[len(locals_used)])
        copy.start()
        locals_used.append(copy)
        return copy

    def at(start, size, unit=128):
        return pl.ds(pl.multiple_of(start, unit), size)

    mine = at(me * shard, shard)
    triple_own = [
        copy_here(
            triple_weight.at[:, at(k * width + rank * quarter, quarter)],
            triple_held.at[mine, k * quarter : (k + 1) * quarter],
        )
        for k in range(3)
    ]
    tile = wide // 4
    expand_views = [row_view(expand_all, shard, at(chip * wide + cut * (wide // 2), wide // 2)) for cut in range(2)]
    expand_own = [
        copy_here(
            expand_weight.at[:, at(((4 * chip + q) * 2 + core) * tile, tile)],
            expand_all.at[mine, at(chip * wide + q * tile, tile)],
        )
        for q in range(4)
    ]
    output_columns = at(core * half + chip * quarter, quarter)
    output_view = row_view(output_held, shard, output_columns)
    shrink_views = [
        lambda i, cut=cut: shrink_all.at[at(i * 4 * deep + cut * deep, deep, 64)] for cut in range(4)
    ]
    shrink_parts = [shrink_weight.at[at((core * 4 + cut) * deep, deep, 64)] for cut in range(4)]
    small_own = copy_here(small, small_held.at[me])
    output_own = copy_here(output_weight.at[:, output_columns], output_view(me))
    shrink_own = [copy_here(shrink_parts[cut], shrink_views[cut](me)) for cut in range(4)]
    moves.greet()

    small_gather = Gather(moves, small, lambda index: small_held.at[index], [small_own]).start()
    far = [moves.go(tokens.at[0], parts.at[0, 2], "ctx", 2)]
    near = [moves.go(tokens.at[0], parts.at[0, 1], "ctx", 1)]
    for copy in triple_own:
        copy.wait()
    triple_view = row_view(triple_held, shard)
    triple_gather = Gather(moves, triple_view(me), triple_view, []).start()
    picked = [moves.go(picks.at[flip(rank, p)], picks_held.at[p], "ctx", p) for p in range(1, 4)]
    near.append(moves.go(tokens.at[1], parts.at[1, 1], "ctx", 1))
    far.append(moves.go(tokens.at[1], parts.at[1, 2], "ctx", 2))
    output_gather = Gather(moves, output_weight.at[:, output_columns], output_view, [output_own], True)
    for copy in expand_own:
        copy.wait()
    expands = [Gather(moves, view(me), view, [], True) for view in expand_views]
    shrinks = [Gather(moves, shrink_parts[cut], shrink_views[cut], [shrink_own[cut]]) for cut in range(4)]
    small_gather.forward()
    triple_gather.forward()
    output_gather.start()
    expands[0].start()
    expands[1].start()
    tangent_move = moves.go(tangent, tangent_other, "ctx", 1)

    for move in picked:
        move.wait_recv()
    count = block_bias.shape[2]
    each = count // 4
    ranks = [flip(rank, p) if p else rank for p in range(4)]
    key_row = lax.broadcasted_iota(jnp.int32, (count, rows), 0)
    key_place = key_row // each
    key_rank = ranks[0]
    for p in range(1, 4):
        key_rank = jnp.where(key_place == p, ranks[p], key_rank)
    key_block = key_rank * each + key_row % each
    lane = lax.broadcasted_iota(jnp.int32, (count, rows), 1) // BLOCK
    for step in range(micro):
        first, second = global_ids[step, 0], global_ids[step, 1]
        key_global = (key_block == first) | (key_block == second)
        for p in range(4):
            source = picks.at[rank] if p == 0 else picks_held.at[p]
            query_block = ranks[p] * each + lane
            base = key_global | (jnp.abs(query_block - key_block) <= 1)
            base = base | (query_block == first) | (query_block == second)
            for head in range(block_bias.shape[1]):
                hit = base
                for pick in range(3):
                    hit = hit | (source[step, head, pick : pick + 1, :] == key_block)
                block_bias[step, head, :, p * rows : (p + 1) * rows] = jnp.where(hit, 0.0, -1e30)

    small_gather.finish()
    small_all[...] = small_held[...]

    def vector(line):
        return jnp.concatenate([small_held[b, line : line + 1, :] for b in range(8)], axis=1)

    gain_one, bias_one, gain_two, bias_two = (vector(line) for line in range(4))

    for step in range(micro):
        far[step].wait_recv()
        near.append(moves.go(parts.at[step, 2], parts.at[step, 3], "ctx", 1))
    mixed_moves = []
    for step in range(micro):
        near[step].wait_recv()
        near[2 + step].wait_recv()
        for p in range(4):
            source = tokens[step] if p == 0 else parts[step, p]
            normed[step, p * rows : (p + 1) * rows, :] = normalize(source, gain_one, bias_one)
        if step == 0:
            output_gather.forward()
            shrinks[0].start()
            triple_gather.finish()
        for p in range(4):
            span = slice(p * rows, (p + 1) * rows)
            triple[step, span, :] = dot(normed[step, span, :], triple_held[...]).astype(BF16)

        def between_first():
            expands[1].forward()
            shrinks[2].start()
            output_gather.second()

        def between_second():
            expands[1].second()
            shrinks[1].forward()

        if step == 0:
            expands[0].forward()
            shrinks[1].start()
        else:
            output_gather.finish()
            piece = output_held.at[:, at(core * half, half)]
            output_move = moves.go(piece, piece, "ctx", 1)
            shrinks[0].forward()
        attend_body(
            triple.at[step],
            block_bias.at[step],
            mixed.at[step],
            lse.at[step],
            between_second if step else between_first,
        )
        own = pl.ds(pl.multiple_of(rank * quarter, quarter), quarter)
        span = slice(step * rows, (step + 1) * rows)
        joined[span, own] = mixed[step, 0]
        for p in range(1, 4):
            mixed_moves.append(moves.go(mixed.at[step, p], joined.at[span, own], "ctx", p))
        if step == 0:
            shrinks[3].start()
            expands[0].second()
        else:
            shrinks[2].forward()
    output_move.wait_recv()
    for move in mixed_moves:
        move.wait_recv()
    keep = [copy_here(triple_held, triple_out), copy_here(output_held, output_out)]
    output_kernel(tokens, joined, gain_two, bias_two, output_held, attended, hidden_held)
    last = [
        moves.go(hidden_held, hidden_other, "ctx", 1),
        moves.go(joined, mixed_other, "ctx", 1),
    ]
    hidden[...] = hidden_held[...]
    joined_out[...] = joined[...]
    shrinks[3].forward()
    for gather in shrinks + expands:
        gather.finish()
    for move in [tangent_move] + last:
        move.wait_recv()
    for copy in keep:
        copy.wait()
    moves.close()


def forward_together(global_ids, tokens, small, picks, triple_weight, output_weight, expand_weight, shrink_weight, tangent):
    micro, rows, width = tokens.shape
    total = micro * rows
    columns = triple_weight.shape[1] // 4
    wide = expand_weight.shape[1] // 2
    length = 4 * rows
    heads = picks.shape[2]
    outs = (
        (VM, (8,) + small.shape, F32),
        (ANY, (width, columns), BF16),
        (ANY, (width, width), BF16),
        (ANY, (width, wide), BF16),
        (ANY, (wide, width), BF16),
        (ANY, (total, width), BF16),
        (VM, (micro, length, columns), BF16),
        (VM, (micro, length, width), BF16),
        (VM, (micro, heads, length // BLOCK, length), F32),
        (VM, (micro, 8, length), F32),
        (VM, (micro, 4, rows, width // 4), BF16),
        (VM, (total, width), BF16),
        (ANY, (total, width), BF16),
        (VM, (total, width), F32),
        (VM, (total, width), BF16),
        (ANY, (total, width), BF16),
    )
    return pl.pallas_call(
        forward_kernel,
        name="forward_together",
        out_shape=tuple(shape(dims, kind) for _, dims, kind in outs),
        in_specs=[SM] + [VM] * 3 + [ANY] * 5,
        out_specs=tuple(spec for spec, _, _ in outs),
        scratch_shapes=[
            pltpu.VMEM((micro, 4, rows, width), BF16),
            pltpu.VMEM((8,) + small.shape, F32),
            pltpu.VMEM(picks.shape, jnp.int32),
            pltpu.VMEM((width, columns), BF16),
            pltpu.VMEM((width, width), BF16),
            pltpu.VMEM((total, width), BF16),
            pltpu.VMEM((total, width), BF16),
            pltpu.SemaphoreType.DMA((FORWARD_MOVES,)),
            pltpu.SemaphoreType.DMA((FORWARD_MOVES,)),
            pltpu.SemaphoreType.DMA((15,)),
        ],
        compiler_params=pltpu.CompilerParams(
            collective_id=0, has_side_effects=True, vmem_limit_bytes=56 * MIB
        ),
        cost_estimate=cost(16 * total * width * width, 64 * MIB),
    )(global_ids, tokens, small, picks, triple_weight, output_weight, expand_weight, shrink_weight, tangent)


class Reduce:
    def __init__(self, moves, sent, came, line):
        self.moves, self.came, self.line = moves, came, line
        self.across = moves.go(sent, came, "fsdp", 1)

    def forward(self, *kept):
        self.across.wait_recv()
        for k in range(4):
            self.came[k] = wide_add(self.came[k], *(part[k] for part in kept)).astype(self.came.dtype)
        self.along = [
            self.moves.go(self.came.at[k], self.line.at[k - 1], "fsdp", 2 * k) for k in range(1, 4)
        ]

    def finish(self):
        for move in self.along:
            move.wait_recv()
        return wide_add(self.came[0], *(self.line[k] for k in range(3)))


BACKWARD_MOVES = 66


def backward_kernel(
    vectors,
    tangent,
    output_weight,
    triple_weight,
    triples,
    biases,
    lses,
    mixed_own,
    shift_in_grad,
    own_hidden,
    other_hidden,
    own_out,
    other_out,
    attended,
    tokens,
    mixed_all,
    mixed_other,
    normeds,
    shrink_sent,
    shrink_kept,
    expand_sent,
    expand_kept,
    result,
    token_grad,
    shrink_out,
    expand_out,
    output_out,
    triple_out,
    early_out,
    late_out,
    came_out,
    came_hidden,
    d_attended,
    stage,
    held,
    d_branch,
    branch_other,
    d_mixed,
    grads,
    d_triples,
    key_total,
    value_total,
    near_parts,
    own_parts,
    near_came,
    far_sent,
    far_came,
    kept_ring,
    expand_own,
    over_came,
    feed_came,
    feed_line,
    output_sent,
    output_kept,
    output_came,
    output_line,
    triple_sent,
    triple_kept,
    triple_came,
    triple_line,
    chip_sent,
    chip_came,
    final,
    triple_final,
    small_all,
    small_sent,
    small_kept,
    small_came,
    small_line,
    small_chip,
    small_chip_came,
    small_core,
    small_core_came,
    send,
    recv,
    local,
):
    moves = Moves(send, recv)
    rank, me = moves.place["ctx"], moves.place["fsdp"]
    core = lax.rem(rank, jnp.int32(2))
    micro, rows, width = tangent.shape
    half, quarter, shard = width // 2, width // 4, width // 8
    moves.greet()
    used = []

    def load(source, target):
        copy = pltpu.make_async_copy(source, target, local.at[len(used)])
        copy.start()
        used.append(copy)
        return copy

    def at(start, size, unit=128):
        return pl.ds(pl.multiple_of(start, unit), size)

    chip = lax.div(rank, jnp.int32(2))
    deep = shrink_sent.shape[1] // 2
    wide = expand_sent.shape[2] // 2
    here, there = at(chip * wide, wide), at((1 - chip) * wide, wide)
    hidden_move = moves.go(other_hidden, came_hidden, "ctx", 1)

    def shrink_begin(i):
        part = shrink_sent.at[:, i * deep : (i + 1) * deep, :]
        return Reduce(moves, part, feed_came.at[i], feed_line.at[i])

    shrinks = [shrink_begin(0)]
    over_moves = [moves.go(expand_sent.at[:, :, there], over_came.at[0], "ctx", 2)]
    loads = [load(own_hidden, d_attended), load(attended, stage)]
    out_move = moves.go(other_out, came_out, "ctx", 1)
    mixed_loads = [load(mixed_all, held.at[0, : 2 * rows, :]), load(mixed_other, held.at[0, 2 * rows :, :])]
    expand_loads = [
        load(expand_sent.at[:, :, here], expand_own.at[0]),
        load(expand_kept.at[:, :, here], expand_own.at[1]),
    ]
    kept_loads = [load(shrink_kept.at[:, i * deep : (i + 1) * deep, :], kept_ring.at[i]) for i in range(2)]

    gain_two, gain_one, shift_out = vectors[0:1, :], vectors[1:2, :], vectors[2:3, :]
    for copy in loads:
        copy.wait()
    hidden_move.wait_recv()
    gain_total = bias_total = shift_total = 0.0
    for step in range(micro):
        span = slice(step * rows, (step + 1) * rows)
        cot = tangent[step].astype(F32)
        unit, inverse = norm_parts(stage[span, :])
        grad = d_attended[span, :] + came_hidden[span, :].astype(F32)
        gain_total = gain_total + jnp.sum(grad * unit, axis=0, keepdims=True)
        bias_total = bias_total + jnp.sum(grad, axis=0, keepdims=True)
        shift_total = shift_total + jnp.sum(cot, axis=0, keepdims=True)
        total = cot + norm_back(grad, unit, inverse, gain_two)
        d_attended[span, :] = total
        d_branch[span, :] = total.astype(BF16)
    theirs = d_branch.at[:, pl.ds(pl.multiple_of((1 - core) * half, half), half)]
    branch_move = moves.go(theirs, branch_other, "ctx", 1)
    grad_moves = []
    for step in range(micro):
        for p in (2, 3, 1, 0):
            start = pl.multiple_of((flip(rank, p) if p else rank) * quarter, quarter)
            part = dot(d_branch[step * rows : (step + 1) * rows, :], output_weight[pl.ds(start, quarter), :], NT)
            if p:
                d_mixed[step, p] = part.astype(BF16)
                grad_moves.append(moves.go(d_mixed.at[step, p], grads.at[step, p], "ctx", p))
            else:
                grads[step, 0] = part.astype(BF16)

    over_moves.append(moves.go(expand_kept.at[:, :, there], over_came.at[1], "ctx", 2))

    def small_row(which, line, vector):
        for b in range(8):
            small_all[which, b, line : line + 1, :] = vector[:, b * shard : (b + 1) * shard]

    def small_begin(which):
        for k in range(4):
            small_sent[which, k] = small_all[which, flip(me, 2 * k + 1)]
            small_kept[which, k] = small_all[which, flip(me, 2 * k) if k else me]
        return Reduce(moves, small_sent.at[which], small_came.at[which], small_line.at[which])

    def small_chips(which):
        small_chip[which] = smalls[which].finish()
        return moves.go(small_chip.at[which], small_chip_came.at[which], "ctx", 2)

    def small_cores(which, move):
        move.wait_recv()
        small_core[which] = small_chip[which] + small_chip_came[which]
        return moves.go(small_core.at[which], small_core_came.at[which], "ctx", 1)

    def small_end(which, move, out):
        move.wait_recv()
        out[...] = small_core[which] + small_core_came[which]

    small_all[...] = jnp.zeros_like(small_all)
    for line, vector in enumerate((gain_total, bias_total, shift_total)):
        small_row(0, line, vector)
    unit_lines = shift_in_grad.shape[1] // 8 // 128
    for b in range(8):
        for line in range(unit_lines):
            lanes = slice((b * unit_lines + line) * 128, (b * unit_lines + line + 1) * 128)
            small_all[0, b, pl.ds(3 + core * unit_lines + line, 1), :] = shift_in_grad[:, lanes]
    smalls = [small_begin(0)]

    for copy in mixed_loads:
        copy.wait()
    branch_move.wait_recv()
    mine = pl.ds(pl.multiple_of(core * half, half), half)

    def output_part(index):
        lanes = pl.ds(pl.multiple_of(index * shard, shard), shard)
        part = dot(held[0, : 2 * rows, lanes], d_branch[:, mine], TN)
        return part + dot(held[0, 2 * rows :, lanes], branch_other[...], TN)

    for k in range(4):
        output_sent[k] = output_part(flip(me, 2 * k + 1)).astype(BF16)
    output_reduce = Reduce(moves, output_sent, output_came, output_line)
    for k in range(4):
        output_kept[k] = output_part(flip(me, 2 * k) if k else me).astype(BF16)
    normed_loads = [load(normeds.at[step], held.at[step]) for step in range(1, micro)]

    norm_moves, far_moves = [], []

    def attention(step):
        for move in grad_moves[3 * step : 3 * step + 3]:
            move.wait_recv()
        attend_back_body(
            triples.at[step],
            biases.at[step],
            lses.at[step],
            grads.at[step],
            mixed_own.at[step],
            d_triples.at[step],
            key_total,
            value_total,
        )
        for p in (3, 1, 2, 0):
            span = slice(p * rows, (p + 1) * rows)
            part = dot(d_triples[step, span, :], triple_weight[...], NT).astype(BF16)
            if p:
                near_parts[step, p - 1] = part
            else:
                own_parts[step] = part
            if p % 2:
                norm_moves.append(moves.go(near_parts.at[step, p - 1], near_came.at[step, p // 2], "ctx", 1))

    def far_part(step):
        norm_moves[2 * step].wait_recv()
        far_sent[step] = wide_add(near_parts[step, 1], near_came[step, 1]).astype(BF16)
        far_moves.append(moves.go(far_sent.at[step], far_came.at[step], "ctx", 2))

    for copy in expand_loads:
        copy.wait()
    over_moves[0].wait_recv()
    for k in range(4):
        expand_own[0, k] = wide_add(expand_own[0, k], over_came[0, k]).astype(BF16)
    expand_reduce = Reduce(moves, expand_own.at[0], feed_came.at[2], feed_line.at[2])
    for copy in kept_loads:
        copy.wait()
    shrinks[0].forward(kept_ring.at[0])
    smalls[0].forward(small_kept.at[0])
    normed_loads.insert(0, load(normeds.at[0], held.at[0]))
    attention(0)
    output_reduce.forward(output_kept)
    over_moves[1].wait_recv()
    expand_reduce.forward(expand_own.at[1], over_came.at[1])
    shrinks.append(shrink_begin(1))
    far_part(0)
    attention(1)
    small_moves = [small_chips(0)]

    for copy in normed_loads:
        copy.wait()

    def triple_part(index):
        lanes = pl.ds(pl.multiple_of(index * shard, shard), shard)
        part = dot(held[0, :, lanes], d_triples[0], TN)
        return part + dot(held[1, :, lanes], d_triples[1], TN)

    for k in range(4):
        triple_sent[k] = triple_part(flip(me, 2 * k + 1)).astype(BF16)
    triple_reduce = Reduce(moves, triple_sent, triple_came, triple_line)
    shrinks[1].forward(kept_ring.at[1])
    far_part(1)
    for k in range(4):
        triple_kept[k] = triple_part(flip(me, 2 * k) if k else me).astype(BF16)
    small_moves[0] = small_cores(0, small_moves[0])

    token_load = load(tokens, held.at[0, : 2 * rows, :])
    out_load = load(own_out, stage)
    out_move.wait_recv()
    came_load = load(came_out, came_hidden)

    chips, ends, stays = {}, [], []

    def chip_begin(i, value):
        columns = value.shape[1]
        chip_sent[i, :, :columns] = value.astype(BF16)
        chips[i] = moves.go(chip_sent.at[i, :, pl.ds(0, columns)], chip_came.at[i, :, pl.ds(0, columns)], "ctx", 2)

    def place(source, target, partners=(1,)):
        for p in partners:
            ends.append(moves.go(source, target, "ctx", p))
        stays.append(load(source, target))

    def chip_end(i):
        chips[i].wait_recv()
        if i < 2:
            final[i] = wide_add(chip_sent[i], chip_came[i]).astype(BF16)
            place(final.at[i], shrink_out.at[at((2 * core + i) * deep, deep), :])
        else:
            final[i, :, :half] = wide_add(chip_sent[i, :, :half], chip_came[i, :, :half]).astype(BF16)
            place(final.at[i, :, :half], output_out.at[:, mine])

    chip_begin(0, shrinks[0].finish())

    token_load.wait()
    for move in norm_moves[1::2] + far_moves:
        move.wait_recv()
    gain_total = bias_total = 0.0
    for step in range(micro):
        span = slice(step * rows, (step + 1) * rows)
        grad = wide_add(own_parts[step], near_came[step, 0], far_came[step])
        unit, inverse = norm_parts(held[0, span, :].astype(F32))
        gain_total = gain_total + jnp.sum(grad * unit, axis=0, keepdims=True)
        bias_total = bias_total + jnp.sum(grad, axis=0, keepdims=True)
        token_grad[step] = (d_attended[span, :] + norm_back(grad, unit, inverse, gain_one)).astype(BF16)
    small_row(1, 0, gain_total)
    small_row(1, 1, bias_total)
    smalls.append(small_begin(1))
    small_end(0, small_moves[0], early_out)
    out_load.wait()
    sum_load = load(attended, d_attended)
    came_load.wait()
    for step in range(micro):
        span = slice(step * rows, (step + 1) * rows)
        stage[span, :] = stage[span, :] + came_hidden[span, :].astype(F32) + shift_out
    sum_load.wait()
    moves.sent(branch_move)
    for step in range(micro):
        span = slice(step * rows, (step + 1) * rows)
        d_branch[span, :] = (d_attended[span, :] + stage[span, :]).astype(BF16)
    result_load = load(d_branch, result)
    final[3] = expand_reduce.finish().astype(BF16)
    place(final.at[3], expand_out.at[rank], (1, 2, 3))
    chip_end(0)
    triple_reduce.forward(triple_kept)
    smalls[1].forward(small_kept.at[1])
    chip_begin(2, output_reduce.finish())
    chip_begin(1, shrinks[1].finish())
    chip_end(2)
    chip_end(1)
    triple_final[...] = triple_reduce.finish().astype(BF16)
    place(triple_final, triple_out.at[rank], (1, 2, 3))
    small_moves.append(small_cores(1, small_chips(1)))
    small_end(1, small_moves[1], late_out)
    for move in ends:
        move.wait_recv()
    for copy in stays + [result_load]:
        copy.wait()
    moves.close()


def backward_together(vectors, tangent, output_weight, triple_weight, triples, biases, lses, mixed_own, shift_in_grad, *late_arrays):
    micro, rows, width = tangent.shape
    total, half, quarter, shard = micro * rows, width // 2, width // 4, width // 8
    columns = triple_weight.shape[1]
    shrink_sent, expand_sent = late_arrays[-4], late_arrays[-2]
    deep, wide = shrink_sent.shape[1], expand_sent.shape[2]
    length = 4 * rows
    outs = (
        (ANY, (total, width), BF16),
        (VM, tangent.shape, BF16),
        (ANY, (2 * deep, width), BF16),
        (ANY, (4, shard, wide // 2), BF16),
        (ANY, (shard, width), BF16),
        (ANY, (4, shard, columns), BF16),
        (VM, (8, 128), F32),
        (VM, (8, 128), F32),
        (ANY, (total, width), BF16),
    )
    scratch = (
        ((total, width), BF16),
        ((total, width), F32),
        ((total, width), F32),
        ((2, length, width), BF16),
        ((total, width), BF16),
        ((total, half), BF16),
        ((micro, 4, rows, quarter), BF16),
        ((micro, 4, rows, quarter), BF16),
        ((micro, length, columns), BF16),
        ((length, 128), F32),
        ((length, 128), F32),
        ((micro, 3, rows, width), BF16),
        ((micro, rows, width), BF16),
        ((micro, 2, rows, width), BF16),
        ((micro, rows, width), BF16),
        ((micro, rows, width), BF16),
        ((2, 4, shard, width), BF16),
        ((2, 4, shard, width), BF16),
        ((2, 4, shard, width), BF16),
        ((3, 4, shard, width), BF16),
        ((3, 3, shard, width), BF16),
        ((4, shard, half), BF16),
        ((4, shard, half), BF16),
        ((4, shard, half), BF16),
        ((3, shard, half), BF16),
        ((4, shard, columns), BF16),
        ((4, shard, columns), BF16),
        ((4, shard, columns), BF16),
        ((3, shard, columns), BF16),
        ((3, shard, width), BF16),
        ((3, shard, width), BF16),
        ((4, shard, width), BF16),
        ((shard, columns), BF16),
        ((2, 8, 8, 128), F32),
        ((2, 4, 8, 128), F32),
        ((2, 4, 8, 128), F32),
        ((2, 4, 8, 128), F32),
        ((2, 3, 8, 128), F32),
        ((2, 8, 128), F32),
        ((2, 8, 128), F32),
        ((2, 8, 128), F32),
        ((2, 8, 128), F32),
    )
    return pl.pallas_call(
        backward_kernel,
        name="backward_together",
        out_shape=tuple(shape(dims, kind) for _, dims, kind in outs),
        in_specs=[VM] * 9 + [ANY] * 13,
        out_specs=tuple(spec for spec, _, _ in outs),
        scratch_shapes=[pltpu.VMEM(dims, kind) for dims, kind in scratch]
        + [
            pltpu.SemaphoreType.DMA((BACKWARD_MOVES,)),
            pltpu.SemaphoreType.DMA((BACKWARD_MOVES,)),
            pltpu.SemaphoreType.DMA((26,)),
        ],
        compiler_params=pltpu.CompilerParams(
            collective_id=1, has_side_effects=True, vmem_limit_bytes=63 * MIB
        ),
        cost_estimate=cost(24 * total * width * width, 64 * MIB),
    )(vectors, tangent, output_weight, triple_weight, triples, biases, lses, mixed_own, shift_in_grad, *late_arrays)


def widen_kernel(shrink, expand, output, triple, token_grad, result, *outs):
    shrink_out, expand_out, output_out, triple_out, token_out, result_out = outs
    token_out[...] = token_grad[...]
    result_out[...] = result[...]
    shrink_out[...] = shrink[...].astype(F32)
    output_out[...] = output[...].astype(F32)
    tile = expand.shape[2] // 4
    quarter = triple.shape[2] // 3
    for chip in range(2):
        for core in range(2):
            rank = 2 * chip + core
            for q in range(4):
                start = ((4 * chip + q) * 2 + core) * tile
                part = expand[rank, :, q * tile : (q + 1) * tile]
                expand_out[:, start : start + tile] = part.astype(F32)
            for k in range(3):
                start = (4 * k + rank) * quarter
                part = triple[rank, :, k * quarter : (k + 1) * quarter]
                triple_out[:, start : start + quarter] = part.astype(F32)


def widen(shrink, expand, output, triple, token_grad, result):
    shard = output.shape[0]
    return pl.pallas_call(
        widen_kernel,
        name="widen",
        out_shape=(
            shape(shrink.shape, F32),
            shape((shard, 4 * expand.shape[2]), F32),
            shape(output.shape, F32),
            shape((shard, 4 * triple.shape[2]), F32),
            shape(token_grad.shape, BF16),
            shape(result.shape, BF16),
        ),
        in_specs=[VM] * 6,
        out_specs=(VM,) * 6,
        compiler_params=params(),
        cost_estimate=cost(0, 16 * MIB),
    )(shrink, expand, output, triple, token_grad, result)


def block_biases(chosen, globals_here, rank, local_blocks):
    heads, count, _ = chosen.shape
    place = jnp.arange(count, dtype=jnp.int32)
    true_block = ((place // local_blocks) ^ rank) * local_blocks + place % local_blocks
    near = jnp.abs(true_block[:, None] - true_block[None, :]) <= 1
    is_global = jnp.any(true_block[:, None] == globals_here[None, :], axis=1)
    picked = jnp.any(chosen[:, None, :, :] == true_block[None, :, None, None], axis=3)
    allowed = near[None] | picked | is_global[None, :, None] | is_global[None, None, :]
    bias = jnp.where(allowed, 0.0, -1e30).astype(F32)
    return jnp.repeat(bias, BLOCK, axis=2)


def on_device(
    tokens,
    cotangent,
    random_blocks,
    global_blocks,
    attend_gain,
    attend_bias,
    triple_weight,
    output_weight,
    hidden_gain,
    hidden_bias,
    expand_weight,
    expand_bias,
    shrink_weight,
    shrink_bias,
):
    tokens, cotangent = tokens[:, 0], cotangent[:, 0]
    micro, rows, width = tokens.shape
    total = micro * rows
    ways = lax.axis_size("fsdp")
    fsdp = lax.axis_index("fsdp")
    rank = lax.axis_index("ctx")
    core = rank % 2
    place = place_id()
    heads_all = random_blocks.shape[2]
    own_heads = heads_all // 4
    local_blocks = rows // BLOCK
    shard = width // ways
    wide = expand_weight.shape[1]
    deep = shrink_weight.shape[0]
    ids = jnp.stack([place, rank, core, jnp.int32(0)])
    ids_sent = jnp.stack([place, rank, core, jnp.int32(1)])

    half_units = wide // (2 * ways)
    vectors = [attend_gain, attend_bias, hidden_gain, hidden_bias, shrink_bias]
    tangent_own = cotangent.reshape(total, width)
    picks = random_blocks[:, 0]
    if ways == 8:
        small = jnp.concatenate(
            [v.reshape(1, shard) for v in vectors]
            + [expand_bias.reshape(-1, shard), jnp.zeros((7, shard), BF16)]
        ).astype(F32)
        sets = picks.reshape(micro, 4, own_heads, local_blocks, -1).transpose(1, 0, 2, 4, 3)
        sets = jnp.pad(jnp.repeat(sets, BLOCK, axis=4), ((0, 0),) * 3 + ((0, 5), (0, 0)))
        (
            table,
            triple_full,
            output_full,
            expand_full,
            shrink_full,
            tangent_other,
            triples,
            normeds,
            biases,
            lses,
            mixed_own,
            mixed_all,
            mixed_other,
            attended,
            hidden,
            hidden_other,
        ) = forward_together(
            global_blocks[:, 0],
            tokens,
            small,
            sets,
            triple_weight,
            output_weight,
            expand_weight,
            shrink_weight,
            tangent_own,
        )
        gain_one, bias_one, gain_two, bias_two, shift_out = (
            table[:, k].reshape(1, width) for k in range(5)
        )
        shift_in = lax.dynamic_slice_in_dim(
            table[:, 5:9].reshape(8, 2, half_units), core, 1, 1
        ).reshape(1, wide // 2)
    else:

        def whole(part):
            return lax.all_gather(part, "fsdp", axis=0, tiled=True)

        triple_part = jnp.concatenate(
            [
                lax.dynamic_slice_in_dim(triple_weight, k * width + rank * (width // 4), width // 4, 1)
                for k in range(3)
            ],
            axis=1,
        )
        expand_part = jnp.concatenate(
            [
                lax.dynamic_slice_in_dim(expand_weight, (2 * k + core) * half_units, half_units, 1)
                for k in range(ways)
            ],
            axis=1,
        )
        shrink_part = lax.dynamic_slice_in_dim(shrink_weight, core * (deep // 2), deep // 2, 0)
        gain_one, bias_one, gain_two, bias_two, shift_out = (
            whole(v).astype(F32).reshape(1, width) for v in vectors
        )
        halves = whole(expand_bias).astype(F32).reshape(ways, 2, half_units)
        shift_in = jnp.where(core == 0, halves[:, 0], halves[:, 1]).reshape(1, wide // 2)
        triple_full, expand_full, shrink_full = whole(triple_part), whole(expand_part), whole(shrink_part)
        output_full = whole(output_weight)
        tangent_other = swap(tangent_own, "ctx", 1)
        far_picks = swap(picks, "ctx", 2)
        all_picks = jnp.stack([picks, swap(picks, "ctx", 1), far_picks, swap(far_picks, "ctx", 1)])
        chosen = lax.dynamic_slice_in_dim(all_picks, rank * own_heads, own_heads, 2)
        chosen = chosen.transpose(1, 2, 0, 3, 4).reshape(micro, own_heads, 4 * local_blocks, -1)
        triples, normeds, biases, lses, mixed_own, joined = [], [], [], [], [], []
        for step in range(micro):
            biases.append(block_biases(chosen[step], global_blocks[step, 0], rank, local_blocks))
            near, far = swap(tokens[step], "ctx", 1), swap(tokens[step], "ctx", 2)
            places = (tokens[step], near, far, swap(far, "ctx", 1))
            triple, normed = project(places, gain_one, bias_one, triple_full)
            mixed, lse = attend(triple, biases[step])
            here = [mixed[0]] + [swap(mixed[p], "ctx", p) for p in range(1, 4)]
            for low_bit, high in ((core == 1, False), (rank >= 2, True)):
                pairs = ((0, 2), (1, 3)) if high else ((0, 1), (2, 3))
                for one, two in pairs:
                    first = jnp.where(low_bit, here[two], here[one])
                    here[two] = jnp.where(low_bit, here[one], here[two])
                    here[one] = first
            joined.append(jnp.concatenate(here, axis=1))
            for kept, value in zip(
                (triples, normeds, lses, mixed_own), (triple, normed, lse, mixed)
            ):
                kept.append(value)
        mixed_all = jnp.concatenate(joined, axis=0)
        mixed_other = swap(mixed_all, "ctx", 1)
        attended, hidden = output_project(tokens, mixed_all, gain_two, bias_two, output_full)
        hidden_other = swap(hidden, "ctx", 1)

    (
        own_out,
        other_out,
        own_hidden,
        other_hidden,
        shift_in_grad,
        shrink_sent,
        shrink_kept,
        expand_sent,
        expand_kept,
    ) = feed(ids, (hidden, hidden_other), (tangent_own, tangent_other), shift_in, expand_full, shrink_full)
    if ways == 8:
        rows_of = jnp.concatenate([gain_two, gain_one, shift_out, jnp.zeros((5, width), F32)])
        (
            result,
            token_grad,
            shrink_grad,
            expand_grad,
            output_grad_all,
            triple_grad_all,
            early,
            late,
            _,
        ) = backward_together(
            rows_of,
            cotangent,
            output_full,
            triple_full,
            triples,
            biases,
            lses,
            mixed_own,
            shift_in_grad,
            own_hidden,
            other_hidden,
            own_out,
            other_out,
            attended,
            tokens.reshape(total, width),
            mixed_all,
            mixed_other,
            normeds,
            shrink_sent,
            shrink_kept,
            expand_sent,
            expand_kept,
        )
        shrink_grad, expand_grad, output_grad_all, triple_grad_all, token_grad, result = widen(
            shrink_grad, expand_grad, output_grad_all, triple_grad_all, token_grad, result.reshape(micro, rows, width)
        )
        early, late = early[:7].reshape(-1), late[:2].reshape(-1)
    else:
        came_hidden = swap(other_hidden, "ctx", 1)
        came_out = swap(other_out, "ctx", 1)
        shrink_mine = scatter_rows(shrink_kept, shrink_sent)
        expand_mine = scatter_rows(expand_kept, expand_sent)
        result, d_attended, d_branch, *grads, gain_two_grad, bias_two_grad, shift_out_grad = branch_back(
            ids,
            attended,
            own_hidden,
            came_hidden,
            cotangent,
            own_out,
            came_out,
            gain_two,
            shift_out,
            output_full,
        )
        half_sent = lax.dynamic_slice_in_dim(d_branch, (1 - core) * (width // 2), width // 2, 1)
        branch_other = swap(half_sent, "ctx", 1)
        output_sent = output_grad(ids_sent, mixed_all, mixed_other, d_branch, branch_other)
        output_kept = output_grad(ids, mixed_all, mixed_other, d_branch, branch_other)
        output_mine = scatter_rows(output_kept, output_sent)

        d_triples, norm_parts_here = [], []
        for step in range(micro):
            here = grads[4 * step : 4 * step + 4]
            here = [here[0]] + [swap(here[p], "ctx", p) for p in range(1, 4)]
            d_triple, parts = attend_back(
                triples[step], biases[step], lses[step], here, mixed_own[step], triple_full
            )
            d_triples.append(d_triple)
            near = swap(parts[1], "ctx", 1)
            far = wide_add(parts[2], swap(parts[3], "ctx", 1)).astype(BF16)
            norm_parts_here += [parts[0], near, swap(far, "ctx", 2)]
        normed_pair = (normeds[0], normeds[1])
        triple_sent = triple_grad(ids_sent, normed_pair, d_triples)
        triple_kept = triple_grad(ids, normed_pair, d_triples)
        triple_mine = scatter_rows(triple_kept, triple_sent)
        token_grad, gain_one_grad, bias_one_grad = first_back(
            tokens, d_attended, gain_one, norm_parts_here
        )

        halves = shift_in_grad.reshape(ways, 1, wide // (2 * ways))
        blank = jnp.zeros_like(halves)
        spread = jnp.where(
            core == 0,
            jnp.concatenate([halves, blank], axis=1),
            jnp.concatenate([blank, halves], axis=1),
        )
        early = sum_everywhere(
            jnp.concatenate(
                [
                    gain_two_grad.reshape(ways, shard),
                    bias_two_grad.reshape(ways, shard),
                    shift_out_grad.reshape(ways, shard),
                    spread.reshape(ways, wide // ways),
                ],
                axis=1,
            )
        )
        late = sum_everywhere(
            jnp.concatenate([gain_one_grad.reshape(ways, shard), bias_one_grad.reshape(ways, shard)], axis=1)
        )

        def over_chips(part):
            low = part.astype(BF16)
            return wide_add(low, swap(low, "ctx", 2))

        def both(own, axis):
            other = swap(own, "ctx", 1)
            first = jnp.where(core == 0, own, other)
            second = jnp.where(core == 0, other, own)
            return jnp.stack([first, second], axis=axis)

        shrink_grad = both(over_chips(shrink_mine), 0).reshape(deep, width)
        expand_half = over_chips(expand_mine).reshape(shard, ways, wide // (2 * ways))
        expand_grad = both(expand_half, 2).reshape(shard, wide)
        output_grad_all = both(over_chips(output_mine), 1).reshape(shard, width)
        low = triple_mine.astype(BF16).reshape(shard, 3, width // 4)
        far = swap(low, "ctx", 2)
        pair = jnp.stack([jnp.where(rank < 2, low, far), jnp.where(rank < 2, far, low)], axis=2)
        triple_grad_all = both(pair, 3).reshape(shard, 3 * width).astype(F32)
        early = lax.dynamic_index_in_dim(early, fsdp, 0, keepdims=False)
        late = lax.dynamic_index_in_dim(late, fsdp, 0, keepdims=False)

    return (
        result[:, None],
        token_grad[:, None],
        late[:shard],
        late[shard:],
        triple_grad_all,
        output_grad_all,
        early[:shard],
        early[shard : 2 * shard],
        expand_grad,
        early[3 * shard :],
        shrink_grad,
        early[2 * shard : 3 * shard],
    )


def solution(mesh):
    token_spec = P(None, "fsdp", "ctx", None)
    flat, rows = P("fsdp"), P("fsdp", None)
    return jax.shard_map(
        on_device,
        mesh=mesh,
        in_specs=(
            token_spec,
            token_spec,
            P(None, "fsdp", None, "ctx", None),
            P(None, "fsdp", None),
            flat,
            flat,
            rows,
            rows,
            flat,
            flat,
            rows,
            flat,
            rows,
            flat,
        ),
        out_specs=(
            token_spec,
            token_spec,
            flat,
            flat,
            rows,
            rows,
            flat,
            flat,
            rows,
            flat,
            rows,
            flat,
        ),
        check_vma=False,
    )
```

```python
import functools

import jax
import jax.numpy as jnp
from jax import lax
from jax.experimental import pallas as pl
from jax.experimental.pallas import tpu as pltpu
from jax.sharding import PartitionSpec as P

HEAD_DIM = 64
BLOCK = 64
EPSILON = 1e-05
F32 = jnp.float32
BF16 = jnp.bfloat16
MIB = 1 << 20

VM = pl.BlockSpec(memory_space=pltpu.VMEM)
SM = pl.BlockSpec(memory_space=pltpu.SMEM)
ANY = pl.BlockSpec(memory_space=pl.ANY)

NN = (((1,), (0,)), ((), ()))
NT = (((1,), (1,)), ((), ()))
TN = (((0,), (0,)), ((), ()))


def dot(left, right, dims=NN):
    return lax.dot_general(left, right, dims, preferred_element_type=F32)


def shape(dims, kind):
    return jax.ShapeDtypeStruct(dims, kind)


def params(limit=56):
    return pltpu.CompilerParams(vmem_limit_bytes=limit * MIB)


def cost(flops, moved, special=0):
    return pl.CostEstimate(flops=flops, bytes_accessed=moved, transcendentals=special)


def swap(value, axis, step):
    size = lax.axis_size(axis)
    return lax.ppermute(value, axis, [(i, i ^ step) for i in range(size)])


def place_id():
    return lax.axis_index("fsdp") if lax.axis_size("fsdp") == 8 else jnp.int32(1)


def wide_add(*terms):
    total = terms[0].astype(F32)
    for term in terms[1:]:
        total = total + term.astype(F32)
    return total


def scatter_rows(kept, sent):
    whole = jnp.stack([sent, kept], axis=1)
    whole = whole.reshape((8 * kept.shape[1],) + kept.shape[2:])
    return lax.psum_scatter(whole.astype(F32), "fsdp", scatter_dimension=0, tiled=True)


def sum_everywhere(vector):
    return lax.psum(vector, ("ctx", "fsdp"))


def norm_parts(values):
    average = jnp.mean(values, axis=-1, keepdims=True)
    centered = values - average
    variance = jnp.mean(centered * centered, axis=-1, keepdims=True)
    inverse = lax.rsqrt(variance + EPSILON)
    return centered * inverse, inverse


def norm_back(grad, unit, inverse, gain):
    scaled = grad * gain
    first = jnp.mean(scaled, axis=-1, keepdims=True)
    second = jnp.mean(scaled * unit, axis=-1, keepdims=True)
    return inverse * (scaled - first - unit * second)


def normalize(source, gain, bias):
    unit, _ = norm_parts(source.astype(F32))
    return (unit * gain + bias).astype(BF16)


def project_kernel(t0, t1, t2, t3, gain, bias, weight, triple, normed):
    rows = t0.shape[0]
    for place, part in enumerate((t0, t1, t2, t3)):
        span = slice(place * rows, (place + 1) * rows)
        normed[span, :] = normalize(part[...], gain[...], bias[...])
        triple[span, :] = dot(normed[span, :], weight[...]).astype(BF16)


def project(parts, gain, bias, weight):
    rows, width = parts[0].shape
    columns = weight.shape[1]
    return pl.pallas_call(
        project_kernel,
        name="project",
        out_shape=(shape((4 * rows, columns), BF16), shape((4 * rows, width), BF16)),
        in_specs=[VM] * 7,
        out_specs=(VM, VM),
        compiler_params=params(),
        cost_estimate=cost(8 * rows * width * columns, 12 * rows * width + 2 * width * columns),
    )(*parts, gain, bias, weight)


def head_mask(rows):
    return lax.broadcasted_iota(jnp.int32, (rows, 2 * HEAD_DIM), 1) // HEAD_DIM


def attend_body(triple, block_bias, mixed, lse, between=None):
    length = triple.shape[0]
    width = triple.shape[1] // 3
    rows = length // 4
    blocks = length // BLOCK
    for pair in range(width // 128):
        keys = triple[:, width + pair * 128 : width + pair * 128 + 128]
        values = triple[:, 2 * width + pair * 128 : 2 * width + pair * 128 + 128]
        values_t = values.astype(F32).T.astype(BF16)

        def step(place, carry):
            start = pl.multiple_of(place * rows, rows)
            queries = triple[pl.ds(start, rows), pair * 128 : pair * 128 + 128]
            queries = queries * jnp.asarray(0.125, BF16)
            side = head_mask(rows)
            halves = []
            for which in range(2):
                head = 2 * pair + which
                one = jnp.where(side == which, queries, jnp.zeros_like(queries))
                scores = dot(keys, one, NT)
                shift = block_bias[head, :, pl.ds(start, rows)]
                scores = scores.reshape(blocks, BLOCK, rows) + shift[:, None, :]
                peak = jnp.max(jnp.max(scores, axis=0), axis=0, keepdims=True)
                powered = jnp.exp(scores - peak[None])
                total = jnp.sum(jnp.sum(powered, axis=0), axis=0, keepdims=True)
                lse[head : head + 1, pl.ds(start, rows)] = peak + jnp.log(total)
                low = powered.astype(BF16).reshape(length, rows)
                part = dot(values_t[which * HEAD_DIM : (which + 1) * HEAD_DIM, :], low)
                halves.append(part / total)
            joined = jnp.concatenate(halves, axis=0)
            mixed[place, :, pair * 128 : pair * 128 + 128] = joined.T.astype(BF16)
            return carry

        lax.fori_loop(0, 4, step, 0)
        if between is not None and pair == 0:
            between()


def attend(triple, block_bias):
    length, columns = triple.shape
    width = columns // 3
    heads = width // HEAD_DIM
    rows = length // 4
    return pl.pallas_call(
        attend_body,
        name="attend",
        out_shape=(shape((4, rows, width), BF16), shape((8, length), F32)),
        in_specs=[VM, VM],
        out_specs=(VM, VM),
        compiler_params=params(),
        cost_estimate=cost(
            32 * heads * length * length * HEAD_DIM, 8 * length * width, heads * length * length
        ),
    )(triple, block_bias)


def attend_back_body(triple, block_bias, lse, grads, mixed, d_triple, key_total, value_total):
    length = triple.shape[0]
    width = triple.shape[1] // 3
    rows = length // 4
    blocks = length // BLOCK
    for pair in range(width // 128):
        lanes = slice(pair * 128, pair * 128 + 128)
        keys = triple[:, width + pair * 128 : width + pair * 128 + 128]
        values = triple[:, 2 * width + pair * 128 : 2 * width + pair * 128 + 128]
        keys_t = keys.astype(F32).T.astype(BF16)
        key_total[...] = jnp.zeros_like(key_total)
        value_total[...] = jnp.zeros_like(value_total)

        def step(place, carry):
            start = pl.multiple_of(place * rows, rows)
            queries = triple[pl.ds(start, rows), lanes] * jnp.asarray(0.125, BF16)
            grad = grads[place, :, lanes]
            product = (grad.astype(F32) * mixed[place, :, lanes].astype(F32)).T
            side = head_mask(rows)
            halves = []
            for which in range(2):
                head = 2 * pair + which
                one = jnp.where(side == which, queries, jnp.zeros_like(queries))
                one_grad = jnp.where(side == which, grad, jnp.zeros_like(grad))
                delta = jnp.sum(
                    product[which * HEAD_DIM : (which + 1) * HEAD_DIM, :], axis=0, keepdims=True
                )
                scores = dot(keys, one, NT)
                shift = block_bias[head, :, pl.ds(start, rows)] - lse[head : head + 1, pl.ds(start, rows)]
                exact = jnp.exp(scores.reshape(blocks, BLOCK, rows) + shift[:, None, :])
                exact = exact.reshape(length, rows)
                value_total[...] += dot(exact.astype(BF16), one_grad)
                d_probs = dot(values, one_grad, NT)
                d_scores = (exact * (d_probs - delta)).astype(BF16)
                key_total[...] += dot(d_scores, one)
                halves.append(dot(keys_t[which * HEAD_DIM : (which + 1) * HEAD_DIM, :], d_scores))
            joined = jnp.concatenate(halves, axis=0) * 0.125
            d_triple[pl.ds(start, rows), lanes] = joined.T.astype(BF16)
            return carry

        lax.fori_loop(0, 4, step, 0)
        d_triple[:, width + pair * 128 : width + pair * 128 + 128] = key_total[...].astype(BF16)
        d_triple[:, 2 * width + pair * 128 : 2 * width + pair * 128 + 128] = value_total[
            ...
        ].astype(BF16)


def attend_back_kernel(triple, block_bias, lse, g0, g1, g2, g3, mixed, weight, d_triple, norm_grad, grads, key_total, value_total):
    rows = g0.shape[0]
    for place, part in enumerate((g0, g1, g2, g3)):
        grads[place] = part[...]
    attend_back_body(triple, block_bias, lse, grads, mixed, d_triple, key_total, value_total)
    for place in range(4):
        part = dot(d_triple[place * rows : (place + 1) * rows, :], weight[...], NT)
        norm_grad[place] = part.astype(BF16)


def attend_back(triple, block_bias, lse, grads, mixed, weight):
    length, columns = triple.shape
    width = columns // 3
    heads = width // HEAD_DIM
    rows = length // 4
    return pl.pallas_call(
        attend_back_kernel,
        name="attend_back",
        out_shape=(shape((length, columns), BF16), shape((4, rows, weight.shape[0]), BF16)),
        in_specs=[VM] * 9,
        out_specs=(VM,) * 2,
        scratch_shapes=[
            pltpu.VMEM((4, rows, width), BF16),
            pltpu.VMEM((length, 128), F32),
            pltpu.VMEM((length, 128), F32),
        ],
        compiler_params=params(),
        cost_estimate=cost(
            80 * heads * length * length * HEAD_DIM, 16 * length * width, heads * length * length
        ),
    )(triple, block_bias, lse, *grads, mixed, weight)


def output_kernel(tokens, joined, gain, bias, weight, attended, normed):
    rows = tokens.shape[1]
    for micro in range(2):
        span = slice(micro * rows, (micro + 1) * rows)
        value = tokens[micro].astype(F32) + dot(joined[span, :], weight[...])
        attended[span, :] = value
        normed[span, :] = normalize(value, gain[...], bias[...])


def output_project(tokens, joined, gain, bias, weight):
    micro, rows, width = tokens.shape
    total = micro * rows
    return pl.pallas_call(
        output_kernel,
        name="output_project",
        out_shape=(shape((total, width), F32), shape((total, width), BF16)),
        in_specs=[VM] * 5,
        out_specs=(VM, VM),
        compiler_params=params(),
        cost_estimate=cost(2 * total * width * width, 12 * total * width + 2 * width * width),
    )(tokens, joined, gain, bias, weight)


CURVE = 0.7978845608028654
CUBIC = 0.044715


def feed_kernel(ids, h0, h1, c0, c1, shift, *rest):
    expand_held, shrink_held = rest[:2]
    own_out, other_out, own_hidden, other_hidden, bias_grad = rest[2:7]
    shrink_sent, shrink_kept, expand_sent, expand_kept = rest[7:11]
    hidden, tangent, hidden_t, out_total, hidden_total = rest[11:]
    base = ids[0]
    rows, width = h0.shape
    tile = shrink_held.shape[0] // 8
    deep = width // 8
    hidden[:rows, :] = h0[...]
    hidden[rows:, :] = h1[...]
    tangent[:rows, :] = c0[...]
    tangent[rows:, :] = c1[...]
    for j in range(8):
        source = pl.multiple_of((base ^ j) * deep, deep)
        hidden_t[j * deep : (j + 1) * deep, :] = (
            hidden[:, pl.ds(source, deep)].astype(F32).T.astype(BF16)
        )
    for step, j in enumerate((1, 3, 5, 7, 0, 2, 4, 6)):
        column = pl.multiple_of((base ^ j) * tile, tile)
        up = expand_held[:, pl.ds(column, tile)]
        down = shrink_held[pl.ds(column, tile), :]
        before = dot(hidden[...], up) + shift[:, pl.ds(column, tile)]
        d_active = dot(tangent[...], down, NT)
        square = before * before
        bend = jnp.tanh(CURVE * before * (1.0 + CUBIC * square))
        plus = 0.5 * (1.0 + bend)
        active = (before * plus).astype(BF16)
        slope = plus + (0.5 * CURVE) * before * (1.0 - bend * bend) * (1.0 + 3 * CUBIC * square)
        d_before = (d_active * slope).astype(BF16)
        bias_grad[:, pl.ds(column, tile)] = jnp.sum(d_before.astype(F32), axis=0, keepdims=True)
        out_part = dot(active, down)
        hidden_part = dot(d_before, up, NT)
        if step == 0:
            out_total[...] = out_part
            hidden_total[...] = hidden_part
        else:
            out_total[...] += out_part
            hidden_total[...] += hidden_part
        shrink_part = dot(active, tangent[...], TN).astype(BF16)
        (shrink_sent if j % 2 else shrink_kept)[j // 2] = shrink_part
        expand_part = dot(hidden_t[...], d_before).astype(BF16)
        for place in range(8):
            target = expand_sent if place % 2 else expand_kept
            target[place // 2, :, pl.ds(column, tile)] = expand_part[
                place * deep : (place + 1) * deep, :
            ]
    own_out[...] = out_total[:rows, :]
    other_out[...] = out_total[rows:, :].astype(BF16)
    own_hidden[...] = hidden_total[:rows, :]
    other_hidden[...] = hidden_total[rows:, :].astype(BF16)


def feed(ids, hidden, tangent, shift, expand, shrink):
    rows, width = hidden[0].shape
    wide = expand.shape[1]
    deep, tile = width // 8, wide // 8
    return pl.pallas_call(
        feed_kernel,
        name="feed",
        out_shape=(
            shape((rows, width), F32),
            shape((rows, width), BF16),
            shape((rows, width), F32),
            shape((rows, width), BF16),
            shape((1, wide), F32),
            shape((4, tile, width), BF16),
            shape((4, tile, width), BF16),
            shape((4, deep, wide), BF16),
            shape((4, deep, wide), BF16),
        ),
        in_specs=[SM] + [VM] * 7,
        out_specs=(VM,) * 9,
        scratch_shapes=[
            pltpu.VMEM((2 * rows, width), BF16),
            pltpu.VMEM((2 * rows, width), BF16),
            pltpu.VMEM((width, 2 * rows), BF16),
            pltpu.VMEM((2 * rows, width), F32),
            pltpu.VMEM((2 * rows, width), F32),
        ],
        compiler_params=params(60),
        cost_estimate=cost(24 * rows * width * wide, 8 * width * wide + 20 * rows * width, 2 * rows * wide),
    )(ids, *hidden, *tangent, shift, expand, shrink)


def branch_kernel(
    ids, attended, own_hidden, came_hidden, tangent, own_out, came_out, gain, shift, weight, *rest
):
    result, d_attended, d_branch = rest[:3]
    grads, (gain_grad, bias_grad, shift_grad) = rest[3:11], rest[11:14]
    rows = tangent.shape[1]
    width = gain.shape[1] // 4
    gain_total = bias_total = shift_total = 0.0
    for micro in range(2):
        span = slice(micro * rows, (micro + 1) * rows)
        value = attended[span, :]
        cot = tangent[micro].astype(F32)
        branch = own_out[span, :] + came_out[span, :].astype(F32) + shift[...]
        result[micro] = (value + branch).astype(BF16)
        unit, inverse = norm_parts(value)
        grad = own_hidden[span, :] + came_hidden[span, :].astype(F32)
        gain_total = gain_total + jnp.sum(grad * unit, axis=0, keepdims=True)
        bias_total = bias_total + jnp.sum(grad, axis=0, keepdims=True)
        shift_total = shift_total + jnp.sum(cot, axis=0, keepdims=True)
        total = cot + norm_back(grad, unit, inverse, gain[...])
        d_attended[span, :] = total
        d_branch[span, :] = total.astype(BF16)
    gain_grad[...] = gain_total
    bias_grad[...] = bias_total
    shift_grad[...] = shift_total
    for micro in range(2):
        for place in range(4):
            start = pl.multiple_of((ids[1] ^ place) * width, width)
            part = dot(d_branch[micro * rows : (micro + 1) * rows, :], weight[pl.ds(start, width), :], NT)
            grads[4 * micro + place][...] = part.astype(BF16)


def branch_back(ids, attended, own_hidden, came_hidden, tangent, own_out, came_out, gain, shift, weight):
    micro, rows, width = tangent.shape
    total = micro * rows
    row = shape((1, width), F32)
    return pl.pallas_call(
        branch_kernel,
        name="branch_back",
        out_shape=(
            shape(tangent.shape, BF16),
            shape((total, width), F32),
            shape((total, width), BF16),
        )
        + tuple(shape((rows, width // 4), BF16) for _ in range(8))
        + (row, row, row),
        in_specs=[SM] + [VM] * 9,
        out_specs=(VM,) * 14,
        compiler_params=params(),
        cost_estimate=cost(2 * total * width * width, 32 * total * width),
    )(ids, attended, own_hidden, came_hidden, tangent, own_out, came_out, gain, shift, weight)


def output_grad_kernel(ids, own_mixed, other_mixed, own_branch, other_branch, out):
    rows = out.shape[1]
    width = own_branch.shape[1]
    half = width // 2
    column = pl.multiple_of(ids[2] * half, half)
    right = own_branch[:, pl.ds(column, half)]
    for k in range(4):
        start = pl.multiple_of((ids[0] ^ (2 * k + ids[3])) * rows, rows)
        part = dot(own_mixed[:, pl.ds(start, rows)], right, TN)
        part += dot(other_mixed[:, pl.ds(start, rows)], other_branch[...], TN)
        out[k] = part.astype(BF16)


def output_grad(ids, own_mixed, other_mixed, own_branch, other_branch):
    total, width = own_mixed.shape
    return pl.pallas_call(
        output_grad_kernel,
        name="output_grad",
        out_shape=shape((4, width // 8, width // 2), BF16),
        in_specs=[SM] + [VM] * 4,
        out_specs=VM,
        compiler_params=params(),
        cost_estimate=cost(total * width * width, 8 * total * width),
    )(ids, own_mixed, other_mixed, own_branch, other_branch)


def triple_grad_kernel(ids, n0, n1, d0, d1, out):
    rows = out.shape[1]
    for k in range(4):
        column = pl.multiple_of((ids[0] ^ (2 * k + ids[3])) * rows, rows)
        part = dot(n0[:, pl.ds(column, rows)], d0[...], TN)
        part += dot(n1[:, pl.ds(column, rows)], d1[...], TN)
        out[k] = part.astype(BF16)


def triple_grad(ids, normed, grads):
    length, width = normed[0].shape
    columns = grads[0].shape[1]
    return pl.pallas_call(
        triple_grad_kernel,
        name="triple_grad",
        out_shape=shape((4, width // 8, columns), BF16),
        in_specs=[SM] + [VM] * 4,
        out_specs=VM,
        compiler_params=params(),
        cost_estimate=cost(2 * length * width * columns, 4 * length * (width + columns)),
    )(ids, *normed, *grads)


def first_back_kernel(tokens, d_attended, gain, *rest):
    parts, (grad_out, gain_grad, bias_grad) = rest[:6], rest[6:]
    rows = tokens.shape[1]
    gain_total = bias_total = 0.0
    for micro in range(2):
        one, two, three = parts[3 * micro : 3 * micro + 3]
        grad = one[...].astype(F32) + two[...].astype(F32) + three[...].astype(F32)
        unit, inverse = norm_parts(tokens[micro].astype(F32))
        gain_total = gain_total + jnp.sum(grad * unit, axis=0, keepdims=True)
        bias_total = bias_total + jnp.sum(grad, axis=0, keepdims=True)
        total = d_attended[micro * rows : (micro + 1) * rows, :]
        grad_out[micro] = (total + norm_back(grad, unit, inverse, gain[...])).astype(BF16)
    gain_grad[...] = gain_total
    bias_grad[...] = bias_total


def first_back(tokens, d_attended, gain, parts):
    micro, rows, width = tokens.shape
    row = shape((1, width), F32)
    return pl.pallas_call(
        first_back_kernel,
        name="first_back",
        out_shape=(shape(tokens.shape, BF16), row, row),
        in_specs=[VM] * 9,
        out_specs=(VM,) * 3,
        compiler_params=params(),
        cost_estimate=cost(20 * micro * rows * width, 16 * micro * rows * width),
    )(tokens, d_attended, gain, *parts)


def flip(index, bits):
    out, bit = index, 1
    while bit <= bits:
        if bits & bit:
            out = out + bit * (1 - 2 * lax.rem(lax.div(index, jnp.int32(bit)), jnp.int32(2)))
        bit *= 2
    return out


class Moves:
    def __init__(self, send, recv):
        self.send, self.recv, self.started, self.freed = send, recv, [], []
        self.place = {"ctx": lax.axis_index("ctx"), "fsdp": lax.axis_index("fsdp")}

    def greet(self):
        barrier = pltpu.get_barrier_semaphore()
        partners = [("ctx", 1), ("ctx", 2), ("ctx", 3), ("fsdp", 1), ("fsdp", 2), ("fsdp", 4), ("fsdp", 6)]
        for axis, bits in partners:
            pl.semaphore_signal(
                barrier,
                inc=1,
                device_id={axis: flip(self.place[axis], bits)},
                device_id_type=pl.DeviceIdType.MESH,
            )
        pl.semaphore_wait(barrier, len(partners))

    def go(self, source, target, axis, bits):
        slot = len(self.started)
        move = pltpu.make_async_remote_copy(
            src_ref=source,
            dst_ref=target,
            send_sem=self.send.at[slot],
            recv_sem=self.recv.at[slot],
            device_id={axis: flip(self.place[axis], bits)},
            device_id_type=pl.DeviceIdType.MESH,
        )
        move.start()
        self.started.append(move)
        return move

    def sent(self, move):
        move.wait_send()
        self.freed.append(move)

    def close(self):
        for move in self.started:
            if not any(move is other for other in self.freed):
                move.wait_send()


class Gather:
    def __init__(self, moves, part, view, own, shared=False):
        self.moves, self.view, self.own, self.shared = moves, view, own, shared
        self.part = part

    def start(self):
        moves, part, view, me = self.moves, self.part, self.view, self.moves.place["fsdp"]
        self.distant = moves.go(part, view(me), "fsdp", 4)
        self.adjacent = moves.go(part, view(me), "fsdp", 2)
        self.across = [moves.go(part, view(me), "fsdp", 1)]
        self.sources = [1]
        self.over = [moves.go(part, view(me), "ctx", 2)] if self.shared else []
        return self

    def over_x(self, bits):
        if self.shared:
            block = self.view(flip(self.moves.place["fsdp"], bits))
            self.over.append(self.moves.go(block, block, "ctx", 2))

    def over_y(self, bits):
        block = self.view(flip(self.moves.place["fsdp"], bits))
        self.across.append(self.moves.go(block, block, "fsdp", 1))
        self.sources.append(bits + 1)
        self.over_x(bits)

    def forward(self):
        self.distant.wait_recv()
        block = self.view(flip(self.moves.place["fsdp"], 4))
        self.last = self.moves.go(block, block, "fsdp", 2)
        self.over_y(4)
        self.adjacent.wait_recv()
        self.over_y(2)

    def third(self):
        self.last.wait_recv()
        self.over_y(6)

    def second(self):
        for bits, move in zip(self.sources, self.across):
            move.wait_recv()
            self.over_x(bits)

    def finish(self):
        if not self.shared:
            self.second()
        for move in self.over:
            move.wait_recv()
        for copy in self.own:
            copy.wait()


FORWARD_MOVES = 106


def row_view(ref, rows, columns=slice(None)):
    return lambda index: ref.at[pl.ds(pl.multiple_of(index * rows, rows), rows), columns]


def forward_kernel(
    global_ids,
    tokens,
    small,
    picks,
    triple_weight,
    output_weight,
    expand_weight,
    shrink_weight,
    tangent,
    small_all,
    triple_out,
    output_out,
    expand_all,
    shrink_all,
    tangent_other,
    triple,
    normed,
    block_bias,
    lse,
    mixed,
    joined_out,
    mixed_other,
    attended,
    hidden,
    hidden_other,
    parts,
    small_held,
    picks_held,
    triple_held,
    output_held,
    joined,
    hidden_held,
    send,
    recv,
    local,
):
    moves = Moves(send, recv)
    rank, me = moves.place["ctx"], moves.place["fsdp"]
    core = lax.rem(rank, jnp.int32(2))
    micro, rows, width = tokens.shape
    half = width // 2
    quarter = width // 4
    shard = triple_weight.shape[0]
    wide = expand_all.shape[1] // 2
    deep = shrink_weight.shape[0] // 8
    chip = lax.div(rank, jnp.int32(2))
    locals_used = []

    def copy_here(source, target):
        copy = pltpu.make_async_copy(source, target, local.at[len(locals_used)])
        copy.start()
        locals_used.append(copy)
        return copy

    def at(start, size, unit=128):
        return pl.ds(pl.multiple_of(start, unit), size)

    mine = at(me * shard, shard)
    triple_own = [
        copy_here(
            triple_weight.at[:, at(k * width + rank * quarter, quarter)],
            triple_held.at[mine, k * quarter : (k + 1) * quarter],
        )
        for k in range(3)
    ]
    tile = wide // 4
    expand_views = [row_view(expand_all, shard, at(chip * wide + cut * (wide // 2), wide // 2)) for cut in range(2)]
    expand_own = [
        copy_here(
            expand_weight.at[:, at(((4 * chip + q) * 2 + core) * tile, tile)],
            expand_all.at[mine, at(chip * wide + q * tile, tile)],
        )
        for q in range(4)
    ]
    output_columns = at(core * half + chip * quarter, quarter)
    output_view = row_view(output_held, shard, output_columns)
    shrink_views = [
        lambda i, cut=cut: shrink_all.at[at(i * 4 * deep + cut * deep, deep, 64)] for cut in range(4)
    ]
    shrink_parts = [shrink_weight.at[at((core * 4 + cut) * deep, deep, 64)] for cut in range(4)]
    small_own = copy_here(small, small_held.at[me])
    output_own = copy_here(output_weight.at[:, output_columns], output_view(me))
    shrink_own = [copy_here(shrink_parts[cut], shrink_views[cut](me)) for cut in range(4)]
    moves.greet()

    small_gather = Gather(moves, small, lambda index: small_held.at[index], [small_own]).start()
    far = [moves.go(tokens.at[0], parts.at[0, 2], "ctx", 2)]
    near = [moves.go(tokens.at[0], parts.at[0, 1], "ctx", 1)]
    for copy in triple_own:
        copy.wait()
    triple_view = row_view(triple_held, shard)
    triple_gather = Gather(moves, triple_view(me), triple_view, []).start()
    picked = [moves.go(picks.at[flip(rank, p)], picks_held.at[p], "ctx", p) for p in range(1, 4)]
    near.append(moves.go(tokens.at[1], parts.at[1, 1], "ctx", 1))
    far.append(moves.go(tokens.at[1], parts.at[1, 2], "ctx", 2))
    output_gather = Gather(moves, output_weight.at[:, output_columns], output_view, [output_own], True)
    for copy in expand_own:
        copy.wait()
    expands = [Gather(moves, view(me), view, [], True) for view in expand_views]
    shrinks = [Gather(moves, shrink_parts[cut], shrink_views[cut], [shrink_own[cut]]) for cut in range(4)]
    small_gather.forward()
    triple_gather.forward()
    output_gather.start()
    expands[0].start()
    small_gather.third()
    triple_gather.third()
    expands[1].start()
    tangent_move = moves.go(tangent, tangent_other, "ctx", 1)

    for move in picked:
        move.wait_recv()
    count = block_bias.shape[2]
    each = count // 4
    ranks = [flip(rank, p) if p else rank for p in range(4)]
    key_row = lax.broadcasted_iota(jnp.int32, (count, rows), 0)
    key_place = key_row // each
    key_rank = ranks[0]
    for p in range(1, 4):
        key_rank = jnp.where(key_place == p, ranks[p], key_rank)
    key_block = key_rank * each + key_row % each
    lane = lax.broadcasted_iota(jnp.int32, (count, rows), 1) // BLOCK
    for step in range(micro):
        first, second = global_ids[step, 0], global_ids[step, 1]
        key_global = (key_block == first) | (key_block == second)
        for p in range(4):
            source = picks.at[rank] if p == 0 else picks_held.at[p]
            query_block = ranks[p] * each + lane
            base = key_global | (jnp.abs(query_block - key_block) <= 1)
            base = base | (query_block == first) | (query_block == second)
            for head in range(block_bias.shape[1]):
                hit = base
                for pick in range(3):
                    hit = hit | (source[step, head, pick : pick + 1, :] == key_block)
                block_bias[step, head, :, p * rows : (p + 1) * rows] = jnp.where(hit, 0.0, -1e30)

    small_gather.finish()
    small_all[...] = small_held[...]

    def vector(line):
        return jnp.concatenate([small_held[b, line : line + 1, :] for b in range(8)], axis=1)

    gain_one, bias_one, gain_two, bias_two = (vector(line) for line in range(4))

    for step in range(micro):
        far[step].wait_recv()
        near.append(moves.go(parts.at[step, 2], parts.at[step, 3], "ctx", 1))
    mixed_moves = []
    for step in range(micro):
        near[step].wait_recv()
        near[2 + step].wait_recv()
        for p in range(4):
            source = tokens[step] if p == 0 else parts[step, p]
            normed[step, p * rows : (p + 1) * rows, :] = normalize(source, gain_one, bias_one)
        if step == 0:
            output_gather.forward()
            expands[0].forward()
            shrinks[0].start()
            triple_gather.finish()
        for p in range(4):
            span = slice(p * rows, (p + 1) * rows)
            triple[step, span, :] = dot(normed[step, span, :], triple_held[...]).astype(BF16)

        def between_first():
            expands[0].third()
            shrinks[0].forward()
            shrinks[2].start()
            output_gather.second()

        def between_second():
            expands[1].second()
            shrinks[3].forward()
            shrinks[2].third()

        if step == 0:
            output_gather.third()
            expands[1].forward()
            shrinks[1].start()
        else:
            output_gather.finish()
            piece = output_held.at[:, at(core * half, half)]
            output_move = moves.go(piece, piece, "ctx", 1)
            shrinks[2].forward()
            shrinks[1].third()
        attend_body(
            triple.at[step],
            block_bias.at[step],
            mixed.at[step],
            lse.at[step],
            between_second if step else between_first,
        )
        own = pl.ds(pl.multiple_of(rank * quarter, quarter), quarter)
        span = slice(step * rows, (step + 1) * rows)
        joined[span, own] = mixed[step, 0]
        for p in range(1, 4):
            mixed_moves.append(moves.go(mixed.at[step, p], joined.at[span, own], "ctx", p))
        if step == 0:
            expands[1].third()
            shrinks[1].forward()
            shrinks[3].start()
            shrinks[0].third()
            expands[0].second()
        else:
            shrinks[3].third()
    output_move.wait_recv()
    for move in mixed_moves:
        move.wait_recv()
    keep = [copy_here(triple_held, triple_out), copy_here(output_held, output_out)]
    output_kernel(tokens, joined, gain_two, bias_two, output_held, attended, hidden_held)
    last = [
        moves.go(hidden_held, hidden_other, "ctx", 1),
        moves.go(joined, mixed_other, "ctx", 1),
    ]
    hidden[...] = hidden_held[...]
    joined_out[...] = joined[...]
    for gather in shrinks + expands:
        gather.finish()
    for move in [tangent_move] + last:
        move.wait_recv()
    for copy in keep:
        copy.wait()
    moves.close()


def forward_together(global_ids, tokens, small, picks, triple_weight, output_weight, expand_weight, shrink_weight, tangent):
    micro, rows, width = tokens.shape
    total = micro * rows
    columns = triple_weight.shape[1] // 4
    wide = expand_weight.shape[1] // 2
    length = 4 * rows
    heads = picks.shape[2]
    outs = (
        (VM, (8,) + small.shape, F32),
        (ANY, (width, columns), BF16),
        (ANY, (width, width), BF16),
        (ANY, (width, wide), BF16),
        (ANY, (wide, width), BF16),
        (ANY, (total, width), BF16),
        (VM, (micro, length, columns), BF16),
        (VM, (micro, length, width), BF16),
        (VM, (micro, heads, length // BLOCK, length), F32),
        (VM, (micro, 8, length), F32),
        (VM, (micro, 4, rows, width // 4), BF16),
        (VM, (total, width), BF16),
        (ANY, (total, width), BF16),
        (VM, (total, width), F32),
        (VM, (total, width), BF16),
        (ANY, (total, width), BF16),
    )
    return pl.pallas_call(
        forward_kernel,
        name="forward_together",
        out_shape=tuple(shape(dims, kind) for _, dims, kind in outs),
        in_specs=[SM] + [VM] * 3 + [ANY] * 5,
        out_specs=tuple(spec for spec, _, _ in outs),
        scratch_shapes=[
            pltpu.VMEM((micro, 4, rows, width), BF16),
            pltpu.VMEM((8,) + small.shape, F32),
            pltpu.VMEM(picks.shape, jnp.int32),
            pltpu.VMEM((width, columns), BF16),
            pltpu.VMEM((width, width), BF16),
            pltpu.VMEM((total, width), BF16),
            pltpu.VMEM((total, width), BF16),
            pltpu.SemaphoreType.DMA((FORWARD_MOVES,)),
            pltpu.SemaphoreType.DMA((FORWARD_MOVES,)),
            pltpu.SemaphoreType.DMA((15,)),
        ],
        compiler_params=pltpu.CompilerParams(
            collective_id=0, has_side_effects=True, vmem_limit_bytes=56 * MIB
        ),
        cost_estimate=cost(16 * total * width * width, 64 * MIB),
    )(global_ids, tokens, small, picks, triple_weight, output_weight, expand_weight, shrink_weight, tangent)


class Reduce:
    def __init__(self, moves, sent, came, line):
        self.moves, self.came, self.line = moves, came, line
        self.across = moves.go(sent, came, "fsdp", 1)

    def forward(self, *kept):
        self.across.wait_recv()
        for k in range(4):
            self.came[k] = wide_add(self.came[k], *(part[k] for part in kept)).astype(self.came.dtype)
        self.along = [
            self.moves.go(self.came.at[k], self.line.at[k - 1], "fsdp", 2 * k) for k in range(1, 4)
        ]

    def finish(self):
        for move in self.along:
            move.wait_recv()
        return wide_add(self.came[0], *(self.line[k] for k in range(3)))


BACKWARD_MOVES = 66


def backward_kernel(
    vectors,
    tangent,
    output_weight,
    triple_weight,
    triples,
    biases,
    lses,
    mixed_own,
    shift_in_grad,
    own_hidden,
    other_hidden,
    own_out,
    other_out,
    attended,
    tokens,
    mixed_all,
    mixed_other,
    normeds,
    shrink_sent,
    shrink_kept,
    expand_sent,
    expand_kept,
    result,
    token_grad,
    shrink_out,
    expand_out,
    output_out,
    triple_out,
    early_out,
    late_out,
    came_out,
    came_hidden,
    d_attended,
    stage,
    held,
    d_branch,
    branch_other,
    d_mixed,
    grads,
    d_triples,
    key_total,
    value_total,
    near_parts,
    own_parts,
    near_came,
    far_sent,
    far_came,
    kept_ring,
    expand_own,
    over_came,
    feed_came,
    feed_line,
    output_sent,
    output_kept,
    output_came,
    output_line,
    triple_sent,
    triple_kept,
    triple_came,
    triple_line,
    chip_sent,
    chip_came,
    final,
    triple_final,
    small_all,
    small_sent,
    small_kept,
    small_came,
    small_line,
    small_chip,
    small_chip_came,
    small_core,
    small_core_came,
    send,
    recv,
    local,
):
    moves = Moves(send, recv)
    rank, me = moves.place["ctx"], moves.place["fsdp"]
    core = lax.rem(rank, jnp.int32(2))
    micro, rows, width = tangent.shape
    half, quarter, shard = width // 2, width // 4, width // 8
    moves.greet()
    used = []

    def load(source, target):
        copy = pltpu.make_async_copy(source, target, local.at[len(used)])
        copy.start()
        used.append(copy)
        return copy

    def at(start, size, unit=128):
        return pl.ds(pl.multiple_of(start, unit), size)

    chip = lax.div(rank, jnp.int32(2))
    deep = shrink_sent.shape[1] // 2
    wide = expand_sent.shape[2] // 2
    here, there = at(chip * wide, wide), at((1 - chip) * wide, wide)
    hidden_move = moves.go(other_hidden, came_hidden, "ctx", 1)

    def shrink_begin(i):
        part = shrink_sent.at[:, i * deep : (i + 1) * deep, :]
        return Reduce(moves, part, feed_came.at[i], feed_line.at[i])

    shrinks = [shrink_begin(0)]
    over_moves = [moves.go(expand_sent.at[:, :, there], over_came.at[0], "ctx", 2)]
    loads = [load(own_hidden, d_attended), load(attended, stage)]
    out_move = moves.go(other_out, came_out, "ctx", 1)
    mixed_loads = [load(mixed_all, held.at[0, : 2 * rows, :]), load(mixed_other, held.at[0, 2 * rows :, :])]
    expand_loads = [
        load(expand_sent.at[:, :, here], expand_own.at[0]),
        load(expand_kept.at[:, :, here], expand_own.at[1]),
    ]
    kept_loads = [load(shrink_kept.at[:, i * deep : (i + 1) * deep, :], kept_ring.at[i]) for i in range(2)]

    gain_two, gain_one, shift_out = vectors[0:1, :], vectors[1:2, :], vectors[2:3, :]
    for copy in loads:
        copy.wait()
    hidden_move.wait_recv()
    gain_total = bias_total = shift_total = 0.0
    for step in range(micro):
        span = slice(step * rows, (step + 1) * rows)
        cot = tangent[step].astype(F32)
        unit, inverse = norm_parts(stage[span, :])
        grad = d_attended[span, :] + came_hidden[span, :].astype(F32)
        gain_total = gain_total + jnp.sum(grad * unit, axis=0, keepdims=True)
        bias_total = bias_total + jnp.sum(grad, axis=0, keepdims=True)
        shift_total = shift_total + jnp.sum(cot, axis=0, keepdims=True)
        total = cot + norm_back(grad, unit, inverse, gain_two)
        d_attended[span, :] = total
        d_branch[span, :] = total.astype(BF16)
    theirs = d_branch.at[:, pl.ds(pl.multiple_of((1 - core) * half, half), half)]
    branch_move = moves.go(theirs, branch_other, "ctx", 1)
    grad_moves = []
    for step in range(micro):
        for p in (2, 3, 1, 0):
            start = pl.multiple_of((flip(rank, p) if p else rank) * quarter, quarter)
            part = dot(d_branch[step * rows : (step + 1) * rows, :], output_weight[pl.ds(start, quarter), :], NT)
            if p:
                d_mixed[step, p] = part.astype(BF16)
                grad_moves.append(moves.go(d_mixed.at[step, p], grads.at[step, p], "ctx", p))
            else:
                grads[step, 0] = part.astype(BF16)

    over_moves.append(moves.go(expand_kept.at[:, :, there], over_came.at[1], "ctx", 2))

    def small_row(which, line, vector):
        for b in range(8):
            small_all[which, b, line : line + 1, :] = vector[:, b * shard : (b + 1) * shard]

    def small_begin(which):
        for k in range(4):
            small_sent[which, k] = small_all[which, flip(me, 2 * k + 1)]
            small_kept[which, k] = small_all[which, flip(me, 2 * k) if k else me]
        return Reduce(moves, small_sent.at[which], small_came.at[which], small_line.at[which])

    def small_chips(which):
        small_chip[which] = smalls[which].finish()
        return moves.go(small_chip.at[which], small_chip_came.at[which], "ctx", 2)

    def small_cores(which, move):
        move.wait_recv()
        small_core[which] = small_chip[which] + small_chip_came[which]
        return moves.go(small_core.at[which], small_core_came.at[which], "ctx", 1)

    def small_end(which, move, out):
        move.wait_recv()
        out[...] = small_core[which] + small_core_came[which]

    small_all[...] = jnp.zeros_like(small_all)
    for line, vector in enumerate((gain_total, bias_total, shift_total)):
        small_row(0, line, vector)
    unit_lines = shift_in_grad.shape[1] // 8 // 128
    for b in range(8):
        for line in range(unit_lines):
            lanes = slice((b * unit_lines + line) * 128, (b * unit_lines + line + 1) * 128)
            small_all[0, b, pl.ds(3 + core * unit_lines + line, 1), :] = shift_in_grad[:, lanes]
    smalls = [small_begin(0)]

    for copy in mixed_loads:
        copy.wait()
    branch_move.wait_recv()
    mine = pl.ds(pl.multiple_of(core * half, half), half)

    def output_part(index):
        lanes = pl.ds(pl.multiple_of(index * shard, shard), shard)
        part = dot(held[0, : 2 * rows, lanes], d_branch[:, mine], TN)
        return part + dot(held[0, 2 * rows :, lanes], branch_other[...], TN)

    for k in range(4):
        output_sent[k] = output_part(flip(me, 2 * k + 1)).astype(BF16)
    output_reduce = Reduce(moves, output_sent, output_came, output_line)
    for k in range(4):
        output_kept[k] = output_part(flip(me, 2 * k) if k else me).astype(BF16)
    normed_loads = [load(normeds.at[step], held.at[step]) for step in range(1, micro)]

    norm_moves, far_moves = [], []

    def attention(step):
        for move in grad_moves[3 * step : 3 * step + 3]:
            move.wait_recv()
        attend_back_body(
            triples.at[step],
            biases.at[step],
            lses.at[step],
            grads.at[step],
            mixed_own.at[step],
            d_triples.at[step],
            key_total,
            value_total,
        )
        for p in (3, 1, 2, 0):
            span = slice(p * rows, (p + 1) * rows)
            part = dot(d_triples[step, span, :], triple_weight[...], NT).astype(BF16)
            if p:
                near_parts[step, p - 1] = part
            else:
                own_parts[step] = part
            if p % 2:
                norm_moves.append(moves.go(near_parts.at[step, p - 1], near_came.at[step, p // 2], "ctx", 1))

    def far_part(step):
        norm_moves[2 * step].wait_recv()
        far_sent[step] = wide_add(near_parts[step, 1], near_came[step, 1]).astype(BF16)
        far_moves.append(moves.go(far_sent.at[step], far_came.at[step], "ctx", 2))

    for copy in expand_loads:
        copy.wait()
    over_moves[0].wait_recv()
    for k in range(4):
        expand_own[0, k] = wide_add(expand_own[0, k], over_came[0, k]).astype(BF16)
    expand_reduce = Reduce(moves, expand_own.at[0], feed_came.at[2], feed_line.at[2])
    for copy in kept_loads:
        copy.wait()
    shrinks[0].forward(kept_ring.at[0])
    smalls[0].forward(small_kept.at[0])
    normed_loads.insert(0, load(normeds.at[0], held.at[0]))
    attention(0)
    output_reduce.forward(output_kept)
    over_moves[1].wait_recv()
    expand_reduce.forward(expand_own.at[1], over_came.at[1])
    shrinks.append(shrink_begin(1))
    far_part(0)
    attention(1)
    small_moves = [small_chips(0)]

    for copy in normed_loads:
        copy.wait()

    def triple_part(index):
        lanes = pl.ds(pl.multiple_of(index * shard, shard), shard)
        part = dot(held[0, :, lanes], d_triples[0], TN)
        return part + dot(held[1, :, lanes], d_triples[1], TN)

    for k in range(4):
        triple_sent[k] = triple_part(flip(me, 2 * k + 1)).astype(BF16)
    triple_reduce = Reduce(moves, triple_sent, triple_came, triple_line)
    shrinks[1].forward(kept_ring.at[1])
    far_part(1)
    for k in range(4):
        triple_kept[k] = triple_part(flip(me, 2 * k) if k else me).astype(BF16)
    small_moves[0] = small_cores(0, small_moves[0])

    token_load = load(tokens, held.at[0, : 2 * rows, :])
    out_load = load(own_out, stage)
    out_move.wait_recv()
    came_load = load(came_out, came_hidden)

    chips, ends, stays = {}, [], []

    def chip_begin(i, value):
        columns = value.shape[1]
        chip_sent[i, :, :columns] = value.astype(BF16)
        chips[i] = moves.go(chip_sent.at[i, :, pl.ds(0, columns)], chip_came.at[i, :, pl.ds(0, columns)], "ctx", 2)

    def place(source, target, partners=(1,)):
        for p in partners:
            ends.append(moves.go(source, target, "ctx", p))
        stays.append(load(source, target))

    def chip_end(i):
        chips[i].wait_recv()
        if i < 2:
            final[i] = wide_add(chip_sent[i], chip_came[i]).astype(BF16)
            place(final.at[i], shrink_out.at[at((2 * core + i) * deep, deep), :])
        else:
            final[i, :, :half] = wide_add(chip_sent[i, :, :half], chip_came[i, :, :half]).astype(BF16)
            place(final.at[i, :, :half], output_out.at[:, mine])

    chip_begin(0, shrinks[0].finish())

    token_load.wait()
    for move in norm_moves[1::2] + far_moves:
        move.wait_recv()
    gain_total = bias_total = 0.0
    for step in range(micro):
        span = slice(step * rows, (step + 1) * rows)
        grad = wide_add(own_parts[step], near_came[step, 0], far_came[step])
        unit, inverse = norm_parts(held[0, span, :].astype(F32))
        gain_total = gain_total + jnp.sum(grad * unit, axis=0, keepdims=True)
        bias_total = bias_total + jnp.sum(grad, axis=0, keepdims=True)
        token_grad[step] = (d_attended[span, :] + norm_back(grad, unit, inverse, gain_one)).astype(BF16)
    small_row(1, 0, gain_total)
    small_row(1, 1, bias_total)
    smalls.append(small_begin(1))
    small_end(0, small_moves[0], early_out)
    out_load.wait()
    sum_load = load(attended, d_attended)
    came_load.wait()
    for step in range(micro):
        span = slice(step * rows, (step + 1) * rows)
        stage[span, :] = stage[span, :] + came_hidden[span, :].astype(F32) + shift_out
    sum_load.wait()
    moves.sent(branch_move)
    for step in range(micro):
        span = slice(step * rows, (step + 1) * rows)
        d_branch[span, :] = (d_attended[span, :] + stage[span, :]).astype(BF16)
    result_load = load(d_branch, result)
    final[3] = expand_reduce.finish().astype(BF16)
    place(final.at[3], expand_out.at[rank], (1, 2, 3))
    chip_end(0)
    triple_reduce.forward(triple_kept)
    smalls[1].forward(small_kept.at[1])
    chip_begin(2, output_reduce.finish())
    chip_begin(1, shrinks[1].finish())
    chip_end(2)
    chip_end(1)
    triple_final[...] = triple_reduce.finish().astype(BF16)
    place(triple_final, triple_out.at[rank], (1, 2, 3))
    small_moves.append(small_cores(1, small_chips(1)))
    small_end(1, small_moves[1], late_out)
    for move in ends:
        move.wait_recv()
    for copy in stays + [result_load]:
        copy.wait()
    moves.close()


def backward_together(vectors, tangent, output_weight, triple_weight, triples, biases, lses, mixed_own, shift_in_grad, *late_arrays):
    micro, rows, width = tangent.shape
    total, half, quarter, shard = micro * rows, width // 2, width // 4, width // 8
    columns = triple_weight.shape[1]
    shrink_sent, expand_sent = late_arrays[-4], late_arrays[-2]
    deep, wide = shrink_sent.shape[1], expand_sent.shape[2]
    length = 4 * rows
    outs = (
        (ANY, (total, width), BF16),
        (VM, tangent.shape, BF16),
        (ANY, (2 * deep, width), BF16),
        (ANY, (4, shard, wide // 2), BF16),
        (ANY, (shard, width), BF16),
        (ANY, (4, shard, columns), BF16),
        (VM, (8, 128), F32),
        (VM, (8, 128), F32),
        (ANY, (total, width), BF16),
    )
    scratch = (
        ((total, width), BF16),
        ((total, width), F32),
        ((total, width), F32),
        ((2, length, width), BF16),
        ((total, width), BF16),
        ((total, half), BF16),
        ((micro, 4, rows, quarter), BF16),
        ((micro, 4, rows, quarter), BF16),
        ((micro, length, columns), BF16),
        ((length, 128), F32),
        ((length, 128), F32),
        ((micro, 3, rows, width), BF16),
        ((micro, rows, width), BF16),
        ((micro, 2, rows, width), BF16),
        ((micro, rows, width), BF16),
        ((micro, rows, width), BF16),
        ((2, 4, shard, width), BF16),
        ((2, 4, shard, width), BF16),
        ((2, 4, shard, width), BF16),
        ((3, 4, shard, width), BF16),
        ((3, 3, shard, width), BF16),
        ((4, shard, half), BF16),
        ((4, shard, half), BF16),
        ((4, shard, half), BF16),
        ((3, shard, half), BF16),
        ((4, shard, columns), BF16),
        ((4, shard, columns), BF16),
        ((4, shard, columns), BF16),
        ((3, shard, columns), BF16),
        ((3, shard, width), BF16),
        ((3, shard, width), BF16),
        ((4, shard, width), BF16),
        ((shard, columns), BF16),
        ((2, 8, 8, 128), F32),
        ((2, 4, 8, 128), F32),
        ((2, 4, 8, 128), F32),
        ((2, 4, 8, 128), F32),
        ((2, 3, 8, 128), F32),
        ((2, 8, 128), F32),
        ((2, 8, 128), F32),
        ((2, 8, 128), F32),
        ((2, 8, 128), F32),
    )
    return pl.pallas_call(
        backward_kernel,
        name="backward_together",
        out_shape=tuple(shape(dims, kind) for _, dims, kind in outs),
        in_specs=[VM] * 9 + [ANY] * 13,
        out_specs=tuple(spec for spec, _, _ in outs),
        scratch_shapes=[pltpu.VMEM(dims, kind) for dims, kind in scratch]
        + [
            pltpu.SemaphoreType.DMA((BACKWARD_MOVES,)),
            pltpu.SemaphoreType.DMA((BACKWARD_MOVES,)),
            pltpu.SemaphoreType.DMA((26,)),
        ],
        compiler_params=pltpu.CompilerParams(
            collective_id=1, has_side_effects=True, vmem_limit_bytes=63 * MIB
        ),
        cost_estimate=cost(24 * total * width * width, 64 * MIB),
    )(vectors, tangent, output_weight, triple_weight, triples, biases, lses, mixed_own, shift_in_grad, *late_arrays)


def widen_kernel(shrink, expand, output, triple, token_grad, result, *outs):
    shrink_out, expand_out, output_out, triple_out, token_out, result_out = outs
    token_out[...] = token_grad[...]
    result_out[...] = result[...]
    shrink_out[...] = shrink[...].astype(F32)
    output_out[...] = output[...].astype(F32)
    tile = expand.shape[2] // 4
    quarter = triple.shape[2] // 3
    for chip in range(2):
        for core in range(2):
            rank = 2 * chip + core
            for q in range(4):
                start = ((4 * chip + q) * 2 + core) * tile
                part = expand[rank, :, q * tile : (q + 1) * tile]
                expand_out[:, start : start + tile] = part.astype(F32)
            for k in range(3):
                start = (4 * k + rank) * quarter
                part = triple[rank, :, k * quarter : (k + 1) * quarter]
                triple_out[:, start : start + quarter] = part.astype(F32)


def widen(shrink, expand, output, triple, token_grad, result):
    shard = output.shape[0]
    return pl.pallas_call(
        widen_kernel,
        name="widen",
        out_shape=(
            shape(shrink.shape, F32),
            shape((shard, 4 * expand.shape[2]), F32),
            shape(output.shape, F32),
            shape((shard, 4 * triple.shape[2]), F32),
            shape(token_grad.shape, BF16),
            shape(result.shape, BF16),
        ),
        in_specs=[VM] * 6,
        out_specs=(VM,) * 6,
        compiler_params=params(),
        cost_estimate=cost(0, 16 * MIB),
    )(shrink, expand, output, triple, token_grad, result)


def block_biases(chosen, globals_here, rank, local_blocks):
    heads, count, _ = chosen.shape
    place = jnp.arange(count, dtype=jnp.int32)
    true_block = ((place // local_blocks) ^ rank) * local_blocks + place % local_blocks
    near = jnp.abs(true_block[:, None] - true_block[None, :]) <= 1
    is_global = jnp.any(true_block[:, None] == globals_here[None, :], axis=1)
    picked = jnp.any(chosen[:, None, :, :] == true_block[None, :, None, None], axis=3)
    allowed = near[None] | picked | is_global[None, :, None] | is_global[None, None, :]
    bias = jnp.where(allowed, 0.0, -1e30).astype(F32)
    return jnp.repeat(bias, BLOCK, axis=2)


def on_device(
    tokens,
    cotangent,
    random_blocks,
    global_blocks,
    attend_gain,
    attend_bias,
    triple_weight,
    output_weight,
    hidden_gain,
    hidden_bias,
    expand_weight,
    expand_bias,
    shrink_weight,
    shrink_bias,
):
    tokens, cotangent = tokens[:, 0], cotangent[:, 0]
    micro, rows, width = tokens.shape
    total = micro * rows
    ways = lax.axis_size("fsdp")
    fsdp = lax.axis_index("fsdp")
    rank = lax.axis_index("ctx")
    core = rank % 2
    place = place_id()
    heads_all = random_blocks.shape[2]
    own_heads = heads_all // 4
    local_blocks = rows // BLOCK
    shard = width // ways
    wide = expand_weight.shape[1]
    deep = shrink_weight.shape[0]
    ids = jnp.stack([place, rank, core, jnp.int32(0)])
    ids_sent = jnp.stack([place, rank, core, jnp.int32(1)])

    half_units = wide // (2 * ways)
    vectors = [attend_gain, attend_bias, hidden_gain, hidden_bias, shrink_bias]
    tangent_own = cotangent.reshape(total, width)
    picks = random_blocks[:, 0]
    if ways == 8:
        small = jnp.concatenate(
            [v.reshape(1, shard) for v in vectors]
            + [expand_bias.reshape(-1, shard), jnp.zeros((7, shard), BF16)]
        ).astype(F32)
        sets = picks.reshape(micro, 4, own_heads, local_blocks, -1).transpose(1, 0, 2, 4, 3)
        sets = jnp.pad(jnp.repeat(sets, BLOCK, axis=4), ((0, 0),) * 3 + ((0, 5), (0, 0)))
        (
            table,
            triple_full,
            output_full,
            expand_full,
            shrink_full,
            tangent_other,
            triples,
            normeds,
            biases,
            lses,
            mixed_own,
            mixed_all,
            mixed_other,
            attended,
            hidden,
            hidden_other,
        ) = forward_together(
            global_blocks[:, 0],
            tokens,
            small,
            sets,
            triple_weight,
            output_weight,
            expand_weight,
            shrink_weight,
            tangent_own,
        )
        gain_one, bias_one, gain_two, bias_two, shift_out = (
            table[:, k].reshape(1, width) for k in range(5)
        )
        shift_in = lax.dynamic_slice_in_dim(
            table[:, 5:9].reshape(8, 2, half_units), core, 1, 1
        ).reshape(1, wide // 2)
    else:

        def whole(part):
            return lax.all_gather(part, "fsdp", axis=0, tiled=True)

        triple_part = jnp.concatenate(
            [
                lax.dynamic_slice_in_dim(triple_weight, k * width + rank * (width // 4), width // 4, 1)
                for k in range(3)
            ],
            axis=1,
        )
        expand_part = jnp.concatenate(
            [
                lax.dynamic_slice_in_dim(expand_weight, (2 * k + core) * half_units, half_units, 1)
                for k in range(ways)
            ],
            axis=1,
        )
        shrink_part = lax.dynamic_slice_in_dim(shrink_weight, core * (deep // 2), deep // 2, 0)
        gain_one, bias_one, gain_two, bias_two, shift_out = (
            whole(v).astype(F32).reshape(1, width) for v in vectors
        )
        halves = whole(expand_bias).astype(F32).reshape(ways, 2, half_units)
        shift_in = jnp.where(core == 0, halves[:, 0], halves[:, 1]).reshape(1, wide // 2)
        triple_full, expand_full, shrink_full = whole(triple_part), whole(expand_part), whole(shrink_part)
        output_full = whole(output_weight)
        tangent_other = swap(tangent_own, "ctx", 1)
        far_picks = swap(picks, "ctx", 2)
        all_picks = jnp.stack([picks, swap(picks, "ctx", 1), far_picks, swap(far_picks, "ctx", 1)])
        chosen = lax.dynamic_slice_in_dim(all_picks, rank * own_heads, own_heads, 2)
        chosen = chosen.transpose(1, 2, 0, 3, 4).reshape(micro, own_heads, 4 * local_blocks, -1)
        triples, normeds, biases, lses, mixed_own, joined = [], [], [], [], [], []
        for step in range(micro):
            biases.append(block_biases(chosen[step], global_blocks[step, 0], rank, local_blocks))
            near, far = swap(tokens[step], "ctx", 1), swap(tokens[step], "ctx", 2)
            places = (tokens[step], near, far, swap(far, "ctx", 1))
            triple, normed = project(places, gain_one, bias_one, triple_full)
            mixed, lse = attend(triple, biases[step])
            here = [mixed[0]] + [swap(mixed[p], "ctx", p) for p in range(1, 4)]
            for low_bit, high in ((core == 1, False), (rank >= 2, True)):
                pairs = ((0, 2), (1, 3)) if high else ((0, 1), (2, 3))
                for one, two in pairs:
                    first = jnp.where(low_bit, here[two], here[one])
                    here[two] = jnp.where(low_bit, here[one], here[two])
                    here[one] = first
            joined.append(jnp.concatenate(here, axis=1))
            for kept, value in zip(
                (triples, normeds, lses, mixed_own), (triple, normed, lse, mixed)
            ):
                kept.append(value)
        mixed_all = jnp.concatenate(joined, axis=0)
        mixed_other = swap(mixed_all, "ctx", 1)
        attended, hidden = output_project(tokens, mixed_all, gain_two, bias_two, output_full)
        hidden_other = swap(hidden, "ctx", 1)

    (
        own_out,
        other_out,
        own_hidden,
        other_hidden,
        shift_in_grad,
        shrink_sent,
        shrink_kept,
        expand_sent,
        expand_kept,
    ) = feed(ids, (hidden, hidden_other), (tangent_own, tangent_other), shift_in, expand_full, shrink_full)
    if ways == 8:
        rows_of = jnp.concatenate([gain_two, gain_one, shift_out, jnp.zeros((5, width), F32)])
        (
            result,
            token_grad,
            shrink_grad,
            expand_grad,
            output_grad_all,
            triple_grad_all,
            early,
            late,
            _,
        ) = backward_together(
            rows_of,
            cotangent,
            output_full,
            triple_full,
            triples,
            biases,
            lses,
            mixed_own,
            shift_in_grad,
            own_hidden,
            other_hidden,
            own_out,
            other_out,
            attended,
            tokens.reshape(total, width),
            mixed_all,
            mixed_other,
            normeds,
            shrink_sent,
            shrink_kept,
            expand_sent,
            expand_kept,
        )
        shrink_grad, expand_grad, output_grad_all, triple_grad_all, token_grad, result = widen(
            shrink_grad, expand_grad, output_grad_all, triple_grad_all, token_grad, result.reshape(micro, rows, width)
        )
        early, late = early[:7].reshape(-1), late[:2].reshape(-1)
    else:
        came_hidden = swap(other_hidden, "ctx", 1)
        came_out = swap(other_out, "ctx", 1)
        shrink_mine = scatter_rows(shrink_kept, shrink_sent)
        expand_mine = scatter_rows(expand_kept, expand_sent)
        result, d_attended, d_branch, *grads, gain_two_grad, bias_two_grad, shift_out_grad = branch_back(
            ids,
            attended,
            own_hidden,
            came_hidden,
            cotangent,
            own_out,
            came_out,
            gain_two,
            shift_out,
            output_full,
        )
        half_sent = lax.dynamic_slice_in_dim(d_branch, (1 - core) * (width // 2), width // 2, 1)
        branch_other = swap(half_sent, "ctx", 1)
        output_sent = output_grad(ids_sent, mixed_all, mixed_other, d_branch, branch_other)
        output_kept = output_grad(ids, mixed_all, mixed_other, d_branch, branch_other)
        output_mine = scatter_rows(output_kept, output_sent)

        d_triples, norm_parts_here = [], []
        for step in range(micro):
            here = grads[4 * step : 4 * step + 4]
            here = [here[0]] + [swap(here[p], "ctx", p) for p in range(1, 4)]
            d_triple, parts = attend_back(
                triples[step], biases[step], lses[step], here, mixed_own[step], triple_full
            )
            d_triples.append(d_triple)
            near = swap(parts[1], "ctx", 1)
            far = wide_add(parts[2], swap(parts[3], "ctx", 1)).astype(BF16)
            norm_parts_here += [parts[0], near, swap(far, "ctx", 2)]
        normed_pair = (normeds[0], normeds[1])
        triple_sent = triple_grad(ids_sent, normed_pair, d_triples)
        triple_kept = triple_grad(ids, normed_pair, d_triples)
        triple_mine = scatter_rows(triple_kept, triple_sent)
        token_grad, gain_one_grad, bias_one_grad = first_back(
            tokens, d_attended, gain_one, norm_parts_here
        )

        halves = shift_in_grad.reshape(ways, 1, wide // (2 * ways))
        blank = jnp.zeros_like(halves)
        spread = jnp.where(
            core == 0,
            jnp.concatenate([halves, blank], axis=1),
            jnp.concatenate([blank, halves], axis=1),
        )
        early = sum_everywhere(
            jnp.concatenate(
                [
                    gain_two_grad.reshape(ways, shard),
                    bias_two_grad.reshape(ways, shard),
                    shift_out_grad.reshape(ways, shard),
                    spread.reshape(ways, wide // ways),
                ],
                axis=1,
            )
        )
        late = sum_everywhere(
            jnp.concatenate([gain_one_grad.reshape(ways, shard), bias_one_grad.reshape(ways, shard)], axis=1)
        )

        def over_chips(part):
            low = part.astype(BF16)
            return wide_add(low, swap(low, "ctx", 2))

        def both(own, axis):
            other = swap(own, "ctx", 1)
            first = jnp.where(core == 0, own, other)
            second = jnp.where(core == 0, other, own)
            return jnp.stack([first, second], axis=axis)

        shrink_grad = both(over_chips(shrink_mine), 0).reshape(deep, width)
        expand_half = over_chips(expand_mine).reshape(shard, ways, wide // (2 * ways))
        expand_grad = both(expand_half, 2).reshape(shard, wide)
        output_grad_all = both(over_chips(output_mine), 1).reshape(shard, width)
        low = triple_mine.astype(BF16).reshape(shard, 3, width // 4)
        far = swap(low, "ctx", 2)
        pair = jnp.stack([jnp.where(rank < 2, low, far), jnp.where(rank < 2, far, low)], axis=2)
        triple_grad_all = both(pair, 3).reshape(shard, 3 * width).astype(F32)
        early = lax.dynamic_index_in_dim(early, fsdp, 0, keepdims=False)
        late = lax.dynamic_index_in_dim(late, fsdp, 0, keepdims=False)

    return (
        result[:, None],
        token_grad[:, None],
        late[:shard],
        late[shard:],
        triple_grad_all,
        output_grad_all,
        early[:shard],
        early[shard : 2 * shard],
        expand_grad,
        early[3 * shard :],
        shrink_grad,
        early[2 * shard : 3 * shard],
    )


def solution(mesh):
    token_spec = P(None, "fsdp", "ctx", None)
    flat, rows = P("fsdp"), P("fsdp", None)
    return jax.shard_map(
        on_device,
        mesh=mesh,
        in_specs=(
            token_spec,
            token_spec,
            P(None, "fsdp", None, "ctx", None),
            P(None, "fsdp", None),
            flat,
            flat,
            rows,
            rows,
            flat,
            flat,
            rows,
            flat,
            rows,
            flat,
        ),
        out_specs=(
            token_spec,
            token_spec,
            flat,
            flat,
            rows,
            rows,
            flat,
            flat,
            rows,
            flat,
            rows,
            flat,
        ),
        check_vma=False,
    )
```

```python
import functools

import jax
import jax.numpy as jnp
from jax import lax
from jax.experimental import pallas as pl
from jax.experimental.pallas import tpu as pltpu
from jax.sharding import PartitionSpec as P

HEAD_DIM = 64
BLOCK = 64
EPSILON = 1e-05
F32 = jnp.float32
BF16 = jnp.bfloat16
MIB = 1 << 20

VM = pl.BlockSpec(memory_space=pltpu.VMEM)
SM = pl.BlockSpec(memory_space=pltpu.SMEM)
ANY = pl.BlockSpec(memory_space=pl.ANY)

NN = (((1,), (0,)), ((), ()))
NT = (((1,), (1,)), ((), ()))
TN = (((0,), (0,)), ((), ()))


def dot(left, right, dims=NN):
    return lax.dot_general(left, right, dims, preferred_element_type=F32)


def shape(dims, kind):
    return jax.ShapeDtypeStruct(dims, kind)


def params(limit=56):
    return pltpu.CompilerParams(vmem_limit_bytes=limit * MIB)


def cost(flops, moved, special=0):
    return pl.CostEstimate(flops=flops, bytes_accessed=moved, transcendentals=special)


def swap(value, axis, step):
    size = lax.axis_size(axis)
    return lax.ppermute(value, axis, [(i, i ^ step) for i in range(size)])


def place_id():
    return lax.axis_index("fsdp") if lax.axis_size("fsdp") == 8 else jnp.int32(1)


def wide_add(*terms):
    total = terms[0].astype(F32)
    for term in terms[1:]:
        total = total + term.astype(F32)
    return total


def scatter_rows(kept, sent):
    whole = jnp.stack([sent, kept], axis=1)
    whole = whole.reshape((8 * kept.shape[1],) + kept.shape[2:])
    return lax.psum_scatter(whole.astype(F32), "fsdp", scatter_dimension=0, tiled=True)


def sum_everywhere(vector):
    return lax.psum(vector, ("ctx", "fsdp"))


def norm_parts(values):
    average = jnp.mean(values, axis=-1, keepdims=True)
    centered = values - average
    variance = jnp.mean(centered * centered, axis=-1, keepdims=True)
    inverse = lax.rsqrt(variance + EPSILON)
    return centered * inverse, inverse


def norm_back(grad, unit, inverse, gain):
    scaled = grad * gain
    first = jnp.mean(scaled, axis=-1, keepdims=True)
    second = jnp.mean(scaled * unit, axis=-1, keepdims=True)
    return inverse * (scaled - first - unit * second)


def normalize(source, gain, bias):
    unit, _ = norm_parts(source.astype(F32))
    return (unit * gain + bias).astype(BF16)


def project_kernel(t0, t1, t2, t3, gain, bias, weight, triple, normed):
    rows = t0.shape[0]
    for place, part in enumerate((t0, t1, t2, t3)):
        span = slice(place * rows, (place + 1) * rows)
        normed[span, :] = normalize(part[...], gain[...], bias[...])
        triple[span, :] = dot(normed[span, :], weight[...]).astype(BF16)


def project(parts, gain, bias, weight):
    rows, width = parts[0].shape
    columns = weight.shape[1]
    return pl.pallas_call(
        project_kernel,
        name="project",
        out_shape=(shape((4 * rows, columns), BF16), shape((4 * rows, width), BF16)),
        in_specs=[VM] * 7,
        out_specs=(VM, VM),
        compiler_params=params(),
        cost_estimate=cost(8 * rows * width * columns, 12 * rows * width + 2 * width * columns),
    )(*parts, gain, bias, weight)


def head_mask(rows):
    return lax.broadcasted_iota(jnp.int32, (rows, 2 * HEAD_DIM), 1) // HEAD_DIM


def attend_body(triple, block_bias, mixed, lse, between=None):
    length = triple.shape[0]
    width = triple.shape[1] // 3
    rows = length // 4
    blocks = length // BLOCK
    for pair in range(width // 128):
        keys = triple[:, width + pair * 128 : width + pair * 128 + 128]
        values = triple[:, 2 * width + pair * 128 : 2 * width + pair * 128 + 128]
        values_t = values.astype(F32).T.astype(BF16)

        def step(place, carry):
            start = pl.multiple_of(place * rows, rows)
            queries = triple[pl.ds(start, rows), pair * 128 : pair * 128 + 128]
            queries = queries * jnp.asarray(0.125, BF16)
            side = head_mask(rows)
            halves = []
            for which in range(2):
                head = 2 * pair + which
                one = jnp.where(side == which, queries, jnp.zeros_like(queries))
                scores = dot(keys, one, NT)
                shift = block_bias[head, :, pl.ds(start, rows)]
                scores = scores.reshape(blocks, BLOCK, rows) + shift[:, None, :]
                peak = jnp.max(jnp.max(scores, axis=0), axis=0, keepdims=True)
                powered = jnp.exp(scores - peak[None])
                total = jnp.sum(jnp.sum(powered, axis=0), axis=0, keepdims=True)
                lse[head : head + 1, pl.ds(start, rows)] = peak + jnp.log(total)
                low = powered.astype(BF16).reshape(length, rows)
                part = dot(values_t[which * HEAD_DIM : (which + 1) * HEAD_DIM, :], low)
                halves.append(part / total)
            joined = jnp.concatenate(halves, axis=0)
            mixed[place, :, pair * 128 : pair * 128 + 128] = joined.T.astype(BF16)
            return carry

        lax.fori_loop(0, 4, step, 0)
        if between is not None and pair == 0:
            between()


def attend(triple, block_bias):
    length, columns = triple.shape
    width = columns // 3
    heads = width // HEAD_DIM
    rows = length // 4
    return pl.pallas_call(
        attend_body,
        name="attend",
        out_shape=(shape((4, rows, width), BF16), shape((8, length), F32)),
        in_specs=[VM, VM],
        out_specs=(VM, VM),
        compiler_params=params(),
        cost_estimate=cost(
            32 * heads * length * length * HEAD_DIM, 8 * length * width, heads * length * length
        ),
    )(triple, block_bias)


def attend_back_body(
    triple, block_bias, lse, grads, mixed, d_triple, key_total, value_total, between=None
):
    length = triple.shape[0]
    width = triple.shape[1] // 3
    rows = length // 4
    blocks = length // BLOCK
    for pair in range(width // 128):
        lanes = slice(pair * 128, pair * 128 + 128)
        keys = triple[:, width + pair * 128 : width + pair * 128 + 128]
        values = triple[:, 2 * width + pair * 128 : 2 * width + pair * 128 + 128]
        keys_t = keys.astype(F32).T.astype(BF16)
        key_total[...] = jnp.zeros_like(key_total)
        value_total[...] = jnp.zeros_like(value_total)

        def step(place, carry):
            start = pl.multiple_of(place * rows, rows)
            queries = triple[pl.ds(start, rows), lanes] * jnp.asarray(0.125, BF16)
            grad = grads[place, :, lanes]
            product = (grad.astype(F32) * mixed[place, :, lanes].astype(F32)).T
            side = head_mask(rows)
            halves = []
            for which in range(2):
                head = 2 * pair + which
                one = jnp.where(side == which, queries, jnp.zeros_like(queries))
                one_grad = jnp.where(side == which, grad, jnp.zeros_like(grad))
                delta = jnp.sum(
                    product[which * HEAD_DIM : (which + 1) * HEAD_DIM, :], axis=0, keepdims=True
                )
                scores = dot(keys, one, NT)
                shift = block_bias[head, :, pl.ds(start, rows)] - lse[head : head + 1, pl.ds(start, rows)]
                exact = jnp.exp(scores.reshape(blocks, BLOCK, rows) + shift[:, None, :])
                exact = exact.reshape(length, rows)
                value_total[...] += dot(exact.astype(BF16), one_grad)
                d_probs = dot(values, one_grad, NT)
                d_scores = (exact * (d_probs - delta)).astype(BF16)
                key_total[...] += dot(d_scores, one)
                halves.append(dot(keys_t[which * HEAD_DIM : (which + 1) * HEAD_DIM, :], d_scores))
            joined = jnp.concatenate(halves, axis=0) * 0.125
            d_triple[pl.ds(start, rows), lanes] = joined.T.astype(BF16)
            return carry

        lax.fori_loop(0, 4, step, 0)
        d_triple[:, width + pair * 128 : width + pair * 128 + 128] = key_total[...].astype(BF16)
        d_triple[:, 2 * width + pair * 128 : 2 * width + pair * 128 + 128] = value_total[
            ...
        ].astype(BF16)
        if between is not None and pair == 0:
            between()


def attend_back_kernel(triple, block_bias, lse, g0, g1, g2, g3, mixed, weight, d_triple, norm_grad, grads, key_total, value_total):
    rows = g0.shape[0]
    for place, part in enumerate((g0, g1, g2, g3)):
        grads[place] = part[...]
    attend_back_body(triple, block_bias, lse, grads, mixed, d_triple, key_total, value_total)
    for place in range(4):
        part = dot(d_triple[place * rows : (place + 1) * rows, :], weight[...], NT)
        norm_grad[place] = part.astype(BF16)


def attend_back(triple, block_bias, lse, grads, mixed, weight):
    length, columns = triple.shape
    width = columns // 3
    heads = width // HEAD_DIM
    rows = length // 4
    return pl.pallas_call(
        attend_back_kernel,
        name="attend_back",
        out_shape=(shape((length, columns), BF16), shape((4, rows, weight.shape[0]), BF16)),
        in_specs=[VM] * 9,
        out_specs=(VM,) * 2,
        scratch_shapes=[
            pltpu.VMEM((4, rows, width), BF16),
            pltpu.VMEM((length, 128), F32),
            pltpu.VMEM((length, 128), F32),
        ],
        compiler_params=params(),
        cost_estimate=cost(
            80 * heads * length * length * HEAD_DIM, 16 * length * width, heads * length * length
        ),
    )(triple, block_bias, lse, *grads, mixed, weight)


def output_kernel(tokens, joined, gain, bias, weight, attended, normed):
    rows = tokens.shape[1]
    for micro in range(2):
        span = slice(micro * rows, (micro + 1) * rows)
        value = tokens[micro].astype(F32) + dot(joined[span, :], weight[...])
        attended[span, :] = value
        normed[span, :] = normalize(value, gain[...], bias[...])


def output_project(tokens, joined, gain, bias, weight):
    micro, rows, width = tokens.shape
    total = micro * rows
    return pl.pallas_call(
        output_kernel,
        name="output_project",
        out_shape=(shape((total, width), F32), shape((total, width), BF16)),
        in_specs=[VM] * 5,
        out_specs=(VM, VM),
        compiler_params=params(),
        cost_estimate=cost(2 * total * width * width, 12 * total * width + 2 * width * width),
    )(tokens, joined, gain, bias, weight)


CURVE = 0.7978845608028654
CUBIC = 0.044715


def feed_kernel(ids, h0, h1, c0, c1, shift, *rest):
    expand_held, shrink_held = rest[:2]
    own_out, other_out, own_hidden, other_hidden, bias_grad = rest[2:7]
    shrink_sent, shrink_kept, expand_sent, expand_kept = rest[7:11]
    hidden, tangent, hidden_t, out_total, hidden_total = rest[11:]
    base = ids[0]
    rows, width = h0.shape
    tile = shrink_held.shape[0] // 8
    deep = width // 8
    hidden[:rows, :] = h0[...]
    hidden[rows:, :] = h1[...]
    tangent[:rows, :] = c0[...]
    tangent[rows:, :] = c1[...]
    for j in range(8):
        source = pl.multiple_of((base ^ j) * deep, deep)
        hidden_t[j * deep : (j + 1) * deep, :] = (
            hidden[:, pl.ds(source, deep)].astype(F32).T.astype(BF16)
        )
    for step, j in enumerate((1, 3, 5, 7, 0, 2, 4, 6)):
        column = pl.multiple_of((base ^ j) * tile, tile)
        up = expand_held[:, pl.ds(column, tile)]
        down = shrink_held[pl.ds(column, tile), :]
        before = dot(hidden[...], up) + shift[:, pl.ds(column, tile)]
        d_active = dot(tangent[...], down, NT)
        square = before * before
        bend = jnp.tanh(CURVE * before * (1.0 + CUBIC * square))
        plus = 0.5 * (1.0 + bend)
        active = (before * plus).astype(BF16)
        slope = plus + (0.5 * CURVE) * before * (1.0 - bend * bend) * (1.0 + 3 * CUBIC * square)
        d_before = (d_active * slope).astype(BF16)
        bias_grad[:, pl.ds(column, tile)] = jnp.sum(d_before.astype(F32), axis=0, keepdims=True)
        out_part = dot(active, down)
        hidden_part = dot(d_before, up, NT)
        if step == 0:
            out_total[...] = out_part
            hidden_total[...] = hidden_part
        else:
            out_total[...] += out_part
            hidden_total[...] += hidden_part
        shrink_part = dot(active, tangent[...], TN).astype(BF16)
        (shrink_sent if j % 2 else shrink_kept)[j // 2] = shrink_part
        expand_part = dot(hidden_t[...], d_before).astype(BF16)
        for place in range(8):
            target = expand_sent if place % 2 else expand_kept
            target[place // 2, :, pl.ds(column, tile)] = expand_part[
                place * deep : (place + 1) * deep, :
            ]
    own_out[...] = out_total[:rows, :]
    other_out[...] = out_total[rows:, :].astype(BF16)
    own_hidden[...] = hidden_total[:rows, :]
    other_hidden[...] = hidden_total[rows:, :].astype(BF16)


def feed(ids, hidden, tangent, shift, expand, shrink):
    rows, width = hidden[0].shape
    wide = expand.shape[1]
    deep, tile = width // 8, wide // 8
    return pl.pallas_call(
        feed_kernel,
        name="feed",
        out_shape=(
            shape((rows, width), F32),
            shape((rows, width), BF16),
            shape((rows, width), F32),
            shape((rows, width), BF16),
            shape((1, wide), F32),
            shape((4, tile, width), BF16),
            shape((4, tile, width), BF16),
            shape((4, deep, wide), BF16),
            shape((4, deep, wide), BF16),
        ),
        in_specs=[SM] + [VM] * 7,
        out_specs=(VM,) * 9,
        scratch_shapes=[
            pltpu.VMEM((2 * rows, width), BF16),
            pltpu.VMEM((2 * rows, width), BF16),
            pltpu.VMEM((width, 2 * rows), BF16),
            pltpu.VMEM((2 * rows, width), F32),
            pltpu.VMEM((2 * rows, width), F32),
        ],
        compiler_params=params(60),
        cost_estimate=cost(24 * rows * width * wide, 8 * width * wide + 20 * rows * width, 2 * rows * wide),
    )(ids, *hidden, *tangent, shift, expand, shrink)


def branch_kernel(
    ids, attended, own_hidden, came_hidden, tangent, own_out, came_out, gain, shift, weight, *rest
):
    result, d_attended, d_branch = rest[:3]
    grads, (gain_grad, bias_grad, shift_grad) = rest[3:11], rest[11:14]
    rows = tangent.shape[1]
    width = gain.shape[1] // 4
    gain_total = bias_total = shift_total = 0.0
    for micro in range(2):
        span = slice(micro * rows, (micro + 1) * rows)
        value = attended[span, :]
        cot = tangent[micro].astype(F32)
        branch = own_out[span, :] + came_out[span, :].astype(F32) + shift[...]
        result[micro] = (value + branch).astype(BF16)
        unit, inverse = norm_parts(value)
        grad = own_hidden[span, :] + came_hidden[span, :].astype(F32)
        gain_total = gain_total + jnp.sum(grad * unit, axis=0, keepdims=True)
        bias_total = bias_total + jnp.sum(grad, axis=0, keepdims=True)
        shift_total = shift_total + jnp.sum(cot, axis=0, keepdims=True)
        total = cot + norm_back(grad, unit, inverse, gain[...])
        d_attended[span, :] = total
        d_branch[span, :] = total.astype(BF16)
    gain_grad[...] = gain_total
    bias_grad[...] = bias_total
    shift_grad[...] = shift_total
    for micro in range(2):
        for place in range(4):
            start = pl.multiple_of((ids[1] ^ place) * width, width)
            part = dot(d_branch[micro * rows : (micro + 1) * rows, :], weight[pl.ds(start, width), :], NT)
            grads[4 * micro + place][...] = part.astype(BF16)


def branch_back(ids, attended, own_hidden, came_hidden, tangent, own_out, came_out, gain, shift, weight):
    micro, rows, width = tangent.shape
    total = micro * rows
    row = shape((1, width), F32)
    return pl.pallas_call(
        branch_kernel,
        name="branch_back",
        out_shape=(
            shape(tangent.shape, BF16),
            shape((total, width), F32),
            shape((total, width), BF16),
        )
        + tuple(shape((rows, width // 4), BF16) for _ in range(8))
        + (row, row, row),
        in_specs=[SM] + [VM] * 9,
        out_specs=(VM,) * 14,
        compiler_params=params(),
        cost_estimate=cost(2 * total * width * width, 32 * total * width),
    )(ids, attended, own_hidden, came_hidden, tangent, own_out, came_out, gain, shift, weight)


def output_grad_kernel(ids, own_mixed, other_mixed, own_branch, other_branch, out):
    rows = out.shape[1]
    width = own_branch.shape[1]
    half = width // 2
    column = pl.multiple_of(ids[2] * half, half)
    right = own_branch[:, pl.ds(column, half)]
    for k in range(4):
        start = pl.multiple_of((ids[0] ^ (2 * k + ids[3])) * rows, rows)
        part = dot(own_mixed[:, pl.ds(start, rows)], right, TN)
        part += dot(other_mixed[:, pl.ds(start, rows)], other_branch[...], TN)
        out[k] = part.astype(BF16)


def output_grad(ids, own_mixed, other_mixed, own_branch, other_branch):
    total, width = own_mixed.shape
    return pl.pallas_call(
        output_grad_kernel,
        name="output_grad",
        out_shape=shape((4, width // 8, width // 2), BF16),
        in_specs=[SM] + [VM] * 4,
        out_specs=VM,
        compiler_params=params(),
        cost_estimate=cost(total * width * width, 8 * total * width),
    )(ids, own_mixed, other_mixed, own_branch, other_branch)


def triple_grad_kernel(ids, n0, n1, d0, d1, out):
    rows = out.shape[1]
    for k in range(4):
        column = pl.multiple_of((ids[0] ^ (2 * k + ids[3])) * rows, rows)
        part = dot(n0[:, pl.ds(column, rows)], d0[...], TN)
        part += dot(n1[:, pl.ds(column, rows)], d1[...], TN)
        out[k] = part.astype(BF16)


def triple_grad(ids, normed, grads):
    length, width = normed[0].shape
    columns = grads[0].shape[1]
    return pl.pallas_call(
        triple_grad_kernel,
        name="triple_grad",
        out_shape=shape((4, width // 8, columns), BF16),
        in_specs=[SM] + [VM] * 4,
        out_specs=VM,
        compiler_params=params(),
        cost_estimate=cost(2 * length * width * columns, 4 * length * (width + columns)),
    )(ids, *normed, *grads)


def first_back_kernel(tokens, d_attended, gain, *rest):
    parts, (grad_out, gain_grad, bias_grad) = rest[:6], rest[6:]
    rows = tokens.shape[1]
    gain_total = bias_total = 0.0
    for micro in range(2):
        one, two, three = parts[3 * micro : 3 * micro + 3]
        grad = one[...].astype(F32) + two[...].astype(F32) + three[...].astype(F32)
        unit, inverse = norm_parts(tokens[micro].astype(F32))
        gain_total = gain_total + jnp.sum(grad * unit, axis=0, keepdims=True)
        bias_total = bias_total + jnp.sum(grad, axis=0, keepdims=True)
        total = d_attended[micro * rows : (micro + 1) * rows, :]
        grad_out[micro] = (total + norm_back(grad, unit, inverse, gain[...])).astype(BF16)
    gain_grad[...] = gain_total
    bias_grad[...] = bias_total


def first_back(tokens, d_attended, gain, parts):
    micro, rows, width = tokens.shape
    row = shape((1, width), F32)
    return pl.pallas_call(
        first_back_kernel,
        name="first_back",
        out_shape=(shape(tokens.shape, BF16), row, row),
        in_specs=[VM] * 9,
        out_specs=(VM,) * 3,
        compiler_params=params(),
        cost_estimate=cost(20 * micro * rows * width, 16 * micro * rows * width),
    )(tokens, d_attended, gain, *parts)


def flip(index, bits):
    out, bit = index, 1
    while bit <= bits:
        if bits & bit:
            out = out + bit * (1 - 2 * lax.rem(lax.div(index, jnp.int32(bit)), jnp.int32(2)))
        bit *= 2
    return out


class Moves:
    def __init__(self, send, recv):
        self.send, self.recv, self.started, self.freed = send, recv, [], []
        self.place = {"ctx": lax.axis_index("ctx"), "fsdp": lax.axis_index("fsdp")}

    def greet(self):
        barrier = pltpu.get_barrier_semaphore()
        partners = [("ctx", 1), ("ctx", 2), ("ctx", 3), ("fsdp", 1), ("fsdp", 2), ("fsdp", 4), ("fsdp", 6)]
        for axis, bits in partners:
            pl.semaphore_signal(
                barrier,
                inc=1,
                device_id={axis: flip(self.place[axis], bits)},
                device_id_type=pl.DeviceIdType.MESH,
            )
        pl.semaphore_wait(barrier, len(partners))

    def go(self, source, target, axis, bits):
        slot = len(self.started)
        move = pltpu.make_async_remote_copy(
            src_ref=source,
            dst_ref=target,
            send_sem=self.send.at[slot],
            recv_sem=self.recv.at[slot],
            device_id={axis: flip(self.place[axis], bits)},
            device_id_type=pl.DeviceIdType.MESH,
        )
        move.start()
        self.started.append(move)
        return move

    def sent(self, move):
        move.wait_send()
        self.freed.append(move)

    def close(self):
        for move in self.started:
            if not any(move is other for other in self.freed):
                move.wait_send()


class Gather:
    def __init__(self, moves, part, view, own, shared=False):
        self.moves, self.view, self.own, self.shared = moves, view, own, shared
        self.part = part

    def start(self):
        moves, part, view, me = self.moves, self.part, self.view, self.moves.place["fsdp"]
        self.distant = moves.go(part, view(me), "fsdp", 4)
        self.adjacent = moves.go(part, view(me), "fsdp", 2)
        self.across = [moves.go(part, view(me), "fsdp", 1)]
        self.sources = [1]
        self.over = [moves.go(part, view(me), "ctx", 2)] if self.shared else []
        return self

    def over_x(self, bits):
        if self.shared:
            block = self.view(flip(self.moves.place["fsdp"], bits))
            self.over.append(self.moves.go(block, block, "ctx", 2))

    def over_y(self, bits):
        block = self.view(flip(self.moves.place["fsdp"], bits))
        self.across.append(self.moves.go(block, block, "fsdp", 1))
        self.sources.append(bits + 1)
        self.over_x(bits)

    def forward(self):
        self.distant.wait_recv()
        block = self.view(flip(self.moves.place["fsdp"], 4))
        self.last = self.moves.go(block, block, "fsdp", 2)
        self.over_y(4)
        self.adjacent.wait_recv()
        self.over_y(2)

    def third(self):
        self.last.wait_recv()
        self.over_y(6)

    def second(self):
        for bits, move in zip(self.sources, self.across):
            move.wait_recv()
            self.over_x(bits)

    def finish(self):
        if not self.shared:
            self.second()
        for move in self.over:
            move.wait_recv()
        for copy in self.own:
            copy.wait()


FORWARD_MOVES = 106


def row_view(ref, rows, columns=slice(None)):
    return lambda index: ref.at[pl.ds(pl.multiple_of(index * rows, rows), rows), columns]


def forward_kernel(
    global_ids,
    tokens,
    small,
    picks,
    triple_weight,
    output_weight,
    expand_weight,
    shrink_weight,
    tangent,
    small_all,
    triple_out,
    output_out,
    expand_all,
    shrink_all,
    tangent_other,
    triple,
    normed,
    block_bias,
    lse,
    mixed,
    joined_out,
    mixed_other,
    attended,
    hidden,
    hidden_other,
    parts,
    small_held,
    picks_held,
    triple_held,
    output_held,
    joined,
    hidden_held,
    send,
    recv,
    local,
):
    moves = Moves(send, recv)
    rank, me = moves.place["ctx"], moves.place["fsdp"]
    core = lax.rem(rank, jnp.int32(2))
    micro, rows, width = tokens.shape
    half = width // 2
    quarter = width // 4
    shard = triple_weight.shape[0]
    wide = expand_all.shape[1] // 2
    deep = shrink_weight.shape[0] // 8
    chip = lax.div(rank, jnp.int32(2))
    locals_used = []

    def copy_here(source, target):
        copy = pltpu.make_async_copy(source, target, local.at[len(locals_used)])
        copy.start()
        locals_used.append(copy)
        return copy

    def at(start, size, unit=128):
        return pl.ds(pl.multiple_of(start, unit), size)

    mine = at(me * shard, shard)
    triple_own = [
        copy_here(
            triple_weight.at[:, at(k * width + rank * quarter, quarter)],
            triple_held.at[mine, k * quarter : (k + 1) * quarter],
        )
        for k in range(3)
    ]
    tile = wide // 4
    expand_views = [row_view(expand_all, shard, at(chip * wide + cut * (wide // 2), wide // 2)) for cut in range(2)]
    expand_own = [
        copy_here(
            expand_weight.at[:, at(((4 * chip + q) * 2 + core) * tile, tile)],
            expand_all.at[mine, at(chip * wide + q * tile, tile)],
        )
        for q in range(4)
    ]
    output_columns = at(core * half + chip * quarter, quarter)
    output_view = row_view(output_held, shard, output_columns)
    shrink_views = [
        lambda i, cut=cut: shrink_all.at[at(i * 4 * deep + cut * deep, deep, 64)] for cut in range(4)
    ]
    shrink_parts = [shrink_weight.at[at((core * 4 + cut) * deep, deep, 64)] for cut in range(4)]
    small_own = copy_here(small, small_held.at[me])
    output_own = copy_here(output_weight.at[:, output_columns], output_view(me))
    shrink_own = [copy_here(shrink_parts[cut], shrink_views[cut](me)) for cut in range(4)]
    moves.greet()

    small_gather = Gather(moves, small, lambda index: small_held.at[index], [small_own]).start()
    far = [moves.go(tokens.at[0], parts.at[0, 2], "ctx", 2)]
    near = [moves.go(tokens.at[0], parts.at[0, 1], "ctx", 1)]
    for copy in triple_own:
        copy.wait()
    triple_view = row_view(triple_held, shard)
    triple_gather = Gather(moves, triple_view(me), triple_view, []).start()
    picked = [moves.go(picks.at[flip(rank, p)], picks_held.at[p], "ctx", p) for p in range(1, 4)]
    near.append(moves.go(tokens.at[1], parts.at[1, 1], "ctx", 1))
    far.append(moves.go(tokens.at[1], parts.at[1, 2], "ctx", 2))
    output_gather = Gather(moves, output_weight.at[:, output_columns], output_view, [output_own], True)
    for copy in expand_own:
        copy.wait()
    expands = [Gather(moves, view(me), view, [], True) for view in expand_views]
    shrinks = [Gather(moves, shrink_parts[cut], shrink_views[cut], [shrink_own[cut]]) for cut in range(4)]
    small_gather.forward()
    triple_gather.forward()
    output_gather.start()
    expands[0].start()
    small_gather.third()
    triple_gather.third()
    expands[1].start()
    tangent_move = moves.go(tangent, tangent_other, "ctx", 1)

    for move in picked:
        move.wait_recv()
    count = block_bias.shape[2]
    each = count // 4
    ranks = [flip(rank, p) if p else rank for p in range(4)]
    key_row = lax.broadcasted_iota(jnp.int32, (count, rows), 0)
    key_place = key_row // each
    key_rank = ranks[0]
    for p in range(1, 4):
        key_rank = jnp.where(key_place == p, ranks[p], key_rank)
    key_block = key_rank * each + key_row % each
    lane = lax.broadcasted_iota(jnp.int32, (count, rows), 1) // BLOCK
    for step in range(micro):
        first, second = global_ids[step, 0], global_ids[step, 1]
        key_global = (key_block == first) | (key_block == second)
        for p in range(4):
            source = picks.at[rank] if p == 0 else picks_held.at[p]
            query_block = ranks[p] * each + lane
            base = key_global | (jnp.abs(query_block - key_block) <= 1)
            base = base | (query_block == first) | (query_block == second)
            for head in range(block_bias.shape[1]):
                hit = base
                for pick in range(3):
                    hit = hit | (source[step, head, pick : pick + 1, :] == key_block)
                block_bias[step, head, :, p * rows : (p + 1) * rows] = jnp.where(hit, 0.0, -1e30)

    small_gather.finish()
    small_all[...] = small_held[...]

    def vector(line):
        return jnp.concatenate([small_held[b, line : line + 1, :] for b in range(8)], axis=1)

    gain_one, bias_one, gain_two, bias_two = (vector(line) for line in range(4))

    for step in range(micro):
        far[step].wait_recv()
        near.append(moves.go(parts.at[step, 2], parts.at[step, 3], "ctx", 1))
    mixed_moves = []
    for step in range(micro):
        near[step].wait_recv()
        near[2 + step].wait_recv()
        for p in range(4):
            source = tokens[step] if p == 0 else parts[step, p]
            normed[step, p * rows : (p + 1) * rows, :] = normalize(source, gain_one, bias_one)
        if step == 0:
            output_gather.forward()
            expands[0].forward()
            shrinks[0].start()
            triple_gather.finish()
        for p in range(4):
            span = slice(p * rows, (p + 1) * rows)
            triple[step, span, :] = dot(normed[step, span, :], triple_held[...]).astype(BF16)

        def between_first():
            expands[0].third()
            shrinks[0].forward()
            shrinks[2].start()
            output_gather.second()

        def between_second():
            expands[1].second()
            shrinks[3].forward()
            shrinks[2].third()

        if step == 0:
            output_gather.third()
            expands[1].forward()
            shrinks[1].start()
        else:
            output_gather.finish()
            piece = output_held.at[:, at(core * half, half)]
            output_move = moves.go(piece, piece, "ctx", 1)
            shrinks[2].forward()
            shrinks[1].third()
        attend_body(
            triple.at[step],
            block_bias.at[step],
            mixed.at[step],
            lse.at[step],
            between_second if step else between_first,
        )
        own = pl.ds(pl.multiple_of(rank * quarter, quarter), quarter)
        span = slice(step * rows, (step + 1) * rows)
        joined[span, own] = mixed[step, 0]
        for p in range(1, 4):
            mixed_moves.append(moves.go(mixed.at[step, p], joined.at[span, own], "ctx", p))
        if step == 0:
            expands[1].third()
            shrinks[1].forward()
            shrinks[3].start()
            shrinks[0].third()
            expands[0].second()
        else:
            shrinks[3].third()
    output_move.wait_recv()
    for move in mixed_moves:
        move.wait_recv()
    keep = [copy_here(triple_held, triple_out), copy_here(output_held, output_out)]
    output_kernel(tokens, joined, gain_two, bias_two, output_held, attended, hidden_held)
    last = [
        moves.go(hidden_held, hidden_other, "ctx", 1),
        moves.go(joined, mixed_other, "ctx", 1),
    ]
    hidden[...] = hidden_held[...]
    joined_out[...] = joined[...]
    for gather in shrinks + expands:
        gather.finish()
    for move in [tangent_move] + last:
        move.wait_recv()
    for copy in keep:
        copy.wait()
    moves.close()


def forward_together(global_ids, tokens, small, picks, triple_weight, output_weight, expand_weight, shrink_weight, tangent):
    micro, rows, width = tokens.shape
    total = micro * rows
    columns = triple_weight.shape[1] // 4
    wide = expand_weight.shape[1] // 2
    length = 4 * rows
    heads = picks.shape[2]
    outs = (
        (VM, (8,) + small.shape, F32),
        (ANY, (width, columns), BF16),
        (ANY, (width, width), BF16),
        (ANY, (width, wide), BF16),
        (ANY, (wide, width), BF16),
        (ANY, (total, width), BF16),
        (VM, (micro, length, columns), BF16),
        (VM, (micro, length, width), BF16),
        (VM, (micro, heads, length // BLOCK, length), F32),
        (VM, (micro, 8, length), F32),
        (VM, (micro, 4, rows, width // 4), BF16),
        (VM, (total, width), BF16),
        (ANY, (total, width), BF16),
        (VM, (total, width), F32),
        (VM, (total, width), BF16),
        (ANY, (total, width), BF16),
    )
    return pl.pallas_call(
        forward_kernel,
        name="forward_together",
        out_shape=tuple(shape(dims, kind) for _, dims, kind in outs),
        in_specs=[SM] + [VM] * 3 + [ANY] * 5,
        out_specs=tuple(spec for spec, _, _ in outs),
        scratch_shapes=[
            pltpu.VMEM((micro, 4, rows, width), BF16),
            pltpu.VMEM((8,) + small.shape, F32),
            pltpu.VMEM(picks.shape, jnp.int32),
            pltpu.VMEM((width, columns), BF16),
            pltpu.VMEM((width, width), BF16),
            pltpu.VMEM((total, width), BF16),
            pltpu.VMEM((total, width), BF16),
            pltpu.SemaphoreType.DMA((FORWARD_MOVES,)),
            pltpu.SemaphoreType.DMA((FORWARD_MOVES,)),
            pltpu.SemaphoreType.DMA((15,)),
        ],
        compiler_params=pltpu.CompilerParams(
            collective_id=0, has_side_effects=True, vmem_limit_bytes=56 * MIB
        ),
        cost_estimate=cost(16 * total * width * width, 64 * MIB),
    )(global_ids, tokens, small, picks, triple_weight, output_weight, expand_weight, shrink_weight, tangent)


class Reduce:
    def __init__(self, moves, sent, came, line):
        self.moves, self.came, self.line = moves, came, line
        self.across = moves.go(sent, came, "fsdp", 1)

    def forward(self, *kept):
        self.across.wait_recv()
        for k in (1, 3, 0, 2):
            self.came[k] = wide_add(self.came[k], *(part[k] for part in kept)).astype(self.came.dtype)
        self.along = [self.moves.go(self.came.at[2 * i + 1], self.line.at[i], "fsdp", 2) for i in range(2)]

    def third(self):
        for move in self.along:
            move.wait_recv()
        self.came[2] = wide_add(self.came[2], self.line[1]).astype(self.came.dtype)
        self.last = self.moves.go(self.came.at[2], self.line.at[2], "fsdp", 4)

    def finish(self):
        self.last.wait_recv()
        return wide_add(self.came[0], self.line[0], self.line[2])


class ReduceAlong:
    def __init__(self, moves, kept, sent, ends, came, line):
        self.moves, self.ends, self.came, self.line = moves, ends, came, line
        sources = (kept.at[1], kept.at[3], sent.at[1], sent.at[3])
        self.along = [moves.go(source, came.at[i], "fsdp", 2) for i, source in enumerate(sources)]

    def forward(self):
        for i in (1, 3, 0, 2):
            self.along[i].wait_recv()
            self.ends[i] = wide_add(self.ends[i], self.came[i]).astype(BF16)
        self.next = [self.moves.go(self.ends.at[2 * i + 1], self.line.at[i], "fsdp", 4) for i in range(2)]

    def third(self):
        for move in self.next:
            move.wait_recv()
        self.ends[2] = wide_add(self.ends[2], self.line[1]).astype(BF16)
        self.last = self.moves.go(self.ends.at[2], self.line.at[2], "fsdp", 1)

    def finish(self):
        self.last.wait_recv()
        return wide_add(self.ends[0], self.line[0], self.line[2])


BACKWARD_MOVES = 96


def backward_kernel(
    vectors,
    tangent,
    output_weight,
    triple_weight,
    triples,
    biases,
    lses,
    mixed_own,
    shift_in_grad,
    own_hidden,
    other_hidden,
    own_out,
    other_out,
    attended,
    tokens,
    mixed_all,
    mixed_other,
    normeds,
    shrink_sent,
    shrink_kept,
    expand_sent,
    expand_kept,
    result,
    token_grad,
    shrink_out,
    expand_out,
    output_out,
    triple_out,
    early_out,
    late_out,
    came_out,
    came_hidden,
    d_attended,
    stage,
    held,
    d_branch,
    branch_other,
    d_mixed,
    grads,
    d_triples,
    key_total,
    value_total,
    near_parts,
    own_parts,
    near_came,
    far_sent,
    far_came,
    shrink_held,
    shrink_came,
    shrink_line,
    along_ends,
    along_came,
    along_line,
    expand_own,
    over_came,
    expand_came,
    expand_line,
    output_sent,
    output_mine,
    output_came,
    output_line,
    first_sent,
    first_mine,
    first_came,
    first_line,
    second_sent,
    second_mine,
    second_came,
    second_line,
    chip_sent,
    chip_came,
    chip_final,
    output_chip,
    expand_final,
    first_final,
    second_final,
    small_all,
    small_sent,
    small_kept,
    small_came,
    small_line,
    small_chip,
    small_chip_came,
    small_core,
    small_core_came,
    send,
    recv,
    local,
):
    moves = Moves(send, recv)
    rank, me = moves.place["ctx"], moves.place["fsdp"]
    core = lax.rem(rank, jnp.int32(2))
    micro, rows, width = tangent.shape
    half, quarter, shard = width // 2, width // 4, width // 8
    moves.greet()
    used = []

    def load(source, target):
        copy = pltpu.make_async_copy(source, target, local.at[len(used)])
        copy.start()
        used.append(copy)
        return copy

    def at(start, size, unit=128):
        return pl.ds(pl.multiple_of(start, unit), size)

    chip = lax.div(rank, jnp.int32(2))
    deep = shrink_sent.shape[1] // 4
    wide = expand_sent.shape[2] // 4
    hidden_move = moves.go(other_hidden, came_hidden, "ctx", 1)

    def rows_of(ref, i):
        return ref.at[:, i * deep : (i + 1) * deep, :]

    def there(ref, e):
        return ref.at[:, :, at((1 - chip) * 2 * wide + e * wide, wide)]

    shrinks = [Reduce(moves, rows_of(shrink_sent, i), shrink_came.at[i], shrink_line.at[i]) for i in range(3)]
    last_kept, last_sent = rows_of(shrink_kept, 3), rows_of(shrink_sent, 3)
    shrinks.append(ReduceAlong(moves, last_kept, last_sent, along_ends, along_came, along_line))
    over_moves = [moves.go(there(expand_sent, 0), over_came.at[0, 0], "ctx", 2)]
    loads = [load(own_hidden, d_attended), load(attended, stage)]
    out_move = moves.go(other_out, came_out, "ctx", 1)
    here = at(chip * 2 * wide, 2 * wide)
    expand_loads = [
        load(expand_sent.at[:, :, here], expand_own.at[0]),
        load(expand_kept.at[:, :, here], expand_own.at[1]),
    ]
    shrink_loads = [load(rows_of(shrink_kept, i), shrink_held.at[i]) for i in range(3)]
    along_loads = [
        load(source.at[2 * k], along_ends.at[2 * i + k])
        for i, source in enumerate((last_kept, last_sent))
        for k in range(2)
    ]
    mixed_loads = [load(mixed_all, held.at[0, : 2 * rows, :]), load(mixed_other, held.at[0, 2 * rows :, :])]

    gain_two, gain_one, shift_out = vectors[0:1, :], vectors[1:2, :], vectors[2:3, :]
    for copy in loads:
        copy.wait()
    hidden_move.wait_recv()
    gain_total = bias_total = shift_total = 0.0
    for step in range(micro):
        span = slice(step * rows, (step + 1) * rows)
        cot = tangent[step].astype(F32)
        unit, inverse = norm_parts(stage[span, :])
        grad = d_attended[span, :] + came_hidden[span, :].astype(F32)
        gain_total = gain_total + jnp.sum(grad * unit, axis=0, keepdims=True)
        bias_total = bias_total + jnp.sum(grad, axis=0, keepdims=True)
        shift_total = shift_total + jnp.sum(cot, axis=0, keepdims=True)
        total = cot + norm_back(grad, unit, inverse, gain_two)
        d_attended[span, :] = total
        d_branch[span, :] = total.astype(BF16)
    theirs = d_branch.at[:, pl.ds(pl.multiple_of((1 - core) * half, half), half)]
    branch_move = moves.go(theirs, branch_other, "ctx", 1)
    grad_moves = []
    for step in range(micro):
        for p in (2, 3, 1, 0):
            start = pl.multiple_of((flip(rank, p) if p else rank) * quarter, quarter)
            part = dot(d_branch[step * rows : (step + 1) * rows, :], output_weight[pl.ds(start, quarter), :], NT)
            if p:
                d_mixed[step, p] = part.astype(BF16)
                grad_moves.append(moves.go(d_mixed.at[step, p], grads.at[step, p], "ctx", p))
            else:
                grads[step, 0] = part.astype(BF16)

    over_moves.append(moves.go(there(expand_sent, 1), over_came.at[0, 1], "ctx", 2))
    over_moves += [moves.go(there(expand_kept, e), over_came.at[1, e], "ctx", 2) for e in range(2)]

    def small_row(which, line, vector):
        for b in range(8):
            small_all[which, b, line : line + 1, :] = vector[:, b * shard : (b + 1) * shard]

    def small_begin(which):
        for k in range(4):
            small_sent[which, k] = small_all[which, flip(me, 2 * k + 1)]
            small_kept[which, k] = small_all[which, flip(me, 2 * k) if k else me]
        return Reduce(moves, small_sent.at[which], small_came.at[which], small_line.at[which])

    def small_chips(which):
        small_chip[which] = smalls[which].finish()
        return moves.go(small_chip.at[which], small_chip_came.at[which], "ctx", 2)

    def small_cores(which, move):
        move.wait_recv()
        small_core[which] = small_chip[which] + small_chip_came[which]
        return moves.go(small_core.at[which], small_core_came.at[which], "ctx", 1)

    def small_end(which, move, out):
        move.wait_recv()
        out[...] = small_core[which] + small_core_came[which]

    small_all[...] = jnp.zeros_like(small_all)
    for line, vector in enumerate((gain_total, bias_total, shift_total)):
        small_row(0, line, vector)
    unit_lines = shift_in_grad.shape[1] // 8 // 128
    for b in range(8):
        for line in range(unit_lines):
            lanes = slice((b * unit_lines + line) * 128, (b * unit_lines + line + 1) * 128)
            small_all[0, b, pl.ds(3 + core * unit_lines + line, 1), :] = shift_in_grad[:, lanes]
    smalls = [small_begin(0)]
    for copy in shrink_loads + along_loads + expand_loads:
        copy.wait()

    def expand_columns(which, e):
        return expand_own.at[which, :, :, e * wide : (e + 1) * wide]

    def expand_begin(e):
        over_moves[e].wait_recv()
        part = expand_columns(0, e)
        for k in range(4):
            part[k] = wide_add(part[k], over_came[0, e, k]).astype(BF16)
        return Reduce(moves, part, expand_came.at[e], expand_line.at[e])

    def expand_forward(e):
        over_moves[2 + e].wait_recv()
        expands[e].forward(expand_columns(1, e), over_came.at[1, e])

    shrinks[0].forward(shrink_held.at[0])
    expands = [expand_begin(0)]

    for copy in mixed_loads:
        copy.wait()
    branch_move.wait_recv()
    mine = pl.ds(pl.multiple_of(core * half, half), half)

    def output_part(index):
        lanes = pl.ds(pl.multiple_of(index * shard, shard), shard)
        part = dot(held[0, : 2 * rows, lanes], d_branch[:, mine], TN)
        return part + dot(held[0, 2 * rows :, lanes], branch_other[...], TN)

    for k in range(4):
        output_sent[k] = output_part(flip(me, 2 * k + 1)).astype(BF16)
    output_reduce = Reduce(moves, output_sent, output_came, output_line)
    for k in range(4):
        output_mine[k] = output_part(flip(me, 2 * k) if k else me).astype(BF16)
    normed_loads = [load(normeds.at[step], held.at[step]) for step in range(1, micro)]

    norm_moves, far_moves = [], []

    def attention(step, between):
        for move in grad_moves[3 * step : 3 * step + 3]:
            move.wait_recv()
        attend_back_body(
            triples.at[step],
            biases.at[step],
            lses.at[step],
            grads.at[step],
            mixed_own.at[step],
            d_triples.at[step],
            key_total,
            value_total,
            between,
        )
        for p in (3, 1, 2, 0):
            span = slice(p * rows, (p + 1) * rows)
            part = dot(d_triples[step, span, :], triple_weight[...], NT).astype(BF16)
            if p:
                near_parts[step, p - 1] = part
            else:
                own_parts[step] = part
            if p % 2:
                norm_moves.append(moves.go(near_parts.at[step, p - 1], near_came.at[step, p // 2], "ctx", 1))

    def far_part(step):
        norm_moves[2 * step].wait_recv()
        far_sent[step] = wide_add(near_parts[step, 1], near_came[step, 1]).astype(BF16)
        far_moves.append(moves.go(far_sent.at[step], far_came.at[step], "ctx", 2))

    def between_first():
        expands.append(expand_begin(1))
        shrinks[1].third()
        shrinks[3].third()

    def between_second():
        shrinks[2].third()
        smalls[0].third()
        expand_forward(0)

    shrinks[3].forward()
    shrinks[1].forward(shrink_held.at[1])
    shrinks[0].third()
    attention(0, between_first)
    shrinks[2].forward(shrink_held.at[2])
    smalls[0].forward(small_kept.at[0])
    far_part(0)
    normed_loads.insert(0, load(normeds.at[0], held.at[0]))
    attention(1, between_second)

    for copy in normed_loads:
        copy.wait()
    split = first_sent.shape[2]

    def triple_part(index, columns):
        lanes = pl.ds(pl.multiple_of(index * shard, shard), shard)
        part = dot(held[0, :, lanes], d_triples[0, :, columns], TN)
        return part + dot(held[1, :, lanes], d_triples[1, :, columns], TN)

    groups = (slice(0, split), slice(split, None))
    triples_out = []
    for columns, sent, came, line in (
        (groups[0], first_sent, first_came, first_line),
        (groups[1], second_sent, second_came, second_line),
    ):
        for k in range(4):
            sent[k] = triple_part(flip(me, 2 * k + 1), columns).astype(BF16)
        triples_out.append(Reduce(moves, sent, came, line))
    expand_forward(1)
    expands[0].third()
    far_part(1)
    small_moves = [small_chips(0)]
    chips = []
    for i in range(4):
        chip_sent[i] = shrinks[i].finish().astype(BF16)
        chips.append(moves.go(chip_sent.at[i], chip_came.at[i], "ctx", 2))
    for columns, target in zip(groups, (first_mine, second_mine)):
        for k in range(4):
            target[k] = triple_part(flip(me, 2 * k) if k else me, columns).astype(BF16)
    small_moves[0] = small_cores(0, small_moves[0])
    output_reduce.forward(output_mine)
    expands[1].third()
    triples_out[0].forward(first_mine)

    token_load = load(tokens, held.at[0, : 2 * rows, :])
    out_load = load(own_out, stage)
    out_move.wait_recv()
    came_load = load(came_out, came_hidden)

    token_load.wait()
    for move in norm_moves[1::2] + far_moves:
        move.wait_recv()
    gain_total = bias_total = 0.0
    for step in range(micro):
        span = slice(step * rows, (step + 1) * rows)
        grad = wide_add(own_parts[step], near_came[step, 0], far_came[step])
        unit, inverse = norm_parts(held[0, span, :].astype(F32))
        gain_total = gain_total + jnp.sum(grad * unit, axis=0, keepdims=True)
        bias_total = bias_total + jnp.sum(grad, axis=0, keepdims=True)
        token_grad[step] = (d_attended[span, :] + norm_back(grad, unit, inverse, gain_one)).astype(BF16)
    small_row(1, 0, gain_total)
    small_row(1, 1, bias_total)
    smalls.append(small_begin(1))
    small_end(0, small_moves[0], early_out)
    output_reduce.third()
    triples_out[1].forward(second_mine)
    smalls[1].forward(small_kept.at[1])
    out_load.wait()
    sum_load = load(attended, d_attended)
    came_load.wait()
    for step in range(micro):
        span = slice(step * rows, (step + 1) * rows)
        stage[span, :] = stage[span, :] + came_hidden[span, :].astype(F32) + shift_out
    sum_load.wait()
    moves.sent(branch_move)
    for step in range(micro):
        span = slice(step * rows, (step + 1) * rows)
        d_branch[span, :] = (d_attended[span, :] + stage[span, :]).astype(BF16)
    result_load = load(d_branch, result)

    ends, stays, crossing = [], [], []

    def place(source, target):
        ends.append(moves.go(source, target, "ctx", 1))
        stays.append(load(source, target))

    def spread(source, view):
        crossing.append((moves.go(source, view(rank), "ctx", 2), view(flip(rank, 2))))
        place(source, view(rank))

    for i in range(4):
        chips[i].wait_recv()
        chip_final[i] = wide_add(chip_sent[i], chip_came[i]).astype(BF16)
        place(chip_final.at[i], shrink_out.at[at((4 * core + i) * deep, deep, 64), :])
    for e in range(2):
        expand_final[e] = expands[e].finish().astype(BF16)
        spread(expand_final.at[e], lambda r, e=e: expand_out.at[r, :, e * wide : (e + 1) * wide])
    triples_out[0].third()
    triples_out[1].third()
    smalls[1].third()
    output_chip[0] = output_reduce.finish().astype(BF16)
    output_move = moves.go(output_chip.at[0], output_chip.at[1], "ctx", 2)
    first_final[...] = triples_out[0].finish().astype(BF16)
    spread(first_final, lambda r: triple_out.at[r, :, groups[0]])
    second_final[...] = triples_out[1].finish().astype(BF16)
    spread(second_final, lambda r: triple_out.at[r, :, split : first_sent.shape[2] + second_sent.shape[2]])
    late_move = small_chips(1)
    output_move.wait_recv()
    output_chip[2] = wide_add(output_chip[0], output_chip[1]).astype(BF16)
    place(output_chip.at[2], output_out.at[:, mine])
    for move, block in crossing:
        move.wait_recv()
        ends.append(moves.go(block, block, "ctx", 1))
    late_move = small_cores(1, late_move)
    small_end(1, late_move, late_out)
    for move in ends:
        move.wait_recv()
    for copy in stays + [result_load]:
        copy.wait()
    moves.close()


def backward_together(vectors, tangent, output_weight, triple_weight, triples, biases, lses, mixed_own, shift_in_grad, *late_arrays):
    micro, rows, width = tangent.shape
    total, half, quarter, shard = micro * rows, width // 2, width // 4, width // 8
    columns = triple_weight.shape[1]
    shrink_sent, expand_sent = late_arrays[-4], late_arrays[-2]
    deep, wide = shrink_sent.shape[1], expand_sent.shape[2]
    length = 4 * rows
    outs = (
        (ANY, (total, width), BF16),
        (VM, tangent.shape, BF16),
        (ANY, (2 * deep, width), BF16),
        (ANY, (4, shard, wide // 2), BF16),
        (ANY, (shard, width), BF16),
        (ANY, (4, shard, columns), BF16),
        (VM, (8, 128), F32),
        (VM, (8, 128), F32),
        (ANY, (total, width), BF16),
    )
    scratch = (
        ((total, width), BF16),
        ((total, width), F32),
        ((total, width), F32),
        ((2, length, width), BF16),
        ((total, width), BF16),
        ((total, half), BF16),
        ((micro, 4, rows, quarter), BF16),
        ((micro, 4, rows, quarter), BF16),
        ((micro, length, columns), BF16),
        ((length, 128), F32),
        ((length, 128), F32),
        ((micro, 3, rows, width), BF16),
        ((micro, rows, width), BF16),
        ((micro, 2, rows, width), BF16),
        ((micro, rows, width), BF16),
        ((micro, rows, width), BF16),
        ((3, 4, deep // 4, width), BF16),
        ((3, 4, deep // 4, width), BF16),
        ((3, 3, deep // 4, width), BF16),
        ((4, deep // 4, width), BF16),
        ((4, deep // 4, width), BF16),
        ((3, deep // 4, width), BF16),
        ((2, 4, shard, wide // 2), BF16),
        ((2, 2, 4, shard, wide // 4), BF16),
        ((2, 4, shard, wide // 4), BF16),
        ((2, 3, shard, wide // 4), BF16),
        ((4, shard, half), BF16),
        ((4, shard, half), BF16),
        ((4, shard, half), BF16),
        ((3, shard, half), BF16),
        ((4, shard, 2 * quarter), BF16),
        ((4, shard, 2 * quarter), BF16),
        ((4, shard, 2 * quarter), BF16),
        ((3, shard, 2 * quarter), BF16),
        ((4, shard, quarter), BF16),
        ((4, shard, quarter), BF16),
        ((4, shard, quarter), BF16),
        ((3, shard, quarter), BF16),
        ((4, deep // 4, width), BF16),
        ((4, deep // 4, width), BF16),
        ((4, deep // 4, width), BF16),
        ((3, shard, half), BF16),
        ((2, shard, wide // 4), BF16),
        ((shard, 2 * quarter), BF16),
        ((shard, quarter), BF16),
        ((2, 8, 8, 128), F32),
        ((2, 4, 8, 128), F32),
        ((2, 4, 8, 128), F32),
        ((2, 4, 8, 128), F32),
        ((2, 3, 8, 128), F32),
        ((2, 8, 128), F32),
        ((2, 8, 128), F32),
        ((2, 8, 128), F32),
        ((2, 8, 128), F32),
    )
    return pl.pallas_call(
        backward_kernel,
        name="backward_together",
        out_shape=tuple(shape(dims, kind) for _, dims, kind in outs),
        in_specs=[VM] * 9 + [ANY] * 13,
        out_specs=tuple(spec for spec, _, _ in outs),
        scratch_shapes=[pltpu.VMEM(dims, kind) for dims, kind in scratch]
        + [
            pltpu.SemaphoreType.DMA((BACKWARD_MOVES,)),
            pltpu.SemaphoreType.DMA((BACKWARD_MOVES,)),
            pltpu.SemaphoreType.DMA((32,)),
        ],
        compiler_params=pltpu.CompilerParams(
            collective_id=1, has_side_effects=True, vmem_limit_bytes=63 * MIB
        ),
        cost_estimate=cost(24 * total * width * width, 64 * MIB),
    )(vectors, tangent, output_weight, triple_weight, triples, biases, lses, mixed_own, shift_in_grad, *late_arrays)


def widen_kernel(shrink, expand, output, triple, token_grad, result, *outs):
    shrink_out, expand_out, output_out, triple_out, token_out, result_out = outs
    token_out[...] = token_grad[...]
    result_out[...] = result[...]
    shrink_out[...] = shrink[...].astype(F32)
    output_out[...] = output[...].astype(F32)
    tile = expand.shape[2] // 4
    quarter = triple.shape[2] // 3
    for chip in range(2):
        for core in range(2):
            rank = 2 * chip + core
            for q in range(4):
                start = ((4 * chip + q) * 2 + core) * tile
                part = expand[rank, :, q * tile : (q + 1) * tile]
                expand_out[:, start : start + tile] = part.astype(F32)
            for k in range(3):
                start = (4 * k + rank) * quarter
                part = triple[rank, :, k * quarter : (k + 1) * quarter]
                triple_out[:, start : start + quarter] = part.astype(F32)


def widen(shrink, expand, output, triple, token_grad, result):
    shard = output.shape[0]
    return pl.pallas_call(
        widen_kernel,
        name="widen",
        out_shape=(
            shape(shrink.shape, F32),
            shape((shard, 4 * expand.shape[2]), F32),
            shape(output.shape, F32),
            shape((shard, 4 * triple.shape[2]), F32),
            shape(token_grad.shape, BF16),
            shape(result.shape, BF16),
        ),
        in_specs=[VM] * 6,
        out_specs=(VM,) * 6,
        compiler_params=params(),
        cost_estimate=cost(0, 16 * MIB),
    )(shrink, expand, output, triple, token_grad, result)


def block_biases(chosen, globals_here, rank, local_blocks):
    heads, count, _ = chosen.shape
    place = jnp.arange(count, dtype=jnp.int32)
    true_block = ((place // local_blocks) ^ rank) * local_blocks + place % local_blocks
    near = jnp.abs(true_block[:, None] - true_block[None, :]) <= 1
    is_global = jnp.any(true_block[:, None] == globals_here[None, :], axis=1)
    picked = jnp.any(chosen[:, None, :, :] == true_block[None, :, None, None], axis=3)
    allowed = near[None] | picked | is_global[None, :, None] | is_global[None, None, :]
    bias = jnp.where(allowed, 0.0, -1e30).astype(F32)
    return jnp.repeat(bias, BLOCK, axis=2)


def on_device(
    tokens,
    cotangent,
    random_blocks,
    global_blocks,
    attend_gain,
    attend_bias,
    triple_weight,
    output_weight,
    hidden_gain,
    hidden_bias,
    expand_weight,
    expand_bias,
    shrink_weight,
    shrink_bias,
):
    tokens, cotangent = tokens[:, 0], cotangent[:, 0]
    micro, rows, width = tokens.shape
    total = micro * rows
    ways = lax.axis_size("fsdp")
    fsdp = lax.axis_index("fsdp")
    rank = lax.axis_index("ctx")
    core = rank % 2
    place = place_id()
    heads_all = random_blocks.shape[2]
    own_heads = heads_all // 4
    local_blocks = rows // BLOCK
    shard = width // ways
    wide = expand_weight.shape[1]
    deep = shrink_weight.shape[0]
    ids = jnp.stack([place, rank, core, jnp.int32(0)])
    ids_sent = jnp.stack([place, rank, core, jnp.int32(1)])

    half_units = wide // (2 * ways)
    vectors = [attend_gain, attend_bias, hidden_gain, hidden_bias, shrink_bias]
    tangent_own = cotangent.reshape(total, width)
    picks = random_blocks[:, 0]
    if ways == 8:
        small = jnp.concatenate(
            [v.reshape(1, shard) for v in vectors]
            + [expand_bias.reshape(-1, shard), jnp.zeros((7, shard), BF16)]
        ).astype(F32)
        sets = picks.reshape(micro, 4, own_heads, local_blocks, -1).transpose(1, 0, 2, 4, 3)
        sets = jnp.pad(jnp.repeat(sets, BLOCK, axis=4), ((0, 0),) * 3 + ((0, 5), (0, 0)))
        (
            table,
            triple_full,
            output_full,
            expand_full,
            shrink_full,
            tangent_other,
            triples,
            normeds,
            biases,
            lses,
            mixed_own,
            mixed_all,
            mixed_other,
            attended,
            hidden,
            hidden_other,
        ) = forward_together(
            global_blocks[:, 0],
            tokens,
            small,
            sets,
            triple_weight,
            output_weight,
            expand_weight,
            shrink_weight,
            tangent_own,
        )
        gain_one, bias_one, gain_two, bias_two, shift_out = (
            table[:, k].reshape(1, width) for k in range(5)
        )
        shift_in = lax.dynamic_slice_in_dim(
            table[:, 5:9].reshape(8, 2, half_units), core, 1, 1
        ).reshape(1, wide // 2)
    else:

        def whole(part):
            return lax.all_gather(part, "fsdp", axis=0, tiled=True)

        triple_part = jnp.concatenate(
            [
                lax.dynamic_slice_in_dim(triple_weight, k * width + rank * (width // 4), width // 4, 1)
                for k in range(3)
            ],
            axis=1,
        )
        expand_part = jnp.concatenate(
            [
                lax.dynamic_slice_in_dim(expand_weight, (2 * k + core) * half_units, half_units, 1)
                for k in range(ways)
            ],
            axis=1,
        )
        shrink_part = lax.dynamic_slice_in_dim(shrink_weight, core * (deep // 2), deep // 2, 0)
        gain_one, bias_one, gain_two, bias_two, shift_out = (
            whole(v).astype(F32).reshape(1, width) for v in vectors
        )
        halves = whole(expand_bias).astype(F32).reshape(ways, 2, half_units)
        shift_in = jnp.where(core == 0, halves[:, 0], halves[:, 1]).reshape(1, wide // 2)
        triple_full, expand_full, shrink_full = whole(triple_part), whole(expand_part), whole(shrink_part)
        output_full = whole(output_weight)
        tangent_other = swap(tangent_own, "ctx", 1)
        far_picks = swap(picks, "ctx", 2)
        all_picks = jnp.stack([picks, swap(picks, "ctx", 1), far_picks, swap(far_picks, "ctx", 1)])
        chosen = lax.dynamic_slice_in_dim(all_picks, rank * own_heads, own_heads, 2)
        chosen = chosen.transpose(1, 2, 0, 3, 4).reshape(micro, own_heads, 4 * local_blocks, -1)
        triples, normeds, biases, lses, mixed_own, joined = [], [], [], [], [], []
        for step in range(micro):
            biases.append(block_biases(chosen[step], global_blocks[step, 0], rank, local_blocks))
            near, far = swap(tokens[step], "ctx", 1), swap(tokens[step], "ctx", 2)
            places = (tokens[step], near, far, swap(far, "ctx", 1))
            triple, normed = project(places, gain_one, bias_one, triple_full)
            mixed, lse = attend(triple, biases[step])
            here = [mixed[0]] + [swap(mixed[p], "ctx", p) for p in range(1, 4)]
            for low_bit, high in ((core == 1, False), (rank >= 2, True)):
                pairs = ((0, 2), (1, 3)) if high else ((0, 1), (2, 3))
                for one, two in pairs:
                    first = jnp.where(low_bit, here[two], here[one])
                    here[two] = jnp.where(low_bit, here[one], here[two])
                    here[one] = first
            joined.append(jnp.concatenate(here, axis=1))
            for kept, value in zip(
                (triples, normeds, lses, mixed_own), (triple, normed, lse, mixed)
            ):
                kept.append(value)
        mixed_all = jnp.concatenate(joined, axis=0)
        mixed_other = swap(mixed_all, "ctx", 1)
        attended, hidden = output_project(tokens, mixed_all, gain_two, bias_two, output_full)
        hidden_other = swap(hidden, "ctx", 1)

    (
        own_out,
        other_out,
        own_hidden,
        other_hidden,
        shift_in_grad,
        shrink_sent,
        shrink_kept,
        expand_sent,
        expand_kept,
    ) = feed(ids, (hidden, hidden_other), (tangent_own, tangent_other), shift_in, expand_full, shrink_full)
    if ways == 8:
        rows_of = jnp.concatenate([gain_two, gain_one, shift_out, jnp.zeros((5, width), F32)])
        (
            result,
            token_grad,
            shrink_grad,
            expand_grad,
            output_grad_all,
            triple_grad_all,
            early,
            late,
            _,
        ) = backward_together(
            rows_of,
            cotangent,
            output_full,
            triple_full,
            triples,
            biases,
            lses,
            mixed_own,
            shift_in_grad,
            own_hidden,
            other_hidden,
            own_out,
            other_out,
            attended,
            tokens.reshape(total, width),
            mixed_all,
            mixed_other,
            normeds,
            shrink_sent,
            shrink_kept,
            expand_sent,
            expand_kept,
        )
        shrink_grad, expand_grad, output_grad_all, triple_grad_all, token_grad, result = widen(
            shrink_grad, expand_grad, output_grad_all, triple_grad_all, token_grad, result.reshape(micro, rows, width)
        )
        early, late = early[:7].reshape(-1), late[:2].reshape(-1)
    else:
        came_hidden = swap(other_hidden, "ctx", 1)
        came_out = swap(other_out, "ctx", 1)
        shrink_mine = scatter_rows(shrink_kept, shrink_sent)
        expand_mine = scatter_rows(expand_kept, expand_sent)
        result, d_attended, d_branch, *grads, gain_two_grad, bias_two_grad, shift_out_grad = branch_back(
            ids,
            attended,
            own_hidden,
            came_hidden,
            cotangent,
            own_out,
            came_out,
            gain_two,
            shift_out,
            output_full,
        )
        half_sent = lax.dynamic_slice_in_dim(d_branch, (1 - core) * (width // 2), width // 2, 1)
        branch_other = swap(half_sent, "ctx", 1)
        output_sent = output_grad(ids_sent, mixed_all, mixed_other, d_branch, branch_other)
        output_kept = output_grad(ids, mixed_all, mixed_other, d_branch, branch_other)
        output_mine = scatter_rows(output_kept, output_sent)

        d_triples, norm_parts_here = [], []
        for step in range(micro):
            here = grads[4 * step : 4 * step + 4]
            here = [here[0]] + [swap(here[p], "ctx", p) for p in range(1, 4)]
            d_triple, parts = attend_back(
                triples[step], biases[step], lses[step], here, mixed_own[step], triple_full
            )
            d_triples.append(d_triple)
            near = swap(parts[1], "ctx", 1)
            far = wide_add(parts[2], swap(parts[3], "ctx", 1)).astype(BF16)
            norm_parts_here += [parts[0], near, swap(far, "ctx", 2)]
        normed_pair = (normeds[0], normeds[1])
        triple_sent = triple_grad(ids_sent, normed_pair, d_triples)
        triple_kept = triple_grad(ids, normed_pair, d_triples)
        triple_mine = scatter_rows(triple_kept, triple_sent)
        token_grad, gain_one_grad, bias_one_grad = first_back(
            tokens, d_attended, gain_one, norm_parts_here
        )

        halves = shift_in_grad.reshape(ways, 1, wide // (2 * ways))
        blank = jnp.zeros_like(halves)
        spread = jnp.where(
            core == 0,
            jnp.concatenate([halves, blank], axis=1),
            jnp.concatenate([blank, halves], axis=1),
        )
        early = sum_everywhere(
            jnp.concatenate(
                [
                    gain_two_grad.reshape(ways, shard),
                    bias_two_grad.reshape(ways, shard),
                    shift_out_grad.reshape(ways, shard),
                    spread.reshape(ways, wide // ways),
                ],
                axis=1,
            )
        )
        late = sum_everywhere(
            jnp.concatenate([gain_one_grad.reshape(ways, shard), bias_one_grad.reshape(ways, shard)], axis=1)
        )

        def over_chips(part):
            low = part.astype(BF16)
            return wide_add(low, swap(low, "ctx", 2))

        def both(own, axis):
            other = swap(own, "ctx", 1)
            first = jnp.where(core == 0, own, other)
            second = jnp.where(core == 0, other, own)
            return jnp.stack([first, second], axis=axis)

        shrink_grad = both(over_chips(shrink_mine), 0).reshape(deep, width)
        expand_half = over_chips(expand_mine).reshape(shard, ways, wide // (2 * ways))
        expand_grad = both(expand_half, 2).reshape(shard, wide)
        output_grad_all = both(over_chips(output_mine), 1).reshape(shard, width)
        low = triple_mine.astype(BF16).reshape(shard, 3, width // 4)
        far = swap(low, "ctx", 2)
        pair = jnp.stack([jnp.where(rank < 2, low, far), jnp.where(rank < 2, far, low)], axis=2)
        triple_grad_all = both(pair, 3).reshape(shard, 3 * width).astype(F32)
        early = lax.dynamic_index_in_dim(early, fsdp, 0, keepdims=False)
        late = lax.dynamic_index_in_dim(late, fsdp, 0, keepdims=False)

    return (
        result[:, None],
        token_grad[:, None],
        late[:shard],
        late[shard:],
        triple_grad_all,
        output_grad_all,
        early[:shard],
        early[shard : 2 * shard],
        expand_grad,
        early[3 * shard :],
        shrink_grad,
        early[2 * shard : 3 * shard],
    )


def solution(mesh):
    token_spec = P(None, "fsdp", "ctx", None)
    flat, rows = P("fsdp"), P("fsdp", None)
    return jax.shard_map(
        on_device,
        mesh=mesh,
        in_specs=(
            token_spec,
            token_spec,
            P(None, "fsdp", None, "ctx", None),
            P(None, "fsdp", None),
            flat,
            flat,
            rows,
            rows,
            flat,
            flat,
            rows,
            flat,
            rows,
            flat,
        ),
        out_specs=(
            token_spec,
            token_spec,
            flat,
            flat,
            rows,
            rows,
            flat,
            flat,
            rows,
            flat,
            rows,
            flat,
        ),
        check_vma=False,
    )
```

```python
import functools

import jax
import jax.numpy as jnp
from jax import lax
from jax.experimental import pallas as pl
from jax.experimental.pallas import tpu as pltpu
from jax.sharding import PartitionSpec as P

HEAD_DIM = 64
BLOCK = 64
EPSILON = 1e-05
F32 = jnp.float32
BF16 = jnp.bfloat16
MIB = 1 << 20

VM = pl.BlockSpec(memory_space=pltpu.VMEM)
SM = pl.BlockSpec(memory_space=pltpu.SMEM)
ANY = pl.BlockSpec(memory_space=pl.ANY)

NN = (((1,), (0,)), ((), ()))
NT = (((1,), (1,)), ((), ()))
TN = (((0,), (0,)), ((), ()))


def dot(left, right, dims=NN):
    return lax.dot_general(left, right, dims, preferred_element_type=F32)


def shape(dims, kind):
    return jax.ShapeDtypeStruct(dims, kind)


def params(limit=56):
    return pltpu.CompilerParams(vmem_limit_bytes=limit * MIB)


def cost(flops, moved, special=0):
    return pl.CostEstimate(flops=flops, bytes_accessed=moved, transcendentals=special)


def swap(value, axis, step):
    size = lax.axis_size(axis)
    return lax.ppermute(value, axis, [(i, i ^ step) for i in range(size)])


def place_id():
    return lax.axis_index("fsdp") if lax.axis_size("fsdp") == 8 else jnp.int32(1)


def wide_add(*terms):
    total = terms[0].astype(F32)
    for term in terms[1:]:
        total = total + term.astype(F32)
    return total


def scatter_rows(kept, sent):
    whole = jnp.stack([sent, kept], axis=1)
    whole = whole.reshape((8 * kept.shape[1],) + kept.shape[2:])
    return lax.psum_scatter(whole.astype(F32), "fsdp", scatter_dimension=0, tiled=True)


def sum_everywhere(vector):
    return lax.psum(vector, ("ctx", "fsdp"))


def norm_parts(values):
    average = jnp.mean(values, axis=-1, keepdims=True)
    centered = values - average
    variance = jnp.mean(centered * centered, axis=-1, keepdims=True)
    inverse = lax.rsqrt(variance + EPSILON)
    return centered * inverse, inverse


def norm_back(grad, unit, inverse, gain):
    scaled = grad * gain
    first = jnp.mean(scaled, axis=-1, keepdims=True)
    second = jnp.mean(scaled * unit, axis=-1, keepdims=True)
    return inverse * (scaled - first - unit * second)


def normalize(source, gain, bias):
    unit, _ = norm_parts(source.astype(F32))
    return (unit * gain + bias).astype(BF16)


def project_kernel(t0, t1, t2, t3, gain, bias, weight, triple, normed):
    rows = t0.shape[0]
    for place, part in enumerate((t0, t1, t2, t3)):
        span = slice(place * rows, (place + 1) * rows)
        normed[span, :] = normalize(part[...], gain[...], bias[...])
        triple[span, :] = dot(normed[span, :], weight[...]).astype(BF16)


def project(parts, gain, bias, weight):
    rows, width = parts[0].shape
    columns = weight.shape[1]
    return pl.pallas_call(
        project_kernel,
        name="project",
        out_shape=(shape((4 * rows, columns), BF16), shape((4 * rows, width), BF16)),
        in_specs=[VM] * 7,
        out_specs=(VM, VM),
        compiler_params=params(),
        cost_estimate=cost(8 * rows * width * columns, 12 * rows * width + 2 * width * columns),
    )(*parts, gain, bias, weight)


def head_mask(rows):
    return lax.broadcasted_iota(jnp.int32, (rows, 2 * HEAD_DIM), 1) // HEAD_DIM


def attend_body(triple, block_bias, mixed, lse, between=None):
    length = triple.shape[0]
    width = triple.shape[1] // 3
    rows = length // 4
    blocks = length // BLOCK
    for pair in range(width // 128):
        keys = triple[:, width + pair * 128 : width + pair * 128 + 128]
        values = triple[:, 2 * width + pair * 128 : 2 * width + pair * 128 + 128]
        values_t = values.astype(F32).T.astype(BF16)

        def step(place, carry):
            start = pl.multiple_of(place * rows, rows)
            queries = triple[pl.ds(start, rows), pair * 128 : pair * 128 + 128]
            queries = queries * jnp.asarray(0.125, BF16)
            side = head_mask(rows)
            halves = []
            for which in range(2):
                head = 2 * pair + which
                one = jnp.where(side == which, queries, jnp.zeros_like(queries))
                scores = dot(keys, one, NT)
                shift = block_bias[head, :, pl.ds(start, rows)]
                scores = scores.reshape(blocks, BLOCK, rows) + shift[:, None, :]
                peak = jnp.max(jnp.max(scores, axis=0), axis=0, keepdims=True)
                powered = jnp.exp(scores - peak[None])
                total = jnp.sum(jnp.sum(powered, axis=0), axis=0, keepdims=True)
                lse[head : head + 1, pl.ds(start, rows)] = peak + jnp.log(total)
                low = powered.astype(BF16).reshape(length, rows)
                part = dot(values_t[which * HEAD_DIM : (which + 1) * HEAD_DIM, :], low)
                halves.append(part / total)
            joined = jnp.concatenate(halves, axis=0)
            mixed[place, :, pair * 128 : pair * 128 + 128] = joined.T.astype(BF16)
            return carry

        lax.fori_loop(0, 4, step, 0)
        if between is not None and pair == 0:
            between()


def attend(triple, block_bias):
    length, columns = triple.shape
    width = columns // 3
    heads = width // HEAD_DIM
    rows = length // 4
    return pl.pallas_call(
        attend_body,
        name="attend",
        out_shape=(shape((4, rows, width), BF16), shape((8, length), F32)),
        in_specs=[VM, VM],
        out_specs=(VM, VM),
        compiler_params=params(),
        cost_estimate=cost(
            32 * heads * length * length * HEAD_DIM, 8 * length * width, heads * length * length
        ),
    )(triple, block_bias)


def attend_back_body(
    triple, block_bias, lse, grads, mixed, d_triple, key_total, value_total, between=None
):
    length = triple.shape[0]
    width = triple.shape[1] // 3
    rows = length // 4
    blocks = length // BLOCK
    for pair in range(width // 128):
        lanes = slice(pair * 128, pair * 128 + 128)
        keys = triple[:, width + pair * 128 : width + pair * 128 + 128]
        values = triple[:, 2 * width + pair * 128 : 2 * width + pair * 128 + 128]
        keys_t = keys.astype(F32).T.astype(BF16)
        key_total[...] = jnp.zeros_like(key_total)
        value_total[...] = jnp.zeros_like(value_total)

        def step(place, carry):
            start = pl.multiple_of(place * rows, rows)
            queries = triple[pl.ds(start, rows), lanes] * jnp.asarray(0.125, BF16)
            grad = grads[place, :, lanes]
            product = (grad.astype(F32) * mixed[place, :, lanes].astype(F32)).T
            side = head_mask(rows)
            halves = []
            for which in range(2):
                head = 2 * pair + which
                one = jnp.where(side == which, queries, jnp.zeros_like(queries))
                one_grad = jnp.where(side == which, grad, jnp.zeros_like(grad))
                delta = jnp.sum(
                    product[which * HEAD_DIM : (which + 1) * HEAD_DIM, :], axis=0, keepdims=True
                )
                scores = dot(keys, one, NT)
                shift = block_bias[head, :, pl.ds(start, rows)] - lse[head : head + 1, pl.ds(start, rows)]
                exact = jnp.exp(scores.reshape(blocks, BLOCK, rows) + shift[:, None, :])
                exact = exact.reshape(length, rows)
                value_total[...] += dot(exact.astype(BF16), one_grad)
                d_probs = dot(values, one_grad, NT)
                d_scores = (exact * (d_probs - delta)).astype(BF16)
                key_total[...] += dot(d_scores, one)
                halves.append(dot(keys_t[which * HEAD_DIM : (which + 1) * HEAD_DIM, :], d_scores))
            joined = jnp.concatenate(halves, axis=0) * 0.125
            d_triple[pl.ds(start, rows), lanes] = joined.T.astype(BF16)
            return carry

        lax.fori_loop(0, 4, step, 0)
        d_triple[:, width + pair * 128 : width + pair * 128 + 128] = key_total[...].astype(BF16)
        d_triple[:, 2 * width + pair * 128 : 2 * width + pair * 128 + 128] = value_total[
            ...
        ].astype(BF16)
        if between is not None and pair == 0:
            between()


def attend_back_kernel(triple, block_bias, lse, g0, g1, g2, g3, mixed, weight, d_triple, norm_grad, grads, key_total, value_total):
    rows = g0.shape[0]
    for place, part in enumerate((g0, g1, g2, g3)):
        grads[place] = part[...]
    attend_back_body(triple, block_bias, lse, grads, mixed, d_triple, key_total, value_total)
    for place in range(4):
        part = dot(d_triple[place * rows : (place + 1) * rows, :], weight[...], NT)
        norm_grad[place] = part.astype(BF16)


def attend_back(triple, block_bias, lse, grads, mixed, weight):
    length, columns = triple.shape
    width = columns // 3
    heads = width // HEAD_DIM
    rows = length // 4
    return pl.pallas_call(
        attend_back_kernel,
        name="attend_back",
        out_shape=(shape((length, columns), BF16), shape((4, rows, weight.shape[0]), BF16)),
        in_specs=[VM] * 9,
        out_specs=(VM,) * 2,
        scratch_shapes=[
            pltpu.VMEM((4, rows, width), BF16),
            pltpu.VMEM((length, 128), F32),
            pltpu.VMEM((length, 128), F32),
        ],
        compiler_params=params(),
        cost_estimate=cost(
            80 * heads * length * length * HEAD_DIM, 16 * length * width, heads * length * length
        ),
    )(triple, block_bias, lse, *grads, mixed, weight)


def output_kernel(tokens, joined, gain, bias, weight, attended, normed):
    rows = tokens.shape[1]
    for micro in range(2):
        span = slice(micro * rows, (micro + 1) * rows)
        value = tokens[micro].astype(F32) + dot(joined[span, :], weight[...])
        attended[span, :] = value
        normed[span, :] = normalize(value, gain[...], bias[...])


def output_project(tokens, joined, gain, bias, weight):
    micro, rows, width = tokens.shape
    total = micro * rows
    return pl.pallas_call(
        output_kernel,
        name="output_project",
        out_shape=(shape((total, width), F32), shape((total, width), BF16)),
        in_specs=[VM] * 5,
        out_specs=(VM, VM),
        compiler_params=params(),
        cost_estimate=cost(2 * total * width * width, 12 * total * width + 2 * width * width),
    )(tokens, joined, gain, bias, weight)


CURVE = 0.7978845608028654
CUBIC = 0.044715


def feed_kernel(ids, h0, h1, c0, c1, shift, *rest):
    expand_held, shrink_held = rest[:2]
    own_out, other_out, own_hidden, other_hidden, bias_grad = rest[2:7]
    shrink_sent, shrink_kept, expand_sent, expand_kept = rest[7:11]
    hidden, tangent, hidden_t, out_total, hidden_total = rest[11:]
    base = ids[0]
    rows, width = h0.shape
    tile = shrink_held.shape[0] // 8
    deep = width // 8
    hidden[:rows, :] = h0[...]
    hidden[rows:, :] = h1[...]
    tangent[:rows, :] = c0[...]
    tangent[rows:, :] = c1[...]
    for j in range(8):
        source = pl.multiple_of((base ^ j) * deep, deep)
        hidden_t[j * deep : (j + 1) * deep, :] = (
            hidden[:, pl.ds(source, deep)].astype(F32).T.astype(BF16)
        )
    for step, j in enumerate((1, 3, 5, 7, 0, 2, 4, 6)):
        column = pl.multiple_of((base ^ j) * tile, tile)
        up = expand_held[:, pl.ds(column, tile)]
        down = shrink_held[pl.ds(column, tile), :]
        before = dot(hidden[...], up) + shift[:, pl.ds(column, tile)]
        d_active = dot(tangent[...], down, NT)
        square = before * before
        bend = jnp.tanh(CURVE * before * (1.0 + CUBIC * square))
        plus = 0.5 * (1.0 + bend)
        active = (before * plus).astype(BF16)
        slope = plus + (0.5 * CURVE) * before * (1.0 - bend * bend) * (1.0 + 3 * CUBIC * square)
        d_before = (d_active * slope).astype(BF16)
        bias_grad[:, pl.ds(column, tile)] = jnp.sum(d_before.astype(F32), axis=0, keepdims=True)
        out_part = dot(active, down)
        hidden_part = dot(d_before, up, NT)
        if step == 0:
            out_total[...] = out_part
            hidden_total[...] = hidden_part
        else:
            out_total[...] += out_part
            hidden_total[...] += hidden_part
        shrink_part = dot(active, tangent[...], TN).astype(BF16)
        (shrink_sent if j % 2 else shrink_kept)[j // 2] = shrink_part
        expand_part = dot(hidden_t[...], d_before).astype(BF16)
        for place in range(8):
            target = expand_sent if place % 2 else expand_kept
            target[place // 2, :, pl.ds(column, tile)] = expand_part[
                place * deep : (place + 1) * deep, :
            ]
    own_out[...] = out_total[:rows, :]
    other_out[...] = out_total[rows:, :].astype(BF16)
    own_hidden[...] = hidden_total[:rows, :]
    other_hidden[...] = hidden_total[rows:, :].astype(BF16)


def feed(ids, hidden, tangent, shift, expand, shrink):
    rows, width = hidden[0].shape
    wide = expand.shape[1]
    deep, tile = width // 8, wide // 8
    return pl.pallas_call(
        feed_kernel,
        name="feed",
        out_shape=(
            shape((rows, width), F32),
            shape((rows, width), BF16),
            shape((rows, width), F32),
            shape((rows, width), BF16),
            shape((1, wide), F32),
            shape((4, tile, width), BF16),
            shape((4, tile, width), BF16),
            shape((4, deep, wide), BF16),
            shape((4, deep, wide), BF16),
        ),
        in_specs=[SM] + [VM] * 7,
        out_specs=(VM,) * 9,
        scratch_shapes=[
            pltpu.VMEM((2 * rows, width), BF16),
            pltpu.VMEM((2 * rows, width), BF16),
            pltpu.VMEM((width, 2 * rows), BF16),
            pltpu.VMEM((2 * rows, width), F32),
            pltpu.VMEM((2 * rows, width), F32),
        ],
        compiler_params=params(60),
        cost_estimate=cost(24 * rows * width * wide, 8 * width * wide + 20 * rows * width, 2 * rows * wide),
    )(ids, *hidden, *tangent, shift, expand, shrink)


def branch_kernel(
    ids, attended, own_hidden, came_hidden, tangent, own_out, came_out, gain, shift, weight, *rest
):
    result, d_attended, d_branch = rest[:3]
    grads, (gain_grad, bias_grad, shift_grad) = rest[3:11], rest[11:14]
    rows = tangent.shape[1]
    width = gain.shape[1] // 4
    gain_total = bias_total = shift_total = 0.0
    for micro in range(2):
        span = slice(micro * rows, (micro + 1) * rows)
        value = attended[span, :]
        cot = tangent[micro].astype(F32)
        branch = own_out[span, :] + came_out[span, :].astype(F32) + shift[...]
        result[micro] = (value + branch).astype(BF16)
        unit, inverse = norm_parts(value)
        grad = own_hidden[span, :] + came_hidden[span, :].astype(F32)
        gain_total = gain_total + jnp.sum(grad * unit, axis=0, keepdims=True)
        bias_total = bias_total + jnp.sum(grad, axis=0, keepdims=True)
        shift_total = shift_total + jnp.sum(cot, axis=0, keepdims=True)
        total = cot + norm_back(grad, unit, inverse, gain[...])
        d_attended[span, :] = total
        d_branch[span, :] = total.astype(BF16)
    gain_grad[...] = gain_total
    bias_grad[...] = bias_total
    shift_grad[...] = shift_total
    for micro in range(2):
        for place in range(4):
            start = pl.multiple_of((ids[1] ^ place) * width, width)
            part = dot(d_branch[micro * rows : (micro + 1) * rows, :], weight[pl.ds(start, width), :], NT)
            grads[4 * micro + place][...] = part.astype(BF16)


def branch_back(ids, attended, own_hidden, came_hidden, tangent, own_out, came_out, gain, shift, weight):
    micro, rows, width = tangent.shape
    total = micro * rows
    row = shape((1, width), F32)
    return pl.pallas_call(
        branch_kernel,
        name="branch_back",
        out_shape=(
            shape(tangent.shape, BF16),
            shape((total, width), F32),
            shape((total, width), BF16),
        )
        + tuple(shape((rows, width // 4), BF16) for _ in range(8))
        + (row, row, row),
        in_specs=[SM] + [VM] * 9,
        out_specs=(VM,) * 14,
        compiler_params=params(),
        cost_estimate=cost(2 * total * width * width, 32 * total * width),
    )(ids, attended, own_hidden, came_hidden, tangent, own_out, came_out, gain, shift, weight)


def output_grad_kernel(ids, own_mixed, other_mixed, own_branch, other_branch, out):
    rows = out.shape[1]
    width = own_branch.shape[1]
    half = width // 2
    column = pl.multiple_of(ids[2] * half, half)
    right = own_branch[:, pl.ds(column, half)]
    for k in range(4):
        start = pl.multiple_of((ids[0] ^ (2 * k + ids[3])) * rows, rows)
        part = dot(own_mixed[:, pl.ds(start, rows)], right, TN)
        part += dot(other_mixed[:, pl.ds(start, rows)], other_branch[...], TN)
        out[k] = part.astype(BF16)


def output_grad(ids, own_mixed, other_mixed, own_branch, other_branch):
    total, width = own_mixed.shape
    return pl.pallas_call(
        output_grad_kernel,
        name="output_grad",
        out_shape=shape((4, width // 8, width // 2), BF16),
        in_specs=[SM] + [VM] * 4,
        out_specs=VM,
        compiler_params=params(),
        cost_estimate=cost(total * width * width, 8 * total * width),
    )(ids, own_mixed, other_mixed, own_branch, other_branch)


def triple_grad_kernel(ids, n0, n1, d0, d1, out):
    rows = out.shape[1]
    for k in range(4):
        column = pl.multiple_of((ids[0] ^ (2 * k + ids[3])) * rows, rows)
        part = dot(n0[:, pl.ds(column, rows)], d0[...], TN)
        part += dot(n1[:, pl.ds(column, rows)], d1[...], TN)
        out[k] = part.astype(BF16)


def triple_grad(ids, normed, grads):
    length, width = normed[0].shape
    columns = grads[0].shape[1]
    return pl.pallas_call(
        triple_grad_kernel,
        name="triple_grad",
        out_shape=shape((4, width // 8, columns), BF16),
        in_specs=[SM] + [VM] * 4,
        out_specs=VM,
        compiler_params=params(),
        cost_estimate=cost(2 * length * width * columns, 4 * length * (width + columns)),
    )(ids, *normed, *grads)


def first_back_kernel(tokens, d_attended, gain, *rest):
    parts, (grad_out, gain_grad, bias_grad) = rest[:6], rest[6:]
    rows = tokens.shape[1]
    gain_total = bias_total = 0.0
    for micro in range(2):
        one, two, three = parts[3 * micro : 3 * micro + 3]
        grad = one[...].astype(F32) + two[...].astype(F32) + three[...].astype(F32)
        unit, inverse = norm_parts(tokens[micro].astype(F32))
        gain_total = gain_total + jnp.sum(grad * unit, axis=0, keepdims=True)
        bias_total = bias_total + jnp.sum(grad, axis=0, keepdims=True)
        total = d_attended[micro * rows : (micro + 1) * rows, :]
        grad_out[micro] = (total + norm_back(grad, unit, inverse, gain[...])).astype(BF16)
    gain_grad[...] = gain_total
    bias_grad[...] = bias_total


def first_back(tokens, d_attended, gain, parts):
    micro, rows, width = tokens.shape
    row = shape((1, width), F32)
    return pl.pallas_call(
        first_back_kernel,
        name="first_back",
        out_shape=(shape(tokens.shape, BF16), row, row),
        in_specs=[VM] * 9,
        out_specs=(VM,) * 3,
        compiler_params=params(),
        cost_estimate=cost(20 * micro * rows * width, 16 * micro * rows * width),
    )(tokens, d_attended, gain, *parts)


def flip(index, bits):
    out, bit = index, 1
    while bit <= bits:
        if bits & bit:
            out = out + bit * (1 - 2 * lax.rem(lax.div(index, jnp.int32(bit)), jnp.int32(2)))
        bit *= 2
    return out


class Moves:
    def __init__(self, send, recv):
        self.send, self.recv, self.started, self.freed = send, recv, [], []
        self.place = {"ctx": lax.axis_index("ctx"), "fsdp": lax.axis_index("fsdp")}

    def greet(self):
        barrier = pltpu.get_barrier_semaphore()
        partners = [("ctx", 1), ("ctx", 2), ("ctx", 3), ("fsdp", 1), ("fsdp", 2), ("fsdp", 4), ("fsdp", 6)]
        for axis, bits in partners:
            pl.semaphore_signal(
                barrier,
                inc=1,
                device_id={axis: flip(self.place[axis], bits)},
                device_id_type=pl.DeviceIdType.MESH,
            )
        pl.semaphore_wait(barrier, len(partners))

    def go(self, source, target, axis, bits):
        slot = len(self.started)
        move = pltpu.make_async_remote_copy(
            src_ref=source,
            dst_ref=target,
            send_sem=self.send.at[slot],
            recv_sem=self.recv.at[slot],
            device_id={axis: flip(self.place[axis], bits)},
            device_id_type=pl.DeviceIdType.MESH,
        )
        move.start()
        self.started.append(move)
        return move

    def sent(self, move):
        move.wait_send()
        self.freed.append(move)

    def close(self):
        for move in self.started:
            if not any(move is other for other in self.freed):
                move.wait_send()


class Gather:
    def __init__(self, moves, part, view, own, shared=False):
        self.moves, self.view, self.own, self.shared = moves, view, own, shared
        self.part = part

    def start(self):
        moves, part, view, me = self.moves, self.part, self.view, self.moves.place["fsdp"]
        self.distant = moves.go(part, view(me), "fsdp", 4)
        self.adjacent = moves.go(part, view(me), "fsdp", 2)
        self.across = [moves.go(part, view(me), "fsdp", 1)]
        self.sources = [1]
        self.over = [moves.go(part, view(me), "ctx", 2)] if self.shared else []
        return self

    def over_x(self, bits):
        if self.shared:
            block = self.view(flip(self.moves.place["fsdp"], bits))
            self.over.append(self.moves.go(block, block, "ctx", 2))

    def over_y(self, bits):
        block = self.view(flip(self.moves.place["fsdp"], bits))
        self.across.append(self.moves.go(block, block, "fsdp", 1))
        self.sources.append(bits + 1)
        self.over_x(bits)

    def forward(self):
        self.distant.wait_recv()
        block = self.view(flip(self.moves.place["fsdp"], 4))
        self.last = self.moves.go(block, block, "fsdp", 2)
        self.over_y(4)
        self.adjacent.wait_recv()
        self.over_y(2)

    def third(self):
        self.last.wait_recv()
        self.over_y(6)

    def second(self):
        for bits, move in zip(self.sources, self.across):
            move.wait_recv()
            self.over_x(bits)

    def finish(self):
        if not self.shared:
            self.second()
        for move in self.over:
            move.wait_recv()
        for copy in self.own:
            copy.wait()


FORWARD_MOVES = 106


def row_view(ref, rows, columns=slice(None)):
    return lambda index: ref.at[pl.ds(pl.multiple_of(index * rows, rows), rows), columns]


def forward_kernel(
    global_ids,
    tokens,
    small,
    picks,
    triple_weight,
    output_weight,
    expand_weight,
    shrink_weight,
    tangent,
    vectors_out,
    shift_in_out,
    triple_out,
    output_out,
    expand_all,
    shrink_all,
    tangent_other,
    triple,
    normed,
    block_bias,
    lse,
    mixed,
    joined_out,
    mixed_other,
    attended,
    hidden,
    hidden_other,
    parts,
    small_held,
    picks_held,
    triple_held,
    output_held,
    joined,
    hidden_held,
    send,
    recv,
    local,
):
    moves = Moves(send, recv)
    rank, me = moves.place["ctx"], moves.place["fsdp"]
    core = lax.rem(rank, jnp.int32(2))
    micro, rows, width = tokens.shape
    half = width // 2
    quarter = width // 4
    shard = triple_weight.shape[0]
    wide = expand_all.shape[1] // 2
    deep = shrink_weight.shape[0] // 8
    chip = lax.div(rank, jnp.int32(2))
    locals_used = []

    def copy_here(source, target):
        copy = pltpu.make_async_copy(source, target, local.at[len(locals_used)])
        copy.start()
        locals_used.append(copy)
        return copy

    def at(start, size, unit=128):
        return pl.ds(pl.multiple_of(start, unit), size)

    mine = at(me * shard, shard)
    triple_own = [
        copy_here(
            triple_weight.at[:, at(k * width + rank * quarter, quarter)],
            triple_held.at[mine, k * quarter : (k + 1) * quarter],
        )
        for k in range(3)
    ]
    tile = wide // 4
    expand_views = [row_view(expand_all, shard, at(chip * wide + cut * (wide // 2), wide // 2)) for cut in range(2)]
    expand_own = [
        copy_here(
            expand_weight.at[:, at(((4 * chip + q) * 2 + core) * tile, tile)],
            expand_all.at[mine, at(chip * wide + q * tile, tile)],
        )
        for q in range(4)
    ]
    output_columns = at(core * half + chip * quarter, quarter)
    output_view = row_view(output_held, shard, output_columns)
    shrink_views = [
        lambda i, cut=cut: shrink_all.at[at(i * 4 * deep + cut * deep, deep, 64)] for cut in range(4)
    ]
    shrink_parts = [shrink_weight.at[at((core * 4 + cut) * deep, deep, 64)] for cut in range(4)]
    small_own = copy_here(small, small_held.at[me])
    output_own = copy_here(output_weight.at[:, output_columns], output_view(me))
    shrink_own = [copy_here(shrink_parts[cut], shrink_views[cut](me)) for cut in range(4)]
    moves.greet()

    small_gather = Gather(moves, small, lambda index: small_held.at[index], [small_own]).start()
    far = [moves.go(tokens.at[0], parts.at[0, 2], "ctx", 2)]
    near = [moves.go(tokens.at[0], parts.at[0, 1], "ctx", 1)]
    for copy in triple_own:
        copy.wait()
    triple_view = row_view(triple_held, shard)
    triple_gather = Gather(moves, triple_view(me), triple_view, []).start()
    picked = [moves.go(picks.at[flip(rank, p)], picks_held.at[p], "ctx", p) for p in range(1, 4)]
    near.append(moves.go(tokens.at[1], parts.at[1, 1], "ctx", 1))
    far.append(moves.go(tokens.at[1], parts.at[1, 2], "ctx", 2))
    output_gather = Gather(moves, output_weight.at[:, output_columns], output_view, [output_own], True)
    for copy in expand_own:
        copy.wait()
    expands = [Gather(moves, view(me), view, [], True) for view in expand_views]
    shrinks = [Gather(moves, shrink_parts[cut], shrink_views[cut], [shrink_own[cut]]) for cut in range(4)]
    small_gather.forward()
    triple_gather.forward()
    output_gather.start()
    expands[0].start()
    small_gather.third()
    triple_gather.third()
    expands[1].start()
    tangent_move = moves.go(tangent, tangent_other, "ctx", 1)

    for move in picked:
        move.wait_recv()
    count = block_bias.shape[2]
    each = count // 4
    ranks = [flip(rank, p) if p else rank for p in range(4)]
    key_row = lax.broadcasted_iota(jnp.int32, (count, rows), 0)
    key_place = key_row // each
    key_rank = ranks[0]
    for p in range(1, 4):
        key_rank = jnp.where(key_place == p, ranks[p], key_rank)
    key_block = key_rank * each + key_row % each
    lane = lax.broadcasted_iota(jnp.int32, (count, rows), 1) // BLOCK
    for step in range(micro):
        first, second = global_ids[step, 0], global_ids[step, 1]
        key_global = (key_block == first) | (key_block == second)
        for p in range(4):
            source = picks.at[rank] if p == 0 else picks_held.at[p]
            query_block = ranks[p] * each + lane
            base = key_global | (jnp.abs(query_block - key_block) <= 1)
            base = base | (query_block == first) | (query_block == second)
            for head in range(block_bias.shape[1]):
                hit = base
                for pick in range(3):
                    hit = hit | (source[step, head, pick : pick + 1, :] == key_block)
                block_bias[step, head, :, p * rows : (p + 1) * rows] = jnp.where(hit, 0.0, -1e30)

    small_gather.finish()
    def vector(line):
        return jnp.concatenate([small_held[b, line : line + 1, :] for b in range(8)], axis=1)

    gain_one, bias_one, gain_two, bias_two, shift_out = (vector(line) for line in range(5))
    vectors_out[...] = jnp.zeros_like(vectors_out)
    for line, value in enumerate((gain_two, gain_one, shift_out)):
        vectors_out[line : line + 1, :] = value
    lines = shift_in_out.shape[1] // 8 // 128
    for b in range(8):
        for i in range(lines):
            lanes = slice((b * lines + i) * 128, (b * lines + i + 1) * 128)
            shift_in_out[:, lanes] = small_held[b, pl.ds(5 + core * lines + i, 1), :]

    for step in range(micro):
        far[step].wait_recv()
        near.append(moves.go(parts.at[step, 2], parts.at[step, 3], "ctx", 1))
    mixed_moves = []
    for step in range(micro):
        near[step].wait_recv()
        near[2 + step].wait_recv()
        for p in range(4):
            source = tokens[step] if p == 0 else parts[step, p]
            normed[step, p * rows : (p + 1) * rows, :] = normalize(source, gain_one, bias_one)
        if step == 0:
            output_gather.forward()
            expands[0].forward()
            shrinks[0].start()
            triple_gather.finish()
        for p in range(4):
            span = slice(p * rows, (p + 1) * rows)
            triple[step, span, :] = dot(normed[step, span, :], triple_held[...]).astype(BF16)

        def between_first():
            expands[0].third()
            shrinks[0].forward()
            shrinks[2].start()
            output_gather.second()

        def between_second():
            expands[1].second()
            shrinks[3].forward()
            shrinks[2].third()

        if step == 0:
            output_gather.third()
            expands[1].forward()
            shrinks[1].start()
        else:
            output_gather.finish()
            piece = output_held.at[:, at(core * half, half)]
            output_move = moves.go(piece, piece, "ctx", 1)
            shrinks[2].forward()
            shrinks[1].third()
        attend_body(
            triple.at[step],
            block_bias.at[step],
            mixed.at[step],
            lse.at[step],
            between_second if step else between_first,
        )
        own = pl.ds(pl.multiple_of(rank * quarter, quarter), quarter)
        span = slice(step * rows, (step + 1) * rows)
        joined[span, own] = mixed[step, 0]
        for p in range(1, 4):
            mixed_moves.append(moves.go(mixed.at[step, p], joined.at[span, own], "ctx", p))
        if step == 0:
            expands[1].third()
            shrinks[1].forward()
            shrinks[3].start()
            shrinks[0].third()
            expands[0].second()
        else:
            shrinks[3].third()
    output_move.wait_recv()
    for move in mixed_moves:
        move.wait_recv()
    keep = [copy_here(triple_held, triple_out), copy_here(output_held, output_out)]
    output_kernel(tokens, joined, gain_two, bias_two, output_held, attended, hidden_held)
    last = [
        moves.go(hidden_held, hidden_other, "ctx", 1),
        moves.go(joined, mixed_other, "ctx", 1),
    ]
    hidden[...] = hidden_held[...]
    joined_out[...] = joined[...]
    for gather in shrinks + expands:
        gather.finish()
    for move in [tangent_move] + last:
        move.wait_recv()
    for copy in keep:
        copy.wait()
    moves.close()


def forward_together(global_ids, tokens, small, picks, triple_weight, output_weight, expand_weight, shrink_weight, tangent):
    micro, rows, width = tokens.shape
    total = micro * rows
    columns = triple_weight.shape[1] // 4
    wide = expand_weight.shape[1] // 2
    length = 4 * rows
    heads = picks.shape[2]
    outs = (
        (VM, (8, width), F32),
        (VM, (1, wide), F32),
        (ANY, (width, columns), BF16),
        (ANY, (width, width), BF16),
        (ANY, (width, wide), BF16),
        (ANY, (wide, width), BF16),
        (ANY, (total, width), BF16),
        (VM, (micro, length, columns), BF16),
        (VM, (micro, length, width), BF16),
        (VM, (micro, heads, length // BLOCK, length), F32),
        (VM, (micro, 8, length), F32),
        (VM, (micro, 4, rows, width // 4), BF16),
        (VM, (total, width), BF16),
        (ANY, (total, width), BF16),
        (VM, (total, width), F32),
        (VM, (total, width), BF16),
        (ANY, (total, width), BF16),
    )
    return pl.pallas_call(
        forward_kernel,
        name="forward_together",
        out_shape=tuple(shape(dims, kind) for _, dims, kind in outs),
        in_specs=[SM] + [VM] * 3 + [ANY] * 5,
        out_specs=tuple(spec for spec, _, _ in outs),
        scratch_shapes=[
            pltpu.VMEM((micro, 4, rows, width), BF16),
            pltpu.VMEM((8,) + small.shape, F32),
            pltpu.VMEM(picks.shape, jnp.int32),
            pltpu.VMEM((width, columns), BF16),
            pltpu.VMEM((width, width), BF16),
            pltpu.VMEM((total, width), BF16),
            pltpu.VMEM((total, width), BF16),
            pltpu.SemaphoreType.DMA((FORWARD_MOVES,)),
            pltpu.SemaphoreType.DMA((FORWARD_MOVES,)),
            pltpu.SemaphoreType.DMA((15,)),
        ],
        compiler_params=pltpu.CompilerParams(
            collective_id=0, has_side_effects=True, vmem_limit_bytes=56 * MIB
        ),
        cost_estimate=cost(16 * total * width * width, 64 * MIB),
    )(global_ids, tokens, small, picks, triple_weight, output_weight, expand_weight, shrink_weight, tangent)


class Reduce:
    def __init__(self, moves, sent, came, line):
        self.moves, self.came, self.line = moves, came, line
        self.across = moves.go(sent, came, "fsdp", 1)

    def forward(self, *kept):
        self.across.wait_recv()
        for k in (1, 3, 0, 2):
            self.came[k] = wide_add(self.came[k], *(part[k] for part in kept)).astype(self.came.dtype)
        self.along = [self.moves.go(self.came.at[2 * i + 1], self.line.at[i], "fsdp", 2) for i in range(2)]

    def third(self):
        for move in self.along:
            move.wait_recv()
        self.came[2] = wide_add(self.came[2], self.line[1]).astype(self.came.dtype)
        self.last = self.moves.go(self.came.at[2], self.line.at[2], "fsdp", 4)

    def finish(self):
        self.last.wait_recv()
        return wide_add(self.came[0], self.line[0], self.line[2])


class ReduceAlong:
    def __init__(self, moves, kept, sent, ends, came, line):
        self.moves, self.ends, self.came, self.line = moves, ends, came, line
        sources = (kept.at[1], kept.at[3], sent.at[1], sent.at[3])
        self.along = [moves.go(source, came.at[i], "fsdp", 2) for i, source in enumerate(sources)]

    def forward(self):
        for i in (1, 3, 0, 2):
            self.along[i].wait_recv()
            self.ends[i] = wide_add(self.ends[i], self.came[i]).astype(BF16)
        self.next = [self.moves.go(self.ends.at[2 * i + 1], self.line.at[i], "fsdp", 4) for i in range(2)]

    def third(self):
        for move in self.next:
            move.wait_recv()
        self.ends[2] = wide_add(self.ends[2], self.line[1]).astype(BF16)
        self.last = self.moves.go(self.ends.at[2], self.line.at[2], "fsdp", 1)

    def finish(self):
        self.last.wait_recv()
        return wide_add(self.ends[0], self.line[0], self.line[2])


BACKWARD_MOVES = 96


def backward_kernel(
    vectors,
    tangent,
    output_weight,
    triple_weight,
    triples,
    biases,
    lses,
    mixed_own,
    shift_in_grad,
    own_hidden,
    other_hidden,
    own_out,
    other_out,
    attended,
    tokens,
    mixed_all,
    mixed_other,
    normeds,
    shrink_sent,
    shrink_kept,
    expand_sent,
    expand_kept,
    result,
    token_grad,
    shrink_out,
    expand_out,
    output_out,
    triple_out,
    early_out,
    late_out,
    came_out,
    came_hidden,
    d_attended,
    stage,
    held,
    d_branch,
    branch_other,
    d_mixed,
    grads,
    d_triples,
    key_total,
    value_total,
    near_parts,
    own_parts,
    near_came,
    far_sent,
    far_came,
    shrink_held,
    shrink_came,
    shrink_line,
    along_ends,
    along_came,
    along_line,
    expand_own,
    over_came,
    expand_came,
    expand_line,
    output_sent,
    output_mine,
    output_came,
    output_line,
    first_sent,
    first_mine,
    first_came,
    first_line,
    second_sent,
    second_mine,
    second_came,
    second_line,
    chip_sent,
    chip_came,
    chip_final,
    output_chip,
    expand_final,
    first_final,
    second_final,
    small_all,
    small_sent,
    small_kept,
    small_came,
    small_line,
    small_chip,
    small_chip_came,
    small_core,
    small_core_came,
    send,
    recv,
    local,
):
    moves = Moves(send, recv)
    rank, me = moves.place["ctx"], moves.place["fsdp"]
    core = lax.rem(rank, jnp.int32(2))
    micro, rows, width = tangent.shape
    half, quarter, shard = width // 2, width // 4, width // 8
    moves.greet()
    used = []

    def load(source, target):
        copy = pltpu.make_async_copy(source, target, local.at[len(used)])
        copy.start()
        used.append(copy)
        return copy

    def at(start, size, unit=128):
        return pl.ds(pl.multiple_of(start, unit), size)

    chip = lax.div(rank, jnp.int32(2))
    deep = shrink_sent.shape[1] // 4
    wide = expand_sent.shape[2] // 4
    hidden_move = moves.go(other_hidden, came_hidden, "ctx", 1)

    def rows_of(ref, i):
        return ref.at[:, i * deep : (i + 1) * deep, :]

    def there(ref, e):
        return ref.at[:, :, at((1 - chip) * 2 * wide + e * wide, wide)]

    shrinks = [Reduce(moves, rows_of(shrink_sent, i), shrink_came.at[i], shrink_line.at[i]) for i in range(3)]
    last_kept, last_sent = rows_of(shrink_kept, 3), rows_of(shrink_sent, 3)
    shrinks.append(ReduceAlong(moves, last_kept, last_sent, along_ends, along_came, along_line))
    over_moves = [moves.go(there(expand_sent, 0), over_came.at[0, 0], "ctx", 2)]
    loads = [load(own_hidden, d_attended), load(attended, stage)]
    out_move = moves.go(other_out, came_out, "ctx", 1)
    here = at(chip * 2 * wide, 2 * wide)
    expand_loads = [
        load(expand_sent.at[:, :, here], expand_own.at[0]),
        load(expand_kept.at[:, :, here], expand_own.at[1]),
    ]
    shrink_loads = [load(rows_of(shrink_kept, i), shrink_held.at[i]) for i in range(3)]
    along_loads = [
        load(source.at[2 * k], along_ends.at[2 * i + k])
        for i, source in enumerate((last_kept, last_sent))
        for k in range(2)
    ]
    mixed_loads = [load(mixed_all, held.at[0, : 2 * rows, :]), load(mixed_other, held.at[0, 2 * rows :, :])]

    gain_two, gain_one, shift_out = vectors[0:1, :], vectors[1:2, :], vectors[2:3, :]
    for copy in loads:
        copy.wait()
    hidden_move.wait_recv()
    gain_total = bias_total = shift_total = 0.0
    for step in range(micro):
        span = slice(step * rows, (step + 1) * rows)
        cot = tangent[step].astype(F32)
        unit, inverse = norm_parts(stage[span, :])
        grad = d_attended[span, :] + came_hidden[span, :].astype(F32)
        gain_total = gain_total + jnp.sum(grad * unit, axis=0, keepdims=True)
        bias_total = bias_total + jnp.sum(grad, axis=0, keepdims=True)
        shift_total = shift_total + jnp.sum(cot, axis=0, keepdims=True)
        total = cot + norm_back(grad, unit, inverse, gain_two)
        d_attended[span, :] = total
        d_branch[span, :] = total.astype(BF16)
    theirs = d_branch.at[:, pl.ds(pl.multiple_of((1 - core) * half, half), half)]
    branch_move = moves.go(theirs, branch_other, "ctx", 1)
    grad_moves = []
    for step in range(micro):
        for p in (2, 3, 1, 0):
            start = pl.multiple_of((flip(rank, p) if p else rank) * quarter, quarter)
            part = dot(d_branch[step * rows : (step + 1) * rows, :], output_weight[pl.ds(start, quarter), :], NT)
            if p:
                d_mixed[step, p] = part.astype(BF16)
                grad_moves.append(moves.go(d_mixed.at[step, p], grads.at[step, p], "ctx", p))
            else:
                grads[step, 0] = part.astype(BF16)

    over_moves.append(moves.go(there(expand_sent, 1), over_came.at[0, 1], "ctx", 2))
    over_moves += [moves.go(there(expand_kept, e), over_came.at[1, e], "ctx", 2) for e in range(2)]

    def small_row(which, line, vector):
        for b in range(8):
            small_all[which, b, line : line + 1, :] = vector[:, b * shard : (b + 1) * shard]

    def small_begin(which):
        for k in range(4):
            small_sent[which, k] = small_all[which, flip(me, 2 * k + 1)]
            small_kept[which, k] = small_all[which, flip(me, 2 * k) if k else me]
        return Reduce(moves, small_sent.at[which], small_came.at[which], small_line.at[which])

    def small_chips(which):
        small_chip[which] = smalls[which].finish()
        return moves.go(small_chip.at[which], small_chip_came.at[which], "ctx", 2)

    def small_cores(which, move):
        move.wait_recv()
        small_core[which] = small_chip[which] + small_chip_came[which]
        return moves.go(small_core.at[which], small_core_came.at[which], "ctx", 1)

    def small_end(which, move, out):
        move.wait_recv()
        out[...] = small_core[which] + small_core_came[which]

    small_all[...] = jnp.zeros_like(small_all)
    for line, vector in enumerate((gain_total, bias_total, shift_total)):
        small_row(0, line, vector)
    unit_lines = shift_in_grad.shape[1] // 8 // 128
    for b in range(8):
        for line in range(unit_lines):
            lanes = slice((b * unit_lines + line) * 128, (b * unit_lines + line + 1) * 128)
            small_all[0, b, pl.ds(3 + core * unit_lines + line, 1), :] = shift_in_grad[:, lanes]
    smalls = [small_begin(0)]
    for copy in shrink_loads + along_loads + expand_loads:
        copy.wait()

    def expand_columns(which, e):
        return expand_own.at[which, :, :, e * wide : (e + 1) * wide]

    def expand_begin(e):
        over_moves[e].wait_recv()
        part = expand_columns(0, e)
        for k in range(4):
            part[k] = wide_add(part[k], over_came[0, e, k]).astype(BF16)
        return Reduce(moves, part, expand_came.at[e], expand_line.at[e])

    def expand_forward(e):
        over_moves[2 + e].wait_recv()
        expands[e].forward(expand_columns(1, e), over_came.at[1, e])

    shrinks[0].forward(shrink_held.at[0])
    expands = [expand_begin(0)]

    for copy in mixed_loads:
        copy.wait()
    branch_move.wait_recv()
    mine = pl.ds(pl.multiple_of(core * half, half), half)

    def output_part(index):
        lanes = pl.ds(pl.multiple_of(index * shard, shard), shard)
        part = dot(held[0, : 2 * rows, lanes], d_branch[:, mine], TN)
        return part + dot(held[0, 2 * rows :, lanes], branch_other[...], TN)

    for k in range(4):
        output_sent[k] = output_part(flip(me, 2 * k + 1)).astype(BF16)
    output_reduce = Reduce(moves, output_sent, output_came, output_line)
    for k in range(4):
        output_mine[k] = output_part(flip(me, 2 * k) if k else me).astype(BF16)
    normed_loads = [load(normeds.at[step], held.at[step]) for step in range(1, micro)]

    norm_moves, far_moves = [], []

    def attention(step, between):
        for move in grad_moves[3 * step : 3 * step + 3]:
            move.wait_recv()
        attend_back_body(
            triples.at[step],
            biases.at[step],
            lses.at[step],
            grads.at[step],
            mixed_own.at[step],
            d_triples.at[step],
            key_total,
            value_total,
            between,
        )
        for p in (3, 1, 2, 0):
            span = slice(p * rows, (p + 1) * rows)
            part = dot(d_triples[step, span, :], triple_weight[...], NT).astype(BF16)
            if p:
                near_parts[step, p - 1] = part
            else:
                own_parts[step] = part
            if p % 2:
                norm_moves.append(moves.go(near_parts.at[step, p - 1], near_came.at[step, p // 2], "ctx", 1))

    def far_part(step):
        norm_moves[2 * step].wait_recv()
        far_sent[step] = wide_add(near_parts[step, 1], near_came[step, 1]).astype(BF16)
        far_moves.append(moves.go(far_sent.at[step], far_came.at[step], "ctx", 2))

    def between_first():
        expands.append(expand_begin(1))
        shrinks[1].third()
        shrinks[3].third()

    def between_second():
        shrinks[2].third()
        smalls[0].third()
        expand_forward(0)

    shrinks[3].forward()
    shrinks[1].forward(shrink_held.at[1])
    shrinks[0].third()
    attention(0, between_first)
    shrinks[2].forward(shrink_held.at[2])
    smalls[0].forward(small_kept.at[0])
    far_part(0)
    normed_loads.insert(0, load(normeds.at[0], held.at[0]))
    attention(1, between_second)

    for copy in normed_loads:
        copy.wait()
    split = first_sent.shape[2]

    def triple_part(index, columns):
        lanes = pl.ds(pl.multiple_of(index * shard, shard), shard)
        part = dot(held[0, :, lanes], d_triples[0, :, columns], TN)
        return part + dot(held[1, :, lanes], d_triples[1, :, columns], TN)

    groups = (slice(0, split), slice(split, None))
    triples_out = []
    for columns, sent, came, line in (
        (groups[0], first_sent, first_came, first_line),
        (groups[1], second_sent, second_came, second_line),
    ):
        for k in range(4):
            sent[k] = triple_part(flip(me, 2 * k + 1), columns).astype(BF16)
        triples_out.append(Reduce(moves, sent, came, line))
    expand_forward(1)
    expands[0].third()
    far_part(1)
    small_moves = [small_chips(0)]
    chips = []
    for i in range(4):
        chip_sent[i] = shrinks[i].finish().astype(BF16)
        chips.append(moves.go(chip_sent.at[i], chip_came.at[i], "ctx", 2))
    for columns, target in zip(groups, (first_mine, second_mine)):
        for k in range(4):
            target[k] = triple_part(flip(me, 2 * k) if k else me, columns).astype(BF16)
    small_moves[0] = small_cores(0, small_moves[0])
    output_reduce.forward(output_mine)
    expands[1].third()
    triples_out[0].forward(first_mine)

    token_load = load(tokens, held.at[0, : 2 * rows, :])
    out_load = load(own_out, stage)
    out_move.wait_recv()
    came_load = load(came_out, came_hidden)

    token_load.wait()
    for move in norm_moves[1::2] + far_moves:
        move.wait_recv()
    gain_total = bias_total = 0.0
    for step in range(micro):
        span = slice(step * rows, (step + 1) * rows)
        grad = wide_add(own_parts[step], near_came[step, 0], far_came[step])
        unit, inverse = norm_parts(held[0, span, :].astype(F32))
        gain_total = gain_total + jnp.sum(grad * unit, axis=0, keepdims=True)
        bias_total = bias_total + jnp.sum(grad, axis=0, keepdims=True)
        token_grad[step] = (d_attended[span, :] + norm_back(grad, unit, inverse, gain_one)).astype(BF16)
    small_row(1, 0, gain_total)
    small_row(1, 1, bias_total)
    smalls.append(small_begin(1))
    small_end(0, small_moves[0], early_out)
    output_reduce.third()
    triples_out[1].forward(second_mine)
    smalls[1].forward(small_kept.at[1])
    out_load.wait()
    sum_load = load(attended, d_attended)
    came_load.wait()
    for step in range(micro):
        span = slice(step * rows, (step + 1) * rows)
        stage[span, :] = stage[span, :] + came_hidden[span, :].astype(F32) + shift_out
    sum_load.wait()
    moves.sent(branch_move)
    for step in range(micro):
        span = slice(step * rows, (step + 1) * rows)
        d_branch[span, :] = (d_attended[span, :] + stage[span, :]).astype(BF16)
    result_load = load(d_branch, result)

    ends, stays, crossing = [], [], []

    def place(source, target):
        ends.append(moves.go(source, target, "ctx", 1))
        stays.append(load(source, target))

    def spread(source, view):
        crossing.append((moves.go(source, view(rank), "ctx", 2), view(flip(rank, 2))))
        place(source, view(rank))

    for i in range(4):
        chips[i].wait_recv()
        chip_final[i] = wide_add(chip_sent[i], chip_came[i]).astype(BF16)
        place(chip_final.at[i], shrink_out.at[at((4 * core + i) * deep, deep, 64), :])
    for e in range(2):
        expand_final[e] = expands[e].finish().astype(BF16)
        spread(expand_final.at[e], lambda r, e=e: expand_out.at[r, :, e * wide : (e + 1) * wide])
    triples_out[0].third()
    triples_out[1].third()
    smalls[1].third()
    output_chip[0] = output_reduce.finish().astype(BF16)
    output_move = moves.go(output_chip.at[0], output_chip.at[1], "ctx", 2)
    first_final[...] = triples_out[0].finish().astype(BF16)
    spread(first_final, lambda r: triple_out.at[r, :, groups[0]])
    second_final[...] = triples_out[1].finish().astype(BF16)
    spread(second_final, lambda r: triple_out.at[r, :, split : first_sent.shape[2] + second_sent.shape[2]])
    late_move = small_chips(1)
    output_move.wait_recv()
    output_chip[2] = wide_add(output_chip[0], output_chip[1]).astype(BF16)
    place(output_chip.at[2], output_out.at[:, mine])
    for move, block in crossing:
        move.wait_recv()
        ends.append(moves.go(block, block, "ctx", 1))
    late_move = small_cores(1, late_move)
    small_end(1, late_move, late_out)
    for move in ends:
        move.wait_recv()
    for copy in stays + [result_load]:
        copy.wait()
    moves.close()


def backward_together(vectors, tangent, output_weight, triple_weight, triples, biases, lses, mixed_own, shift_in_grad, *late_arrays):
    micro, rows, width = tangent.shape
    total, half, quarter, shard = micro * rows, width // 2, width // 4, width // 8
    columns = triple_weight.shape[1]
    shrink_sent, expand_sent = late_arrays[-4], late_arrays[-2]
    deep, wide = shrink_sent.shape[1], expand_sent.shape[2]
    length = 4 * rows
    outs = (
        (ANY, (total, width), BF16),
        (VM, tangent.shape, BF16),
        (ANY, (2 * deep, width), BF16),
        (ANY, (4, shard, wide // 2), BF16),
        (ANY, (shard, width), BF16),
        (ANY, (4, shard, columns), BF16),
        (VM, (8, 128), F32),
        (VM, (8, 128), F32),
        (ANY, (total, width), BF16),
    )
    scratch = (
        ((total, width), BF16),
        ((total, width), F32),
        ((total, width), F32),
        ((2, length, width), BF16),
        ((total, width), BF16),
        ((total, half), BF16),
        ((micro, 4, rows, quarter), BF16),
        ((micro, 4, rows, quarter), BF16),
        ((micro, length, columns), BF16),
        ((length, 128), F32),
        ((length, 128), F32),
        ((micro, 3, rows, width), BF16),
        ((micro, rows, width), BF16),
        ((micro, 2, rows, width), BF16),
        ((micro, rows, width), BF16),
        ((micro, rows, width), BF16),
        ((3, 4, deep // 4, width), BF16),
        ((3, 4, deep // 4, width), BF16),
        ((3, 3, deep // 4, width), BF16),
        ((4, deep // 4, width), BF16),
        ((4, deep // 4, width), BF16),
        ((3, deep // 4, width), BF16),
        ((2, 4, shard, wide // 2), BF16),
        ((2, 2, 4, shard, wide // 4), BF16),
        ((2, 4, shard, wide // 4), BF16),
        ((2, 3, shard, wide // 4), BF16),
        ((4, shard, half), BF16),
        ((4, shard, half), BF16),
        ((4, shard, half), BF16),
        ((3, shard, half), BF16),
        ((4, shard, 2 * quarter), BF16),
        ((4, shard, 2 * quarter), BF16),
        ((4, shard, 2 * quarter), BF16),
        ((3, shard, 2 * quarter), BF16),
        ((4, shard, quarter), BF16),
        ((4, shard, quarter), BF16),
        ((4, shard, quarter), BF16),
        ((3, shard, quarter), BF16),
        ((4, deep // 4, width), BF16),
        ((4, deep // 4, width), BF16),
        ((4, deep // 4, width), BF16),
        ((3, shard, half), BF16),
        ((2, shard, wide // 4), BF16),
        ((shard, 2 * quarter), BF16),
        ((shard, quarter), BF16),
        ((2, 8, 8, 128), F32),
        ((2, 4, 8, 128), F32),
        ((2, 4, 8, 128), F32),
        ((2, 4, 8, 128), F32),
        ((2, 3, 8, 128), F32),
        ((2, 8, 128), F32),
        ((2, 8, 128), F32),
        ((2, 8, 128), F32),
        ((2, 8, 128), F32),
    )
    return pl.pallas_call(
        backward_kernel,
        name="backward_together",
        out_shape=tuple(shape(dims, kind) for _, dims, kind in outs),
        in_specs=[VM] * 9 + [ANY] * 13,
        out_specs=tuple(spec for spec, _, _ in outs),
        scratch_shapes=[pltpu.VMEM(dims, kind) for dims, kind in scratch]
        + [
            pltpu.SemaphoreType.DMA((BACKWARD_MOVES,)),
            pltpu.SemaphoreType.DMA((BACKWARD_MOVES,)),
            pltpu.SemaphoreType.DMA((32,)),
        ],
        compiler_params=pltpu.CompilerParams(
            collective_id=1, has_side_effects=True, vmem_limit_bytes=63 * MIB
        ),
        cost_estimate=cost(24 * total * width * width, 64 * MIB),
    )(vectors, tangent, output_weight, triple_weight, triples, biases, lses, mixed_own, shift_in_grad, *late_arrays)


def widen_kernel(shrink, expand, output, triple, token_grad, result, early, late, *outs):
    shrink_out, expand_out, output_out, triple_out, token_out, result_out = outs[:6]
    shift_in_out, small_outs = outs[6], outs[7:]
    for line in range(3):
        small_outs[line][...] = early[line : line + 1, :]
    for line in range(2):
        small_outs[3 + line][...] = late[line : line + 1, :]
    for line in range(shift_in_out.shape[1] // 128):
        shift_in_out[:, line * 128 : (line + 1) * 128] = early[3 + line : 4 + line, :]
    token_out[...] = token_grad[...]
    result_out[...] = result[...]
    shrink_out[...] = shrink[...].astype(F32)
    output_out[...] = output[...].astype(F32)
    tile = expand.shape[2] // 4
    quarter = triple.shape[2] // 3
    for chip in range(2):
        for core in range(2):
            rank = 2 * chip + core
            for q in range(4):
                start = ((4 * chip + q) * 2 + core) * tile
                part = expand[rank, :, q * tile : (q + 1) * tile]
                expand_out[:, start : start + tile] = part.astype(F32)
            for k in range(3):
                start = (4 * k + rank) * quarter
                part = triple[rank, :, k * quarter : (k + 1) * quarter]
                triple_out[:, start : start + quarter] = part.astype(F32)


def widen(shrink, expand, output, triple, token_grad, result, early, late):
    shard = output.shape[0]
    return pl.pallas_call(
        widen_kernel,
        name="widen",
        out_shape=(
            shape(shrink.shape, F32),
            shape((shard, 4 * expand.shape[2]), F32),
            shape(output.shape, F32),
            shape((shard, 4 * triple.shape[2]), F32),
            shape(token_grad.shape, BF16),
            shape(result.shape, BF16),
            shape((1, shrink.shape[0]), F32),
        )
        + tuple(shape((1, 128), F32) for _ in range(5)),
        in_specs=[VM] * 8,
        out_specs=(VM,) * 12,
        compiler_params=params(),
        cost_estimate=cost(0, 16 * MIB),
    )(shrink, expand, output, triple, token_grad, result, early, late)


def block_biases(chosen, globals_here, rank, local_blocks):
    heads, count, _ = chosen.shape
    place = jnp.arange(count, dtype=jnp.int32)
    true_block = ((place // local_blocks) ^ rank) * local_blocks + place % local_blocks
    near = jnp.abs(true_block[:, None] - true_block[None, :]) <= 1
    is_global = jnp.any(true_block[:, None] == globals_here[None, :], axis=1)
    picked = jnp.any(chosen[:, None, :, :] == true_block[None, :, None, None], axis=3)
    allowed = near[None] | picked | is_global[None, :, None] | is_global[None, None, :]
    bias = jnp.where(allowed, 0.0, -1e30).astype(F32)
    return jnp.repeat(bias, BLOCK, axis=2)


def on_device(
    tokens,
    cotangent,
    random_blocks,
    global_blocks,
    attend_gain,
    attend_bias,
    triple_weight,
    output_weight,
    hidden_gain,
    hidden_bias,
    expand_weight,
    expand_bias,
    shrink_weight,
    shrink_bias,
):
    tokens, cotangent = tokens[:, 0], cotangent[:, 0]
    micro, rows, width = tokens.shape
    total = micro * rows
    ways = lax.axis_size("fsdp")
    fsdp = lax.axis_index("fsdp")
    rank = lax.axis_index("ctx")
    core = rank % 2
    place = place_id()
    heads_all = random_blocks.shape[2]
    own_heads = heads_all // 4
    local_blocks = rows // BLOCK
    shard = width // ways
    wide = expand_weight.shape[1]
    deep = shrink_weight.shape[0]
    ids = jnp.stack([place, rank, core, jnp.int32(0)])
    ids_sent = jnp.stack([place, rank, core, jnp.int32(1)])

    half_units = wide // (2 * ways)
    vectors = [attend_gain, attend_bias, hidden_gain, hidden_bias, shrink_bias]
    tangent_own = cotangent.reshape(total, width)
    picks = random_blocks[:, 0]
    if ways == 8:
        small = jnp.concatenate(
            [v.reshape(1, shard) for v in vectors]
            + [expand_bias.reshape(-1, shard), jnp.zeros((7, shard), BF16)]
        ).astype(F32)
        sets = picks.reshape(micro, 4, own_heads, local_blocks, -1).transpose(1, 0, 2, 4, 3)
        sets = jnp.pad(jnp.repeat(sets, BLOCK, axis=4), ((0, 0),) * 3 + ((0, 5), (0, 0)))
        (
            vectors_here,
            shift_in,
            triple_full,
            output_full,
            expand_full,
            shrink_full,
            tangent_other,
            triples,
            normeds,
            biases,
            lses,
            mixed_own,
            mixed_all,
            mixed_other,
            attended,
            hidden,
            hidden_other,
        ) = forward_together(
            global_blocks[:, 0],
            tokens,
            small,
            sets,
            triple_weight,
            output_weight,
            expand_weight,
            shrink_weight,
            tangent_own,
        )
    else:

        def whole(part):
            return lax.all_gather(part, "fsdp", axis=0, tiled=True)

        triple_part = jnp.concatenate(
            [
                lax.dynamic_slice_in_dim(triple_weight, k * width + rank * (width // 4), width // 4, 1)
                for k in range(3)
            ],
            axis=1,
        )
        expand_part = jnp.concatenate(
            [
                lax.dynamic_slice_in_dim(expand_weight, (2 * k + core) * half_units, half_units, 1)
                for k in range(ways)
            ],
            axis=1,
        )
        shrink_part = lax.dynamic_slice_in_dim(shrink_weight, core * (deep // 2), deep // 2, 0)
        gain_one, bias_one, gain_two, bias_two, shift_out = (
            whole(v).astype(F32).reshape(1, width) for v in vectors
        )
        halves = whole(expand_bias).astype(F32).reshape(ways, 2, half_units)
        shift_in = jnp.where(core == 0, halves[:, 0], halves[:, 1]).reshape(1, wide // 2)
        triple_full, expand_full, shrink_full = whole(triple_part), whole(expand_part), whole(shrink_part)
        output_full = whole(output_weight)
        tangent_other = swap(tangent_own, "ctx", 1)
        far_picks = swap(picks, "ctx", 2)
        all_picks = jnp.stack([picks, swap(picks, "ctx", 1), far_picks, swap(far_picks, "ctx", 1)])
        chosen = lax.dynamic_slice_in_dim(all_picks, rank * own_heads, own_heads, 2)
        chosen = chosen.transpose(1, 2, 0, 3, 4).reshape(micro, own_heads, 4 * local_blocks, -1)
        triples, normeds, biases, lses, mixed_own, joined = [], [], [], [], [], []
        for step in range(micro):
            biases.append(block_biases(chosen[step], global_blocks[step, 0], rank, local_blocks))
            near, far = swap(tokens[step], "ctx", 1), swap(tokens[step], "ctx", 2)
            places = (tokens[step], near, far, swap(far, "ctx", 1))
            triple, normed = project(places, gain_one, bias_one, triple_full)
            mixed, lse = attend(triple, biases[step])
            here = [mixed[0]] + [swap(mixed[p], "ctx", p) for p in range(1, 4)]
            for low_bit, high in ((core == 1, False), (rank >= 2, True)):
                pairs = ((0, 2), (1, 3)) if high else ((0, 1), (2, 3))
                for one, two in pairs:
                    first = jnp.where(low_bit, here[two], here[one])
                    here[two] = jnp.where(low_bit, here[one], here[two])
                    here[one] = first
            joined.append(jnp.concatenate(here, axis=1))
            for kept, value in zip(
                (triples, normeds, lses, mixed_own), (triple, normed, lse, mixed)
            ):
                kept.append(value)
        mixed_all = jnp.concatenate(joined, axis=0)
        mixed_other = swap(mixed_all, "ctx", 1)
        attended, hidden = output_project(tokens, mixed_all, gain_two, bias_two, output_full)
        hidden_other = swap(hidden, "ctx", 1)

    (
        own_out,
        other_out,
        own_hidden,
        other_hidden,
        shift_in_grad,
        shrink_sent,
        shrink_kept,
        expand_sent,
        expand_kept,
    ) = feed(ids, (hidden, hidden_other), (tangent_own, tangent_other), shift_in, expand_full, shrink_full)
    if ways == 8:
        (
            result,
            token_grad,
            shrink_grad,
            expand_grad,
            output_grad_all,
            triple_grad_all,
            early,
            late,
            _,
        ) = backward_together(
            vectors_here,
            cotangent,
            output_full,
            triple_full,
            triples,
            biases,
            lses,
            mixed_own,
            shift_in_grad,
            own_hidden,
            other_hidden,
            own_out,
            other_out,
            attended,
            tokens.reshape(total, width),
            mixed_all,
            mixed_other,
            normeds,
            shrink_sent,
            shrink_kept,
            expand_sent,
            expand_kept,
        )
        shrink_grad, expand_grad, output_grad_all, triple_grad_all, token_grad, result, *smalls = widen(
            shrink_grad,
            expand_grad,
            output_grad_all,
            triple_grad_all,
            token_grad,
            result.reshape(micro, rows, width),
            early,
            late,
        )
        shift_in_grad, gain_two_grad, bias_two_grad, shift_out_grad, gain_one_grad, bias_one_grad = (
            value.reshape(-1) for value in smalls
        )
    else:
        came_hidden = swap(other_hidden, "ctx", 1)
        came_out = swap(other_out, "ctx", 1)
        shrink_mine = scatter_rows(shrink_kept, shrink_sent)
        expand_mine = scatter_rows(expand_kept, expand_sent)
        result, d_attended, d_branch, *grads, gain_two_grad, bias_two_grad, shift_out_grad = branch_back(
            ids,
            attended,
            own_hidden,
            came_hidden,
            cotangent,
            own_out,
            came_out,
            gain_two,
            shift_out,
            output_full,
        )
        half_sent = lax.dynamic_slice_in_dim(d_branch, (1 - core) * (width // 2), width // 2, 1)
        branch_other = swap(half_sent, "ctx", 1)
        output_sent = output_grad(ids_sent, mixed_all, mixed_other, d_branch, branch_other)
        output_kept = output_grad(ids, mixed_all, mixed_other, d_branch, branch_other)
        output_mine = scatter_rows(output_kept, output_sent)

        d_triples, norm_parts_here = [], []
        for step in range(micro):
            here = grads[4 * step : 4 * step + 4]
            here = [here[0]] + [swap(here[p], "ctx", p) for p in range(1, 4)]
            d_triple, parts = attend_back(
                triples[step], biases[step], lses[step], here, mixed_own[step], triple_full
            )
            d_triples.append(d_triple)
            near = swap(parts[1], "ctx", 1)
            far = wide_add(parts[2], swap(parts[3], "ctx", 1)).astype(BF16)
            norm_parts_here += [parts[0], near, swap(far, "ctx", 2)]
        normed_pair = (normeds[0], normeds[1])
        triple_sent = triple_grad(ids_sent, normed_pair, d_triples)
        triple_kept = triple_grad(ids, normed_pair, d_triples)
        triple_mine = scatter_rows(triple_kept, triple_sent)
        token_grad, gain_one_grad, bias_one_grad = first_back(
            tokens, d_attended, gain_one, norm_parts_here
        )

        halves = shift_in_grad.reshape(ways, 1, wide // (2 * ways))
        blank = jnp.zeros_like(halves)
        spread = jnp.where(
            core == 0,
            jnp.concatenate([halves, blank], axis=1),
            jnp.concatenate([blank, halves], axis=1),
        )
        early = sum_everywhere(
            jnp.concatenate(
                [
                    gain_two_grad.reshape(ways, shard),
                    bias_two_grad.reshape(ways, shard),
                    shift_out_grad.reshape(ways, shard),
                    spread.reshape(ways, wide // ways),
                ],
                axis=1,
            )
        )
        late = sum_everywhere(
            jnp.concatenate([gain_one_grad.reshape(ways, shard), bias_one_grad.reshape(ways, shard)], axis=1)
        )

        def over_chips(part):
            low = part.astype(BF16)
            return wide_add(low, swap(low, "ctx", 2))

        def both(own, axis):
            other = swap(own, "ctx", 1)
            first = jnp.where(core == 0, own, other)
            second = jnp.where(core == 0, other, own)
            return jnp.stack([first, second], axis=axis)

        shrink_grad = both(over_chips(shrink_mine), 0).reshape(deep, width)
        expand_half = over_chips(expand_mine).reshape(shard, ways, wide // (2 * ways))
        expand_grad = both(expand_half, 2).reshape(shard, wide)
        output_grad_all = both(over_chips(output_mine), 1).reshape(shard, width)
        low = triple_mine.astype(BF16).reshape(shard, 3, width // 4)
        far = swap(low, "ctx", 2)
        pair = jnp.stack([jnp.where(rank < 2, low, far), jnp.where(rank < 2, far, low)], axis=2)
        triple_grad_all = both(pair, 3).reshape(shard, 3 * width).astype(F32)
        early = lax.dynamic_index_in_dim(early, fsdp, 0, keepdims=False)
        late = lax.dynamic_index_in_dim(late, fsdp, 0, keepdims=False)
        gain_one_grad, bias_one_grad = late[:shard], late[shard:]
        gain_two_grad, bias_two_grad = early[:shard], early[shard : 2 * shard]
        shift_out_grad, shift_in_grad = early[2 * shard : 3 * shard], early[3 * shard :]

    return (
        result[:, None],
        token_grad[:, None],
        gain_one_grad,
        bias_one_grad,
        triple_grad_all,
        output_grad_all,
        gain_two_grad,
        bias_two_grad,
        expand_grad,
        shift_in_grad,
        shrink_grad,
        shift_out_grad,
    )


def solution(mesh):
    token_spec = P(None, "fsdp", "ctx", None)
    flat, rows = P("fsdp"), P("fsdp", None)
    return jax.shard_map(
        on_device,
        mesh=mesh,
        in_specs=(
            token_spec,
            token_spec,
            P(None, "fsdp", None, "ctx", None),
            P(None, "fsdp", None),
            flat,
            flat,
            rows,
            rows,
            flat,
            flat,
            rows,
            flat,
            rows,
            flat,
        ),
        out_specs=(
            token_spec,
            token_spec,
            flat,
            flat,
            rows,
            rows,
            flat,
            flat,
            rows,
            flat,
            rows,
            flat,
        ),
        check_vma=False,
    )
```

```python
import functools

import jax
import jax.numpy as jnp
from jax import lax
from jax.experimental import pallas as pl
from jax.experimental.pallas import tpu as pltpu
from jax.sharding import PartitionSpec as P

HEAD_DIM = 64
BLOCK = 64
EPSILON = 1e-05
F32 = jnp.float32
BF16 = jnp.bfloat16
MIB = 1 << 20

VM = pl.BlockSpec(memory_space=pltpu.VMEM)
SM = pl.BlockSpec(memory_space=pltpu.SMEM)
ANY = pl.BlockSpec(memory_space=pl.ANY)

NN = (((1,), (0,)), ((), ()))
NT = (((1,), (1,)), ((), ()))
TN = (((0,), (0,)), ((), ()))


def dot(left, right, dims=NN):
    return lax.dot_general(left, right, dims, preferred_element_type=F32)


def shape(dims, kind):
    return jax.ShapeDtypeStruct(dims, kind)


def params(limit=56):
    return pltpu.CompilerParams(vmem_limit_bytes=limit * MIB)


def cost(flops, moved, special=0):
    return pl.CostEstimate(flops=flops, bytes_accessed=moved, transcendentals=special)


def swap(value, axis, step):
    size = lax.axis_size(axis)
    return lax.ppermute(value, axis, [(i, i ^ step) for i in range(size)])


def place_id():
    return lax.axis_index("fsdp") if lax.axis_size("fsdp") == 8 else jnp.int32(1)


def wide_add(*terms):
    total = terms[0].astype(F32)
    for term in terms[1:]:
        total = total + term.astype(F32)
    return total


def scatter_rows(kept, sent):
    whole = jnp.stack([sent, kept], axis=1)
    whole = whole.reshape((8 * kept.shape[1],) + kept.shape[2:])
    return lax.psum_scatter(whole.astype(F32), "fsdp", scatter_dimension=0, tiled=True)


def sum_everywhere(vector):
    return lax.psum(vector, ("ctx", "fsdp"))


def norm_parts(values):
    average = jnp.mean(values, axis=-1, keepdims=True)
    centered = values - average
    variance = jnp.mean(centered * centered, axis=-1, keepdims=True)
    inverse = lax.rsqrt(variance + EPSILON)
    return centered * inverse, inverse


def norm_back(grad, unit, inverse, gain):
    scaled = grad * gain
    first = jnp.mean(scaled, axis=-1, keepdims=True)
    second = jnp.mean(scaled * unit, axis=-1, keepdims=True)
    return inverse * (scaled - first - unit * second)


def normalize(source, gain, bias):
    unit, _ = norm_parts(source.astype(F32))
    return (unit * gain + bias).astype(BF16)


def project_kernel(t0, t1, t2, t3, gain, bias, weight, triple, normed):
    rows = t0.shape[0]
    for place, part in enumerate((t0, t1, t2, t3)):
        span = slice(place * rows, (place + 1) * rows)
        normed[span, :] = normalize(part[...], gain[...], bias[...])
        triple[span, :] = dot(normed[span, :], weight[...]).astype(BF16)


def project(parts, gain, bias, weight):
    rows, width = parts[0].shape
    columns = weight.shape[1]
    return pl.pallas_call(
        project_kernel,
        name="project",
        out_shape=(shape((4 * rows, columns), BF16), shape((4 * rows, width), BF16)),
        in_specs=[VM] * 7,
        out_specs=(VM, VM),
        compiler_params=params(),
        cost_estimate=cost(8 * rows * width * columns, 12 * rows * width + 2 * width * columns),
    )(*parts, gain, bias, weight)


def head_mask(rows):
    return lax.broadcasted_iota(jnp.int32, (rows, 2 * HEAD_DIM), 1) // HEAD_DIM


def attend_body(triple, block_bias, mixed, lse, between=None):
    length = triple.shape[0]
    width = triple.shape[1] // 3
    rows = length // 4
    blocks = length // BLOCK
    for pair in range(width // 128):
        keys = triple[:, width + pair * 128 : width + pair * 128 + 128]
        values = triple[:, 2 * width + pair * 128 : 2 * width + pair * 128 + 128]
        values_t = values.astype(F32).T.astype(BF16)

        def step(place, carry):
            start = pl.multiple_of(place * rows, rows)
            queries = triple[pl.ds(start, rows), pair * 128 : pair * 128 + 128]
            queries = queries * jnp.asarray(0.125, BF16)
            side = head_mask(rows)
            halves = []
            for which in range(2):
                head = 2 * pair + which
                one = jnp.where(side == which, queries, jnp.zeros_like(queries))
                scores = dot(keys, one, NT)
                shift = block_bias[head, :, pl.ds(start, rows)]
                scores = scores.reshape(blocks, BLOCK, rows) + shift[:, None, :]
                peak = jnp.max(jnp.max(scores, axis=0), axis=0, keepdims=True)
                powered = jnp.exp(scores - peak[None])
                total = jnp.sum(jnp.sum(powered, axis=0), axis=0, keepdims=True)
                lse[head : head + 1, pl.ds(start, rows)] = peak + jnp.log(total)
                low = powered.astype(BF16).reshape(length, rows)
                part = dot(values_t[which * HEAD_DIM : (which + 1) * HEAD_DIM, :], low)
                halves.append(part / total)
            joined = jnp.concatenate(halves, axis=0)
            mixed[place, :, pair * 128 : pair * 128 + 128] = joined.T.astype(BF16)
            return carry

        lax.fori_loop(0, 4, step, 0)
        if between is not None and pair == 0:
            between()


def attend(triple, block_bias):
    length, columns = triple.shape
    width = columns // 3
    heads = width // HEAD_DIM
    rows = length // 4
    return pl.pallas_call(
        attend_body,
        name="attend",
        out_shape=(shape((4, rows, width), BF16), shape((8, length), F32)),
        in_specs=[VM, VM],
        out_specs=(VM, VM),
        compiler_params=params(),
        cost_estimate=cost(
            32 * heads * length * length * HEAD_DIM, 8 * length * width, heads * length * length
        ),
    )(triple, block_bias)


def attend_back_body(
    triple, block_bias, lse, grads, mixed, d_triple, key_total, value_total, between=None
):
    length = triple.shape[0]
    width = triple.shape[1] // 3
    rows = length // 4
    blocks = length // BLOCK
    for pair in range(width // 128):
        lanes = slice(pair * 128, pair * 128 + 128)
        keys = triple[:, width + pair * 128 : width + pair * 128 + 128]
        values = triple[:, 2 * width + pair * 128 : 2 * width + pair * 128 + 128]
        keys_t = keys.astype(F32).T.astype(BF16)
        key_total[...] = jnp.zeros_like(key_total)
        value_total[...] = jnp.zeros_like(value_total)

        def step(place, carry):
            start = pl.multiple_of(place * rows, rows)
            queries = triple[pl.ds(start, rows), lanes] * jnp.asarray(0.125, BF16)
            grad = grads[place, :, lanes]
            product = (grad.astype(F32) * mixed[place, :, lanes].astype(F32)).T
            side = head_mask(rows)
            halves = []
            for which in range(2):
                head = 2 * pair + which
                one = jnp.where(side == which, queries, jnp.zeros_like(queries))
                one_grad = jnp.where(side == which, grad, jnp.zeros_like(grad))
                delta = jnp.sum(
                    product[which * HEAD_DIM : (which + 1) * HEAD_DIM, :], axis=0, keepdims=True
                )
                scores = dot(keys, one, NT)
                shift = block_bias[head, :, pl.ds(start, rows)] - lse[head : head + 1, pl.ds(start, rows)]
                exact = jnp.exp(scores.reshape(blocks, BLOCK, rows) + shift[:, None, :])
                exact = exact.reshape(length, rows)
                value_total[...] += dot(exact.astype(BF16), one_grad)
                d_probs = dot(values, one_grad, NT)
                d_scores = (exact * (d_probs - delta)).astype(BF16)
                key_total[...] += dot(d_scores, one)
                halves.append(dot(keys_t[which * HEAD_DIM : (which + 1) * HEAD_DIM, :], d_scores))
            joined = jnp.concatenate(halves, axis=0) * 0.125
            d_triple[pl.ds(start, rows), lanes] = joined.T.astype(BF16)
            return carry

        lax.fori_loop(0, 4, step, 0)
        d_triple[:, width + pair * 128 : width + pair * 128 + 128] = key_total[...].astype(BF16)
        d_triple[:, 2 * width + pair * 128 : 2 * width + pair * 128 + 128] = value_total[
            ...
        ].astype(BF16)
        if between is not None and pair == 0:
            between()


def attend_back_kernel(triple, block_bias, lse, g0, g1, g2, g3, mixed, weight, d_triple, norm_grad, grads, key_total, value_total):
    rows = g0.shape[0]
    for place, part in enumerate((g0, g1, g2, g3)):
        grads[place] = part[...]
    attend_back_body(triple, block_bias, lse, grads, mixed, d_triple, key_total, value_total)
    for place in range(4):
        part = dot(d_triple[place * rows : (place + 1) * rows, :], weight[...], NT)
        norm_grad[place] = part.astype(BF16)


def attend_back(triple, block_bias, lse, grads, mixed, weight):
    length, columns = triple.shape
    width = columns // 3
    heads = width // HEAD_DIM
    rows = length // 4
    return pl.pallas_call(
        attend_back_kernel,
        name="attend_back",
        out_shape=(shape((length, columns), BF16), shape((4, rows, weight.shape[0]), BF16)),
        in_specs=[VM] * 9,
        out_specs=(VM,) * 2,
        scratch_shapes=[
            pltpu.VMEM((4, rows, width), BF16),
            pltpu.VMEM((length, 128), F32),
            pltpu.VMEM((length, 128), F32),
        ],
        compiler_params=params(),
        cost_estimate=cost(
            80 * heads * length * length * HEAD_DIM, 16 * length * width, heads * length * length
        ),
    )(triple, block_bias, lse, *grads, mixed, weight)


def output_kernel(tokens, joined, gain, bias, weight, attended, normed):
    rows = tokens.shape[1]
    for micro in range(2):
        span = slice(micro * rows, (micro + 1) * rows)
        value = tokens[micro].astype(F32) + dot(joined[span, :], weight[...])
        attended[span, :] = value
        normed[span, :] = normalize(value, gain[...], bias[...])


def output_project(tokens, joined, gain, bias, weight):
    micro, rows, width = tokens.shape
    total = micro * rows
    return pl.pallas_call(
        output_kernel,
        name="output_project",
        out_shape=(shape((total, width), F32), shape((total, width), BF16)),
        in_specs=[VM] * 5,
        out_specs=(VM, VM),
        compiler_params=params(),
        cost_estimate=cost(2 * total * width * width, 12 * total * width + 2 * width * width),
    )(tokens, joined, gain, bias, weight)


CURVE = 0.7978845608028654
CUBIC = 0.044715


def feed_kernel(ids, h0, h1, c0, c1, shift, *rest):
    expand_held, shrink_held = rest[:2]
    own_out, other_out, own_hidden, other_hidden, bias_grad = rest[2:7]
    shrink_sent, shrink_kept, expand_sent, expand_kept = rest[7:11]
    hidden, tangent, hidden_t, out_total, hidden_total = rest[11:]
    base = ids[0]
    rows, width = h0.shape
    tile = shrink_held.shape[0] // 8
    deep = width // 8
    hidden[:rows, :] = h0[...]
    hidden[rows:, :] = h1[...]
    tangent[:rows, :] = c0[...]
    tangent[rows:, :] = c1[...]
    for j in range(8):
        source = pl.multiple_of((base ^ j) * deep, deep)
        hidden_t[j * deep : (j + 1) * deep, :] = (
            hidden[:, pl.ds(source, deep)].astype(F32).T.astype(BF16)
        )
    for step, j in enumerate((1, 3, 5, 7, 0, 2, 4, 6)):
        column = pl.multiple_of((base ^ j) * tile, tile)
        up = expand_held[:, pl.ds(column, tile)]
        down = shrink_held[pl.ds(column, tile), :]
        before = dot(hidden[...], up) + shift[:, pl.ds(column, tile)]
        d_active = dot(tangent[...], down, NT)
        square = before * before
        bend = jnp.tanh(CURVE * before * (1.0 + CUBIC * square))
        plus = 0.5 * (1.0 + bend)
        active = (before * plus).astype(BF16)
        slope = plus + (0.5 * CURVE) * before * (1.0 - bend * bend) * (1.0 + 3 * CUBIC * square)
        d_before = (d_active * slope).astype(BF16)
        bias_grad[:, pl.ds(column, tile)] = jnp.sum(d_before.astype(F32), axis=0, keepdims=True)
        out_part = dot(active, down)
        hidden_part = dot(d_before, up, NT)
        if step == 0:
            out_total[...] = out_part
            hidden_total[...] = hidden_part
        else:
            out_total[...] += out_part
            hidden_total[...] += hidden_part
        shrink_part = dot(active, tangent[...], TN).astype(BF16)
        (shrink_sent if j % 2 else shrink_kept)[j // 2] = shrink_part
        expand_part = dot(hidden_t[...], d_before).astype(BF16)
        for place in range(8):
            target = expand_sent if place % 2 else expand_kept
            target[place // 2, :, pl.ds(column, tile)] = expand_part[
                place * deep : (place + 1) * deep, :
            ]
    own_out[...] = out_total[:rows, :]
    other_out[...] = out_total[rows:, :].astype(BF16)
    own_hidden[...] = hidden_total[:rows, :]
    other_hidden[...] = hidden_total[rows:, :].astype(BF16)


def feed(ids, hidden, tangent, shift, expand, shrink):
    rows, width = hidden[0].shape
    wide = expand.shape[1]
    deep, tile = width // 8, wide // 8
    return pl.pallas_call(
        feed_kernel,
        name="feed",
        out_shape=(
            shape((rows, width), F32),
            shape((rows, width), BF16),
            shape((rows, width), F32),
            shape((rows, width), BF16),
            shape((1, wide), F32),
            shape((4, tile, width), BF16),
            shape((4, tile, width), BF16),
            shape((4, deep, wide), BF16),
            shape((4, deep, wide), BF16),
        ),
        in_specs=[SM] + [VM] * 7,
        out_specs=(VM,) * 9,
        scratch_shapes=[
            pltpu.VMEM((2 * rows, width), BF16),
            pltpu.VMEM((2 * rows, width), BF16),
            pltpu.VMEM((width, 2 * rows), BF16),
            pltpu.VMEM((2 * rows, width), F32),
            pltpu.VMEM((2 * rows, width), F32),
        ],
        compiler_params=params(60),
        cost_estimate=cost(24 * rows * width * wide, 8 * width * wide + 20 * rows * width, 2 * rows * wide),
    )(ids, *hidden, *tangent, shift, expand, shrink)


def branch_kernel(
    ids, attended, own_hidden, came_hidden, tangent, own_out, came_out, gain, shift, weight, *rest
):
    result, d_attended, d_branch = rest[:3]
    grads, (gain_grad, bias_grad, shift_grad) = rest[3:11], rest[11:14]
    rows = tangent.shape[1]
    width = gain.shape[1] // 4
    gain_total = bias_total = shift_total = 0.0
    for micro in range(2):
        span = slice(micro * rows, (micro + 1) * rows)
        value = attended[span, :]
        cot = tangent[micro].astype(F32)
        branch = own_out[span, :] + came_out[span, :].astype(F32) + shift[...]
        result[micro] = (value + branch).astype(BF16)
        unit, inverse = norm_parts(value)
        grad = own_hidden[span, :] + came_hidden[span, :].astype(F32)
        gain_total = gain_total + jnp.sum(grad * unit, axis=0, keepdims=True)
        bias_total = bias_total + jnp.sum(grad, axis=0, keepdims=True)
        shift_total = shift_total + jnp.sum(cot, axis=0, keepdims=True)
        total = cot + norm_back(grad, unit, inverse, gain[...])
        d_attended[span, :] = total
        d_branch[span, :] = total.astype(BF16)
    gain_grad[...] = gain_total
    bias_grad[...] = bias_total
    shift_grad[...] = shift_total
    for micro in range(2):
        for place in range(4):
            start = pl.multiple_of((ids[1] ^ place) * width, width)
            part = dot(d_branch[micro * rows : (micro + 1) * rows, :], weight[pl.ds(start, width), :], NT)
            grads[4 * micro + place][...] = part.astype(BF16)


def branch_back(ids, attended, own_hidden, came_hidden, tangent, own_out, came_out, gain, shift, weight):
    micro, rows, width = tangent.shape
    total = micro * rows
    row = shape((1, width), F32)
    return pl.pallas_call(
        branch_kernel,
        name="branch_back",
        out_shape=(
            shape(tangent.shape, BF16),
            shape((total, width), F32),
            shape((total, width), BF16),
        )
        + tuple(shape((rows, width // 4), BF16) for _ in range(8))
        + (row, row, row),
        in_specs=[SM] + [VM] * 9,
        out_specs=(VM,) * 14,
        compiler_params=params(),
        cost_estimate=cost(2 * total * width * width, 32 * total * width),
    )(ids, attended, own_hidden, came_hidden, tangent, own_out, came_out, gain, shift, weight)


def output_grad_kernel(ids, own_mixed, other_mixed, own_branch, other_branch, out):
    rows = out.shape[1]
    width = own_branch.shape[1]
    half = width // 2
    column = pl.multiple_of(ids[2] * half, half)
    right = own_branch[:, pl.ds(column, half)]
    for k in range(4):
        start = pl.multiple_of((ids[0] ^ (2 * k + ids[3])) * rows, rows)
        part = dot(own_mixed[:, pl.ds(start, rows)], right, TN)
        part += dot(other_mixed[:, pl.ds(start, rows)], other_branch[...], TN)
        out[k] = part.astype(BF16)


def output_grad(ids, own_mixed, other_mixed, own_branch, other_branch):
    total, width = own_mixed.shape
    return pl.pallas_call(
        output_grad_kernel,
        name="output_grad",
        out_shape=shape((4, width // 8, width // 2), BF16),
        in_specs=[SM] + [VM] * 4,
        out_specs=VM,
        compiler_params=params(),
        cost_estimate=cost(total * width * width, 8 * total * width),
    )(ids, own_mixed, other_mixed, own_branch, other_branch)


def triple_grad_kernel(ids, n0, n1, d0, d1, out):
    rows = out.shape[1]
    for k in range(4):
        column = pl.multiple_of((ids[0] ^ (2 * k + ids[3])) * rows, rows)
        part = dot(n0[:, pl.ds(column, rows)], d0[...], TN)
        part += dot(n1[:, pl.ds(column, rows)], d1[...], TN)
        out[k] = part.astype(BF16)


def triple_grad(ids, normed, grads):
    length, width = normed[0].shape
    columns = grads[0].shape[1]
    return pl.pallas_call(
        triple_grad_kernel,
        name="triple_grad",
        out_shape=shape((4, width // 8, columns), BF16),
        in_specs=[SM] + [VM] * 4,
        out_specs=VM,
        compiler_params=params(),
        cost_estimate=cost(2 * length * width * columns, 4 * length * (width + columns)),
    )(ids, *normed, *grads)


def first_back_kernel(tokens, d_attended, gain, *rest):
    parts, (grad_out, gain_grad, bias_grad) = rest[:6], rest[6:]
    rows = tokens.shape[1]
    gain_total = bias_total = 0.0
    for micro in range(2):
        one, two, three = parts[3 * micro : 3 * micro + 3]
        grad = one[...].astype(F32) + two[...].astype(F32) + three[...].astype(F32)
        unit, inverse = norm_parts(tokens[micro].astype(F32))
        gain_total = gain_total + jnp.sum(grad * unit, axis=0, keepdims=True)
        bias_total = bias_total + jnp.sum(grad, axis=0, keepdims=True)
        total = d_attended[micro * rows : (micro + 1) * rows, :]
        grad_out[micro] = (total + norm_back(grad, unit, inverse, gain[...])).astype(BF16)
    gain_grad[...] = gain_total
    bias_grad[...] = bias_total


def first_back(tokens, d_attended, gain, parts):
    micro, rows, width = tokens.shape
    row = shape((1, width), F32)
    return pl.pallas_call(
        first_back_kernel,
        name="first_back",
        out_shape=(shape(tokens.shape, BF16), row, row),
        in_specs=[VM] * 9,
        out_specs=(VM,) * 3,
        compiler_params=params(),
        cost_estimate=cost(20 * micro * rows * width, 16 * micro * rows * width),
    )(tokens, d_attended, gain, *parts)


def flip(index, bits):
    out, bit = index, 1
    while bit <= bits:
        if bits & bit:
            out = out + bit * (1 - 2 * lax.rem(lax.div(index, jnp.int32(bit)), jnp.int32(2)))
        bit *= 2
    return out


class Moves:
    def __init__(self, send, recv):
        self.send, self.recv, self.started, self.freed = send, recv, [], []
        self.place = {"ctx": lax.axis_index("ctx"), "fsdp": lax.axis_index("fsdp")}

    def greet(self):
        barrier = pltpu.get_barrier_semaphore()
        partners = [("ctx", 1), ("ctx", 2), ("ctx", 3), ("fsdp", 1), ("fsdp", 2), ("fsdp", 4), ("fsdp", 6)]
        for axis, bits in partners:
            pl.semaphore_signal(
                barrier,
                inc=1,
                device_id={axis: flip(self.place[axis], bits)},
                device_id_type=pl.DeviceIdType.MESH,
            )
        pl.semaphore_wait(barrier, len(partners))

    def go(self, source, target, axis, bits):
        slot = len(self.started)
        move = pltpu.make_async_remote_copy(
            src_ref=source,
            dst_ref=target,
            send_sem=self.send.at[slot],
            recv_sem=self.recv.at[slot],
            device_id={axis: flip(self.place[axis], bits)},
            device_id_type=pl.DeviceIdType.MESH,
        )
        move.start()
        self.started.append(move)
        return move

    def sent(self, move):
        move.wait_send()
        self.freed.append(move)

    def close(self):
        for move in self.started:
            if not any(move is other for other in self.freed):
                move.wait_send()


class Gather:
    def __init__(self, moves, part, view, own, shared=False):
        self.moves, self.view, self.own, self.shared = moves, view, own, shared
        self.part = part

    def start(self):
        moves, part, view, me = self.moves, self.part, self.view, self.moves.place["fsdp"]
        self.distant = moves.go(part, view(me), "fsdp", 4)
        self.adjacent = moves.go(part, view(me), "fsdp", 2)
        self.across = [moves.go(part, view(me), "fsdp", 1)]
        self.sources = [1]
        self.over = [moves.go(part, view(me), "ctx", 2)] if self.shared else []
        return self

    def over_x(self, bits):
        if self.shared:
            block = self.view(flip(self.moves.place["fsdp"], bits))
            self.over.append(self.moves.go(block, block, "ctx", 2))

    def over_y(self, bits):
        block = self.view(flip(self.moves.place["fsdp"], bits))
        self.across.append(self.moves.go(block, block, "fsdp", 1))
        self.sources.append(bits + 1)
        self.over_x(bits)

    def forward(self):
        self.distant.wait_recv()
        block = self.view(flip(self.moves.place["fsdp"], 4))
        self.last = self.moves.go(block, block, "fsdp", 2)
        self.over_y(4)
        self.adjacent.wait_recv()
        self.over_y(2)

    def third(self):
        self.last.wait_recv()
        self.over_y(6)

    def second(self):
        for bits, move in zip(self.sources, self.across):
            move.wait_recv()
            self.over_x(bits)

    def finish(self):
        if not self.shared:
            self.second()
        for move in self.over:
            move.wait_recv()
        for copy in self.own:
            copy.wait()


FORWARD_MOVES = 106


def row_view(ref, rows, columns=slice(None)):
    return lambda index: ref.at[pl.ds(pl.multiple_of(index * rows, rows), rows), columns]


def forward_kernel(
    global_ids,
    tokens,
    small,
    picks,
    triple_weight,
    output_weight,
    expand_weight,
    shrink_weight,
    tangent,
    vectors_out,
    shift_in_out,
    triple_out,
    output_out,
    expand_all,
    shrink_all,
    tangent_other,
    triple,
    normed,
    block_bias,
    lse,
    mixed,
    joined_out,
    mixed_other,
    attended,
    hidden,
    hidden_other,
    parts,
    small_held,
    picks_held,
    triple_held,
    output_held,
    joined,
    hidden_held,
    send,
    recv,
    local,
):
    moves = Moves(send, recv)
    rank, me = moves.place["ctx"], moves.place["fsdp"]
    core = lax.rem(rank, jnp.int32(2))
    micro, rows, width = tokens.shape
    half = width // 2
    quarter = width // 4
    shard = triple_weight.shape[0]
    wide = expand_all.shape[1] // 2
    deep = shrink_weight.shape[0] // 8
    chip = lax.div(rank, jnp.int32(2))
    locals_used = []

    def copy_here(source, target):
        copy = pltpu.make_async_copy(source, target, local.at[len(locals_used)])
        copy.start()
        locals_used.append(copy)
        return copy

    def at(start, size, unit=128):
        return pl.ds(pl.multiple_of(start, unit), size)

    mine = at(me * shard, shard)
    triple_own = [
        copy_here(
            triple_weight.at[:, at(k * width + rank * quarter, quarter)],
            triple_held.at[mine, k * quarter : (k + 1) * quarter],
        )
        for k in range(3)
    ]
    tile = wide // 4
    expand_views = [row_view(expand_all, shard, at(chip * wide + cut * (wide // 2), wide // 2)) for cut in range(2)]
    expand_own = [
        copy_here(
            expand_weight.at[:, at(((4 * chip + q) * 2 + core) * tile, tile)],
            expand_all.at[mine, at(chip * wide + q * tile, tile)],
        )
        for q in range(4)
    ]
    output_columns = at(core * half + chip * quarter, quarter)
    output_view = row_view(output_held, shard, output_columns)
    shrink_views = [
        lambda i, cut=cut: shrink_all.at[at(i * 4 * deep + cut * deep, deep, 64)] for cut in range(4)
    ]
    shrink_parts = [shrink_weight.at[at((core * 4 + cut) * deep, deep, 64)] for cut in range(4)]
    small_held[me] = small[...].astype(F32)
    output_own = copy_here(output_weight.at[:, output_columns], output_view(me))
    shrink_own = [copy_here(shrink_parts[cut], shrink_views[cut](me)) for cut in range(4)]
    moves.greet()

    small_gather = Gather(moves, small_held.at[me], lambda index: small_held.at[index], []).start()
    far = [moves.go(tokens.at[0], parts.at[0, 2], "ctx", 2)]
    near = [moves.go(tokens.at[0], parts.at[0, 1], "ctx", 1)]
    for copy in triple_own:
        copy.wait()
    triple_view = row_view(triple_held, shard)
    triple_gather = Gather(moves, triple_view(me), triple_view, []).start()
    picked = [moves.go(picks.at[flip(rank, p)], picks_held.at[p], "ctx", p) for p in range(1, 4)]
    near.append(moves.go(tokens.at[1], parts.at[1, 1], "ctx", 1))
    far.append(moves.go(tokens.at[1], parts.at[1, 2], "ctx", 2))
    output_gather = Gather(moves, output_weight.at[:, output_columns], output_view, [output_own], True)
    for copy in expand_own:
        copy.wait()
    expands = [Gather(moves, view(me), view, [], True) for view in expand_views]
    shrinks = [Gather(moves, shrink_parts[cut], shrink_views[cut], [shrink_own[cut]]) for cut in range(4)]
    small_gather.forward()
    triple_gather.forward()
    output_gather.start()
    expands[0].start()
    small_gather.third()
    triple_gather.third()
    expands[1].start()
    tangent_move = moves.go(tangent, tangent_other, "ctx", 1)

    for move in picked:
        move.wait_recv()
    count = block_bias.shape[2]
    each = count // 4
    ranks = [flip(rank, p) if p else rank for p in range(4)]
    key_row = lax.broadcasted_iota(jnp.int32, (count, rows), 0)
    key_place = key_row // each
    key_rank = ranks[0]
    for p in range(1, 4):
        key_rank = jnp.where(key_place == p, ranks[p], key_rank)
    key_block = key_rank * each + key_row % each
    lane = lax.broadcasted_iota(jnp.int32, (count, rows), 1) // BLOCK
    for step in range(micro):
        first, second = global_ids[step, 0], global_ids[step, 1]
        key_global = (key_block == first) | (key_block == second)
        for p in range(4):
            source = picks.at[rank] if p == 0 else picks_held.at[p]
            query_block = ranks[p] * each + lane
            base = key_global | (jnp.abs(query_block - key_block) <= 1)
            base = base | (query_block == first) | (query_block == second)
            for head in range(block_bias.shape[1]):
                hit = base
                for pick in range(3):
                    hit = hit | (source[step, head, pick : pick + 1, :] == key_block)
                block_bias[step, head, :, p * rows : (p + 1) * rows] = jnp.where(hit, 0.0, -1e30)

    small_gather.finish()
    def vector(line):
        return jnp.concatenate([small_held[b, line : line + 1, :] for b in range(8)], axis=1)

    gain_one, bias_one, gain_two, bias_two, shift_out = (vector(line) for line in range(5))
    vectors_out[...] = jnp.zeros_like(vectors_out)
    for line, value in enumerate((gain_two, gain_one, shift_out)):
        vectors_out[line : line + 1, :] = value
    lines = shift_in_out.shape[1] // 8 // 128
    for b in range(8):
        for i in range(lines):
            lanes = slice((b * lines + i) * 128, (b * lines + i + 1) * 128)
            shift_in_out[:, lanes] = small_held[b, pl.ds(5 + core * lines + i, 1), :]

    for step in range(micro):
        far[step].wait_recv()
        near.append(moves.go(parts.at[step, 2], parts.at[step, 3], "ctx", 1))
    mixed_moves = []
    for step in range(micro):
        near[step].wait_recv()
        near[2 + step].wait_recv()
        for p in range(4):
            source = tokens[step] if p == 0 else parts[step, p]
            normed[step, p * rows : (p + 1) * rows, :] = normalize(source, gain_one, bias_one)
        if step == 0:
            output_gather.forward()
            expands[0].forward()
            shrinks[0].start()
            triple_gather.finish()
        for p in range(4):
            span = slice(p * rows, (p + 1) * rows)
            triple[step, span, :] = dot(normed[step, span, :], triple_held[...]).astype(BF16)

        def between_first():
            expands[0].third()
            shrinks[0].forward()
            shrinks[2].start()
            output_gather.second()

        def between_second():
            expands[1].second()
            shrinks[3].forward()
            shrinks[2].third()

        if step == 0:
            output_gather.third()
            expands[1].forward()
            shrinks[1].start()
        else:
            output_gather.finish()
            piece = output_held.at[:, at(core * half, half)]
            output_move = moves.go(piece, piece, "ctx", 1)
            shrinks[2].forward()
            shrinks[1].third()
        attend_body(
            triple.at[step],
            block_bias.at[step],
            mixed.at[step],
            lse.at[step],
            between_second if step else between_first,
        )
        own = pl.ds(pl.multiple_of(rank * quarter, quarter), quarter)
        span = slice(step * rows, (step + 1) * rows)
        joined[span, own] = mixed[step, 0]
        for p in range(1, 4):
            mixed_moves.append(moves.go(mixed.at[step, p], joined.at[span, own], "ctx", p))
        if step == 0:
            expands[1].third()
            shrinks[1].forward()
            shrinks[3].start()
            shrinks[0].third()
            expands[0].second()
        else:
            shrinks[3].third()
    output_move.wait_recv()
    for move in mixed_moves:
        move.wait_recv()
    keep = [copy_here(triple_held, triple_out), copy_here(output_held, output_out)]
    output_kernel(tokens, joined, gain_two, bias_two, output_held, attended, hidden_held)
    last = [
        moves.go(hidden_held, hidden_other, "ctx", 1),
        moves.go(joined, mixed_other, "ctx", 1),
    ]
    hidden[...] = hidden_held[...]
    joined_out[...] = joined[...]
    for gather in shrinks + expands:
        gather.finish()
    for move in [tangent_move] + last:
        move.wait_recv()
    for copy in keep:
        copy.wait()
    moves.close()


def forward_together(global_ids, tokens, small, picks, triple_weight, output_weight, expand_weight, shrink_weight, tangent):
    micro, rows, width = tokens.shape
    total = micro * rows
    columns = triple_weight.shape[1] // 4
    wide = expand_weight.shape[1] // 2
    length = 4 * rows
    heads = picks.shape[2]
    outs = (
        (VM, (8, width), F32),
        (VM, (1, wide), F32),
        (ANY, (width, columns), BF16),
        (ANY, (width, width), BF16),
        (ANY, (width, wide), BF16),
        (ANY, (wide, width), BF16),
        (ANY, (total, width), BF16),
        (VM, (micro, length, columns), BF16),
        (VM, (micro, length, width), BF16),
        (VM, (micro, heads, length // BLOCK, length), F32),
        (VM, (micro, 8, length), F32),
        (VM, (micro, 4, rows, width // 4), BF16),
        (VM, (total, width), BF16),
        (ANY, (total, width), BF16),
        (VM, (total, width), F32),
        (VM, (total, width), BF16),
        (ANY, (total, width), BF16),
    )
    return pl.pallas_call(
        forward_kernel,
        name="forward_together",
        out_shape=tuple(shape(dims, kind) for _, dims, kind in outs),
        in_specs=[SM] + [VM] * 3 + [ANY] * 5,
        out_specs=tuple(spec for spec, _, _ in outs),
        scratch_shapes=[
            pltpu.VMEM((micro, 4, rows, width), BF16),
            pltpu.VMEM((8,) + small.shape, F32),
            pltpu.VMEM(picks.shape, jnp.int32),
            pltpu.VMEM((width, columns), BF16),
            pltpu.VMEM((width, width), BF16),
            pltpu.VMEM((total, width), BF16),
            pltpu.VMEM((total, width), BF16),
            pltpu.SemaphoreType.DMA((FORWARD_MOVES,)),
            pltpu.SemaphoreType.DMA((FORWARD_MOVES,)),
            pltpu.SemaphoreType.DMA((15,)),
        ],
        compiler_params=pltpu.CompilerParams(
            collective_id=0, has_side_effects=True, vmem_limit_bytes=56 * MIB
        ),
        cost_estimate=cost(16 * total * width * width, 64 * MIB),
    )(global_ids, tokens, small, picks, triple_weight, output_weight, expand_weight, shrink_weight, tangent)


class Reduce:
    def __init__(self, moves, sent, came, line):
        self.moves, self.came, self.line = moves, came, line
        self.across = moves.go(sent, came, "fsdp", 1)

    def forward(self, *kept):
        self.across.wait_recv()
        for k in (1, 3, 0, 2):
            self.came[k] = wide_add(self.came[k], *(part[k] for part in kept)).astype(self.came.dtype)
        self.along = [self.moves.go(self.came.at[2 * i + 1], self.line.at[i], "fsdp", 2) for i in range(2)]

    def third(self):
        for move in self.along:
            move.wait_recv()
        self.came[2] = wide_add(self.came[2], self.line[1]).astype(self.came.dtype)
        self.last = self.moves.go(self.came.at[2], self.line.at[2], "fsdp", 4)

    def finish(self):
        self.last.wait_recv()
        return wide_add(self.came[0], self.line[0], self.line[2])


class ReduceAlong:
    def __init__(self, moves, kept, sent, ends, came, line):
        self.moves, self.ends, self.came, self.line = moves, ends, came, line
        sources = (kept.at[1], kept.at[3], sent.at[1], sent.at[3])
        self.along = [moves.go(source, came.at[i], "fsdp", 2) for i, source in enumerate(sources)]

    def forward(self):
        for i in (1, 3, 0, 2):
            self.along[i].wait_recv()
            self.ends[i] = wide_add(self.ends[i], self.came[i]).astype(BF16)
        self.next = [self.moves.go(self.ends.at[2 * i + 1], self.line.at[i], "fsdp", 4) for i in range(2)]

    def third(self):
        for move in self.next:
            move.wait_recv()
        self.ends[2] = wide_add(self.ends[2], self.line[1]).astype(BF16)
        self.last = self.moves.go(self.ends.at[2], self.line.at[2], "fsdp", 1)

    def finish(self):
        self.last.wait_recv()
        return wide_add(self.ends[0], self.line[0], self.line[2])


BACKWARD_MOVES = 96


def backward_kernel(
    vectors,
    tangent,
    output_weight,
    triple_weight,
    triples,
    biases,
    lses,
    mixed_own,
    shift_in_grad,
    own_hidden,
    other_hidden,
    own_out,
    other_out,
    attended,
    tokens,
    mixed_all,
    mixed_other,
    normeds,
    shrink_sent,
    shrink_kept,
    expand_sent,
    expand_kept,
    result,
    token_grad,
    shrink_out,
    expand_out,
    output_out,
    triple_out,
    early_out,
    late_out,
    came_out,
    came_hidden,
    d_attended,
    stage,
    held,
    d_branch,
    branch_other,
    d_mixed,
    grads,
    d_triples,
    key_total,
    value_total,
    near_parts,
    own_parts,
    near_came,
    far_sent,
    far_came,
    shrink_held,
    shrink_came,
    shrink_line,
    along_ends,
    along_came,
    along_line,
    expand_own,
    over_came,
    expand_came,
    expand_line,
    output_sent,
    output_mine,
    output_came,
    output_line,
    first_sent,
    first_mine,
    first_came,
    first_line,
    second_sent,
    second_mine,
    second_came,
    second_line,
    chip_sent,
    chip_came,
    chip_final,
    output_chip,
    expand_final,
    first_final,
    second_final,
    small_all,
    small_sent,
    small_kept,
    small_came,
    small_line,
    small_chip,
    small_chip_came,
    small_core,
    small_core_came,
    send,
    recv,
    local,
):
    moves = Moves(send, recv)
    rank, me = moves.place["ctx"], moves.place["fsdp"]
    core = lax.rem(rank, jnp.int32(2))
    micro, rows, width = tangent.shape
    half, quarter, shard = width // 2, width // 4, width // 8
    moves.greet()
    used = []

    def load(source, target):
        copy = pltpu.make_async_copy(source, target, local.at[len(used)])
        copy.start()
        used.append(copy)
        return copy

    def at(start, size, unit=128):
        return pl.ds(pl.multiple_of(start, unit), size)

    chip = lax.div(rank, jnp.int32(2))
    deep = shrink_sent.shape[1] // 4
    wide = expand_sent.shape[2] // 4
    hidden_move = moves.go(other_hidden, came_hidden, "ctx", 1)

    def rows_of(ref, i):
        return ref.at[:, i * deep : (i + 1) * deep, :]

    def there(ref, e):
        return ref.at[:, :, at((1 - chip) * 2 * wide + e * wide, wide)]

    shrinks = [Reduce(moves, rows_of(shrink_sent, i), shrink_came.at[i], shrink_line.at[i]) for i in range(3)]
    last_kept, last_sent = rows_of(shrink_kept, 3), rows_of(shrink_sent, 3)
    shrinks.append(ReduceAlong(moves, last_kept, last_sent, along_ends, along_came, along_line))
    over_moves = [moves.go(there(expand_sent, 0), over_came.at[0, 0], "ctx", 2)]
    loads = [load(own_hidden, d_attended), load(attended, stage)]
    out_move = moves.go(other_out, came_out, "ctx", 1)
    here = at(chip * 2 * wide, 2 * wide)
    expand_loads = [
        load(expand_sent.at[:, :, here], expand_own.at[0]),
        load(expand_kept.at[:, :, here], expand_own.at[1]),
    ]
    shrink_loads = [load(rows_of(shrink_kept, i), shrink_held.at[i]) for i in range(3)]
    along_loads = [
        load(source.at[2 * k], along_ends.at[2 * i + k])
        for i, source in enumerate((last_kept, last_sent))
        for k in range(2)
    ]
    mixed_loads = [load(mixed_all, held.at[0, : 2 * rows, :]), load(mixed_other, held.at[0, 2 * rows :, :])]

    gain_two, gain_one, shift_out = vectors[0:1, :], vectors[1:2, :], vectors[2:3, :]
    for copy in loads:
        copy.wait()
    hidden_move.wait_recv()
    gain_total = bias_total = shift_total = 0.0
    for step in range(micro):
        span = slice(step * rows, (step + 1) * rows)
        cot = tangent[step].astype(F32)
        unit, inverse = norm_parts(stage[span, :])
        grad = d_attended[span, :] + came_hidden[span, :].astype(F32)
        gain_total = gain_total + jnp.sum(grad * unit, axis=0, keepdims=True)
        bias_total = bias_total + jnp.sum(grad, axis=0, keepdims=True)
        shift_total = shift_total + jnp.sum(cot, axis=0, keepdims=True)
        total = cot + norm_back(grad, unit, inverse, gain_two)
        d_attended[span, :] = total
        d_branch[span, :] = total.astype(BF16)
    theirs = d_branch.at[:, pl.ds(pl.multiple_of((1 - core) * half, half), half)]
    branch_move = moves.go(theirs, branch_other, "ctx", 1)
    grad_moves = []
    for step in range(micro):
        for p in (2, 3, 1, 0):
            start = pl.multiple_of((flip(rank, p) if p else rank) * quarter, quarter)
            part = dot(d_branch[step * rows : (step + 1) * rows, :], output_weight[pl.ds(start, quarter), :], NT)
            if p:
                d_mixed[step, p] = part.astype(BF16)
                grad_moves.append(moves.go(d_mixed.at[step, p], grads.at[step, p], "ctx", p))
            else:
                grads[step, 0] = part.astype(BF16)

    over_moves.append(moves.go(there(expand_sent, 1), over_came.at[0, 1], "ctx", 2))
    over_moves += [moves.go(there(expand_kept, e), over_came.at[1, e], "ctx", 2) for e in range(2)]

    def small_row(which, line, vector):
        for b in range(8):
            small_all[which, b, line : line + 1, :] = vector[:, b * shard : (b + 1) * shard]

    def small_begin(which):
        for k in range(4):
            small_sent[which, k] = small_all[which, flip(me, 2 * k + 1)]
            small_kept[which, k] = small_all[which, flip(me, 2 * k) if k else me]
        return Reduce(moves, small_sent.at[which], small_came.at[which], small_line.at[which])

    def small_chips(which):
        small_chip[which] = smalls[which].finish()
        return moves.go(small_chip.at[which], small_chip_came.at[which], "ctx", 2)

    def small_cores(which, move):
        move.wait_recv()
        small_core[which] = small_chip[which] + small_chip_came[which]
        return moves.go(small_core.at[which], small_core_came.at[which], "ctx", 1)

    def small_end(which, move, out):
        move.wait_recv()
        out[...] = small_core[which] + small_core_came[which]

    small_all[...] = jnp.zeros_like(small_all)
    for line, vector in enumerate((gain_total, bias_total, shift_total)):
        small_row(0, line, vector)
    unit_lines = shift_in_grad.shape[1] // 8 // 128
    for b in range(8):
        for line in range(unit_lines):
            lanes = slice((b * unit_lines + line) * 128, (b * unit_lines + line + 1) * 128)
            small_all[0, b, pl.ds(3 + core * unit_lines + line, 1), :] = shift_in_grad[:, lanes]
    smalls = [small_begin(0)]
    for copy in shrink_loads + along_loads + expand_loads:
        copy.wait()

    def expand_columns(which, e):
        return expand_own.at[which, :, :, e * wide : (e + 1) * wide]

    def expand_begin(e):
        over_moves[e].wait_recv()
        part = expand_columns(0, e)
        for k in range(4):
            part[k] = wide_add(part[k], over_came[0, e, k]).astype(BF16)
        return Reduce(moves, part, expand_came.at[e], expand_line.at[e])

    def expand_forward(e):
        over_moves[2 + e].wait_recv()
        expands[e].forward(expand_columns(1, e), over_came.at[1, e])

    shrinks[0].forward(shrink_held.at[0])
    expands = [expand_begin(0)]

    for copy in mixed_loads:
        copy.wait()
    branch_move.wait_recv()
    mine = pl.ds(pl.multiple_of(core * half, half), half)

    def output_part(index):
        lanes = pl.ds(pl.multiple_of(index * shard, shard), shard)
        part = dot(held[0, : 2 * rows, lanes], d_branch[:, mine], TN)
        return part + dot(held[0, 2 * rows :, lanes], branch_other[...], TN)

    for k in range(4):
        output_sent[k] = output_part(flip(me, 2 * k + 1)).astype(BF16)
    output_reduce = Reduce(moves, output_sent, output_came, output_line)
    for k in range(4):
        output_mine[k] = output_part(flip(me, 2 * k) if k else me).astype(BF16)
    normed_loads = [load(normeds.at[step], held.at[step]) for step in range(1, micro)]

    norm_moves, far_moves = [], []

    def attention(step, between):
        for move in grad_moves[3 * step : 3 * step + 3]:
            move.wait_recv()
        attend_back_body(
            triples.at[step],
            biases.at[step],
            lses.at[step],
            grads.at[step],
            mixed_own.at[step],
            d_triples.at[step],
            key_total,
            value_total,
            between,
        )
        for p in (3, 1, 2, 0):
            span = slice(p * rows, (p + 1) * rows)
            part = dot(d_triples[step, span, :], triple_weight[...], NT).astype(BF16)
            if p:
                near_parts[step, p - 1] = part
            else:
                own_parts[step] = part
            if p % 2:
                norm_moves.append(moves.go(near_parts.at[step, p - 1], near_came.at[step, p // 2], "ctx", 1))

    def far_part(step):
        norm_moves[2 * step].wait_recv()
        far_sent[step] = wide_add(near_parts[step, 1], near_came[step, 1]).astype(BF16)
        far_moves.append(moves.go(far_sent.at[step], far_came.at[step], "ctx", 2))

    def between_first():
        expands.append(expand_begin(1))
        shrinks[1].third()
        shrinks[3].third()

    def between_second():
        shrinks[2].third()
        smalls[0].third()
        expand_forward(0)

    shrinks[3].forward()
    shrinks[1].forward(shrink_held.at[1])
    shrinks[0].third()
    attention(0, between_first)
    shrinks[2].forward(shrink_held.at[2])
    smalls[0].forward(small_kept.at[0])
    far_part(0)
    normed_loads.insert(0, load(normeds.at[0], held.at[0]))
    attention(1, between_second)

    for copy in normed_loads:
        copy.wait()
    split = first_sent.shape[2]

    def triple_part(index, columns):
        lanes = pl.ds(pl.multiple_of(index * shard, shard), shard)
        part = dot(held[0, :, lanes], d_triples[0, :, columns], TN)
        return part + dot(held[1, :, lanes], d_triples[1, :, columns], TN)

    groups = (slice(0, split), slice(split, None))
    triples_out = []
    for columns, sent, came, line in (
        (groups[0], first_sent, first_came, first_line),
        (groups[1], second_sent, second_came, second_line),
    ):
        for k in range(4):
            sent[k] = triple_part(flip(me, 2 * k + 1), columns).astype(BF16)
        triples_out.append(Reduce(moves, sent, came, line))
    expand_forward(1)
    expands[0].third()
    far_part(1)
    small_moves = [small_chips(0)]
    chips = []
    for i in range(4):
        chip_sent[i] = shrinks[i].finish().astype(BF16)
        chips.append(moves.go(chip_sent.at[i], chip_came.at[i], "ctx", 2))
    for columns, target in zip(groups, (first_mine, second_mine)):
        for k in range(4):
            target[k] = triple_part(flip(me, 2 * k) if k else me, columns).astype(BF16)
    small_moves[0] = small_cores(0, small_moves[0])
    output_reduce.forward(output_mine)
    expands[1].third()
    triples_out[0].forward(first_mine)

    token_load = load(tokens, held.at[0, : 2 * rows, :])
    out_load = load(own_out, stage)
    out_move.wait_recv()
    came_load = load(came_out, came_hidden)

    token_load.wait()
    for move in norm_moves[1::2] + far_moves:
        move.wait_recv()
    gain_total = bias_total = 0.0
    for step in range(micro):
        span = slice(step * rows, (step + 1) * rows)
        grad = wide_add(own_parts[step], near_came[step, 0], far_came[step])
        unit, inverse = norm_parts(held[0, span, :].astype(F32))
        gain_total = gain_total + jnp.sum(grad * unit, axis=0, keepdims=True)
        bias_total = bias_total + jnp.sum(grad, axis=0, keepdims=True)
        token_grad[step] = (d_attended[span, :] + norm_back(grad, unit, inverse, gain_one)).astype(BF16)
    small_row(1, 0, gain_total)
    small_row(1, 1, bias_total)
    smalls.append(small_begin(1))
    small_end(0, small_moves[0], early_out)
    output_reduce.third()
    triples_out[1].forward(second_mine)
    smalls[1].forward(small_kept.at[1])
    out_load.wait()
    sum_load = load(attended, d_attended)
    came_load.wait()
    for step in range(micro):
        span = slice(step * rows, (step + 1) * rows)
        stage[span, :] = stage[span, :] + came_hidden[span, :].astype(F32) + shift_out
    sum_load.wait()
    moves.sent(branch_move)
    for step in range(micro):
        span = slice(step * rows, (step + 1) * rows)
        d_branch[span, :] = (d_attended[span, :] + stage[span, :]).astype(BF16)
    result_load = load(d_branch, result)

    ends, stays, crossing = [], [], []

    def place(source, target):
        ends.append(moves.go(source, target, "ctx", 1))
        stays.append(load(source, target))

    def spread(source, view):
        crossing.append((moves.go(source, view(rank), "ctx", 2), view(flip(rank, 2))))
        place(source, view(rank))

    for i in range(4):
        chips[i].wait_recv()
        chip_final[i] = wide_add(chip_sent[i], chip_came[i]).astype(BF16)
        place(chip_final.at[i], shrink_out.at[at((4 * core + i) * deep, deep, 64), :])
    for e in range(2):
        expand_final[e] = expands[e].finish().astype(BF16)
        spread(expand_final.at[e], lambda r, e=e: expand_out.at[r, :, e * wide : (e + 1) * wide])
    triples_out[0].third()
    triples_out[1].third()
    smalls[1].third()
    output_chip[0] = output_reduce.finish().astype(BF16)
    output_move = moves.go(output_chip.at[0], output_chip.at[1], "ctx", 2)
    first_final[...] = triples_out[0].finish().astype(BF16)
    spread(first_final, lambda r: triple_out.at[r, :, groups[0]])
    second_final[...] = triples_out[1].finish().astype(BF16)
    spread(second_final, lambda r: triple_out.at[r, :, split : first_sent.shape[2] + second_sent.shape[2]])
    late_move = small_chips(1)
    output_move.wait_recv()
    output_chip[2] = wide_add(output_chip[0], output_chip[1]).astype(BF16)
    place(output_chip.at[2], output_out.at[:, mine])
    for move, block in crossing:
        move.wait_recv()
        ends.append(moves.go(block, block, "ctx", 1))
    late_move = small_cores(1, late_move)
    small_end(1, late_move, late_out)
    for move in ends:
        move.wait_recv()
    for copy in stays + [result_load]:
        copy.wait()
    moves.close()


def backward_together(vectors, tangent, output_weight, triple_weight, triples, biases, lses, mixed_own, shift_in_grad, *late_arrays):
    micro, rows, width = tangent.shape
    total, half, quarter, shard = micro * rows, width // 2, width // 4, width // 8
    columns = triple_weight.shape[1]
    shrink_sent, expand_sent = late_arrays[-4], late_arrays[-2]
    deep, wide = shrink_sent.shape[1], expand_sent.shape[2]
    length = 4 * rows
    outs = (
        (ANY, (total, width), BF16),
        (VM, tangent.shape, BF16),
        (ANY, (2 * deep, width), BF16),
        (ANY, (4, shard, wide // 2), BF16),
        (ANY, (shard, width), BF16),
        (ANY, (4, shard, columns), BF16),
        (VM, (8, 128), F32),
        (VM, (8, 128), F32),
        (ANY, (total, width), BF16),
    )
    scratch = (
        ((total, width), BF16),
        ((total, width), F32),
        ((total, width), F32),
        ((2, length, width), BF16),
        ((total, width), BF16),
        ((total, half), BF16),
        ((micro, 4, rows, quarter), BF16),
        ((micro, 4, rows, quarter), BF16),
        ((micro, length, columns), BF16),
        ((length, 128), F32),
        ((length, 128), F32),
        ((micro, 3, rows, width), BF16),
        ((micro, rows, width), BF16),
        ((micro, 2, rows, width), BF16),
        ((micro, rows, width), BF16),
        ((micro, rows, width), BF16),
        ((3, 4, deep // 4, width), BF16),
        ((3, 4, deep // 4, width), BF16),
        ((3, 3, deep // 4, width), BF16),
        ((4, deep // 4, width), BF16),
        ((4, deep // 4, width), BF16),
        ((3, deep // 4, width), BF16),
        ((2, 4, shard, wide // 2), BF16),
        ((2, 2, 4, shard, wide // 4), BF16),
        ((2, 4, shard, wide // 4), BF16),
        ((2, 3, shard, wide // 4), BF16),
        ((4, shard, half), BF16),
        ((4, shard, half), BF16),
        ((4, shard, half), BF16),
        ((3, shard, half), BF16),
        ((4, shard, 2 * quarter), BF16),
        ((4, shard, 2 * quarter), BF16),
        ((4, shard, 2 * quarter), BF16),
        ((3, shard, 2 * quarter), BF16),
        ((4, shard, quarter), BF16),
        ((4, shard, quarter), BF16),
        ((4, shard, quarter), BF16),
        ((3, shard, quarter), BF16),
        ((4, deep // 4, width), BF16),
        ((4, deep // 4, width), BF16),
        ((4, deep // 4, width), BF16),
        ((3, shard, half), BF16),
        ((2, shard, wide // 4), BF16),
        ((shard, 2 * quarter), BF16),
        ((shard, quarter), BF16),
        ((2, 8, 8, 128), F32),
        ((2, 4, 8, 128), F32),
        ((2, 4, 8, 128), F32),
        ((2, 4, 8, 128), F32),
        ((2, 3, 8, 128), F32),
        ((2, 8, 128), F32),
        ((2, 8, 128), F32),
        ((2, 8, 128), F32),
        ((2, 8, 128), F32),
    )
    return pl.pallas_call(
        backward_kernel,
        name="backward_together",
        out_shape=tuple(shape(dims, kind) for _, dims, kind in outs),
        in_specs=[VM] * 9 + [ANY] * 13,
        out_specs=tuple(spec for spec, _, _ in outs),
        scratch_shapes=[pltpu.VMEM(dims, kind) for dims, kind in scratch]
        + [
            pltpu.SemaphoreType.DMA((BACKWARD_MOVES,)),
            pltpu.SemaphoreType.DMA((BACKWARD_MOVES,)),
            pltpu.SemaphoreType.DMA((32,)),
        ],
        compiler_params=pltpu.CompilerParams(
            collective_id=1, has_side_effects=True, vmem_limit_bytes=63 * MIB
        ),
        cost_estimate=cost(24 * total * width * width, 64 * MIB),
    )(vectors, tangent, output_weight, triple_weight, triples, biases, lses, mixed_own, shift_in_grad, *late_arrays)


def widen_kernel(shrink, expand, output, triple, token_grad, result, early, late, *outs):
    shrink_out, expand_out, output_out, triple_out, token_out, result_out = outs[:6]
    shift_in_out, small_outs = outs[6], outs[7:]
    for line in range(3):
        small_outs[line][...] = early[line : line + 1, :]
    for line in range(2):
        small_outs[3 + line][...] = late[line : line + 1, :]
    for line in range(shift_in_out.shape[1] // 128):
        shift_in_out[:, line * 128 : (line + 1) * 128] = early[3 + line : 4 + line, :]
    token_out[...] = token_grad[...]
    result_out[...] = result[...]
    shrink_out[...] = shrink[...].astype(F32)
    output_out[...] = output[...].astype(F32)
    tile = expand.shape[2] // 4
    quarter = triple.shape[2] // 3
    for chip in range(2):
        for core in range(2):
            rank = 2 * chip + core
            for q in range(4):
                start = ((4 * chip + q) * 2 + core) * tile
                part = expand[rank, :, q * tile : (q + 1) * tile]
                expand_out[:, start : start + tile] = part.astype(F32)
            for k in range(3):
                start = (4 * k + rank) * quarter
                part = triple[rank, :, k * quarter : (k + 1) * quarter]
                triple_out[:, start : start + quarter] = part.astype(F32)


def widen(shrink, expand, output, triple, token_grad, result, early, late):
    shard = output.shape[0]
    return pl.pallas_call(
        widen_kernel,
        name="widen",
        out_shape=(
            shape(shrink.shape, F32),
            shape((shard, 4 * expand.shape[2]), F32),
            shape(output.shape, F32),
            shape((shard, 4 * triple.shape[2]), F32),
            shape(token_grad.shape, BF16),
            shape(result.shape, BF16),
            shape((1, shrink.shape[0]), F32),
        )
        + tuple(shape((1, 128), F32) for _ in range(5)),
        in_specs=[VM] * 8,
        out_specs=(VM,) * 12,
        compiler_params=params(),
        cost_estimate=cost(0, 16 * MIB),
    )(shrink, expand, output, triple, token_grad, result, early, late)


def block_biases(chosen, globals_here, rank, local_blocks):
    heads, count, _ = chosen.shape
    place = jnp.arange(count, dtype=jnp.int32)
    true_block = ((place // local_blocks) ^ rank) * local_blocks + place % local_blocks
    near = jnp.abs(true_block[:, None] - true_block[None, :]) <= 1
    is_global = jnp.any(true_block[:, None] == globals_here[None, :], axis=1)
    picked = jnp.any(chosen[:, None, :, :] == true_block[None, :, None, None], axis=3)
    allowed = near[None] | picked | is_global[None, :, None] | is_global[None, None, :]
    bias = jnp.where(allowed, 0.0, -1e30).astype(F32)
    return jnp.repeat(bias, BLOCK, axis=2)


def on_device(
    tokens,
    cotangent,
    random_blocks,
    global_blocks,
    attend_gain,
    attend_bias,
    triple_weight,
    output_weight,
    hidden_gain,
    hidden_bias,
    expand_weight,
    expand_bias,
    shrink_weight,
    shrink_bias,
):
    tokens, cotangent = tokens[:, 0], cotangent[:, 0]
    micro, rows, width = tokens.shape
    total = micro * rows
    ways = lax.axis_size("fsdp")
    fsdp = lax.axis_index("fsdp")
    rank = lax.axis_index("ctx")
    core = rank % 2
    place = place_id()
    heads_all = random_blocks.shape[2]
    own_heads = heads_all // 4
    local_blocks = rows // BLOCK
    shard = width // ways
    wide = expand_weight.shape[1]
    deep = shrink_weight.shape[0]
    ids = jnp.stack([place, rank, core, jnp.int32(0)])
    ids_sent = jnp.stack([place, rank, core, jnp.int32(1)])

    half_units = wide // (2 * ways)
    vectors = [attend_gain, attend_bias, hidden_gain, hidden_bias, shrink_bias]
    tangent_own = cotangent.reshape(total, width)
    picks = random_blocks[:, 0]
    if ways == 8:
        small = jnp.concatenate(vectors + [expand_bias, jnp.zeros((7 * shard,), BF16)]).reshape(16, shard)
        sets = picks.reshape(micro, 4, own_heads, local_blocks, -1).transpose(1, 0, 2, 4, 3)
        sets = jnp.pad(jnp.repeat(sets, BLOCK, axis=4), ((0, 0),) * 3 + ((0, 5), (0, 0)))
        (
            vectors_here,
            shift_in,
            triple_full,
            output_full,
            expand_full,
            shrink_full,
            tangent_other,
            triples,
            normeds,
            biases,
            lses,
            mixed_own,
            mixed_all,
            mixed_other,
            attended,
            hidden,
            hidden_other,
        ) = forward_together(
            global_blocks[:, 0],
            tokens,
            small,
            sets,
            triple_weight,
            output_weight,
            expand_weight,
            shrink_weight,
            tangent_own,
        )
    else:

        def whole(part):
            return lax.all_gather(part, "fsdp", axis=0, tiled=True)

        triple_part = jnp.concatenate(
            [
                lax.dynamic_slice_in_dim(triple_weight, k * width + rank * (width // 4), width // 4, 1)
                for k in range(3)
            ],
            axis=1,
        )
        expand_part = jnp.concatenate(
            [
                lax.dynamic_slice_in_dim(expand_weight, (2 * k + core) * half_units, half_units, 1)
                for k in range(ways)
            ],
            axis=1,
        )
        shrink_part = lax.dynamic_slice_in_dim(shrink_weight, core * (deep // 2), deep // 2, 0)
        gain_one, bias_one, gain_two, bias_two, shift_out = (
            whole(v).astype(F32).reshape(1, width) for v in vectors
        )
        halves = whole(expand_bias).astype(F32).reshape(ways, 2, half_units)
        shift_in = jnp.where(core == 0, halves[:, 0], halves[:, 1]).reshape(1, wide // 2)
        triple_full, expand_full, shrink_full = whole(triple_part), whole(expand_part), whole(shrink_part)
        output_full = whole(output_weight)
        tangent_other = swap(tangent_own, "ctx", 1)
        far_picks = swap(picks, "ctx", 2)
        all_picks = jnp.stack([picks, swap(picks, "ctx", 1), far_picks, swap(far_picks, "ctx", 1)])
        chosen = lax.dynamic_slice_in_dim(all_picks, rank * own_heads, own_heads, 2)
        chosen = chosen.transpose(1, 2, 0, 3, 4).reshape(micro, own_heads, 4 * local_blocks, -1)
        triples, normeds, biases, lses, mixed_own, joined = [], [], [], [], [], []
        for step in range(micro):
            biases.append(block_biases(chosen[step], global_blocks[step, 0], rank, local_blocks))
            near, far = swap(tokens[step], "ctx", 1), swap(tokens[step], "ctx", 2)
            places = (tokens[step], near, far, swap(far, "ctx", 1))
            triple, normed = project(places, gain_one, bias_one, triple_full)
            mixed, lse = attend(triple, biases[step])
            here = [mixed[0]] + [swap(mixed[p], "ctx", p) for p in range(1, 4)]
            for low_bit, high in ((core == 1, False), (rank >= 2, True)):
                pairs = ((0, 2), (1, 3)) if high else ((0, 1), (2, 3))
                for one, two in pairs:
                    first = jnp.where(low_bit, here[two], here[one])
                    here[two] = jnp.where(low_bit, here[one], here[two])
                    here[one] = first
            joined.append(jnp.concatenate(here, axis=1))
            for kept, value in zip(
                (triples, normeds, lses, mixed_own), (triple, normed, lse, mixed)
            ):
                kept.append(value)
        mixed_all = jnp.concatenate(joined, axis=0)
        mixed_other = swap(mixed_all, "ctx", 1)
        attended, hidden = output_project(tokens, mixed_all, gain_two, bias_two, output_full)
        hidden_other = swap(hidden, "ctx", 1)

    (
        own_out,
        other_out,
        own_hidden,
        other_hidden,
        shift_in_grad,
        shrink_sent,
        shrink_kept,
        expand_sent,
        expand_kept,
    ) = feed(ids, (hidden, hidden_other), (tangent_own, tangent_other), shift_in, expand_full, shrink_full)
    if ways == 8:
        (
            result,
            token_grad,
            shrink_grad,
            expand_grad,
            output_grad_all,
            triple_grad_all,
            early,
            late,
            _,
        ) = backward_together(
            vectors_here,
            cotangent,
            output_full,
            triple_full,
            triples,
            biases,
            lses,
            mixed_own,
            shift_in_grad,
            own_hidden,
            other_hidden,
            own_out,
            other_out,
            attended,
            tokens.reshape(total, width),
            mixed_all,
            mixed_other,
            normeds,
            shrink_sent,
            shrink_kept,
            expand_sent,
            expand_kept,
        )
        shrink_grad, expand_grad, output_grad_all, triple_grad_all, token_grad, result, *smalls = widen(
            shrink_grad,
            expand_grad,
            output_grad_all,
            triple_grad_all,
            token_grad,
            result.reshape(micro, rows, width),
            early,
            late,
        )
        shift_in_grad, gain_two_grad, bias_two_grad, shift_out_grad, gain_one_grad, bias_one_grad = (
            value.reshape(-1) for value in smalls
        )
    else:
        came_hidden = swap(other_hidden, "ctx", 1)
        came_out = swap(other_out, "ctx", 1)
        shrink_mine = scatter_rows(shrink_kept, shrink_sent)
        expand_mine = scatter_rows(expand_kept, expand_sent)
        result, d_attended, d_branch, *grads, gain_two_grad, bias_two_grad, shift_out_grad = branch_back(
            ids,
            attended,
            own_hidden,
            came_hidden,
            cotangent,
            own_out,
            came_out,
            gain_two,
            shift_out,
            output_full,
        )
        half_sent = lax.dynamic_slice_in_dim(d_branch, (1 - core) * (width // 2), width // 2, 1)
        branch_other = swap(half_sent, "ctx", 1)
        output_sent = output_grad(ids_sent, mixed_all, mixed_other, d_branch, branch_other)
        output_kept = output_grad(ids, mixed_all, mixed_other, d_branch, branch_other)
        output_mine = scatter_rows(output_kept, output_sent)

        d_triples, norm_parts_here = [], []
        for step in range(micro):
            here = grads[4 * step : 4 * step + 4]
            here = [here[0]] + [swap(here[p], "ctx", p) for p in range(1, 4)]
            d_triple, parts = attend_back(
                triples[step], biases[step], lses[step], here, mixed_own[step], triple_full
            )
            d_triples.append(d_triple)
            near = swap(parts[1], "ctx", 1)
            far = wide_add(parts[2], swap(parts[3], "ctx", 1)).astype(BF16)
            norm_parts_here += [parts[0], near, swap(far, "ctx", 2)]
        normed_pair = (normeds[0], normeds[1])
        triple_sent = triple_grad(ids_sent, normed_pair, d_triples)
        triple_kept = triple_grad(ids, normed_pair, d_triples)
        triple_mine = scatter_rows(triple_kept, triple_sent)
        token_grad, gain_one_grad, bias_one_grad = first_back(
            tokens, d_attended, gain_one, norm_parts_here
        )

        halves = shift_in_grad.reshape(ways, 1, wide // (2 * ways))
        blank = jnp.zeros_like(halves)
        spread = jnp.where(
            core == 0,
            jnp.concatenate([halves, blank], axis=1),
            jnp.concatenate([blank, halves], axis=1),
        )
        early = sum_everywhere(
            jnp.concatenate(
                [
                    gain_two_grad.reshape(ways, shard),
                    bias_two_grad.reshape(ways, shard),
                    shift_out_grad.reshape(ways, shard),
                    spread.reshape(ways, wide // ways),
                ],
                axis=1,
            )
        )
        late = sum_everywhere(
            jnp.concatenate([gain_one_grad.reshape(ways, shard), bias_one_grad.reshape(ways, shard)], axis=1)
        )

        def over_chips(part):
            low = part.astype(BF16)
            return wide_add(low, swap(low, "ctx", 2))

        def both(own, axis):
            other = swap(own, "ctx", 1)
            first = jnp.where(core == 0, own, other)
            second = jnp.where(core == 0, other, own)
            return jnp.stack([first, second], axis=axis)

        shrink_grad = both(over_chips(shrink_mine), 0).reshape(deep, width)
        expand_half = over_chips(expand_mine).reshape(shard, ways, wide // (2 * ways))
        expand_grad = both(expand_half, 2).reshape(shard, wide)
        output_grad_all = both(over_chips(output_mine), 1).reshape(shard, width)
        low = triple_mine.astype(BF16).reshape(shard, 3, width // 4)
        far = swap(low, "ctx", 2)
        pair = jnp.stack([jnp.where(rank < 2, low, far), jnp.where(rank < 2, far, low)], axis=2)
        triple_grad_all = both(pair, 3).reshape(shard, 3 * width).astype(F32)
        early = lax.dynamic_index_in_dim(early, fsdp, 0, keepdims=False)
        late = lax.dynamic_index_in_dim(late, fsdp, 0, keepdims=False)
        gain_one_grad, bias_one_grad = late[:shard], late[shard:]
        gain_two_grad, bias_two_grad = early[:shard], early[shard : 2 * shard]
        shift_out_grad, shift_in_grad = early[2 * shard : 3 * shard], early[3 * shard :]

    return (
        result[:, None],
        token_grad[:, None],
        gain_one_grad,
        bias_one_grad,
        triple_grad_all,
        output_grad_all,
        gain_two_grad,
        bias_two_grad,
        expand_grad,
        shift_in_grad,
        shrink_grad,
        shift_out_grad,
    )


def solution(mesh):
    token_spec = P(None, "fsdp", "ctx", None)
    flat, rows = P("fsdp"), P("fsdp", None)
    return jax.shard_map(
        on_device,
        mesh=mesh,
        in_specs=(
            token_spec,
            token_spec,
            P(None, "fsdp", None, "ctx", None),
            P(None, "fsdp", None),
            flat,
            flat,
            rows,
            rows,
            flat,
            flat,
            rows,
            flat,
            rows,
            flat,
        ),
        out_specs=(
            token_spec,
            token_spec,
            flat,
            flat,
            rows,
            rows,
            flat,
            flat,
            rows,
            flat,
            rows,
            flat,
        ),
        check_vma=False,
    )
```
